128 devices in a mesh: grid: 16 (over z_lo, y, core), sta: 8 (over z_hi, x).
Axes of the slice: x: 4, y: 4, z: 4 (z_hi: 2, z_lo: 2; z = z_hi * 2 + z_lo), core: 2. Of those that a mesh axis runs over, the one named last changes fastest.
Arguments:
- spectra: bfloat16 [64, 2, 6144], P(None, None, 'sta'), may hold values from -6 to 6
- lag_samples: int32 [16, 6144], P('grid', 'sta'), may hold values from 0 to 5999
- slowness: bfloat16 [16, 3, 6144], P('grid', None, 'sta'), may hold values from -3 to 3
- spread_taps: float32 [3, 17], replicated, may hold values from 0.02 to 0.2
Outputs:
- stacked: float32 [16, 32, 8, 128], P('grid')
- deblurred: float32 [16, 32, 8, 128], P('grid')
The draws below stay inside these ranges and needn't reach their ends.
All inputs are finite; a program needn't handle non-finite values.
Results may differ from the reference program's by a relative error of at most 0.0015.
Values may be sent and summed in bfloat16 or wider, within the bound.
A program may use at most 64 MiB of HBM per device.

```python
import math
import jax
import jax.numpy as jnp
from jax import lax

STATIONS = 6144
FREQS = 64
F0 = 600
NT = 6000
TAPS = 17
HALF = 8
ITERS = 4
CX = 32
CY = 8
CZ = 128
TX = 16
TY = 1
TILES = 16


def with_ends(drawn, own_key, low, largest):
    extent = drawn.shape
    index_at = [jax.random.randint(jax.random.fold_in(own_key, axis), (), 0, extent[axis]) for axis in range(len(extent))]
    drawn = drawn.at[tuple(index_at)].set(low)
    longest = extent.index(max(extent))
    index_at[longest] = (index_at[longest] + 1) % extent[longest]
    return drawn.at[tuple(index_at)].set(largest)


def level_of(stream_key, dims, pieces, low, largest):
    factor_of, own = 1.0, jax.random.fold_in(stream_key, 6)
    for dim, parts in pieces:
        draws = jnp.exp(jax.random.uniform(jax.random.fold_in(own, dim), (parts,), jnp.float32, low / len(pieces), largest / len(pieces)))
        factor_of = factor_of * jnp.repeat(draws, dims[dim] // parts).reshape([-1 if axis == dim else 1 for axis in range(len(dims))])
    return factor_of


def centred(key, extent, width, limit, split=(), kind=jnp.bfloat16):
    values = jax.random.normal(key, extent, jnp.float32) * width
    if len(split) > 0:
        values = level_of(key, extent, split, -0.22, 0.18) * values
    return jnp.clip(values, min=-limit, max=limit).astype(kind)


def setup_inputs(seed: int = 0) -> dict:
    key_of = jax.random.split(jax.random.key(seed), 5)
    spectra = centred(key_of[0], (FREQS, 2, STATIONS), 1.0, 6.0, ((2, 8),))
    lag_samples = with_ends(jax.random.randint(key_of[1], (TILES, STATIONS), 0, NT), jax.random.fold_in(key_of[1], 1), 0, NT - 1).astype(jnp.int32)
    slowness = jnp.clip(jax.random.uniform(key_of[2], (TILES, 3, STATIONS), jnp.float32, -3.0, 3.0) * level_of(key_of[2], (TILES, 3, STATIONS), ((0, 16), (2, 8)), -0.4, 0.0), -3.0, 3.0).astype(jnp.bfloat16)
    spread_taps = jnp.clip(jnp.exp(jax.random.uniform(key_of[3], (3, TAPS), jnp.float32, math.log(0.02), math.log(0.2))), 0.02, 0.2)
    return dict(spectra=spectra, lag_samples=lag_samples, slowness=slowness, spread_taps=spread_taps)


TWO_PI = 2.0 * math.pi
BACKGROUND = 0.05


def align_rows(spectra, lag_row):
    bins = (F0 + jnp.arange(FREQS, dtype=jnp.int32)).astype(jnp.int32)
    cycles = (bins[:, None] * lag_row[None, :].astype(jnp.int32)) % NT
    turned = cycles.astype(jnp.float32) * (TWO_PI / NT)
    cosine = jnp.cos(turned)
    sine = jnp.sin(turned)
    real_in = spectra[:, 0, :].astype(jnp.float32)
    imag_in = spectra[:, 1, :].astype(jnp.float32)
    real_out = real_in * cosine + imag_in * sine
    imag_out = imag_in * cosine - real_in * sine
    return jnp.stack([real_out, imag_out], axis=1).astype(jnp.bfloat16)


def beam_freq(freq, aligned_row, slow_rows):
    omega = (F0 + freq).astype(jnp.float32) * (TWO_PI / NT)
    slow = slow_rows.astype(jnp.float32)
    x_coord = jnp.arange(CX, dtype=jnp.float32) - (CX - 1) / 2.0
    y_coord = jnp.arange(CY, dtype=jnp.float32) - (CY - 1) / 2.0
    z_coord = jnp.arange(CZ, dtype=jnp.float32) - (CZ - 1) / 2.0
    phase_x = (omega * slow[0])[None, :] * x_coord[:, None]
    phase_y = (omega * slow[1])[None, :] * y_coord[:, None]
    phase = phase_x[:, None, :] + phase_y[None, :, :]
    cosine = jnp.cos(phase)
    sine = jnp.sin(phase)
    real_in = aligned_row[0].astype(jnp.float32)[None, None, :]
    imag_in = aligned_row[1].astype(jnp.float32)[None, None, :]
    front_real = (real_in * cosine + imag_in * sine).astype(jnp.bfloat16).reshape(CX * CY, -1)
    front_imag = (imag_in * cosine - real_in * sine).astype(jnp.bfloat16).reshape(CX * CY, -1)
    left_side = jnp.concatenate([front_real, front_imag], axis=1)
    phase_z = (omega * slow[2])[:, None] * z_coord[None, :]
    depth_real = jnp.cos(phase_z).astype(jnp.bfloat16)
    depth_imag = jnp.sin(phase_z).astype(jnp.bfloat16)
    upper_rows = jnp.concatenate([depth_real, -depth_imag], axis=1)
    lower_rows = jnp.concatenate([depth_imag, depth_real], axis=1)
    right_side = jnp.concatenate([upper_rows, lower_rows], axis=0)
    return jnp.dot(left_side, right_side, preferred_element_type=jnp.float32)


def tile_power(lag_row, slow_rows, spectra):
    aligned = align_rows(spectra, lag_row)

    def step(total, freq):
        row = lax.dynamic_index_in_dim(aligned, freq, 0, keepdims=False)
        beams = beam_freq(freq, row, slow_rows)
        squares = beams * beams
        return total + squares[:, :CZ] + squares[:, CZ:], None

    total, unused = lax.scan(step, jnp.zeros((CX * CY, CZ), jnp.float32), jnp.arange(FREQS, dtype=jnp.int32))
    return (total / (FREQS * STATIONS) + BACKGROUND).reshape(CX, CY, CZ)


def to_grid(tiles):
    return tiles.reshape(TY, TX, CX, CY, CZ).transpose(1, 2, 0, 3, 4).reshape(TX * CX, TY * CY, CZ)


def to_tiles(volume):
    return volume.reshape(TX, CX, TY, CY, CZ).transpose(2, 0, 1, 3, 4).reshape(TY * TX, CX, CY, CZ)


def blur(volume, spread_taps):
    for axis in range(3):
        widths = [(0, 0), (0, 0), (0, 0)]
        widths[axis] = (HALF, HALF)
        padded = jnp.pad(volume, widths)
        total = jnp.zeros_like(volume)
        for offset in range(TAPS):
            total = total + spread_taps[axis, offset] * lax.slice_in_dim(padded, offset, offset + volume.shape[axis], axis=axis)
        volume = total
    return volume


def reference(spectra, lag_samples, slowness, spread_taps):
    stacked = lax.map(lambda tile_entry: tile_power(tile_entry[0], tile_entry[1], spectra), (lag_samples, slowness))
    observed = to_grid(stacked)
    estimate = observed
    for sweep in range(ITERS):
        blurred = blur(estimate, spread_taps)
        estimate = estimate * blur(observed / blurred, spread_taps)
    return stacked, to_tiles(estimate)
```

```python
import math

import jax
import jax.numpy as jnp
from jax import lax
from jax.sharding import PartitionSpec as P
from jax.experimental import pallas as pl
from jax.experimental.pallas import tpu as pltpu

STATIONS = 6144
FREQS = 64
F0 = 600
NT = 6000
TAPS = 17
HALF = 8
ITERS = 4
CX = 32
CY = 8
CZ = 128


TWO_PI = 2.0 * math.pi
BACKGROUND = 0.05


def with_halo(array, sides, width):
    for axis, dim in sides:
        size, length = (lax.axis_size(axis), array.shape[dim])
        up = [(i, (i + 1) % size) for i in range(size - 1)]
        down = [(j, i) for i, j in up]
        last = lax.slice_in_dim(array, length - width, length, axis=dim)
        leading = lax.slice_in_dim(array, 0, width, axis=dim)
        before = lax.ppermute(last, axis, up)
        after = lax.ppermute(leading, axis, down)
        array = jnp.concatenate([before, array, after], axis=dim)
    return array


def align_rows(spectra, lag_row):
    bins = F0 + jnp.arange(FREQS, dtype=jnp.int32)
    cycles = bins[:, None] * lag_row[None, :] % NT
    turned = cycles.astype(jnp.float32) * (TWO_PI / NT)
    cosine = jnp.cos(turned)
    sine = jnp.sin(turned)
    real_in = spectra[:, 0, :].astype(jnp.float32)
    imag_in = spectra[:, 1, :].astype(jnp.float32)
    real_out = real_in * cosine + imag_in * sine
    imag_out = imag_in * cosine - real_in * sine
    return jnp.stack([real_out, imag_out], axis=1).astype(jnp.bfloat16)


def beam_freq(freq, aligned_row, slow_rows):
    omega = (F0 + freq).astype(jnp.float32) * (TWO_PI / NT)
    slow = slow_rows.astype(jnp.float32)
    x_coord = jnp.arange(CX, dtype=jnp.float32) - (CX - 1) / 2.0
    y_coord = jnp.arange(CY, dtype=jnp.float32) - (CY - 1) / 2.0
    z_coord = jnp.arange(CZ, dtype=jnp.float32) - (CZ - 1) / 2.0
    phase_x = (omega * slow[0])[None, :] * x_coord[:, None]
    phase_y = (omega * slow[1])[None, :] * y_coord[:, None]
    phase = phase_x[:, None, :] + phase_y[None, :, :]
    cosine = jnp.cos(phase)
    sine = jnp.sin(phase)
    real_in = aligned_row[0].astype(jnp.float32)[None, None, :]
    imag_in = aligned_row[1].astype(jnp.float32)[None, None, :]
    front_real = (real_in * cosine + imag_in * sine).astype(jnp.bfloat16).reshape(CX * CY, -1)
    front_imag = (imag_in * cosine - real_in * sine).astype(jnp.bfloat16).reshape(CX * CY, -1)
    left_side = jnp.concatenate([front_real, front_imag], axis=1)
    phase_z = (omega * slow[2])[:, None] * z_coord[None, :]
    depth_real = jnp.cos(phase_z).astype(jnp.bfloat16)
    depth_imag = jnp.sin(phase_z).astype(jnp.bfloat16)
    upper_rows = jnp.concatenate([depth_real, -depth_imag], axis=1)
    lower_rows = jnp.concatenate([depth_imag, depth_real], axis=1)
    right_side = jnp.concatenate([upper_rows, lower_rows], axis=0)
    return jnp.dot(left_side, right_side, preferred_element_type=jnp.float32)


CHUNK = 256


def exp_neg(angle):
    return jnp.cos(angle), -jnp.sin(angle)


def beam_kernel(omega_ref, aligned_ref, slow_ref, power_ref, acc_ref, left_ref, right_ref):
    bins, stations = aligned_ref.shape[0], aligned_ref.shape[2]
    width = CHUNK
    rows8 = lax.broadcasted_iota(jnp.int32, (8, width), 0).astype(jnp.float32)
    rows16 = lax.broadcasted_iota(jnp.int32, (16, width), 0).astype(jnp.float32)
    power_ref[...] = jnp.zeros_like(power_ref)

    def per_bin(f, carry):
        omega = omega_ref[f]
        acc_ref[...] = jnp.zeros_like(acc_ref)

        def per_chunk(k, inner):
            cols = pl.ds(pl.multiple_of(k * width, width), width)
            turn_x = omega * slow_ref[0:1, cols].astype(jnp.float32)
            turn_y = omega * slow_ref[1:2, cols].astype(jnp.float32)
            turn_z = omega * slow_ref[2:3, cols].astype(jnp.float32)
            real_in = aligned_ref[f, 0:1, cols].astype(jnp.float32)
            imag_in = aligned_ref[f, 1:2, cols].astype(jnp.float32)
            a_r, a_i = exp_neg(turn_x * (rows8 - 3.5))
            b_r, b_i = exp_neg(turn_x * (8.0 * (rows8 - 1.5)))
            y_r, y_i = exp_neg(turn_y * (rows8 - 3.5))
            c_r, c_i = exp_neg(turn_z * (rows16 - 7.5))
            d_r, d_i = exp_neg(turn_z * (16.0 * (rows8 - 3.5)))
            for m in range(CX // 8):
                bm_r, bm_i = b_r[m : m + 1], b_i[m : m + 1]
                x_r = bm_r * a_r - bm_i * a_i
                x_i = bm_r * a_i + bm_i * a_r
                p_r = real_in * x_r - imag_in * x_i
                p_i = real_in * x_i + imag_in * x_r
                for j in range(0, 8, 2):
                    parts_r, parts_i = [], []
                    for jj in (j, j + 1):
                        px_r, px_i = p_r[jj : jj + 1], p_i[jj : jj + 1]
                        parts_r.append(px_r * y_r - px_i * y_i)
                        parts_i.append(px_r * y_i + px_i * y_r)
                    row = (8 * m + j) * CY
                    left_ref[row : row + 16, 0:width] = jnp.concatenate(parts_r, axis=0).astype(jnp.bfloat16)
                    left_ref[row : row + 16, width : 2 * width] = jnp.concatenate(parts_i, axis=0).astype(jnp.bfloat16)
            for m in range(CZ // 16):
                dm_r, dm_i = d_r[m : m + 1], d_i[m : m + 1]
                z_r = dm_r * c_r - dm_i * c_i
                z_i = dm_r * c_i + dm_i * c_r
                cos_z = z_r.astype(jnp.bfloat16)
                sin_z = (-z_i).astype(jnp.bfloat16)
                row = 16 * m
                right_ref[row : row + 16, 0:width] = cos_z
                right_ref[row : row + 16, width : 2 * width] = sin_z
                right_ref[CZ + row : CZ + row + 16, 0:width] = -sin_z
                right_ref[CZ + row : CZ + row + 16, width : 2 * width] = cos_z
            acc_ref[...] += lax.dot_general(
                left_ref[...], right_ref[...], (((1,), (1,)), ((), ())), preferred_element_type=jnp.float32
            )
            return inner

        lax.fori_loop(0, stations // width, per_chunk, 0)
        beams = acc_ref[...]
        squares = beams * beams
        power_ref[...] += squares[:, :CZ] + squares[:, CZ:]
        return carry

    lax.fori_loop(0, bins, per_bin, 0)


def beam_power(omegas, aligned_rows, slow_rows):
    width = CHUNK
    return pl.pallas_call(
        beam_kernel,
        out_shape=jax.ShapeDtypeStruct((CX * CY, CZ), jnp.float32),
        in_specs=[
            pl.BlockSpec(memory_space=pltpu.SMEM),
            pl.BlockSpec(memory_space=pltpu.VMEM),
            pl.BlockSpec(memory_space=pltpu.VMEM),
        ],
        out_specs=pl.BlockSpec(memory_space=pltpu.VMEM),
        scratch_shapes=[
            pltpu.VMEM((CX * CY, 2 * CZ), jnp.float32),
            pltpu.VMEM((CX * CY, 2 * width), jnp.bfloat16),
            pltpu.VMEM((2 * CZ, 2 * width), jnp.bfloat16),
        ],
    )(omegas, aligned_rows, slow_rows)


def freq_beams(freq_ids, aligned_rows, slow_rows):
    return lax.map(lambda pair: beam_freq(pair[0], pair[1], slow_rows), (freq_ids, aligned_rows))


def band_matrix(taps, length):
    rows = jnp.arange(length, dtype=jnp.int32)[:, None]
    columns = jnp.arange(length + 2 * HALF, dtype=jnp.int32)[None, :]
    offset = columns - rows
    picks = jnp.arange(TAPS, dtype=jnp.int32)[:, None, None]
    return jnp.sum(jnp.where(offset[None] == picks, taps[:, None, None], 0.0), axis=0)


def blur(volume, bands):
    band_x, square_y, square_z = bands
    padded = with_halo(volume.astype(jnp.bfloat16), (("grid", 0),), HALF).astype(volume.dtype)
    along_x = jnp.einsum("ip,pyz->iyz", band_x, padded, precision=lax.Precision.HIGHEST)
    along_y = jnp.einsum("jq,xqz->xjz", square_y, along_x, precision=lax.Precision.HIGHEST)
    return jnp.einsum("xyw,kw->xyk", along_y, square_z, precision=lax.Precision.HIGHEST)


def per_device(spectra, lag_samples, slowness, spread_taps):
    groups = lax.axis_size("sta")
    own_count = FREQS // groups
    first_bin = lax.axis_index("sta") * own_count
    aligned = align_rows(spectra, lag_samples[0])
    own_ids = first_bin + jnp.arange(own_count, dtype=jnp.int32)
    rows = lax.dynamic_slice_in_dim(
        lax.all_gather(aligned, "sta", axis=2, tiled=True), first_bin, own_count, 0
    )
    omegas = (F0 + own_ids).astype(jnp.float32) * (TWO_PI / NT)
    local_power = beam_power(omegas, rows, lax.all_gather(slowness, "sta", axis=2, tiled=True)[0])
    summed = lax.psum(local_power, "sta")
    stacked = (summed / (FREQS * STATIONS) + BACKGROUND).reshape(CX, CY, CZ)
    square_y = band_matrix(spread_taps[1], CY)[:, HALF : HALF + CY]
    square_z = band_matrix(spread_taps[2], CZ)[:, HALF : HALF + CZ]
    bands = (band_matrix(spread_taps[0], CX), square_y, square_z)
    estimate = stacked
    for sweep in range(ITERS):
        blurred = blur(estimate, bands)
        estimate = estimate * blur(stacked / blurred, bands)
    return (stacked[None], estimate[None])


def solution(mesh):
    placed = (P(None, None, "sta"), P("grid", "sta"), P("grid", None, "sta"), P())
    return jax.shard_map(
        per_device,
        mesh=mesh,
        in_specs=placed,
        out_specs=(P("grid", None, None, None), P("grid", None, None, None)),
        check_vma=False,
    )
```

```python
import math

import jax
import jax.numpy as jnp
from jax import lax
from jax.sharding import PartitionSpec as P
from jax.experimental import pallas as pl
from jax.experimental.pallas import tpu as pltpu

STATIONS = 6144
FREQS = 64
F0 = 600
NT = 6000
TAPS = 17
HALF = 8
ITERS = 4
CX = 32
CY = 8
CZ = 128


TWO_PI = 2.0 * math.pi
BACKGROUND = 0.05


def with_halo(array, sides, width):
    for axis, dim in sides:
        size, length = (lax.axis_size(axis), array.shape[dim])
        up = [(i, (i + 1) % size) for i in range(size - 1)]
        down = [(j, i) for i, j in up]
        last = lax.slice_in_dim(array, length - width, length, axis=dim)
        leading = lax.slice_in_dim(array, 0, width, axis=dim)
        before = lax.ppermute(last, axis, up)
        after = lax.ppermute(leading, axis, down)
        array = jnp.concatenate([before, array, after], axis=dim)
    return array


def align_rows(spectra, lag_row):
    bins = F0 + jnp.arange(FREQS, dtype=jnp.int32)
    cycles = bins[:, None] * lag_row[None, :] % NT
    turned = cycles.astype(jnp.float32) * (TWO_PI / NT)
    cosine = jnp.cos(turned)
    sine = jnp.sin(turned)
    real_in = spectra[:, 0, :].astype(jnp.float32)
    imag_in = spectra[:, 1, :].astype(jnp.float32)
    real_out = real_in * cosine + imag_in * sine
    imag_out = imag_in * cosine - real_in * sine
    return jnp.stack([real_out, imag_out], axis=1).astype(jnp.bfloat16)


def beam_freq(freq, aligned_row, slow_rows):
    omega = (F0 + freq).astype(jnp.float32) * (TWO_PI / NT)
    slow = slow_rows.astype(jnp.float32)
    x_coord = jnp.arange(CX, dtype=jnp.float32) - (CX - 1) / 2.0
    y_coord = jnp.arange(CY, dtype=jnp.float32) - (CY - 1) / 2.0
    z_coord = jnp.arange(CZ, dtype=jnp.float32) - (CZ - 1) / 2.0
    phase_x = (omega * slow[0])[None, :] * x_coord[:, None]
    phase_y = (omega * slow[1])[None, :] * y_coord[:, None]
    phase = phase_x[:, None, :] + phase_y[None, :, :]
    cosine = jnp.cos(phase)
    sine = jnp.sin(phase)
    real_in = aligned_row[0].astype(jnp.float32)[None, None, :]
    imag_in = aligned_row[1].astype(jnp.float32)[None, None, :]
    front_real = (real_in * cosine + imag_in * sine).astype(jnp.bfloat16).reshape(CX * CY, -1)
    front_imag = (imag_in * cosine - real_in * sine).astype(jnp.bfloat16).reshape(CX * CY, -1)
    left_side = jnp.concatenate([front_real, front_imag], axis=1)
    phase_z = (omega * slow[2])[:, None] * z_coord[None, :]
    depth_real = jnp.cos(phase_z).astype(jnp.bfloat16)
    depth_imag = jnp.sin(phase_z).astype(jnp.bfloat16)
    upper_rows = jnp.concatenate([depth_real, -depth_imag], axis=1)
    lower_rows = jnp.concatenate([depth_imag, depth_real], axis=1)
    right_side = jnp.concatenate([upper_rows, lower_rows], axis=0)
    return jnp.dot(left_side, right_side, preferred_element_type=jnp.float32)


CHUNK = 256


def exp_neg(angle):
    return jnp.cos(angle), -jnp.sin(angle)


def beam_kernel(omega_ref, aligned_ref, slow_ref, power_ref, acc_ref, left_ref, right_ref):
    bins, stations = aligned_ref.shape[0], aligned_ref.shape[2]
    width = CHUNK
    rows8 = lax.broadcasted_iota(jnp.int32, (8, width), 0).astype(jnp.float32)
    rows16 = lax.broadcasted_iota(jnp.int32, (16, width), 0).astype(jnp.float32)
    power_ref[...] = jnp.zeros_like(power_ref)

    def per_bin(f, carry):
        omega = omega_ref[f]
        acc_ref[...] = jnp.zeros_like(acc_ref)

        def per_chunk(k, inner):
            cols = pl.ds(pl.multiple_of(k * width, width), width)
            turn_x = omega * slow_ref[0:1, cols].astype(jnp.float32)
            turn_y = omega * slow_ref[1:2, cols].astype(jnp.float32)
            turn_z = omega * slow_ref[2:3, cols].astype(jnp.float32)
            real_in = aligned_ref[f, 0:1, cols].astype(jnp.float32)
            imag_in = aligned_ref[f, 1:2, cols].astype(jnp.float32)
            a_r, a_i = exp_neg(turn_x * (rows8 - 3.5))
            b_r, b_i = exp_neg(turn_x * (8.0 * (rows8 - 1.5)))
            y_r, y_i = exp_neg(turn_y * (rows8 - 3.5))
            c_r, c_i = exp_neg(turn_z * (rows16 - 7.5))
            d_r, d_i = exp_neg(turn_z * (16.0 * (rows8 - 3.5)))
            for m in range(CX // 8):
                bm_r, bm_i = b_r[m : m + 1], b_i[m : m + 1]
                x_r = bm_r * a_r - bm_i * a_i
                x_i = bm_r * a_i + bm_i * a_r
                p_r = real_in * x_r - imag_in * x_i
                p_i = real_in * x_i + imag_in * x_r
                for j in range(0, 8, 2):
                    parts_r, parts_i = [], []
                    for jj in (j, j + 1):
                        px_r, px_i = p_r[jj : jj + 1], p_i[jj : jj + 1]
                        parts_r.append(px_r * y_r - px_i * y_i)
                        parts_i.append(px_r * y_i + px_i * y_r)
                    row = (8 * m + j) * CY
                    left_ref[row : row + 16, 0:width] = jnp.concatenate(parts_r, axis=0).astype(jnp.bfloat16)
                    left_ref[row : row + 16, width : 2 * width] = jnp.concatenate(parts_i, axis=0).astype(jnp.bfloat16)
            for m in range(CZ // 16):
                dm_r, dm_i = d_r[m : m + 1], d_i[m : m + 1]
                z_r = dm_r * c_r - dm_i * c_i
                z_i = dm_r * c_i + dm_i * c_r
                cos_z = z_r.astype(jnp.bfloat16)
                sin_z = (-z_i).astype(jnp.bfloat16)
                row = 16 * m
                right_ref[row : row + 16, 0:width] = cos_z
                right_ref[row : row + 16, width : 2 * width] = sin_z
                right_ref[CZ + row : CZ + row + 16, 0:width] = -sin_z
                right_ref[CZ + row : CZ + row + 16, width : 2 * width] = cos_z
            acc_ref[...] += lax.dot_general(
                left_ref[...], right_ref[...], (((1,), (1,)), ((), ())), preferred_element_type=jnp.float32
            )
            return inner

        lax.fori_loop(0, stations // width, per_chunk, 0)
        beams = acc_ref[...]
        squares = beams * beams
        power_ref[...] += squares[:, :CZ] + squares[:, CZ:]
        return carry

    lax.fori_loop(0, bins, per_bin, 0)


def beam_power(omegas, aligned_rows, slow_rows):
    width = CHUNK
    return pl.pallas_call(
        beam_kernel,
        out_shape=jax.ShapeDtypeStruct((CX * CY, CZ), jnp.float32),
        in_specs=[
            pl.BlockSpec(memory_space=pltpu.SMEM),
            pl.BlockSpec(memory_space=pltpu.VMEM),
            pl.BlockSpec(memory_space=pltpu.VMEM),
        ],
        out_specs=pl.BlockSpec(memory_space=pltpu.VMEM),
        scratch_shapes=[
            pltpu.VMEM((CX * CY, 2 * CZ), jnp.float32),
            pltpu.VMEM((CX * CY, 2 * width), jnp.bfloat16),
            pltpu.VMEM((2 * CZ, 2 * width), jnp.bfloat16),
        ],
    )(omegas, aligned_rows, slow_rows)


def sum_kernel(part_ref, out_ref, recv_ref, local_sem, send_sem, recv_sem):
    count = recv_ref.shape[0]
    me = lax.axis_index("sta")
    tile = lax.axis_index("grid")
    barrier = pltpu.get_barrier_semaphore()
    for shift in range(1, count):
        peer = lax.rem(me + shift, count)
        pl.semaphore_signal(barrier, inc=1, device_id=(tile, peer), device_id_type=pl.DeviceIdType.MESH)
    pl.semaphore_wait(barrier, count - 1)
    own = pltpu.make_async_copy(part_ref, recv_ref.at[me], local_sem.at[0])
    own.start()
    copies = []
    for shift in range(1, count):
        peer = lax.rem(me + shift, count)
        copy = pltpu.make_async_remote_copy(
            src_ref=part_ref,
            dst_ref=recv_ref.at[me],
            send_sem=send_sem.at[shift],
            recv_sem=recv_sem.at[me],
            device_id=(tile, peer),
            device_id_type=pl.DeviceIdType.MESH,
        )
        copy.start()
        copies.append(copy)
    own.wait()
    for shift in range(1, count):
        copies[shift - 1].wait_send()
        source = lax.rem(me + count - shift, count)
        pltpu.make_async_remote_copy(
            src_ref=part_ref,
            dst_ref=recv_ref.at[source],
            send_sem=send_sem.at[shift],
            recv_sem=recv_sem.at[source],
            device_id=(tile, source),
            device_id_type=pl.DeviceIdType.MESH,
        ).wait_recv()
    total = recv_ref[0]
    for source in range(1, count):
        total = total + recv_ref[source]
    out_ref[...] = total


def sum_over_sta(part):
    count = lax.axis_size("sta")
    return pl.pallas_call(
        sum_kernel,
        out_shape=jax.ShapeDtypeStruct(part.shape, jnp.float32),
        in_specs=[pl.BlockSpec(memory_space=pltpu.VMEM)],
        out_specs=pl.BlockSpec(memory_space=pltpu.VMEM),
        scratch_shapes=[
            pltpu.VMEM((count,) + part.shape, jnp.float32),
            pltpu.SemaphoreType.DMA((1,)),
            pltpu.SemaphoreType.DMA((count,)),
            pltpu.SemaphoreType.DMA((count,)),
        ],
        compiler_params=pltpu.CompilerParams(collective_id=0, has_side_effects=True),
    )(part)


def freq_beams(freq_ids, aligned_rows, slow_rows):
    return lax.map(lambda pair: beam_freq(pair[0], pair[1], slow_rows), (freq_ids, aligned_rows))


def band_matrix(taps, length):
    rows = jnp.arange(length, dtype=jnp.int32)[:, None]
    columns = jnp.arange(length + 2 * HALF, dtype=jnp.int32)[None, :]
    offset = columns - rows
    picks = jnp.arange(TAPS, dtype=jnp.int32)[:, None, None]
    return jnp.sum(jnp.where(offset[None] == picks, taps[:, None, None], 0.0), axis=0)


def blur(volume, bands):
    band_x, square_y, square_z = bands
    padded = with_halo(volume.astype(jnp.bfloat16), (("grid", 0),), HALF).astype(volume.dtype)
    along_x = jnp.einsum("ip,pyz->iyz", band_x, padded, precision=lax.Precision.HIGHEST)
    along_y = jnp.einsum("jq,xqz->xjz", square_y, along_x, precision=lax.Precision.HIGHEST)
    return jnp.einsum("xyw,kw->xyk", along_y, square_z, precision=lax.Precision.HIGHEST)


def per_device(spectra, lag_samples, slowness, spread_taps):
    groups = lax.axis_size("sta")
    own_count = FREQS // groups
    first_bin = lax.axis_index("sta") * own_count
    aligned = align_rows(spectra, lag_samples[0])
    own_ids = first_bin + jnp.arange(own_count, dtype=jnp.int32)
    rows = lax.dynamic_slice_in_dim(
        lax.all_gather(aligned, "sta", axis=2, tiled=True), first_bin, own_count, 0
    )
    omegas = (F0 + own_ids).astype(jnp.float32) * (TWO_PI / NT)
    local_power = beam_power(omegas, rows, lax.all_gather(slowness, "sta", axis=2, tiled=True)[0])
    summed = sum_over_sta(local_power)
    stacked = (summed / (FREQS * STATIONS) + BACKGROUND).reshape(CX, CY, CZ)
    square_y = band_matrix(spread_taps[1], CY)[:, HALF : HALF + CY]
    square_z = band_matrix(spread_taps[2], CZ)[:, HALF : HALF + CZ]
    bands = (band_matrix(spread_taps[0], CX), square_y, square_z)
    estimate = stacked
    for sweep in range(ITERS):
        blurred = blur(estimate, bands)
        estimate = estimate * blur(stacked / blurred, bands)
    return (stacked[None], estimate[None])


def solution(mesh):
    placed = (P(None, None, "sta"), P("grid", "sta"), P("grid", None, "sta"), P())
    return jax.shard_map(
        per_device,
        mesh=mesh,
        in_specs=placed,
        out_specs=(P("grid", None, None, None), P("grid", None, None, None)),
        check_vma=False,
    )
```

```python
import math

import jax
import jax.numpy as jnp
from jax import lax
from jax.sharding import PartitionSpec as P
from jax.experimental import pallas as pl
from jax.experimental.pallas import tpu as pltpu

STATIONS = 6144
FREQS = 64
F0 = 600
NT = 6000
TAPS = 17
HALF = 8
ITERS = 4
CX = 32
CY = 8
CZ = 128


TWO_PI = 2.0 * math.pi
BACKGROUND = 0.05


def with_halo(array, sides, width):
    for axis, dim in sides:
        size, length = (lax.axis_size(axis), array.shape[dim])
        up = [(i, (i + 1) % size) for i in range(size - 1)]
        down = [(j, i) for i, j in up]
        last = lax.slice_in_dim(array, length - width, length, axis=dim)
        leading = lax.slice_in_dim(array, 0, width, axis=dim)
        before = lax.ppermute(last, axis, up)
        after = lax.ppermute(leading, axis, down)
        array = jnp.concatenate([before, array, after], axis=dim)
    return array


def align_rows(spectra, lag_row):
    bins = F0 + jnp.arange(FREQS, dtype=jnp.int32)
    cycles = bins[:, None] * lag_row[None, :] % NT
    turned = cycles.astype(jnp.float32) * (TWO_PI / NT)
    cosine = jnp.cos(turned)
    sine = jnp.sin(turned)
    real_in = spectra[:, 0, :].astype(jnp.float32)
    imag_in = spectra[:, 1, :].astype(jnp.float32)
    real_out = real_in * cosine + imag_in * sine
    imag_out = imag_in * cosine - real_in * sine
    return jnp.stack([real_out, imag_out], axis=1).astype(jnp.bfloat16)


def beam_freq(freq, aligned_row, slow_rows):
    omega = (F0 + freq).astype(jnp.float32) * (TWO_PI / NT)
    slow = slow_rows.astype(jnp.float32)
    x_coord = jnp.arange(CX, dtype=jnp.float32) - (CX - 1) / 2.0
    y_coord = jnp.arange(CY, dtype=jnp.float32) - (CY - 1) / 2.0
    z_coord = jnp.arange(CZ, dtype=jnp.float32) - (CZ - 1) / 2.0
    phase_x = (omega * slow[0])[None, :] * x_coord[:, None]
    phase_y = (omega * slow[1])[None, :] * y_coord[:, None]
    phase = phase_x[:, None, :] + phase_y[None, :, :]
    cosine = jnp.cos(phase)
    sine = jnp.sin(phase)
    real_in = aligned_row[0].astype(jnp.float32)[None, None, :]
    imag_in = aligned_row[1].astype(jnp.float32)[None, None, :]
    front_real = (real_in * cosine + imag_in * sine).astype(jnp.bfloat16).reshape(CX * CY, -1)
    front_imag = (imag_in * cosine - real_in * sine).astype(jnp.bfloat16).reshape(CX * CY, -1)
    left_side = jnp.concatenate([front_real, front_imag], axis=1)
    phase_z = (omega * slow[2])[:, None] * z_coord[None, :]
    depth_real = jnp.cos(phase_z).astype(jnp.bfloat16)
    depth_imag = jnp.sin(phase_z).astype(jnp.bfloat16)
    upper_rows = jnp.concatenate([depth_real, -depth_imag], axis=1)
    lower_rows = jnp.concatenate([depth_imag, depth_real], axis=1)
    right_side = jnp.concatenate([upper_rows, lower_rows], axis=0)
    return jnp.dot(left_side, right_side, preferred_element_type=jnp.float32)


CHUNK = 256


def exp_neg(angle):
    return jnp.cos(angle), -jnp.sin(angle)


def beam_kernel(omega_ref, aligned_ref, slow_ref, power_ref, acc_ref, left_ref, right_ref):
    bins, stations = aligned_ref.shape[0], aligned_ref.shape[2]
    width = CHUNK
    rows8 = lax.broadcasted_iota(jnp.int32, (8, width), 0).astype(jnp.float32)
    rows16 = lax.broadcasted_iota(jnp.int32, (16, width), 0).astype(jnp.float32)
    power_ref[...] = jnp.zeros_like(power_ref)

    def per_bin(f, carry):
        omega = omega_ref[f]
        acc_ref[...] = jnp.zeros_like(acc_ref)

        def per_chunk(k, inner):
            cols = pl.ds(pl.multiple_of(k * width, width), width)
            turn_x = omega * slow_ref[0:1, cols].astype(jnp.float32)
            turn_y = omega * slow_ref[1:2, cols].astype(jnp.float32)
            turn_z = omega * slow_ref[2:3, cols].astype(jnp.float32)
            real_in = aligned_ref[f, 0:1, cols].astype(jnp.float32)
            imag_in = aligned_ref[f, 1:2, cols].astype(jnp.float32)
            a_r, a_i = exp_neg(turn_x * (rows8 - 3.5))
            b_r, b_i = exp_neg(turn_x * (8.0 * (rows8 - 1.5)))
            y_r, y_i = exp_neg(turn_y * (rows8 - 3.5))
            c_r, c_i = exp_neg(turn_z * (rows16 - 7.5))
            d_r, d_i = exp_neg(turn_z * (16.0 * (rows8 - 3.5)))
            for m in range(CX // 8):
                bm_r, bm_i = b_r[m : m + 1], b_i[m : m + 1]
                x_r = bm_r * a_r - bm_i * a_i
                x_i = bm_r * a_i + bm_i * a_r
                p_r = real_in * x_r - imag_in * x_i
                p_i = real_in * x_i + imag_in * x_r
                for j in range(0, 8, 2):
                    parts_r, parts_i = [], []
                    for jj in (j, j + 1):
                        px_r, px_i = p_r[jj : jj + 1], p_i[jj : jj + 1]
                        parts_r.append(px_r * y_r - px_i * y_i)
                        parts_i.append(px_r * y_i + px_i * y_r)
                    row = (8 * m + j) * CY
                    left_ref[row : row + 16, 0:width] = jnp.concatenate(parts_r, axis=0).astype(jnp.bfloat16)
                    left_ref[row : row + 16, width : 2 * width] = jnp.concatenate(parts_i, axis=0).astype(jnp.bfloat16)
            for m in range(CZ // 16):
                dm_r, dm_i = d_r[m : m + 1], d_i[m : m + 1]
                z_r = dm_r * c_r - dm_i * c_i
                z_i = dm_r * c_i + dm_i * c_r
                cos_z = z_r.astype(jnp.bfloat16)
                sin_z = (-z_i).astype(jnp.bfloat16)
                row = 16 * m
                right_ref[row : row + 16, 0:width] = cos_z
                right_ref[row : row + 16, width : 2 * width] = sin_z
                right_ref[CZ + row : CZ + row + 16, 0:width] = -sin_z
                right_ref[CZ + row : CZ + row + 16, width : 2 * width] = cos_z
            acc_ref[...] += lax.dot_general(
                left_ref[...], right_ref[...], (((1,), (1,)), ((), ())), preferred_element_type=jnp.float32
            )
            return inner

        lax.fori_loop(0, stations // width, per_chunk, 0)
        beams = acc_ref[...]
        squares = beams * beams
        power_ref[...] += squares[:, :CZ] + squares[:, CZ:]
        return carry

    lax.fori_loop(0, bins, per_bin, 0)


def beam_power(omegas, aligned_rows, slow_rows):
    width = CHUNK
    return pl.pallas_call(
        beam_kernel,
        out_shape=jax.ShapeDtypeStruct((CX * CY, CZ), jnp.float32),
        in_specs=[
            pl.BlockSpec(memory_space=pltpu.SMEM),
            pl.BlockSpec(memory_space=pltpu.VMEM),
            pl.BlockSpec(memory_space=pltpu.VMEM),
        ],
        out_specs=pl.BlockSpec(memory_space=pltpu.VMEM),
        scratch_shapes=[
            pltpu.VMEM((CX * CY, 2 * CZ), jnp.float32),
            pltpu.VMEM((CX * CY, 2 * width), jnp.bfloat16),
            pltpu.VMEM((2 * CZ, 2 * width), jnp.bfloat16),
        ],
    )(omegas, aligned_rows, slow_rows)


def sum_kernel(part_ref, out_ref, recv_ref, local_sem, send_sem, recv_sem):
    count = recv_ref.shape[0]
    me = lax.axis_index("sta")
    tile = lax.axis_index("grid")
    barrier = pltpu.get_barrier_semaphore()
    for shift in range(1, count):
        peer = lax.rem(me + shift, count)
        pl.semaphore_signal(barrier, inc=1, device_id=(tile, peer), device_id_type=pl.DeviceIdType.MESH)
    pl.semaphore_wait(barrier, count - 1)
    own = pltpu.make_async_copy(part_ref, recv_ref.at[me], local_sem.at[0])
    own.start()
    copies = []
    for shift in range(1, count):
        peer = lax.rem(me + shift, count)
        copy = pltpu.make_async_remote_copy(
            src_ref=part_ref,
            dst_ref=recv_ref.at[me],
            send_sem=send_sem.at[shift],
            recv_sem=recv_sem.at[me],
            device_id=(tile, peer),
            device_id_type=pl.DeviceIdType.MESH,
        )
        copy.start()
        copies.append(copy)
    own.wait()
    for shift in range(1, count):
        copies[shift - 1].wait_send()
        source = lax.rem(me + count - shift, count)
        pltpu.make_async_remote_copy(
            src_ref=part_ref,
            dst_ref=recv_ref.at[source],
            send_sem=send_sem.at[shift],
            recv_sem=recv_sem.at[source],
            device_id=(tile, source),
            device_id_type=pl.DeviceIdType.MESH,
        ).wait_recv()
    total = recv_ref[0]
    for source in range(1, count):
        total = total + recv_ref[source]
    out_ref[...] = total


def sum_over_sta(part):
    count = lax.axis_size("sta")
    return pl.pallas_call(
        sum_kernel,
        out_shape=jax.ShapeDtypeStruct(part.shape, jnp.float32),
        in_specs=[pl.BlockSpec(memory_space=pltpu.VMEM)],
        out_specs=pl.BlockSpec(memory_space=pltpu.VMEM),
        scratch_shapes=[
            pltpu.VMEM((count,) + part.shape, jnp.float32),
            pltpu.SemaphoreType.DMA((1,)),
            pltpu.SemaphoreType.DMA((count,)),
            pltpu.SemaphoreType.DMA((count,)),
        ],
        compiler_params=pltpu.CompilerParams(collective_id=0, has_side_effects=True),
    )(part)


def freq_beams(freq_ids, aligned_rows, slow_rows):
    return lax.map(lambda pair: beam_freq(pair[0], pair[1], slow_rows), (freq_ids, aligned_rows))


def band_matrix(taps, length):
    rows = jnp.arange(length, dtype=jnp.int32)[:, None]
    columns = jnp.arange(length + 2 * HALF, dtype=jnp.int32)[None, :]
    offset = columns - rows
    picks = jnp.arange(TAPS, dtype=jnp.int32)[:, None, None]
    return jnp.sum(jnp.where(offset[None] == picks, taps[:, None, None], 0.0), axis=0)


def blur(volume, bands):
    band_x, square_y, square_z = bands
    padded = with_halo(volume.astype(jnp.bfloat16), (("grid", 0),), HALF).astype(volume.dtype)
    along_x = jnp.einsum("ip,pyz->iyz", band_x, padded, precision=lax.Precision.HIGHEST)
    along_y = jnp.einsum("jq,xqz->xjz", square_y, along_x, precision=lax.Precision.HIGHEST)
    return jnp.einsum("xyw,kw->xyk", along_y, square_z, precision=lax.Precision.HIGHEST)


def blur_narrowing(volume, taps, square_y, square_z):
    band_x = band_matrix(taps, volume.shape[0] - 2 * HALF)
    along_x = jnp.einsum("ip,pyz->iyz", band_x, volume, precision=lax.Precision.HIGHEST)
    along_y = jnp.einsum("jq,xqz->xjz", square_y, along_x, precision=lax.Precision.HIGHEST)
    return jnp.einsum("xyw,kw->xyk", along_y, square_z, precision=lax.Precision.HIGHEST)


def deblur(stacked, spread_taps):
    tiles = lax.axis_size("grid")
    me = lax.axis_index("grid")
    reach = ITERS * 2 * HALF
    halo_tiles = -(-reach // CX)
    before = [
        lax.ppermute(stacked, "grid", [(i, i + k) for i in range(tiles - k)])
        for k in range(halo_tiles, 0, -1)
    ]
    after = [
        lax.ppermute(stacked, "grid", [(i + k, i) for i in range(tiles - k)])
        for k in range(1, halo_tiles + 1)
    ]
    cut = halo_tiles * CX - reach
    observed = jnp.concatenate(before + [stacked] + after, axis=0)
    observed = observed[cut : observed.shape[0] - cut]
    width = observed.shape[0]
    cell = (me - halo_tiles) * CX + cut + jnp.arange(width, dtype=jnp.int32)
    inside = (cell >= 0) & (cell < tiles * CX)
    square_y = band_matrix(spread_taps[1], CY)[:, HALF : HALF + CY]
    square_z = band_matrix(spread_taps[2], CZ)[:, HALF : HALF + CZ]
    estimate = observed
    for sweep in range(ITERS):
        low = 2 * HALF * sweep + HALF
        blurred = blur_narrowing(estimate, spread_taps[0], square_y, square_z)
        ratio = jnp.where(
            inside[low : width - low, None, None], observed[low : width - low] / blurred, 0.0
        )
        estimate = estimate[2 * HALF : estimate.shape[0] - 2 * HALF] * blur_narrowing(
            ratio, spread_taps[0], square_y, square_z
        )
    return estimate


def per_device(spectra, lag_samples, slowness, spread_taps):
    groups = lax.axis_size("sta")
    own_count = FREQS // groups
    first_bin = lax.axis_index("sta") * own_count
    aligned = align_rows(spectra, lag_samples[0])
    own_ids = first_bin + jnp.arange(own_count, dtype=jnp.int32)
    rows = lax.dynamic_slice_in_dim(
        lax.all_gather(aligned, "sta", axis=2, tiled=True), first_bin, own_count, 0
    )
    omegas = (F0 + own_ids).astype(jnp.float32) * (TWO_PI / NT)
    local_power = beam_power(omegas, rows, lax.all_gather(slowness, "sta", axis=2, tiled=True)[0])
    summed = sum_over_sta(local_power)
    stacked = (summed / (FREQS * STATIONS) + BACKGROUND).reshape(CX, CY, CZ)
    estimate = deblur(stacked, spread_taps)
    return (stacked[None], estimate[None])


def solution(mesh):
    placed = (P(None, None, "sta"), P("grid", "sta"), P("grid", None, "sta"), P())
    return jax.shard_map(
        per_device,
        mesh=mesh,
        in_specs=placed,
        out_specs=(P("grid", None, None, None), P("grid", None, None, None)),
        check_vma=False,
    )
```

```python
import math

import jax
import jax.numpy as jnp
from jax import lax
from jax.sharding import PartitionSpec as P
from jax.experimental import pallas as pl
from jax.experimental.pallas import tpu as pltpu

STATIONS = 6144
FREQS = 64
F0 = 600
NT = 6000
TAPS = 17
HALF = 8
ITERS = 4
CX = 32
CY = 8
CZ = 128


TWO_PI = 2.0 * math.pi
BACKGROUND = 0.05


def with_halo(array, sides, width):
    for axis, dim in sides:
        size, length = (lax.axis_size(axis), array.shape[dim])
        up = [(i, (i + 1) % size) for i in range(size - 1)]
        down = [(j, i) for i, j in up]
        last = lax.slice_in_dim(array, length - width, length, axis=dim)
        leading = lax.slice_in_dim(array, 0, width, axis=dim)
        before = lax.ppermute(last, axis, up)
        after = lax.ppermute(leading, axis, down)
        array = jnp.concatenate([before, array, after], axis=dim)
    return array


def align_rows(spectra, lag_row):
    bins = F0 + jnp.arange(FREQS, dtype=jnp.int32)
    cycles = bins[:, None] * lag_row[None, :] % NT
    turned = cycles.astype(jnp.float32) * (TWO_PI / NT)
    cosine = jnp.cos(turned)
    sine = jnp.sin(turned)
    real_in = spectra[:, 0, :].astype(jnp.float32)
    imag_in = spectra[:, 1, :].astype(jnp.float32)
    real_out = real_in * cosine + imag_in * sine
    imag_out = imag_in * cosine - real_in * sine
    return jnp.stack([real_out, imag_out], axis=1).astype(jnp.bfloat16)


def beam_freq(freq, aligned_row, slow_rows):
    omega = (F0 + freq).astype(jnp.float32) * (TWO_PI / NT)
    slow = slow_rows.astype(jnp.float32)
    x_coord = jnp.arange(CX, dtype=jnp.float32) - (CX - 1) / 2.0
    y_coord = jnp.arange(CY, dtype=jnp.float32) - (CY - 1) / 2.0
    z_coord = jnp.arange(CZ, dtype=jnp.float32) - (CZ - 1) / 2.0
    phase_x = (omega * slow[0])[None, :] * x_coord[:, None]
    phase_y = (omega * slow[1])[None, :] * y_coord[:, None]
    phase = phase_x[:, None, :] + phase_y[None, :, :]
    cosine = jnp.cos(phase)
    sine = jnp.sin(phase)
    real_in = aligned_row[0].astype(jnp.float32)[None, None, :]
    imag_in = aligned_row[1].astype(jnp.float32)[None, None, :]
    front_real = (real_in * cosine + imag_in * sine).astype(jnp.bfloat16).reshape(CX * CY, -1)
    front_imag = (imag_in * cosine - real_in * sine).astype(jnp.bfloat16).reshape(CX * CY, -1)
    left_side = jnp.concatenate([front_real, front_imag], axis=1)
    phase_z = (omega * slow[2])[:, None] * z_coord[None, :]
    depth_real = jnp.cos(phase_z).astype(jnp.bfloat16)
    depth_imag = jnp.sin(phase_z).astype(jnp.bfloat16)
    upper_rows = jnp.concatenate([depth_real, -depth_imag], axis=1)
    lower_rows = jnp.concatenate([depth_imag, depth_real], axis=1)
    right_side = jnp.concatenate([upper_rows, lower_rows], axis=0)
    return jnp.dot(left_side, right_side, preferred_element_type=jnp.float32)


CHUNK = 256


def exp_neg(angle):
    return jnp.cos(angle), -jnp.sin(angle)


def exchange_inputs(spec_ref, lag_ref, slow_ref, spec_in, lag_in, slow_in, local_sem, send_sem, recv_sem):
    count = spec_in.shape[0]
    me = lax.axis_index("sta")
    tile = lax.axis_index("grid")
    mesh_ids = pl.DeviceIdType.MESH
    barrier = pltpu.get_barrier_semaphore()
    for shift in range(1, count):
        peer = lax.rem(me + shift, count)
        pl.semaphore_signal(barrier, inc=1, device_id=(tile, peer), device_id_type=mesh_ids)
    pl.semaphore_wait(barrier, count - 1)
    pairs = ((spec_ref, spec_in), (lag_ref, lag_in), (slow_ref, slow_in))
    local = []
    for kind, (source, target) in enumerate(pairs):
        own = source.at[me] if kind == 0 else source
        copy = pltpu.make_async_copy(own, target.at[me], local_sem.at[kind])
        copy.start()
        local.append(copy)
    sends = []
    for shift in range(1, count):
        peer = lax.rem(me + shift, count)
        for kind, (source, target) in enumerate(pairs):
            part = source.at[peer] if kind == 0 else source
            copy = pltpu.make_async_remote_copy(
                src_ref=part,
                dst_ref=target.at[me],
                send_sem=send_sem.at[kind, shift],
                recv_sem=recv_sem.at[kind, me],
                device_id=(tile, peer),
                device_id_type=mesh_ids,
            )
            copy.start()
            sends.append(copy)
    for copy in local:
        copy.wait()
    for copy in sends:
        copy.wait_send()
    for shift in range(1, count):
        source_id = lax.rem(me + count - shift, count)
        for kind, (source, target) in enumerate(pairs):
            part = source.at[source_id] if kind == 0 else source
            pltpu.make_async_remote_copy(
                src_ref=part,
                dst_ref=target.at[source_id],
                send_sem=send_sem.at[kind, shift],
                recv_sem=recv_sem.at[kind, source_id],
                device_id=(tile, source_id),
                device_id_type=mesh_ids,
            ).wait_recv()


def align_inputs(spec_in, lag_in, slow_in, real_ref, imag_ref, turn_ref):
    count, bins, block = spec_in.shape[0], spec_in.shape[2], spec_in.shape[3]
    first_bin = lax.axis_index("sta") * bins
    bin_rows = (F0 + first_bin + lax.broadcasted_iota(jnp.int32, (bins, block), 0)).astype(jnp.float32)
    for source in range(count):
        cols = slice(source * block, (source + 1) * block)
        product = bin_rows * lag_in[source].astype(jnp.float32)
        whole = jnp.floor(product * (1.0 / NT))
        left = product - whole * NT
        left = jnp.where(left < 0.0, left + NT, left)
        left = jnp.where(left >= NT, left - NT, left)
        turned = left * (TWO_PI / NT)
        cosine = jnp.cos(turned)
        sine = jnp.sin(turned)
        real_in = spec_in[source, 0].astype(jnp.float32)
        imag_in = spec_in[source, 1].astype(jnp.float32)
        real_ref[:, cols] = (real_in * cosine + imag_in * sine).astype(jnp.bfloat16).astype(jnp.float32)
        imag_ref[:, cols] = (imag_in * cosine - real_in * sine).astype(jnp.bfloat16).astype(jnp.float32)
        turn_ref[:, cols] = slow_in[source].astype(jnp.float32)


def beam_kernel(spec_ref, lag_ref, slow_ref, power_ref, spec_in, lag_in, slow_in, local_sem, send_sem, recv_sem,
                real_ref, imag_ref, turn_ref, acc_ref, left_ref, right_ref):
    exchange_inputs(spec_ref, lag_ref, slow_ref, spec_in, lag_in, slow_in, local_sem, send_sem, recv_sem)
    align_inputs(spec_in, lag_in, slow_in, real_ref, imag_ref, turn_ref)
    bins, stations = real_ref.shape
    first_bin = lax.axis_index("sta") * bins
    width = CHUNK
    rows8 = lax.broadcasted_iota(jnp.int32, (8, width), 0).astype(jnp.float32)
    rows16 = lax.broadcasted_iota(jnp.int32, (16, width), 0).astype(jnp.float32)
    power_ref[...] = jnp.zeros_like(power_ref)

    def per_bin(f, carry):
        omega = (F0 + first_bin + f).astype(jnp.float32) * (TWO_PI / NT)
        acc_ref[...] = jnp.zeros_like(acc_ref)

        def per_chunk(k, inner):
            cols = pl.ds(pl.multiple_of(k * width, width), width)
            turn_x = omega * turn_ref[0:1, cols]
            turn_y = omega * turn_ref[1:2, cols]
            turn_z = omega * turn_ref[2:3, cols]
            real_in = real_ref[pl.ds(f, 1), cols]
            imag_in = imag_ref[pl.ds(f, 1), cols]
            a_r, a_i = exp_neg(turn_x * (rows8 - 3.5))
            b_r, b_i = exp_neg(turn_x * (8.0 * (rows8 - 1.5)))
            y_r, y_i = exp_neg(turn_y * (rows8 - 3.5))
            c_r, c_i = exp_neg(turn_z * (rows16 - 7.5))
            d_r, d_i = exp_neg(turn_z * (16.0 * (rows8 - 3.5)))
            for m in range(CX // 8):
                bm_r, bm_i = b_r[m : m + 1], b_i[m : m + 1]
                x_r = bm_r * a_r - bm_i * a_i
                x_i = bm_r * a_i + bm_i * a_r
                p_r = real_in * x_r - imag_in * x_i
                p_i = real_in * x_i + imag_in * x_r
                for j in range(0, 8, 2):
                    parts_r, parts_i = [], []
                    for jj in (j, j + 1):
                        px_r, px_i = p_r[jj : jj + 1], p_i[jj : jj + 1]
                        parts_r.append(px_r * y_r - px_i * y_i)
                        parts_i.append(px_r * y_i + px_i * y_r)
                    row = (8 * m + j) * CY
                    left_ref[row : row + 16, 0:width] = jnp.concatenate(parts_r, axis=0).astype(jnp.bfloat16)
                    left_ref[row : row + 16, width : 2 * width] = jnp.concatenate(parts_i, axis=0).astype(jnp.bfloat16)
            for m in range(CZ // 16):
                dm_r, dm_i = d_r[m : m + 1], d_i[m : m + 1]
                z_r = dm_r * c_r - dm_i * c_i
                z_i = dm_r * c_i + dm_i * c_r
                cos_z = z_r.astype(jnp.bfloat16)
                sin_z = (-z_i).astype(jnp.bfloat16)
                row = 16 * m
                right_ref[row : row + 16, 0:width] = cos_z
                right_ref[row : row + 16, width : 2 * width] = sin_z
                right_ref[CZ + row : CZ + row + 16, 0:width] = -sin_z
                right_ref[CZ + row : CZ + row + 16, width : 2 * width] = cos_z
            acc_ref[...] += lax.dot_general(
                left_ref[...], right_ref[...], (((1,), (1,)), ((), ())), preferred_element_type=jnp.float32
            )
            return inner

        lax.fori_loop(0, stations // width, per_chunk, 0)
        beams = acc_ref[...]
        squares = beams * beams
        power_ref[...] += squares[:, :CZ] + squares[:, CZ:]
        return carry

    lax.fori_loop(0, bins, per_bin, 0)


def beam_power(spec_send, lag_row, slow_rows):
    count = spec_send.shape[0]
    bins, block = spec_send.shape[2], spec_send.shape[3]
    width = CHUNK
    stations = count * block
    vmem = pl.BlockSpec(memory_space=pltpu.VMEM)
    return pl.pallas_call(
        beam_kernel,
        out_shape=jax.ShapeDtypeStruct((CX * CY, CZ), jnp.float32),
        in_specs=[vmem, vmem, vmem],
        out_specs=vmem,
        scratch_shapes=[
            pltpu.VMEM((count,) + spec_send.shape[1:], jnp.bfloat16),
            pltpu.VMEM((count,) + lag_row.shape, jnp.int32),
            pltpu.VMEM((count,) + slow_rows.shape, jnp.bfloat16),
            pltpu.SemaphoreType.DMA((3,)),
            pltpu.SemaphoreType.DMA((3, count)),
            pltpu.SemaphoreType.DMA((3, count)),
            pltpu.VMEM((bins, stations), jnp.float32),
            pltpu.VMEM((bins, stations), jnp.float32),
            pltpu.VMEM((slow_rows.shape[0], stations), jnp.float32),
            pltpu.VMEM((CX * CY, 2 * CZ), jnp.float32),
            pltpu.VMEM((CX * CY, 2 * width), jnp.bfloat16),
            pltpu.VMEM((2 * CZ, 2 * width), jnp.bfloat16),
        ],
        compiler_params=pltpu.CompilerParams(collective_id=1, has_side_effects=True),
    )(spec_send, lag_row, slow_rows)


def sum_kernel(part_ref, out_ref, recv_ref, local_sem, send_sem, recv_sem):
    count = recv_ref.shape[0]
    me = lax.axis_index("sta")
    tile = lax.axis_index("grid")
    barrier = pltpu.get_barrier_semaphore()
    for shift in range(1, count):
        peer = lax.rem(me + shift, count)
        pl.semaphore_signal(barrier, inc=1, device_id=(tile, peer), device_id_type=pl.DeviceIdType.MESH)
    pl.semaphore_wait(barrier, count - 1)
    own = pltpu.make_async_copy(part_ref, recv_ref.at[me], local_sem.at[0])
    own.start()
    copies = []
    for shift in range(1, count):
        peer = lax.rem(me + shift, count)
        copy = pltpu.make_async_remote_copy(
            src_ref=part_ref,
            dst_ref=recv_ref.at[me],
            send_sem=send_sem.at[shift],
            recv_sem=recv_sem.at[me],
            device_id=(tile, peer),
            device_id_type=pl.DeviceIdType.MESH,
        )
        copy.start()
        copies.append(copy)
    own.wait()
    for shift in range(1, count):
        copies[shift - 1].wait_send()
        source = lax.rem(me + count - shift, count)
        pltpu.make_async_remote_copy(
            src_ref=part_ref,
            dst_ref=recv_ref.at[source],
            send_sem=send_sem.at[shift],
            recv_sem=recv_sem.at[source],
            device_id=(tile, source),
            device_id_type=pl.DeviceIdType.MESH,
        ).wait_recv()
    total = recv_ref[0]
    for source in range(1, count):
        total = total + recv_ref[source]
    out_ref[...] = total


def sum_over_sta(part):
    count = lax.axis_size("sta")
    return pl.pallas_call(
        sum_kernel,
        out_shape=jax.ShapeDtypeStruct(part.shape, jnp.float32),
        in_specs=[pl.BlockSpec(memory_space=pltpu.VMEM)],
        out_specs=pl.BlockSpec(memory_space=pltpu.VMEM),
        scratch_shapes=[
            pltpu.VMEM((count,) + part.shape, jnp.float32),
            pltpu.SemaphoreType.DMA((1,)),
            pltpu.SemaphoreType.DMA((count,)),
            pltpu.SemaphoreType.DMA((count,)),
        ],
        compiler_params=pltpu.CompilerParams(collective_id=0, has_side_effects=True),
    )(part)


def freq_beams(freq_ids, aligned_rows, slow_rows):
    return lax.map(lambda pair: beam_freq(pair[0], pair[1], slow_rows), (freq_ids, aligned_rows))


def band_matrix(taps, length):
    rows = jnp.arange(length, dtype=jnp.int32)[:, None]
    columns = jnp.arange(length + 2 * HALF, dtype=jnp.int32)[None, :]
    offset = columns - rows
    picks = jnp.arange(TAPS, dtype=jnp.int32)[:, None, None]
    return jnp.sum(jnp.where(offset[None] == picks, taps[:, None, None], 0.0), axis=0)


def blur(volume, bands):
    band_x, square_y, square_z = bands
    padded = with_halo(volume.astype(jnp.bfloat16), (("grid", 0),), HALF).astype(volume.dtype)
    along_x = jnp.einsum("ip,pyz->iyz", band_x, padded, precision=lax.Precision.HIGHEST)
    along_y = jnp.einsum("jq,xqz->xjz", square_y, along_x, precision=lax.Precision.HIGHEST)
    return jnp.einsum("xyw,kw->xyk", along_y, square_z, precision=lax.Precision.HIGHEST)


def blur_narrowing(volume, taps, square_y, square_z):
    band_x = band_matrix(taps, volume.shape[0] - 2 * HALF)
    along_x = jnp.einsum("ip,pyz->iyz", band_x, volume, precision=lax.Precision.HIGHEST)
    along_y = jnp.einsum("jq,xqz->xjz", square_y, along_x, precision=lax.Precision.HIGHEST)
    return jnp.einsum("xyw,kw->xyk", along_y, square_z, precision=lax.Precision.HIGHEST)


def deblur(stacked, spread_taps):
    tiles = lax.axis_size("grid")
    me = lax.axis_index("grid")
    reach = ITERS * 2 * HALF
    halo_tiles = -(-reach // CX)
    before = [
        lax.ppermute(stacked, "grid", [(i, i + k) for i in range(tiles - k)])
        for k in range(halo_tiles, 0, -1)
    ]
    after = [
        lax.ppermute(stacked, "grid", [(i + k, i) for i in range(tiles - k)])
        for k in range(1, halo_tiles + 1)
    ]
    cut = halo_tiles * CX - reach
    observed = jnp.concatenate(before + [stacked] + after, axis=0)
    observed = observed[cut : observed.shape[0] - cut]
    width = observed.shape[0]
    cell = (me - halo_tiles) * CX + cut + jnp.arange(width, dtype=jnp.int32)
    inside = (cell >= 0) & (cell < tiles * CX)
    square_y = band_matrix(spread_taps[1], CY)[:, HALF : HALF + CY]
    square_z = band_matrix(spread_taps[2], CZ)[:, HALF : HALF + CZ]
    estimate = observed
    for sweep in range(ITERS):
        low = 2 * HALF * sweep + HALF
        blurred = blur_narrowing(estimate, spread_taps[0], square_y, square_z)
        ratio = jnp.where(
            inside[low : width - low, None, None], observed[low : width - low] / blurred, 0.0
        )
        estimate = estimate[2 * HALF : estimate.shape[0] - 2 * HALF] * blur_narrowing(
            ratio, spread_taps[0], square_y, square_z
        )
    return estimate


def per_device(spectra, lag_samples, slowness, spread_taps):
    groups = lax.axis_size("sta")
    own_count = FREQS // groups
    first_bin = lax.axis_index("sta") * own_count
    block = spectra.shape[2]
    spec_send = spectra.reshape(groups, own_count, 2, block).transpose(0, 2, 1, 3)
    local_power = beam_power(spec_send, lag_samples, slowness[0])
    summed = sum_over_sta(local_power)
    stacked = (summed / (FREQS * STATIONS) + BACKGROUND).reshape(CX, CY, CZ)
    estimate = deblur(stacked, spread_taps)
    return (stacked[None], estimate[None])


def solution(mesh):
    placed = (P(None, None, "sta"), P("grid", "sta"), P("grid", None, "sta"), P())
    return jax.shard_map(
        per_device,
        mesh=mesh,
        in_specs=placed,
        out_specs=(P("grid", None, None, None), P("grid", None, None, None)),
        check_vma=False,
    )
```

```python
import math

import jax
import jax.numpy as jnp
from jax import lax
from jax.sharding import PartitionSpec as P
from jax.experimental import pallas as pl
from jax.experimental.pallas import tpu as pltpu

STATIONS = 6144
FREQS = 64
F0 = 600
NT = 6000
TAPS = 17
HALF = 8
ITERS = 4
CX = 32
CY = 8
CZ = 128


TWO_PI = 2.0 * math.pi
BACKGROUND = 0.05


def with_halo(array, sides, width):
    for axis, dim in sides:
        size, length = (lax.axis_size(axis), array.shape[dim])
        up = [(i, (i + 1) % size) for i in range(size - 1)]
        down = [(j, i) for i, j in up]
        last = lax.slice_in_dim(array, length - width, length, axis=dim)
        leading = lax.slice_in_dim(array, 0, width, axis=dim)
        before = lax.ppermute(last, axis, up)
        after = lax.ppermute(leading, axis, down)
        array = jnp.concatenate([before, array, after], axis=dim)
    return array


def align_rows(spectra, lag_row):
    bins = F0 + jnp.arange(FREQS, dtype=jnp.int32)
    cycles = bins[:, None] * lag_row[None, :] % NT
    turned = cycles.astype(jnp.float32) * (TWO_PI / NT)
    cosine = jnp.cos(turned)
    sine = jnp.sin(turned)
    real_in = spectra[:, 0, :].astype(jnp.float32)
    imag_in = spectra[:, 1, :].astype(jnp.float32)
    real_out = real_in * cosine + imag_in * sine
    imag_out = imag_in * cosine - real_in * sine
    return jnp.stack([real_out, imag_out], axis=1).astype(jnp.bfloat16)


def beam_freq(freq, aligned_row, slow_rows):
    omega = (F0 + freq).astype(jnp.float32) * (TWO_PI / NT)
    slow = slow_rows.astype(jnp.float32)
    x_coord = jnp.arange(CX, dtype=jnp.float32) - (CX - 1) / 2.0
    y_coord = jnp.arange(CY, dtype=jnp.float32) - (CY - 1) / 2.0
    z_coord = jnp.arange(CZ, dtype=jnp.float32) - (CZ - 1) / 2.0
    phase_x = (omega * slow[0])[None, :] * x_coord[:, None]
    phase_y = (omega * slow[1])[None, :] * y_coord[:, None]
    phase = phase_x[:, None, :] + phase_y[None, :, :]
    cosine = jnp.cos(phase)
    sine = jnp.sin(phase)
    real_in = aligned_row[0].astype(jnp.float32)[None, None, :]
    imag_in = aligned_row[1].astype(jnp.float32)[None, None, :]
    front_real = (real_in * cosine + imag_in * sine).astype(jnp.bfloat16).reshape(CX * CY, -1)
    front_imag = (imag_in * cosine - real_in * sine).astype(jnp.bfloat16).reshape(CX * CY, -1)
    left_side = jnp.concatenate([front_real, front_imag], axis=1)
    phase_z = (omega * slow[2])[:, None] * z_coord[None, :]
    depth_real = jnp.cos(phase_z).astype(jnp.bfloat16)
    depth_imag = jnp.sin(phase_z).astype(jnp.bfloat16)
    upper_rows = jnp.concatenate([depth_real, -depth_imag], axis=1)
    lower_rows = jnp.concatenate([depth_imag, depth_real], axis=1)
    right_side = jnp.concatenate([upper_rows, lower_rows], axis=0)
    return jnp.dot(left_side, right_side, preferred_element_type=jnp.float32)


CHUNK = 256


def exp_neg(angle):
    return jnp.cos(angle), -jnp.sin(angle)


def exchange_inputs(spec_ref, lag_ref, slow_ref, spec_in, lag_in, slow_in, local_sem, send_sem, recv_sem):
    count = spec_in.shape[0]
    me = lax.axis_index("sta")
    tile = lax.axis_index("grid")
    mesh_ids = pl.DeviceIdType.MESH
    barrier = pltpu.get_barrier_semaphore()
    for shift in range(1, count):
        peer = lax.rem(me + shift, count)
        pl.semaphore_signal(barrier, inc=1, device_id=(tile, peer), device_id_type=mesh_ids)
    pl.semaphore_wait(barrier, count - 1)
    pairs = ((spec_ref, spec_in), (lag_ref, lag_in), (slow_ref, slow_in))
    local = []
    for kind, (source, target) in enumerate(pairs):
        own = source.at[me] if kind == 0 else source
        copy = pltpu.make_async_copy(own, target.at[me], local_sem.at[kind])
        copy.start()
        local.append(copy)
    sends = []
    for shift in range(1, count):
        peer = lax.rem(me + shift, count)
        for kind, (source, target) in enumerate(pairs):
            part = source.at[peer] if kind == 0 else source
            copy = pltpu.make_async_remote_copy(
                src_ref=part,
                dst_ref=target.at[me],
                send_sem=send_sem.at[kind, shift],
                recv_sem=recv_sem.at[kind, me],
                device_id=(tile, peer),
                device_id_type=mesh_ids,
            )
            copy.start()
            sends.append(copy)
    for copy in local:
        copy.wait()
    for copy in sends:
        copy.wait_send()
    for shift in range(1, count):
        source_id = lax.rem(me + count - shift, count)
        for kind, (source, target) in enumerate(pairs):
            part = source.at[source_id] if kind == 0 else source
            pltpu.make_async_remote_copy(
                src_ref=part,
                dst_ref=target.at[source_id],
                send_sem=send_sem.at[kind, shift],
                recv_sem=recv_sem.at[kind, source_id],
                device_id=(tile, source_id),
                device_id_type=mesh_ids,
            ).wait_recv()


def align_inputs(spec_in, lag_in, slow_in, real_ref, imag_ref, turn_ref):
    count, bins, block = spec_in.shape[0], spec_in.shape[2], spec_in.shape[3]
    first_bin = lax.axis_index("sta") * bins
    bin_rows = (F0 + first_bin + lax.broadcasted_iota(jnp.int32, (bins, block), 0)).astype(jnp.float32)
    for source in range(count):
        cols = slice(source * block, (source + 1) * block)
        product = bin_rows * lag_in[source].astype(jnp.float32)
        whole = jnp.floor(product * (1.0 / NT))
        left = product - whole * NT
        left = jnp.where(left < 0.0, left + NT, left)
        left = jnp.where(left >= NT, left - NT, left)
        turned = left * (TWO_PI / NT)
        cosine = jnp.cos(turned)
        sine = jnp.sin(turned)
        real_in = spec_in[source, 0].astype(jnp.float32)
        imag_in = spec_in[source, 1].astype(jnp.float32)
        real_ref[:, cols] = (real_in * cosine + imag_in * sine).astype(jnp.bfloat16).astype(jnp.float32)
        imag_ref[:, cols] = (imag_in * cosine - real_in * sine).astype(jnp.bfloat16).astype(jnp.float32)
        turn_ref[:, cols] = slow_in[source].astype(jnp.float32)


def complex_times(left, right):
    return left[0] * right[0] - left[1] * right[1], left[0] * right[1] + left[1] * right[0]


def factor_rows(turn_x, turn_y, turn_z, rows8, rows16):
    return (
        exp_neg(turn_x * (rows8 - 3.5)),
        exp_neg(turn_x * (8.0 * (rows8 - 1.5))),
        exp_neg(turn_y * (rows8 - 3.5)),
        exp_neg(turn_z * (rows16 - 7.5)),
        exp_neg(turn_z * (16.0 * (rows8 - 3.5))),
    )


def beam_kernel(spec_ref, lag_ref, slow_ref, power_ref, spec_in, lag_in, slow_in, local_sem, send_sem, recv_sem,
                real_ref, imag_ref, turn_ref, acc_ref, left_ref, right_ref):
    exchange_inputs(spec_ref, lag_ref, slow_ref, spec_in, lag_in, slow_in, local_sem, send_sem, recv_sem)
    align_inputs(spec_in, lag_in, slow_in, real_ref, imag_ref, turn_ref)
    bins, stations = real_ref.shape
    first_bin = lax.axis_index("sta") * bins
    width = CHUNK
    rows8 = lax.broadcasted_iota(jnp.int32, (8, width), 0).astype(jnp.float32)
    rows16 = lax.broadcasted_iota(jnp.int32, (16, width), 0).astype(jnp.float32)
    omega0 = (F0 + first_bin).astype(jnp.float32) * (TWO_PI / NT)
    step = TWO_PI / NT
    acc_ref[...] = jnp.zeros_like(acc_ref)

    def per_chunk(k, carry):
        cols = pl.ds(pl.multiple_of(k * width, width), width)
        slow_x = turn_ref[0:1, cols]
        slow_y = turn_ref[1:2, cols]
        slow_z = turn_ref[2:3, cols]
        start = factor_rows(omega0 * slow_x, omega0 * slow_y, omega0 * slow_z, rows8, rows16)
        ratio = factor_rows(step * slow_x, step * slow_y, step * slow_z, rows8, rows16)

        def per_bin(f, state):
            (a_r, a_i), (b_r, b_i), (y_r, y_i), (c_r, c_i), (d_r, d_i) = state
            real_in = real_ref[pl.ds(f, 1), cols]
            imag_in = imag_ref[pl.ds(f, 1), cols]
            groups_r, groups_i = [], []
            for m in range(CX // 8):
                x_r, x_i = complex_times((b_r[m : m + 1], b_i[m : m + 1]), (a_r, a_i))
                groups_r.append(real_in * x_r - imag_in * x_i)
                groups_i.append(real_in * x_i + imag_in * x_r)
            for y in range(CY):
                yy_r, yy_i = y_r[y : y + 1], y_i[y : y + 1]
                for m in range(0, CX // 8, 2):
                    parts_r, parts_i = [], []
                    for mm in (m, m + 1):
                        parts_r.append(groups_r[mm] * yy_r - groups_i[mm] * yy_i)
                        parts_i.append(groups_r[mm] * yy_i + groups_i[mm] * yy_r)
                    row = y * CX + 8 * m
                    left_ref[row : row + 16, 0:width] = jnp.concatenate(parts_r, axis=0).astype(jnp.bfloat16)
                    left_ref[row : row + 16, width : 2 * width] = jnp.concatenate(parts_i, axis=0).astype(jnp.bfloat16)
            for m in range(CZ // 16):
                z_r, z_i = complex_times((d_r[m : m + 1], d_i[m : m + 1]), (c_r, c_i))
                cos_z = z_r.astype(jnp.bfloat16)
                sin_z = (-z_i).astype(jnp.bfloat16)
                row = 16 * m
                right_ref[row : row + 16, 0:width] = cos_z
                right_ref[row : row + 16, width : 2 * width] = sin_z
                right_ref[CZ + row : CZ + row + 16, 0:width] = -sin_z
                right_ref[CZ + row : CZ + row + 16, width : 2 * width] = cos_z
            acc_ref[f] += lax.dot_general(
                left_ref[...], right_ref[...], (((1,), (1,)), ((), ())), preferred_element_type=jnp.float32
            )
            return tuple(complex_times(now, turn) for now, turn in zip(state, ratio))

        lax.fori_loop(0, bins, per_bin, start)
        return carry

    lax.fori_loop(0, stations // width, per_chunk, 0)
    total = jnp.zeros(power_ref.shape, jnp.float32)
    for f in range(bins):
        beams = acc_ref[f]
        squares = beams * beams
        total = total + squares[:, :CZ] + squares[:, CZ:]
    power_ref[...] = total


def beam_power(spec_send, lag_row, slow_rows):
    count = spec_send.shape[0]
    bins, block = spec_send.shape[2], spec_send.shape[3]
    width = CHUNK
    stations = count * block
    vmem = pl.BlockSpec(memory_space=pltpu.VMEM)
    return pl.pallas_call(
        beam_kernel,
        out_shape=jax.ShapeDtypeStruct((CX * CY, CZ), jnp.float32),
        in_specs=[vmem, vmem, vmem],
        out_specs=vmem,
        scratch_shapes=[
            pltpu.VMEM((count,) + spec_send.shape[1:], jnp.bfloat16),
            pltpu.VMEM((count,) + lag_row.shape, jnp.int32),
            pltpu.VMEM((count,) + slow_rows.shape, jnp.bfloat16),
            pltpu.SemaphoreType.DMA((3,)),
            pltpu.SemaphoreType.DMA((3, count)),
            pltpu.SemaphoreType.DMA((3, count)),
            pltpu.VMEM((bins, stations), jnp.float32),
            pltpu.VMEM((bins, stations), jnp.float32),
            pltpu.VMEM((slow_rows.shape[0], stations), jnp.float32),
            pltpu.VMEM((bins, CX * CY, 2 * CZ), jnp.float32),
            pltpu.VMEM((CX * CY, 2 * width), jnp.bfloat16),
            pltpu.VMEM((2 * CZ, 2 * width), jnp.bfloat16),
        ],
        compiler_params=pltpu.CompilerParams(collective_id=1, has_side_effects=True),
    )(spec_send, lag_row, slow_rows)


def sum_kernel(part_ref, out_ref, recv_ref, local_sem, send_sem, recv_sem):
    count = recv_ref.shape[0]
    me = lax.axis_index("sta")
    tile = lax.axis_index("grid")
    barrier = pltpu.get_barrier_semaphore()
    for shift in range(1, count):
        peer = lax.rem(me + shift, count)
        pl.semaphore_signal(barrier, inc=1, device_id=(tile, peer), device_id_type=pl.DeviceIdType.MESH)
    pl.semaphore_wait(barrier, count - 1)
    own = pltpu.make_async_copy(part_ref, recv_ref.at[me], local_sem.at[0])
    own.start()
    copies = []
    for shift in range(1, count):
        peer = lax.rem(me + shift, count)
        copy = pltpu.make_async_remote_copy(
            src_ref=part_ref,
            dst_ref=recv_ref.at[me],
            send_sem=send_sem.at[shift],
            recv_sem=recv_sem.at[me],
            device_id=(tile, peer),
            device_id_type=pl.DeviceIdType.MESH,
        )
        copy.start()
        copies.append(copy)
    own.wait()
    for shift in range(1, count):
        copies[shift - 1].wait_send()
        source = lax.rem(me + count - shift, count)
        pltpu.make_async_remote_copy(
            src_ref=part_ref,
            dst_ref=recv_ref.at[source],
            send_sem=send_sem.at[shift],
            recv_sem=recv_sem.at[source],
            device_id=(tile, source),
            device_id_type=pl.DeviceIdType.MESH,
        ).wait_recv()
    total = recv_ref[0]
    for source in range(1, count):
        total = total + recv_ref[source]
    out_ref[...] = total


def sum_over_sta(part):
    count = lax.axis_size("sta")
    return pl.pallas_call(
        sum_kernel,
        out_shape=jax.ShapeDtypeStruct(part.shape, jnp.float32),
        in_specs=[pl.BlockSpec(memory_space=pltpu.VMEM)],
        out_specs=pl.BlockSpec(memory_space=pltpu.VMEM),
        scratch_shapes=[
            pltpu.VMEM((count,) + part.shape, jnp.float32),
            pltpu.SemaphoreType.DMA((1,)),
            pltpu.SemaphoreType.DMA((count,)),
            pltpu.SemaphoreType.DMA((count,)),
        ],
        compiler_params=pltpu.CompilerParams(collective_id=0, has_side_effects=True),
    )(part)


def freq_beams(freq_ids, aligned_rows, slow_rows):
    return lax.map(lambda pair: beam_freq(pair[0], pair[1], slow_rows), (freq_ids, aligned_rows))


def band_matrix(taps, length):
    rows = jnp.arange(length, dtype=jnp.int32)[:, None]
    columns = jnp.arange(length + 2 * HALF, dtype=jnp.int32)[None, :]
    offset = columns - rows
    picks = jnp.arange(TAPS, dtype=jnp.int32)[:, None, None]
    return jnp.sum(jnp.where(offset[None] == picks, taps[:, None, None], 0.0), axis=0)


def blur(volume, bands):
    band_x, square_y, square_z = bands
    padded = with_halo(volume.astype(jnp.bfloat16), (("grid", 0),), HALF).astype(volume.dtype)
    along_x = jnp.einsum("ip,pyz->iyz", band_x, padded, precision=lax.Precision.HIGHEST)
    along_y = jnp.einsum("jq,xqz->xjz", square_y, along_x, precision=lax.Precision.HIGHEST)
    return jnp.einsum("xyw,kw->xyk", along_y, square_z, precision=lax.Precision.HIGHEST)


def blur_narrowing(volume, taps, square_y, square_z):
    band_x = band_matrix(taps, volume.shape[0] - 2 * HALF)
    along_x = jnp.einsum("ip,pyz->iyz", band_x, volume, precision=lax.Precision.HIGHEST)
    along_y = jnp.einsum("jq,xqz->xjz", square_y, along_x, precision=lax.Precision.HIGHEST)
    return jnp.einsum("xyw,kw->xyk", along_y, square_z, precision=lax.Precision.HIGHEST)


def deblur(stacked, spread_taps):
    tiles = lax.axis_size("grid")
    me = lax.axis_index("grid")
    reach = ITERS * 2 * HALF
    halo_tiles = -(-reach // CX)
    before = [
        lax.ppermute(stacked, "grid", [(i, i + k) for i in range(tiles - k)])
        for k in range(halo_tiles, 0, -1)
    ]
    after = [
        lax.ppermute(stacked, "grid", [(i + k, i) for i in range(tiles - k)])
        for k in range(1, halo_tiles + 1)
    ]
    cut = halo_tiles * CX - reach
    observed = jnp.concatenate(before + [stacked] + after, axis=0)
    observed = observed[cut : observed.shape[0] - cut]
    width = observed.shape[0]
    cell = (me - halo_tiles) * CX + cut + jnp.arange(width, dtype=jnp.int32)
    inside = (cell >= 0) & (cell < tiles * CX)
    square_y = band_matrix(spread_taps[1], CY)[:, HALF : HALF + CY]
    square_z = band_matrix(spread_taps[2], CZ)[:, HALF : HALF + CZ]
    estimate = observed
    for sweep in range(ITERS):
        low = 2 * HALF * sweep + HALF
        blurred = blur_narrowing(estimate, spread_taps[0], square_y, square_z)
        ratio = jnp.where(
            inside[low : width - low, None, None], observed[low : width - low] / blurred, 0.0
        )
        estimate = estimate[2 * HALF : estimate.shape[0] - 2 * HALF] * blur_narrowing(
            ratio, spread_taps[0], square_y, square_z
        )
    return estimate


def per_device(spectra, lag_samples, slowness, spread_taps):
    groups = lax.axis_size("sta")
    own_count = FREQS // groups
    first_bin = lax.axis_index("sta") * own_count
    block = spectra.shape[2]
    spec_send = spectra.reshape(groups, own_count, 2, block).transpose(0, 2, 1, 3)
    local_power = beam_power(spec_send, lag_samples, slowness[0])
    summed = sum_over_sta(local_power)
    stacked = (summed / (FREQS * STATIONS) + BACKGROUND).reshape(CY, CX, CZ).transpose(1, 0, 2)
    estimate = deblur(stacked, spread_taps)
    return (stacked[None], estimate[None])


def solution(mesh):
    placed = (P(None, None, "sta"), P("grid", "sta"), P("grid", None, "sta"), P())
    return jax.shard_map(
        per_device,
        mesh=mesh,
        in_specs=placed,
        out_specs=(P("grid", None, None, None), P("grid", None, None, None)),
        check_vma=False,
    )
```

```python
import math

import jax
import jax.numpy as jnp
from jax import lax
from jax.sharding import PartitionSpec as P
from jax.experimental import pallas as pl
from jax.experimental.pallas import tpu as pltpu

STATIONS = 6144
FREQS = 64
F0 = 600
NT = 6000
TAPS = 17
HALF = 8
ITERS = 4
CX = 32
CY = 8
CZ = 128


TWO_PI = 2.0 * math.pi
BACKGROUND = 0.05


def with_halo(array, sides, width):
    for axis, dim in sides:
        size, length = (lax.axis_size(axis), array.shape[dim])
        up = [(i, (i + 1) % size) for i in range(size - 1)]
        down = [(j, i) for i, j in up]
        last = lax.slice_in_dim(array, length - width, length, axis=dim)
        leading = lax.slice_in_dim(array, 0, width, axis=dim)
        before = lax.ppermute(last, axis, up)
        after = lax.ppermute(leading, axis, down)
        array = jnp.concatenate([before, array, after], axis=dim)
    return array


def align_rows(spectra, lag_row):
    bins = F0 + jnp.arange(FREQS, dtype=jnp.int32)
    cycles = bins[:, None] * lag_row[None, :] % NT
    turned = cycles.astype(jnp.float32) * (TWO_PI / NT)
    cosine = jnp.cos(turned)
    sine = jnp.sin(turned)
    real_in = spectra[:, 0, :].astype(jnp.float32)
    imag_in = spectra[:, 1, :].astype(jnp.float32)
    real_out = real_in * cosine + imag_in * sine
    imag_out = imag_in * cosine - real_in * sine
    return jnp.stack([real_out, imag_out], axis=1).astype(jnp.bfloat16)


def beam_freq(freq, aligned_row, slow_rows):
    omega = (F0 + freq).astype(jnp.float32) * (TWO_PI / NT)
    slow = slow_rows.astype(jnp.float32)
    x_coord = jnp.arange(CX, dtype=jnp.float32) - (CX - 1) / 2.0
    y_coord = jnp.arange(CY, dtype=jnp.float32) - (CY - 1) / 2.0
    z_coord = jnp.arange(CZ, dtype=jnp.float32) - (CZ - 1) / 2.0
    phase_x = (omega * slow[0])[None, :] * x_coord[:, None]
    phase_y = (omega * slow[1])[None, :] * y_coord[:, None]
    phase = phase_x[:, None, :] + phase_y[None, :, :]
    cosine = jnp.cos(phase)
    sine = jnp.sin(phase)
    real_in = aligned_row[0].astype(jnp.float32)[None, None, :]
    imag_in = aligned_row[1].astype(jnp.float32)[None, None, :]
    front_real = (real_in * cosine + imag_in * sine).astype(jnp.bfloat16).reshape(CX * CY, -1)
    front_imag = (imag_in * cosine - real_in * sine).astype(jnp.bfloat16).reshape(CX * CY, -1)
    left_side = jnp.concatenate([front_real, front_imag], axis=1)
    phase_z = (omega * slow[2])[:, None] * z_coord[None, :]
    depth_real = jnp.cos(phase_z).astype(jnp.bfloat16)
    depth_imag = jnp.sin(phase_z).astype(jnp.bfloat16)
    upper_rows = jnp.concatenate([depth_real, -depth_imag], axis=1)
    lower_rows = jnp.concatenate([depth_imag, depth_real], axis=1)
    right_side = jnp.concatenate([upper_rows, lower_rows], axis=0)
    return jnp.dot(left_side, right_side, preferred_element_type=jnp.float32)


CHUNK = 256


def exp_neg(angle):
    return jnp.cos(angle), -jnp.sin(angle)


def exchange_inputs(spec_ref, lag_ref, slow_ref, spec_in, lag_in, slow_in, local_sem, send_sem, recv_sem):
    count = spec_in.shape[0]
    me = lax.axis_index("sta")
    tile = lax.axis_index("grid")
    mesh_ids = pl.DeviceIdType.MESH
    barrier = pltpu.get_barrier_semaphore()
    for shift in range(1, count):
        peer = lax.rem(me + shift, count)
        pl.semaphore_signal(barrier, inc=1, device_id=(tile, peer), device_id_type=mesh_ids)
    pl.semaphore_wait(barrier, count - 1)
    pairs = ((spec_ref, spec_in), (lag_ref, lag_in), (slow_ref, slow_in))
    local = []
    for kind, (source, target) in enumerate(pairs):
        own = source.at[me] if kind == 0 else source
        copy = pltpu.make_async_copy(own, target.at[me], local_sem.at[kind])
        copy.start()
        local.append(copy)
    sends = []
    for shift in range(1, count):
        peer = lax.rem(me + shift, count)
        for kind, (source, target) in enumerate(pairs):
            part = source.at[peer] if kind == 0 else source
            copy = pltpu.make_async_remote_copy(
                src_ref=part,
                dst_ref=target.at[me],
                send_sem=send_sem.at[kind, shift],
                recv_sem=recv_sem.at[kind, me],
                device_id=(tile, peer),
                device_id_type=mesh_ids,
            )
            copy.start()
            sends.append(copy)
    for copy in local:
        copy.wait()
    for copy in sends:
        copy.wait_send()
    for shift in range(1, count):
        source_id = lax.rem(me + count - shift, count)
        for kind, (source, target) in enumerate(pairs):
            part = source.at[source_id] if kind == 0 else source
            pltpu.make_async_remote_copy(
                src_ref=part,
                dst_ref=target.at[source_id],
                send_sem=send_sem.at[kind, shift],
                recv_sem=recv_sem.at[kind, source_id],
                device_id=(tile, source_id),
                device_id_type=mesh_ids,
            ).wait_recv()


def align_inputs(spec_in, lag_in, slow_in, real_ref, imag_ref, turn_ref):
    count, bins, block = spec_in.shape[0], spec_in.shape[2], spec_in.shape[3]
    first_bin = lax.axis_index("sta") * bins
    bin_rows = (F0 + first_bin + lax.broadcasted_iota(jnp.int32, (bins, block), 0)).astype(jnp.float32)
    for source in range(count):
        cols = slice(source * block, (source + 1) * block)
        product = bin_rows * lag_in[source].astype(jnp.float32)
        whole = jnp.floor(product * (1.0 / NT))
        left = product - whole * NT
        left = jnp.where(left < 0.0, left + NT, left)
        left = jnp.where(left >= NT, left - NT, left)
        turned = left * (TWO_PI / NT)
        cosine = jnp.cos(turned)
        sine = jnp.sin(turned)
        real_in = spec_in[source, 0].astype(jnp.float32)
        imag_in = spec_in[source, 1].astype(jnp.float32)
        real_ref[:, cols] = (real_in * cosine + imag_in * sine).astype(jnp.bfloat16).astype(jnp.float32)
        imag_ref[:, cols] = (imag_in * cosine - real_in * sine).astype(jnp.bfloat16).astype(jnp.float32)
        turn_ref[:, cols] = slow_in[source].astype(jnp.float32)


def complex_times(left, right):
    return left[0] * right[0] - left[1] * right[1], left[0] * right[1] + left[1] * right[0]


def factor_rows(turn_x, turn_y, turn_z, rows8, rows16):
    return (
        exp_neg(turn_x * (rows8 - 3.5)),
        exp_neg(turn_x * (8.0 * (rows8 - 1.5))),
        exp_neg(turn_y * (rows8 - 3.5)),
        exp_neg(turn_z * (rows16 - 7.5)),
        exp_neg(turn_z * (16.0 * (rows8 - 3.5))),
    )


def beam_kernel(spec_ref, lag_ref, slow_ref, power_ref, spec_in, lag_in, slow_in, local_sem, send_sem, recv_sem,
                real_ref, imag_ref, turn_ref, acc_ref, left_ref, right_ref):
    exchange_inputs(spec_ref, lag_ref, slow_ref, spec_in, lag_in, slow_in, local_sem, send_sem, recv_sem)
    align_inputs(spec_in, lag_in, slow_in, real_ref, imag_ref, turn_ref)
    bins, stations = real_ref.shape
    first_bin = lax.axis_index("sta") * bins
    width = CHUNK
    rows8 = lax.broadcasted_iota(jnp.int32, (8, width), 0).astype(jnp.float32)
    rows16 = lax.broadcasted_iota(jnp.int32, (16, width), 0).astype(jnp.float32)
    omega0 = (F0 + first_bin).astype(jnp.float32) * (TWO_PI / NT)
    step = TWO_PI / NT
    acc_ref[...] = jnp.zeros_like(acc_ref)

    def per_chunk(k, carry):
        cols = pl.ds(pl.multiple_of(k * width, width), width)
        slow_x = turn_ref[0:1, cols]
        slow_y = turn_ref[1:2, cols]
        slow_z = turn_ref[2:3, cols]
        start = factor_rows(omega0 * slow_x, omega0 * slow_y, omega0 * slow_z, rows8, rows16)
        ratio = factor_rows(step * slow_x, step * slow_y, step * slow_z, rows8, rows16)

        def per_bin(f, state):
            (a_r, a_i), (b_r, b_i), (y_r, y_i), (c_r, c_i), (d_r, d_i) = state
            real_in = real_ref[pl.ds(f, 1), cols]
            imag_in = imag_ref[pl.ds(f, 1), cols]
            groups_r, groups_i = [], []
            for m in range(CX // 8):
                x_r, x_i = complex_times((b_r[m : m + 1], b_i[m : m + 1]), (a_r, a_i))
                groups_r.append(real_in * x_r - imag_in * x_i)
                groups_i.append(real_in * x_i + imag_in * x_r)
            for y in range(CY):
                yy_r, yy_i = y_r[y : y + 1], y_i[y : y + 1]
                for m in range(0, CX // 8, 2):
                    parts_r, parts_i = [], []
                    for mm in (m, m + 1):
                        parts_r.append(groups_r[mm] * yy_r - groups_i[mm] * yy_i)
                        parts_i.append(groups_r[mm] * yy_i + groups_i[mm] * yy_r)
                    row = y * CX + 8 * m
                    left_ref[row : row + 16, 0:width] = jnp.concatenate(parts_r, axis=0).astype(jnp.bfloat16)
                    left_ref[row : row + 16, width : 2 * width] = jnp.concatenate(parts_i, axis=0).astype(jnp.bfloat16)
            for m in range(CZ // 16):
                z_r, z_i = complex_times((d_r[m : m + 1], d_i[m : m + 1]), (c_r, c_i))
                cos_z = z_r.astype(jnp.bfloat16)
                sin_z = (-z_i).astype(jnp.bfloat16)
                row = 16 * m
                right_ref[row : row + 16, 0:width] = cos_z
                right_ref[row : row + 16, width : 2 * width] = sin_z
                right_ref[CZ + row : CZ + row + 16, 0:width] = -sin_z
                right_ref[CZ + row : CZ + row + 16, width : 2 * width] = cos_z
            acc_ref[f] += lax.dot_general(
                left_ref[...], right_ref[...], (((1,), (1,)), ((), ())), preferred_element_type=jnp.float32
            )
            return tuple(complex_times(now, turn) for now, turn in zip(state, ratio))

        lax.fori_loop(0, bins, per_bin, start)
        return carry

    lax.fori_loop(0, stations // width, per_chunk, 0)
    total = jnp.zeros(power_ref.shape, jnp.float32)
    for f in range(bins):
        beams = acc_ref[f]
        squares = beams * beams
        total = total + squares[:, :CZ] + squares[:, CZ:]
    power_ref[...] = total


def beam_power(spec_send, lag_row, slow_rows):
    count = spec_send.shape[0]
    bins, block = spec_send.shape[2], spec_send.shape[3]
    width = CHUNK
    stations = count * block
    vmem = pl.BlockSpec(memory_space=pltpu.VMEM)
    return pl.pallas_call(
        beam_kernel,
        out_shape=jax.ShapeDtypeStruct((CX * CY, CZ), jnp.float32),
        in_specs=[vmem, vmem, vmem],
        out_specs=vmem,
        scratch_shapes=[
            pltpu.VMEM((count,) + spec_send.shape[1:], jnp.bfloat16),
            pltpu.VMEM((count,) + lag_row.shape, jnp.int32),
            pltpu.VMEM((count,) + slow_rows.shape, jnp.bfloat16),
            pltpu.SemaphoreType.DMA((3,)),
            pltpu.SemaphoreType.DMA((3, count)),
            pltpu.SemaphoreType.DMA((3, count)),
            pltpu.VMEM((bins, stations), jnp.float32),
            pltpu.VMEM((bins, stations), jnp.float32),
            pltpu.VMEM((slow_rows.shape[0], stations), jnp.float32),
            pltpu.VMEM((bins, CX * CY, 2 * CZ), jnp.float32),
            pltpu.VMEM((CX * CY, 2 * width), jnp.bfloat16),
            pltpu.VMEM((2 * CZ, 2 * width), jnp.bfloat16),
        ],
        compiler_params=pltpu.CompilerParams(collective_id=1, has_side_effects=True),
    )(spec_send, lag_row, slow_rows)


def share_kernel(part_ref, out_ref, pieces, send_rs, recv_rs, send_ag, recv_ag, local_sem):
    count = pieces.shape[0]
    slots = out_ref.shape[0]
    reach = slots // 2
    rows = pieces.shape[1]
    me = lax.axis_index("sta")
    tile = lax.axis_index("grid")
    tiles = lax.axis_size("grid")
    mesh_ids = pl.DeviceIdType.MESH
    barrier = pltpu.get_barrier_semaphore()
    for shift in range(1, count):
        pl.semaphore_signal(barrier, inc=1, device_id=(tile, lax.rem(me + shift, count)), device_id_type=mesh_ids)
    neighbours = jnp.int32(0)
    for k in range(-reach, reach + 1):
        if k == 0:
            continue
        there = (tile + k >= 0) & (tile + k < tiles)
        neighbours = neighbours + there.astype(jnp.int32)

        @pl.when(there)
        def _():
            for peer in range(count):
                pl.semaphore_signal(barrier, inc=1, device_id=(tile + k, peer), device_id_type=mesh_ids)

    pl.semaphore_wait(barrier, count - 1 + count * neighbours)
    own = pltpu.make_async_copy(part_ref.at[pl.ds(pl.multiple_of(me * rows, 8), rows)], pieces.at[me], local_sem.at[0])
    own.start()
    sends = []
    for shift in range(1, count):
        peer = lax.rem(me + shift, count)
        copy = pltpu.make_async_remote_copy(
            src_ref=part_ref.at[pl.ds(pl.multiple_of(peer * rows, 8), rows)],
            dst_ref=pieces.at[me],
            send_sem=send_rs.at[shift],
            recv_sem=recv_rs.at[me],
            device_id=(tile, peer),
            device_id_type=mesh_ids,
        )
        copy.start()
        sends.append(copy)
    own.wait()
    for copy in sends:
        copy.wait_send()
    for shift in range(1, count):
        source = lax.rem(me + count - shift, count)
        pltpu.make_async_remote_copy(
            src_ref=pieces.at[source],
            dst_ref=pieces.at[source],
            send_sem=send_rs.at[shift],
            recv_sem=recv_rs.at[source],
            device_id=(tile, source),
            device_id_type=mesh_ids,
        ).wait_recv()
    total = pieces[0]
    for source in range(1, count):
        total = total + pieces[source]
    mine = pl.ds(pl.multiple_of(me * rows, 8), rows)
    out_ref[reach, mine] = total
    block = out_ref.at[reach, mine]

    def gather_copy(k, peer, slot):
        return pltpu.make_async_remote_copy(
            src_ref=block,
            dst_ref=out_ref.at[slot, mine],
            send_sem=send_ag.at[slot, peer],
            recv_sem=recv_ag.at[slot, me],
            device_id=(tile + k, peer),
            device_id_type=mesh_ids,
        )

    peers = []
    for shift in range(1, count):
        copy = gather_copy(0, lax.rem(me + shift, count), reach)
        copy.start()
        peers.append(copy)
    for k in range(-reach, reach + 1):
        if k == 0:
            continue
        there = (tile + k >= 0) & (tile + k < tiles)

        @pl.when(there)
        def _():
            for peer in range(count):
                gather_copy(k, peer, reach - k).start()

        @pl.when(jnp.logical_not(there))
        def _():
            out_ref[reach + k] = jnp.zeros(out_ref.shape[1:], out_ref.dtype)

    for copy in peers:
        copy.wait_send()
    for shift in range(1, count):
        source = lax.rem(me + count - shift, count)
        pltpu.make_async_remote_copy(
            src_ref=block,
            dst_ref=out_ref.at[reach, pl.ds(pl.multiple_of(source * rows, 8), rows)],
            send_sem=send_ag.at[reach, source],
            recv_sem=recv_ag.at[reach, source],
            device_id=(tile, source),
            device_id_type=mesh_ids,
        ).wait_recv()
    for k in range(-reach, reach + 1):
        if k == 0:
            continue
        there = (tile + k >= 0) & (tile + k < tiles)

        @pl.when(there)
        def _():
            for peer in range(count):
                gather_copy(k, peer, reach - k).wait_send()
                pltpu.make_async_remote_copy(
                    src_ref=block,
                    dst_ref=out_ref.at[reach + k, pl.ds(peer * rows, rows)],
                    send_sem=send_ag.at[reach + k, peer],
                    recv_sem=recv_ag.at[reach + k, peer],
                    device_id=(tile + k, peer),
                    device_id_type=mesh_ids,
                ).wait_recv()


def share_power(part, reach):
    count = lax.axis_size("sta")
    rows = part.shape[0] // count
    slots = 2 * reach + 1
    return pl.pallas_call(
        share_kernel,
        out_shape=jax.ShapeDtypeStruct((slots,) + part.shape, jnp.float32),
        in_specs=[pl.BlockSpec(memory_space=pltpu.VMEM)],
        out_specs=pl.BlockSpec(memory_space=pltpu.VMEM),
        scratch_shapes=[
            pltpu.VMEM((count, rows, part.shape[1]), jnp.float32),
            pltpu.SemaphoreType.DMA((count,)),
            pltpu.SemaphoreType.DMA((count,)),
            pltpu.SemaphoreType.DMA((slots, count)),
            pltpu.SemaphoreType.DMA((slots, count)),
            pltpu.SemaphoreType.DMA((1,)),
        ],
        compiler_params=pltpu.CompilerParams(collective_id=0, has_side_effects=True),
    )(part)


def freq_beams(freq_ids, aligned_rows, slow_rows):
    return lax.map(lambda pair: beam_freq(pair[0], pair[1], slow_rows), (freq_ids, aligned_rows))


def band_matrix(taps, length):
    rows = jnp.arange(length, dtype=jnp.int32)[:, None]
    columns = jnp.arange(length + 2 * HALF, dtype=jnp.int32)[None, :]
    offset = columns - rows
    picks = jnp.arange(TAPS, dtype=jnp.int32)[:, None, None]
    return jnp.sum(jnp.where(offset[None] == picks, taps[:, None, None], 0.0), axis=0)


def blur(volume, bands):
    band_x, square_y, square_z = bands
    padded = with_halo(volume.astype(jnp.bfloat16), (("grid", 0),), HALF).astype(volume.dtype)
    along_x = jnp.einsum("ip,pyz->iyz", band_x, padded, precision=lax.Precision.HIGHEST)
    along_y = jnp.einsum("jq,xqz->xjz", square_y, along_x, precision=lax.Precision.HIGHEST)
    return jnp.einsum("xyw,kw->xyk", along_y, square_z, precision=lax.Precision.HIGHEST)


def blur_narrowing(volume, taps, square_y, square_z):
    band_x = band_matrix(taps, volume.shape[0] - 2 * HALF)
    along_x = jnp.einsum("ip,pyz->iyz", band_x, volume, precision=lax.Precision.HIGHEST)
    along_y = jnp.einsum("jq,xqz->xjz", square_y, along_x, precision=lax.Precision.HIGHEST)
    return jnp.einsum("xyw,kw->xyk", along_y, square_z, precision=lax.Precision.HIGHEST)


def deblur(observed, halo_tiles, spread_taps):
    tiles = lax.axis_size("grid")
    me = lax.axis_index("grid")
    reach = ITERS * 2 * HALF
    cut = halo_tiles * CX - reach
    observed = observed[cut : observed.shape[0] - cut]
    width = observed.shape[0]
    cell = (me - halo_tiles) * CX + cut + jnp.arange(width, dtype=jnp.int32)
    inside = (cell >= 0) & (cell < tiles * CX)
    square_y = band_matrix(spread_taps[1], CY)[:, HALF : HALF + CY]
    square_z = band_matrix(spread_taps[2], CZ)[:, HALF : HALF + CZ]
    estimate = jnp.where(inside[:, None, None], observed, 0.0)
    for sweep in range(ITERS):
        low = 2 * HALF * sweep + HALF
        blurred = blur_narrowing(estimate, spread_taps[0], square_y, square_z)
        ratio = jnp.where(
            inside[low : width - low, None, None], observed[low : width - low] / blurred, 0.0
        )
        estimate = estimate[2 * HALF : estimate.shape[0] - 2 * HALF] * blur_narrowing(
            ratio, spread_taps[0], square_y, square_z
        )
    return estimate


def per_device(spectra, lag_samples, slowness, spread_taps):
    groups = lax.axis_size("sta")
    own_count = FREQS // groups
    first_bin = lax.axis_index("sta") * own_count
    block = spectra.shape[2]
    spec_send = spectra.reshape(groups, own_count, 2, block).transpose(0, 2, 1, 3)
    local_power = beam_power(spec_send, lag_samples, slowness[0])
    halo_tiles = -(-(ITERS * 2 * HALF) // CX)
    summed = share_power(local_power, halo_tiles)
    observed = (summed / (FREQS * STATIONS) + BACKGROUND).reshape(-1, CY, CX, CZ).transpose(0, 2, 1, 3)
    stacked = observed[halo_tiles]
    estimate = deblur(observed.reshape(-1, CY, CZ), halo_tiles, spread_taps)
    return (stacked[None], estimate[None])


def solution(mesh):
    placed = (P(None, None, "sta"), P("grid", "sta"), P("grid", None, "sta"), P())
    return jax.shard_map(
        per_device,
        mesh=mesh,
        in_specs=placed,
        out_specs=(P("grid", None, None, None), P("grid", None, None, None)),
        check_vma=False,
    )
```

```python
import math

import jax
import jax.numpy as jnp
from jax import lax
from jax.sharding import PartitionSpec as P
from jax.experimental import pallas as pl
from jax.experimental.pallas import tpu as pltpu

STATIONS = 6144
FREQS = 64
F0 = 600
NT = 6000
TAPS = 17
HALF = 8
ITERS = 4
CX = 32
CY = 8
CZ = 128


TWO_PI = 2.0 * math.pi
BACKGROUND = 0.05


def with_halo(array, sides, width):
    for axis, dim in sides:
        size, length = (lax.axis_size(axis), array.shape[dim])
        up = [(i, (i + 1) % size) for i in range(size - 1)]
        down = [(j, i) for i, j in up]
        last = lax.slice_in_dim(array, length - width, length, axis=dim)
        leading = lax.slice_in_dim(array, 0, width, axis=dim)
        before = lax.ppermute(last, axis, up)
        after = lax.ppermute(leading, axis, down)
        array = jnp.concatenate([before, array, after], axis=dim)
    return array


def align_rows(spectra, lag_row):
    bins = F0 + jnp.arange(FREQS, dtype=jnp.int32)
    cycles = bins[:, None] * lag_row[None, :] % NT
    turned = cycles.astype(jnp.float32) * (TWO_PI / NT)
    cosine = jnp.cos(turned)
    sine = jnp.sin(turned)
    real_in = spectra[:, 0, :].astype(jnp.float32)
    imag_in = spectra[:, 1, :].astype(jnp.float32)
    real_out = real_in * cosine + imag_in * sine
    imag_out = imag_in * cosine - real_in * sine
    return jnp.stack([real_out, imag_out], axis=1).astype(jnp.bfloat16)


def beam_freq(freq, aligned_row, slow_rows):
    omega = (F0 + freq).astype(jnp.float32) * (TWO_PI / NT)
    slow = slow_rows.astype(jnp.float32)
    x_coord = jnp.arange(CX, dtype=jnp.float32) - (CX - 1) / 2.0
    y_coord = jnp.arange(CY, dtype=jnp.float32) - (CY - 1) / 2.0
    z_coord = jnp.arange(CZ, dtype=jnp.float32) - (CZ - 1) / 2.0
    phase_x = (omega * slow[0])[None, :] * x_coord[:, None]
    phase_y = (omega * slow[1])[None, :] * y_coord[:, None]
    phase = phase_x[:, None, :] + phase_y[None, :, :]
    cosine = jnp.cos(phase)
    sine = jnp.sin(phase)
    real_in = aligned_row[0].astype(jnp.float32)[None, None, :]
    imag_in = aligned_row[1].astype(jnp.float32)[None, None, :]
    front_real = (real_in * cosine + imag_in * sine).astype(jnp.bfloat16).reshape(CX * CY, -1)
    front_imag = (imag_in * cosine - real_in * sine).astype(jnp.bfloat16).reshape(CX * CY, -1)
    left_side = jnp.concatenate([front_real, front_imag], axis=1)
    phase_z = (omega * slow[2])[:, None] * z_coord[None, :]
    depth_real = jnp.cos(phase_z).astype(jnp.bfloat16)
    depth_imag = jnp.sin(phase_z).astype(jnp.bfloat16)
    upper_rows = jnp.concatenate([depth_real, -depth_imag], axis=1)
    lower_rows = jnp.concatenate([depth_imag, depth_real], axis=1)
    right_side = jnp.concatenate([upper_rows, lower_rows], axis=0)
    return jnp.dot(left_side, right_side, preferred_element_type=jnp.float32)


CHUNK = 256


def exp_neg(angle):
    return jnp.cos(angle), -jnp.sin(angle)


def exchange_inputs(spec_ref, lag_ref, slow_ref, spec_in, lag_in, slow_in, local_sem, send_sem, recv_sem, then):
    count = spec_in.shape[0]
    me = lax.axis_index("sta")
    tile = lax.axis_index("grid")
    mesh_ids = pl.DeviceIdType.MESH
    barrier = pltpu.get_barrier_semaphore()
    for shift in range(1, count):
        peer = lax.rem(me + shift, count)
        pl.semaphore_signal(barrier, inc=1, device_id=(tile, peer), device_id_type=mesh_ids)
    pl.semaphore_wait(barrier, count - 1)
    pairs = ((spec_ref, spec_in), (lag_ref, lag_in), (slow_ref, slow_in))
    local = []
    for kind, (source, target) in enumerate(pairs):
        own = source.at[me] if kind == 0 else source
        copy = pltpu.make_async_copy(own, target.at[me], local_sem.at[kind])
        copy.start()
        local.append(copy)
    sends = []
    for shift in range(1, count):
        peer = lax.rem(me + shift, count)
        for kind, (source, target) in enumerate(pairs):
            part = source.at[peer] if kind == 0 else source
            copy = pltpu.make_async_remote_copy(
                src_ref=part,
                dst_ref=target.at[me],
                send_sem=send_sem.at[kind, shift],
                recv_sem=recv_sem.at[kind, me],
                device_id=(tile, peer),
                device_id_type=mesh_ids,
            )
            copy.start()
            sends.append(copy)
    then()
    for copy in local:
        copy.wait()
    for copy in sends:
        copy.wait_send()
    for shift in range(1, count):
        source_id = lax.rem(me + count - shift, count)
        for kind, (source, target) in enumerate(pairs):
            part = source.at[source_id] if kind == 0 else source
            pltpu.make_async_remote_copy(
                src_ref=part,
                dst_ref=target.at[source_id],
                send_sem=send_sem.at[kind, shift],
                recv_sem=recv_sem.at[kind, source_id],
                device_id=(tile, source_id),
                device_id_type=mesh_ids,
            ).wait_recv()


def align_block(spec, lag, slow, source, real_ref, imag_ref, turn_ref):
    bins, block = spec.shape[1], spec.shape[2]
    first_bin = lax.axis_index("sta") * bins
    bin_rows = (F0 + first_bin + lax.broadcasted_iota(jnp.int32, (bins, block), 0)).astype(jnp.float32)
    cols = pl.ds(pl.multiple_of(source * block, 128), block)
    product = bin_rows * lag.astype(jnp.float32)
    whole = jnp.floor(product * (1.0 / NT))
    left = product - whole * NT
    left = jnp.where(left < 0.0, left + NT, left)
    left = jnp.where(left >= NT, left - NT, left)
    turned = left * (TWO_PI / NT)
    cosine = jnp.cos(turned)
    sine = jnp.sin(turned)
    real_in = spec[0].astype(jnp.float32)
    imag_in = spec[1].astype(jnp.float32)
    real_ref[:, cols] = (real_in * cosine + imag_in * sine).astype(jnp.bfloat16).astype(jnp.float32)
    imag_ref[:, cols] = (imag_in * cosine - real_in * sine).astype(jnp.bfloat16).astype(jnp.float32)
    turn_ref[:, cols] = slow.astype(jnp.float32)


def complex_times(left, right):
    return left[0] * right[0] - left[1] * right[1], left[0] * right[1] + left[1] * right[0]


def factor_rows(turn_x, turn_y, turn_z, rows8, rows16):
    return (
        exp_neg(turn_x * (rows8 - 3.5)),
        exp_neg(turn_x * (8.0 * (rows8 - 1.5))),
        exp_neg(turn_y * (rows8 - 3.5)),
        exp_neg(turn_z * (rows16 - 7.5)),
        exp_neg(turn_z * (16.0 * (rows8 - 3.5))),
    )


def beam_kernel(spec_ref, lag_ref, slow_ref, power_ref, spec_in, lag_in, slow_in, local_sem, send_sem, recv_sem,
                real_ref, imag_ref, turn_ref, acc_ref, left_ref, right_ref):
    count, bins, block = spec_in.shape[0], spec_in.shape[2], spec_in.shape[3]
    me = lax.axis_index("sta")
    first_bin = me * bins
    width = CHUNK
    per_block = block // width
    half_z = CZ // 2
    rows8 = lax.broadcasted_iota(jnp.int32, (8, width), 0).astype(jnp.float32)
    rows16 = lax.broadcasted_iota(jnp.int32, (16, width), 0).astype(jnp.float32)
    omega0 = (F0 + first_bin).astype(jnp.float32) * (TWO_PI / NT)
    step = TWO_PI / NT
    acc_ref[...] = jnp.zeros_like(acc_ref)

    def per_chunk(k, carry):
        source = lax.rem(me + k // per_block, count)
        cols = pl.ds(pl.multiple_of(source * block + lax.rem(k, per_block) * width, 128), width)
        slow_x = turn_ref[0:1, cols]
        slow_y = turn_ref[1:2, cols]
        slow_z = turn_ref[2:3, cols]
        start = factor_rows(omega0 * slow_x, omega0 * slow_y, omega0 * slow_z, rows8, rows16)
        ratio = factor_rows(step * slow_x, step * slow_y, step * slow_z, rows8, rows16)

        def per_bin(f, state):
            (a_r, a_i), (b_r, b_i), (y_r, y_i), (c_r, c_i), (d_r, d_i) = state
            real_in = real_ref[pl.ds(f, 1), cols]
            imag_in = imag_ref[pl.ds(f, 1), cols]
            groups_r, groups_i = [], []
            for m in range(CX // 8):
                x_r, x_i = complex_times((b_r[m : m + 1], b_i[m : m + 1]), (a_r, a_i))
                groups_r.append(real_in * x_r - imag_in * x_i)
                groups_i.append(real_in * x_i + imag_in * x_r)
            for y in range(CY):
                yy_r, yy_i = y_r[y : y + 1], y_i[y : y + 1]
                for m in range(0, CX // 8, 2):
                    parts_r, parts_i = [], []
                    for mm in (m, m + 1):
                        parts_r.append(groups_r[mm] * yy_r - groups_i[mm] * yy_i)
                        parts_i.append(groups_r[mm] * yy_i + groups_i[mm] * yy_r)
                    row = y * CX + 8 * m
                    left_ref[row : row + 16, :] = jnp.concatenate(parts_r, axis=0).astype(jnp.bfloat16)
                    left_ref[CX * CY + row : CX * CY + row + 16, :] = jnp.concatenate(parts_i, axis=0).astype(jnp.bfloat16)
            for m in range(half_z // 16):
                z_r, z_i = complex_times((d_r[m : m + 1], d_i[m : m + 1]), (c_r, c_i))
                row = 16 * m
                right_ref[row : row + 16, :] = z_r.astype(jnp.bfloat16)
                right_ref[half_z + row : half_z + row + 16, :] = z_i.astype(jnp.bfloat16)
            acc_ref[f] += lax.dot_general(
                left_ref[...], right_ref[...], (((1,), (1,)), ((), ())), preferred_element_type=jnp.float32
            )
            return tuple(complex_times(now, turn) for now, turn in zip(state, ratio))

        lax.fori_loop(0, bins, per_bin, start)
        return carry

    def own_block():
        align_block(spec_ref[me], lag_ref[...], slow_ref[...], me, real_ref, imag_ref, turn_ref)
        lax.fori_loop(0, per_block, per_chunk, 0)

    exchange_inputs(spec_ref, lag_ref, slow_ref, spec_in, lag_in, slow_in, local_sem, send_sem, recv_sem, own_block)

    def align_other(shift, carry):
        source = lax.rem(me + shift, count)
        align_block(spec_in[source], lag_in[source], slow_in[source], source, real_ref, imag_ref, turn_ref)
        return carry

    lax.fori_loop(1, count, align_other, 0)
    lax.fori_loop(per_block, count * per_block, per_chunk, 0)
    cells = CX * CY
    low = jnp.zeros((cells, half_z), jnp.float32)
    high = jnp.zeros((cells, half_z), jnp.float32)
    for f in range(bins):
        sums = acc_ref[f]
        u, w = sums[:cells, :half_z], sums[:cells, half_z:]
        x, v = sums[cells:, :half_z], sums[cells:, half_z:]
        low = low + ((u - v) * (u - v) + (w + x) * (w + x))
        high = high + ((u + v) * (u + v) + (x - w) * (x - w))
    power_ref[:, :half_z] = low
    power_ref[:, half_z:] = high


def beam_power(spec_send, lag_row, slow_rows):
    count = spec_send.shape[0]
    bins, block = spec_send.shape[2], spec_send.shape[3]
    width = CHUNK
    stations = count * block
    vmem = pl.BlockSpec(memory_space=pltpu.VMEM)
    return pl.pallas_call(
        beam_kernel,
        out_shape=jax.ShapeDtypeStruct((CX * CY, CZ), jnp.float32),
        in_specs=[vmem, vmem, vmem],
        out_specs=vmem,
        scratch_shapes=[
            pltpu.VMEM((count,) + spec_send.shape[1:], jnp.bfloat16),
            pltpu.VMEM((count,) + lag_row.shape, jnp.int32),
            pltpu.VMEM((count,) + slow_rows.shape, jnp.bfloat16),
            pltpu.SemaphoreType.DMA((3,)),
            pltpu.SemaphoreType.DMA((3, count)),
            pltpu.SemaphoreType.DMA((3, count)),
            pltpu.VMEM((bins, stations), jnp.float32),
            pltpu.VMEM((bins, stations), jnp.float32),
            pltpu.VMEM((slow_rows.shape[0], stations), jnp.float32),
            pltpu.VMEM((bins, 2 * CX * CY, CZ), jnp.float32),
            pltpu.VMEM((2 * CX * CY, width), jnp.bfloat16),
            pltpu.VMEM((CZ, width), jnp.bfloat16),
        ],
        compiler_params=pltpu.CompilerParams(collective_id=1, has_side_effects=True),
    )(spec_send, lag_row, slow_rows)


def share_kernel(part_ref, out_ref, pieces, send_rs, recv_rs, send_ag, recv_ag, local_sem):
    count = pieces.shape[0]
    slots = out_ref.shape[0]
    reach = slots // 2
    rows = pieces.shape[1]
    me = lax.axis_index("sta")
    tile = lax.axis_index("grid")
    tiles = lax.axis_size("grid")
    mesh_ids = pl.DeviceIdType.MESH
    barrier = pltpu.get_barrier_semaphore()
    for shift in range(1, count):
        pl.semaphore_signal(barrier, inc=1, device_id=(tile, lax.rem(me + shift, count)), device_id_type=mesh_ids)
    neighbours = jnp.int32(0)
    for k in range(-reach, reach + 1):
        if k == 0:
            continue
        there = (tile + k >= 0) & (tile + k < tiles)
        neighbours = neighbours + there.astype(jnp.int32)

        @pl.when(there)
        def _():
            for peer in range(count):
                pl.semaphore_signal(barrier, inc=1, device_id=(tile + k, peer), device_id_type=mesh_ids)

    pl.semaphore_wait(barrier, count - 1 + count * neighbours)
    own = pltpu.make_async_copy(part_ref.at[pl.ds(pl.multiple_of(me * rows, 8), rows)], pieces.at[me], local_sem.at[0])
    own.start()
    sends = []
    for shift in range(1, count):
        peer = lax.rem(me + shift, count)
        copy = pltpu.make_async_remote_copy(
            src_ref=part_ref.at[pl.ds(pl.multiple_of(peer * rows, 8), rows)],
            dst_ref=pieces.at[me],
            send_sem=send_rs.at[shift],
            recv_sem=recv_rs.at[me],
            device_id=(tile, peer),
            device_id_type=mesh_ids,
        )
        copy.start()
        sends.append(copy)
    own.wait()
    for copy in sends:
        copy.wait_send()
    for shift in range(1, count):
        source = lax.rem(me + count - shift, count)
        pltpu.make_async_remote_copy(
            src_ref=pieces.at[source],
            dst_ref=pieces.at[source],
            send_sem=send_rs.at[shift],
            recv_sem=recv_rs.at[source],
            device_id=(tile, source),
            device_id_type=mesh_ids,
        ).wait_recv()
    total = pieces[0]
    for source in range(1, count):
        total = total + pieces[source]
    mine = pl.ds(pl.multiple_of(me * rows, 8), rows)
    out_ref[reach, mine] = total
    block = out_ref.at[reach, mine]

    def gather_copy(k, peer, slot):
        return pltpu.make_async_remote_copy(
            src_ref=block,
            dst_ref=out_ref.at[slot, mine],
            send_sem=send_ag.at[slot, peer],
            recv_sem=recv_ag.at[slot, me],
            device_id=(tile + k, peer),
            device_id_type=mesh_ids,
        )

    peers = []
    for shift in range(1, count):
        copy = gather_copy(0, lax.rem(me + shift, count), reach)
        copy.start()
        peers.append(copy)
    for k in range(-reach, reach + 1):
        if k == 0:
            continue
        there = (tile + k >= 0) & (tile + k < tiles)

        @pl.when(there)
        def _():
            for peer in range(count):
                gather_copy(k, peer, reach - k).start()

        @pl.when(jnp.logical_not(there))
        def _():
            out_ref[reach + k] = jnp.zeros(out_ref.shape[1:], out_ref.dtype)

    for copy in peers:
        copy.wait_send()
    for shift in range(1, count):
        source = lax.rem(me + count - shift, count)
        pltpu.make_async_remote_copy(
            src_ref=block,
            dst_ref=out_ref.at[reach, pl.ds(pl.multiple_of(source * rows, 8), rows)],
            send_sem=send_ag.at[reach, source],
            recv_sem=recv_ag.at[reach, source],
            device_id=(tile, source),
            device_id_type=mesh_ids,
        ).wait_recv()
    for k in range(-reach, reach + 1):
        if k == 0:
            continue
        there = (tile + k >= 0) & (tile + k < tiles)

        @pl.when(there)
        def _():
            for peer in range(count):
                gather_copy(k, peer, reach - k).wait_send()
                pltpu.make_async_remote_copy(
                    src_ref=block,
                    dst_ref=out_ref.at[reach + k, pl.ds(peer * rows, rows)],
                    send_sem=send_ag.at[reach + k, peer],
                    recv_sem=recv_ag.at[reach + k, peer],
                    device_id=(tile + k, peer),
                    device_id_type=mesh_ids,
                ).wait_recv()


def share_power(part, reach):
    count = lax.axis_size("sta")
    rows = part.shape[0] // count
    slots = 2 * reach + 1
    return pl.pallas_call(
        share_kernel,
        out_shape=jax.ShapeDtypeStruct((slots,) + part.shape, jnp.float32),
        in_specs=[pl.BlockSpec(memory_space=pltpu.VMEM)],
        out_specs=pl.BlockSpec(memory_space=pltpu.VMEM),
        scratch_shapes=[
            pltpu.VMEM((count, rows, part.shape[1]), jnp.float32),
            pltpu.SemaphoreType.DMA((count,)),
            pltpu.SemaphoreType.DMA((count,)),
            pltpu.SemaphoreType.DMA((slots, count)),
            pltpu.SemaphoreType.DMA((slots, count)),
            pltpu.SemaphoreType.DMA((1,)),
        ],
        compiler_params=pltpu.CompilerParams(collective_id=0, has_side_effects=True),
    )(part)


def freq_beams(freq_ids, aligned_rows, slow_rows):
    return lax.map(lambda pair: beam_freq(pair[0], pair[1], slow_rows), (freq_ids, aligned_rows))


def band_matrix(taps, length):
    rows = jnp.arange(length, dtype=jnp.int32)[:, None]
    columns = jnp.arange(length + 2 * HALF, dtype=jnp.int32)[None, :]
    offset = columns - rows
    picks = jnp.arange(TAPS, dtype=jnp.int32)[:, None, None]
    return jnp.sum(jnp.where(offset[None] == picks, taps[:, None, None], 0.0), axis=0)


def blur(volume, bands):
    band_x, square_y, square_z = bands
    padded = with_halo(volume.astype(jnp.bfloat16), (("grid", 0),), HALF).astype(volume.dtype)
    along_x = jnp.einsum("ip,pyz->iyz", band_x, padded, precision=lax.Precision.HIGHEST)
    along_y = jnp.einsum("jq,xqz->xjz", square_y, along_x, precision=lax.Precision.HIGHEST)
    return jnp.einsum("xyw,kw->xyk", along_y, square_z, precision=lax.Precision.HIGHEST)


def blur_narrowing(volume, taps, square_y, square_z):
    band_x = band_matrix(taps, volume.shape[0] - 2 * HALF)
    along_x = jnp.einsum("ip,pyz->iyz", band_x, volume, precision=lax.Precision.HIGHEST)
    along_y = jnp.einsum("jq,xqz->xjz", square_y, along_x, precision=lax.Precision.HIGHEST)
    return jnp.einsum("xyw,kw->xyk", along_y, square_z, precision=lax.Precision.HIGHEST)


def deblur(observed, halo_tiles, spread_taps):
    tiles = lax.axis_size("grid")
    me = lax.axis_index("grid")
    reach = ITERS * 2 * HALF
    cut = halo_tiles * CX - reach
    observed = observed[cut : observed.shape[0] - cut]
    width = observed.shape[0]
    cell = (me - halo_tiles) * CX + cut + jnp.arange(width, dtype=jnp.int32)
    inside = (cell >= 0) & (cell < tiles * CX)
    square_y = band_matrix(spread_taps[1], CY)[:, HALF : HALF + CY]
    square_z = band_matrix(spread_taps[2], CZ)[:, HALF : HALF + CZ]
    estimate = jnp.where(inside[:, None, None], observed, 0.0)
    for sweep in range(ITERS):
        low = 2 * HALF * sweep + HALF
        blurred = blur_narrowing(estimate, spread_taps[0], square_y, square_z)
        ratio = jnp.where(
            inside[low : width - low, None, None], observed[low : width - low] / blurred, 0.0
        )
        estimate = estimate[2 * HALF : estimate.shape[0] - 2 * HALF] * blur_narrowing(
            ratio, spread_taps[0], square_y, square_z
        )
    return estimate


def per_device(spectra, lag_samples, slowness, spread_taps):
    groups = lax.axis_size("sta")
    own_count = FREQS // groups
    first_bin = lax.axis_index("sta") * own_count
    block = spectra.shape[2]
    spec_send = spectra.reshape(groups, own_count, 2, block).transpose(0, 2, 1, 3)
    local_power = beam_power(spec_send, lag_samples, slowness[0])
    halo_tiles = -(-(ITERS * 2 * HALF) // CX)
    summed = share_power(local_power, halo_tiles)
    summed = jnp.concatenate([summed[..., : CZ // 2], summed[..., CZ // 2 :][..., ::-1]], axis=-1)
    observed = (summed / (FREQS * STATIONS) + BACKGROUND).reshape(-1, CY, CX, CZ).transpose(0, 2, 1, 3)
    stacked = observed[halo_tiles]
    estimate = deblur(observed.reshape(-1, CY, CZ), halo_tiles, spread_taps)
    return (stacked[None], estimate[None])


def solution(mesh):
    placed = (P(None, None, "sta"), P("grid", "sta"), P("grid", None, "sta"), P())
    return jax.shard_map(
        per_device,
        mesh=mesh,
        in_specs=placed,
        out_specs=(P("grid", None, None, None), P("grid", None, None, None)),
        check_vma=False,
    )
```

```python
import math

import jax
import jax.numpy as jnp
from jax import lax
from jax.sharding import PartitionSpec as P
from jax.experimental import pallas as pl
from jax.experimental.pallas import tpu as pltpu

STATIONS = 6144
FREQS = 64
F0 = 600
NT = 6000
TAPS = 17
HALF = 8
ITERS = 4
CX = 32
CY = 8
CZ = 128


TWO_PI = 2.0 * math.pi
BACKGROUND = 0.05


def with_halo(array, sides, width):
    for axis, dim in sides:
        size, length = (lax.axis_size(axis), array.shape[dim])
        up = [(i, (i + 1) % size) for i in range(size - 1)]
        down = [(j, i) for i, j in up]
        last = lax.slice_in_dim(array, length - width, length, axis=dim)
        leading = lax.slice_in_dim(array, 0, width, axis=dim)
        before = lax.ppermute(last, axis, up)
        after = lax.ppermute(leading, axis, down)
        array = jnp.concatenate([before, array, after], axis=dim)
    return array


def align_rows(spectra, lag_row):
    bins = F0 + jnp.arange(FREQS, dtype=jnp.int32)
    cycles = bins[:, None] * lag_row[None, :] % NT
    turned = cycles.astype(jnp.float32) * (TWO_PI / NT)
    cosine = jnp.cos(turned)
    sine = jnp.sin(turned)
    real_in = spectra[:, 0, :].astype(jnp.float32)
    imag_in = spectra[:, 1, :].astype(jnp.float32)
    real_out = real_in * cosine + imag_in * sine
    imag_out = imag_in * cosine - real_in * sine
    return jnp.stack([real_out, imag_out], axis=1).astype(jnp.bfloat16)


def beam_freq(freq, aligned_row, slow_rows):
    omega = (F0 + freq).astype(jnp.float32) * (TWO_PI / NT)
    slow = slow_rows.astype(jnp.float32)
    x_coord = jnp.arange(CX, dtype=jnp.float32) - (CX - 1) / 2.0
    y_coord = jnp.arange(CY, dtype=jnp.float32) - (CY - 1) / 2.0
    z_coord = jnp.arange(CZ, dtype=jnp.float32) - (CZ - 1) / 2.0
    phase_x = (omega * slow[0])[None, :] * x_coord[:, None]
    phase_y = (omega * slow[1])[None, :] * y_coord[:, None]
    phase = phase_x[:, None, :] + phase_y[None, :, :]
    cosine = jnp.cos(phase)
    sine = jnp.sin(phase)
    real_in = aligned_row[0].astype(jnp.float32)[None, None, :]
    imag_in = aligned_row[1].astype(jnp.float32)[None, None, :]
    front_real = (real_in * cosine + imag_in * sine).astype(jnp.bfloat16).reshape(CX * CY, -1)
    front_imag = (imag_in * cosine - real_in * sine).astype(jnp.bfloat16).reshape(CX * CY, -1)
    left_side = jnp.concatenate([front_real, front_imag], axis=1)
    phase_z = (omega * slow[2])[:, None] * z_coord[None, :]
    depth_real = jnp.cos(phase_z).astype(jnp.bfloat16)
    depth_imag = jnp.sin(phase_z).astype(jnp.bfloat16)
    upper_rows = jnp.concatenate([depth_real, -depth_imag], axis=1)
    lower_rows = jnp.concatenate([depth_imag, depth_real], axis=1)
    right_side = jnp.concatenate([upper_rows, lower_rows], axis=0)
    return jnp.dot(left_side, right_side, preferred_element_type=jnp.float32)


CHUNK = 256


def exp_neg(angle):
    return jnp.cos(angle), -jnp.sin(angle)


def exchange_inputs(spec_ref, lag_ref, slow_ref, spec_in, lag_in, slow_in, local_sem, send_sem, recv_sem, then):
    count = spec_in.shape[0]
    me = lax.axis_index("sta")
    tile = lax.axis_index("grid")
    mesh_ids = pl.DeviceIdType.MESH
    barrier = pltpu.get_barrier_semaphore()
    for shift in range(1, count):
        peer = lax.rem(me + shift, count)
        pl.semaphore_signal(barrier, inc=1, device_id=(tile, peer), device_id_type=mesh_ids)
    pl.semaphore_wait(barrier, count - 1)
    pairs = ((spec_ref, spec_in), (lag_ref, lag_in), (slow_ref, slow_in))
    local = []
    for kind, (source, target) in enumerate(pairs):
        own = source.at[me] if kind == 0 else source
        copy = pltpu.make_async_copy(own, target.at[me], local_sem.at[kind])
        copy.start()
        local.append(copy)
    sends = []
    for shift in range(1, count):
        peer = lax.rem(me + shift, count)
        for kind, (source, target) in enumerate(pairs):
            part = source.at[peer] if kind == 0 else source
            copy = pltpu.make_async_remote_copy(
                src_ref=part,
                dst_ref=target.at[me],
                send_sem=send_sem.at[kind, shift],
                recv_sem=recv_sem.at[kind, me],
                device_id=(tile, peer),
                device_id_type=mesh_ids,
            )
            copy.start()
            sends.append(copy)
    then()
    for copy in local:
        copy.wait()
    for copy in sends:
        copy.wait_send()
    for shift in range(1, count):
        source_id = lax.rem(me + count - shift, count)
        for kind, (source, target) in enumerate(pairs):
            part = source.at[source_id] if kind == 0 else source
            pltpu.make_async_remote_copy(
                src_ref=part,
                dst_ref=target.at[source_id],
                send_sem=send_sem.at[kind, shift],
                recv_sem=recv_sem.at[kind, source_id],
                device_id=(tile, source_id),
                device_id_type=mesh_ids,
            ).wait_recv()


def align_block(spec, lag, slow, source, real_ref, imag_ref, turn_ref):
    bins, block = spec.shape[1], spec.shape[2]
    first_bin = lax.axis_index("sta") * bins
    bin_rows = (F0 + first_bin + lax.broadcasted_iota(jnp.int32, (bins, block), 0)).astype(jnp.float32)
    cols = pl.ds(pl.multiple_of(source * block, 128), block)
    product = bin_rows * lag.astype(jnp.float32)
    whole = jnp.floor(product * (1.0 / NT))
    left = product - whole * NT
    left = jnp.where(left < 0.0, left + NT, left)
    left = jnp.where(left >= NT, left - NT, left)
    turned = left * (TWO_PI / NT)
    cosine = jnp.cos(turned)
    sine = jnp.sin(turned)
    real_in = spec[0].astype(jnp.float32)
    imag_in = spec[1].astype(jnp.float32)
    real_ref[:, cols] = (real_in * cosine + imag_in * sine).astype(jnp.bfloat16).astype(jnp.float32)
    imag_ref[:, cols] = (imag_in * cosine - real_in * sine).astype(jnp.bfloat16).astype(jnp.float32)
    turn_ref[:, cols] = slow.astype(jnp.float32)


def complex_times(left, right):
    return left[0] * right[0] - left[1] * right[1], left[0] * right[1] + left[1] * right[0]


def factor_rows(turn_x, turn_y, turn_z, rows8, rows16):
    return (
        exp_neg(turn_x * (rows8 - 3.5)),
        exp_neg(turn_x * (8.0 * (rows8 - 1.5))),
        exp_neg(turn_y * (rows8 - 3.5)),
        exp_neg(turn_z * (rows16 - 7.5)),
        exp_neg(turn_z * (16.0 * (rows8 - 3.5))),
    )


def beam_kernel(spec_ref, lag_ref, slow_ref, power_ref, spec_in, lag_in, slow_in, local_sem, send_sem, recv_sem,
                real_ref, imag_ref, turn_ref, acc_ref, left_ref, right_ref):
    count, bins, block = spec_in.shape[0], spec_in.shape[2], spec_in.shape[3]
    me = lax.axis_index("sta")
    first_bin = me * bins
    width = CHUNK
    per_block = block // width
    half_z = CZ // 2
    rows8 = lax.broadcasted_iota(jnp.int32, (8, width), 0).astype(jnp.float32)
    rows16 = lax.broadcasted_iota(jnp.int32, (16, width), 0).astype(jnp.float32)
    omega0 = (F0 + first_bin).astype(jnp.float32) * (TWO_PI / NT)
    step = TWO_PI / NT
    acc_ref[...] = jnp.zeros_like(acc_ref)

    def per_chunk(k, carry):
        source = lax.rem(me + k // per_block, count)
        cols = pl.ds(pl.multiple_of(source * block + lax.rem(k, per_block) * width, 128), width)
        slow_x = turn_ref[0:1, cols]
        slow_y = turn_ref[1:2, cols]
        slow_z = turn_ref[2:3, cols]
        start = factor_rows(omega0 * slow_x, omega0 * slow_y, omega0 * slow_z, rows8, rows16)
        ratio = factor_rows(step * slow_x, step * slow_y, step * slow_z, rows8, rows16)

        def per_bin(f, state):
            (a_r, a_i), (b_r, b_i), (y_r, y_i), (c_r, c_i), (d_r, d_i) = state
            real_in = real_ref[pl.ds(f, 1), cols]
            imag_in = imag_ref[pl.ds(f, 1), cols]
            groups_r, groups_i = [], []
            for m in range(CX // 8):
                x_r, x_i = complex_times((b_r[m : m + 1], b_i[m : m + 1]), (a_r, a_i))
                groups_r.append(real_in * x_r - imag_in * x_i)
                groups_i.append(real_in * x_i + imag_in * x_r)
            for y in range(CY):
                yy_r, yy_i = y_r[y : y + 1], y_i[y : y + 1]
                for m in range(0, CX // 8, 2):
                    parts_r, parts_i = [], []
                    for mm in (m, m + 1):
                        parts_r.append(groups_r[mm] * yy_r - groups_i[mm] * yy_i)
                        parts_i.append(groups_r[mm] * yy_i + groups_i[mm] * yy_r)
                    row = y * CX + 8 * m
                    left_ref[row : row + 16, :] = jnp.concatenate(parts_r, axis=0).astype(jnp.bfloat16)
                    left_ref[CX * CY + row : CX * CY + row + 16, :] = jnp.concatenate(parts_i, axis=0).astype(jnp.bfloat16)
            for m in range(half_z // 16):
                z_r, z_i = complex_times((d_r[m : m + 1], d_i[m : m + 1]), (c_r, c_i))
                row = 16 * m
                right_ref[row : row + 16, :] = z_r.astype(jnp.bfloat16)
                right_ref[half_z + row : half_z + row + 16, :] = z_i.astype(jnp.bfloat16)
            acc_ref[f] += lax.dot_general(
                left_ref[...], right_ref[...], (((1,), (1,)), ((), ())), preferred_element_type=jnp.float32
            )
            return tuple(complex_times(now, turn) for now, turn in zip(state, ratio))

        lax.fori_loop(0, bins, per_bin, start)
        return carry

    def own_block():
        align_block(spec_ref[me], lag_ref[...], slow_ref[...], me, real_ref, imag_ref, turn_ref)
        lax.fori_loop(0, per_block, per_chunk, 0)

    exchange_inputs(spec_ref, lag_ref, slow_ref, spec_in, lag_in, slow_in, local_sem, send_sem, recv_sem, own_block)

    def align_other(shift, carry):
        source = lax.rem(me + shift, count)
        align_block(spec_in[source], lag_in[source], slow_in[source], source, real_ref, imag_ref, turn_ref)
        return carry

    lax.fori_loop(1, count, align_other, 0)
    lax.fori_loop(per_block, count * per_block, per_chunk, 0)
    cells = CX * CY
    low = jnp.zeros((cells, half_z), jnp.float32)
    high = jnp.zeros((cells, half_z), jnp.float32)
    for f in range(bins):
        sums = acc_ref[f]
        u, w = sums[:cells, :half_z], sums[:cells, half_z:]
        x, v = sums[cells:, :half_z], sums[cells:, half_z:]
        low = low + ((u - v) * (u - v) + (w + x) * (w + x))
        high = high + ((u + v) * (u + v) + (x - w) * (x - w))
    power_ref[:, :half_z] = low
    power_ref[:, half_z:] = high


def beam_power(spec_send, lag_row, slow_rows):
    count = spec_send.shape[0]
    bins, block = spec_send.shape[2], spec_send.shape[3]
    width = CHUNK
    stations = count * block
    vmem = pl.BlockSpec(memory_space=pltpu.VMEM)
    return pl.pallas_call(
        beam_kernel,
        out_shape=jax.ShapeDtypeStruct((CX * CY, CZ), jnp.float32),
        in_specs=[vmem, vmem, vmem],
        out_specs=vmem,
        scratch_shapes=[
            pltpu.VMEM((count,) + spec_send.shape[1:], jnp.bfloat16),
            pltpu.VMEM((count,) + lag_row.shape, jnp.int32),
            pltpu.VMEM((count,) + slow_rows.shape, jnp.bfloat16),
            pltpu.SemaphoreType.DMA((3,)),
            pltpu.SemaphoreType.DMA((3, count)),
            pltpu.SemaphoreType.DMA((3, count)),
            pltpu.VMEM((bins, stations), jnp.float32),
            pltpu.VMEM((bins, stations), jnp.float32),
            pltpu.VMEM((slow_rows.shape[0], stations), jnp.float32),
            pltpu.VMEM((bins, 2 * CX * CY, CZ), jnp.float32),
            pltpu.VMEM((2 * CX * CY, width), jnp.bfloat16),
            pltpu.VMEM((CZ, width), jnp.bfloat16),
        ],
        compiler_params=pltpu.CompilerParams(collective_id=1, has_side_effects=True),
    )(spec_send, lag_row, slow_rows)


def share_kernel(part_ref, out_ref, pieces, send_rs, recv_rs, send_ag, recv_ag, local_sem):
    count = pieces.shape[0]
    slots = out_ref.shape[0]
    reach = slots // 2
    rows = pieces.shape[1]
    me = lax.axis_index("sta")
    tile = lax.axis_index("grid")
    tiles = lax.axis_size("grid")
    mesh_ids = pl.DeviceIdType.MESH
    barrier = pltpu.get_barrier_semaphore()
    for shift in range(1, count):
        pl.semaphore_signal(barrier, inc=1, device_id=(tile, lax.rem(me + shift, count)), device_id_type=mesh_ids)
    neighbours = jnp.int32(0)
    for k in range(-reach, reach + 1):
        if k == 0:
            continue
        there = (tile + k >= 0) & (tile + k < tiles)
        neighbours = neighbours + there.astype(jnp.int32)

        @pl.when(there)
        def _():
            for peer in range(count):
                pl.semaphore_signal(barrier, inc=1, device_id=(tile + k, peer), device_id_type=mesh_ids)

    pl.semaphore_wait(barrier, count - 1 + count * neighbours)
    own = pltpu.make_async_copy(part_ref.at[pl.ds(pl.multiple_of(me * rows, 8), rows)], pieces.at[me], local_sem.at[0])
    own.start()
    sends = []
    for shift in range(1, count):
        peer = lax.rem(me + shift, count)
        copy = pltpu.make_async_remote_copy(
            src_ref=part_ref.at[pl.ds(pl.multiple_of(peer * rows, 8), rows)],
            dst_ref=pieces.at[me],
            send_sem=send_rs.at[shift],
            recv_sem=recv_rs.at[me],
            device_id=(tile, peer),
            device_id_type=mesh_ids,
        )
        copy.start()
        sends.append(copy)
    own.wait()
    for copy in sends:
        copy.wait_send()
    for shift in range(1, count):
        source = lax.rem(me + count - shift, count)
        pltpu.make_async_remote_copy(
            src_ref=pieces.at[source],
            dst_ref=pieces.at[source],
            send_sem=send_rs.at[shift],
            recv_sem=recv_rs.at[source],
            device_id=(tile, source),
            device_id_type=mesh_ids,
        ).wait_recv()
    total = pieces[0]
    for source in range(1, count):
        total = total + pieces[source]
    mine = pl.ds(pl.multiple_of(me * rows, 8), rows)
    out_ref[reach, mine] = total
    block = out_ref.at[reach, mine]

    def gather_copy(k, peer, slot):
        return pltpu.make_async_remote_copy(
            src_ref=block,
            dst_ref=out_ref.at[slot, mine],
            send_sem=send_ag.at[slot, peer],
            recv_sem=recv_ag.at[slot, me],
            device_id=(tile + k, peer),
            device_id_type=mesh_ids,
        )

    peers = []
    for shift in range(1, count):
        copy = gather_copy(0, lax.rem(me + shift, count), reach)
        copy.start()
        peers.append(copy)
    for k in range(-reach, reach + 1):
        if k == 0:
            continue
        there = (tile + k >= 0) & (tile + k < tiles)

        @pl.when(there)
        def _():
            for peer in range(count):
                gather_copy(k, peer, reach - k).start()

        @pl.when(jnp.logical_not(there))
        def _():
            out_ref[reach + k] = jnp.zeros(out_ref.shape[1:], out_ref.dtype)

    for copy in peers:
        copy.wait_send()
    for shift in range(1, count):
        source = lax.rem(me + count - shift, count)
        pltpu.make_async_remote_copy(
            src_ref=block,
            dst_ref=out_ref.at[reach, pl.ds(pl.multiple_of(source * rows, 8), rows)],
            send_sem=send_ag.at[reach, source],
            recv_sem=recv_ag.at[reach, source],
            device_id=(tile, source),
            device_id_type=mesh_ids,
        ).wait_recv()
    for k in range(-reach, reach + 1):
        if k == 0:
            continue
        there = (tile + k >= 0) & (tile + k < tiles)

        @pl.when(there)
        def _():
            for peer in range(count):
                gather_copy(k, peer, reach - k).wait_send()
                pltpu.make_async_remote_copy(
                    src_ref=block,
                    dst_ref=out_ref.at[reach + k, pl.ds(peer * rows, rows)],
                    send_sem=send_ag.at[reach + k, peer],
                    recv_sem=recv_ag.at[reach + k, peer],
                    device_id=(tile + k, peer),
                    device_id_type=mesh_ids,
                ).wait_recv()


def share_power(part, reach):
    count = lax.axis_size("sta")
    rows = part.shape[0] // count
    slots = 2 * reach + 1
    return pl.pallas_call(
        share_kernel,
        out_shape=jax.ShapeDtypeStruct((slots,) + part.shape, jnp.float32),
        in_specs=[pl.BlockSpec(memory_space=pltpu.VMEM)],
        out_specs=pl.BlockSpec(memory_space=pltpu.VMEM),
        scratch_shapes=[
            pltpu.VMEM((count, rows, part.shape[1]), jnp.float32),
            pltpu.SemaphoreType.DMA((count,)),
            pltpu.SemaphoreType.DMA((count,)),
            pltpu.SemaphoreType.DMA((slots, count)),
            pltpu.SemaphoreType.DMA((slots, count)),
            pltpu.SemaphoreType.DMA((1,)),
        ],
        compiler_params=pltpu.CompilerParams(collective_id=0, has_side_effects=True),
    )(part)


def freq_beams(freq_ids, aligned_rows, slow_rows):
    return lax.map(lambda pair: beam_freq(pair[0], pair[1], slow_rows), (freq_ids, aligned_rows))


def band_matrix(taps, length):
    rows = jnp.arange(length, dtype=jnp.int32)[:, None]
    columns = jnp.arange(length + 2 * HALF, dtype=jnp.int32)[None, :]
    offset = columns - rows
    picks = jnp.arange(TAPS, dtype=jnp.int32)[:, None, None]
    return jnp.sum(jnp.where(offset[None] == picks, taps[:, None, None], 0.0), axis=0)


def blur(volume, bands):
    band_x, square_y, square_z = bands
    padded = with_halo(volume.astype(jnp.bfloat16), (("grid", 0),), HALF).astype(volume.dtype)
    along_x = jnp.einsum("ip,pyz->iyz", band_x, padded, precision=lax.Precision.HIGHEST)
    along_y = jnp.einsum("jq,xqz->xjz", square_y, along_x, precision=lax.Precision.HIGHEST)
    return jnp.einsum("xyw,kw->xyk", along_y, square_z, precision=lax.Precision.HIGHEST)


def blur_narrowing(volume, taps, square_y, square_z):
    band_x = band_matrix(taps, volume.shape[0] - 2 * HALF)
    along_x = jnp.einsum("ip,pyz->iyz", band_x, volume, precision=lax.Precision.HIGHEST)
    along_y = jnp.einsum("jq,xqz->xjz", square_y, along_x, precision=lax.Precision.HIGHEST)
    return jnp.einsum("xyw,kw->xyk", along_y, square_z, precision=lax.Precision.HIGHEST)


def deblur(observed, halo_tiles, spread_taps):
    tiles = lax.axis_size("grid")
    me = lax.axis_index("grid")
    reach = ITERS * 2 * HALF
    cut = halo_tiles * CX - reach
    observed = observed[cut : observed.shape[0] - cut]
    width = observed.shape[0]
    cell = (me - halo_tiles) * CX + cut + jnp.arange(width, dtype=jnp.int32)
    inside = (cell >= 0) & (cell < tiles * CX)
    square_y = band_matrix(spread_taps[1], CY)[:, HALF : HALF + CY]
    square_z = band_matrix(spread_taps[2], CZ)[:, HALF : HALF + CZ]
    estimate = jnp.where(inside[:, None, None], observed, 0.0)
    for sweep in range(ITERS):
        low = 2 * HALF * sweep + HALF
        blurred = blur_narrowing(estimate, spread_taps[0], square_y, square_z)
        ratio = jnp.where(
            inside[low : width - low, None, None], observed[low : width - low] / blurred, 0.0
        )
        estimate = estimate[2 * HALF : estimate.shape[0] - 2 * HALF] * blur_narrowing(
            ratio, spread_taps[0], square_y, square_z
        )
    return estimate


def deblur_kernel(taps_ref, obs_ref, kx_ref, kz_ref, out_ref):
    tiles = lax.axis_size("grid")
    me = lax.axis_index("grid")
    planes, width, depth = obs_ref.shape
    halo_tiles = (width - CX) // (2 * CX)
    highest = lax.Precision.HIGHEST

    def inside(low, size):
        cell = (me - halo_tiles) * CX + low + lax.broadcasted_iota(jnp.int32, (size, depth), 0)
        return (cell >= 0) & (cell < tiles * CX)

    def blur(volume):
        size_in = volume[0].shape[0]
        size_out = size_in - 2 * HALF
        band = kx_ref[0:size_out, 0:size_in]
        along_x = [jnp.dot(band, plane, precision=highest, preferred_element_type=jnp.float32) for plane in volume]
        along_y = []
        for y in range(planes):
            total = None
            for q in range(planes):
                term = taps_ref[1, q - y + HALF] * along_x[q]
                total = term if total is None else total + term
            along_y.append(total)
        joined = jnp.concatenate(along_y, axis=0)
        along_z = jnp.dot(joined, kz_ref[...], precision=highest, preferred_element_type=jnp.float32)
        return [along_z[y * size_out : (y + 1) * size_out] for y in range(planes)]

    observed = [obs_ref[y] for y in range(planes)]
    mask = inside(0, width)
    estimate = [jnp.where(mask, plane, 0.0) for plane in observed]
    for sweep in range(ITERS):
        low = 2 * HALF * sweep + HALF
        blurred = blur(estimate)
        size = blurred[0].shape[0]
        mask = inside(low, size)
        ratio = [jnp.where(mask, observed[y][low : low + size] / blurred[y], 0.0) for y in range(planes)]
        spread = blur(ratio)
        estimate = [estimate[y][2 * HALF : 2 * HALF + spread[y].shape[0]] * spread[y] for y in range(planes)]
    for y in range(planes):
        out_ref[y] = estimate[y]


def deblur_tile(observed, spread_taps, order):
    planes, width, depth = observed.shape
    band_x = band_matrix(spread_taps[0], width - 2 * HALF)
    square_z = band_matrix(spread_taps[2], CZ)[:, HALF : HALF + CZ]
    band_z = square_z[order][:, order].T
    vmem = pl.BlockSpec(memory_space=pltpu.VMEM)
    return pl.pallas_call(
        deblur_kernel,
        out_shape=jax.ShapeDtypeStruct((planes, CX, depth), jnp.float32),
        in_specs=[pl.BlockSpec(memory_space=pltpu.SMEM), vmem, vmem, vmem],
        out_specs=vmem,
    )(spread_taps, observed, band_x, band_z)


def per_device(spectra, lag_samples, slowness, spread_taps):
    groups = lax.axis_size("sta")
    own_count = FREQS // groups
    first_bin = lax.axis_index("sta") * own_count
    block = spectra.shape[2]
    spec_send = spectra.reshape(groups, own_count, 2, block).transpose(0, 2, 1, 3)
    local_power = beam_power(spec_send, lag_samples, slowness[0])
    halo_tiles = -(-(ITERS * 2 * HALF) // CX)
    summed = share_power(local_power, halo_tiles)
    order = jnp.concatenate([jnp.arange(CZ // 2), jnp.arange(CZ - 1, CZ // 2 - 1, -1)])
    observed = summed / (FREQS * STATIONS) + BACKGROUND
    slots = observed.shape[0]
    planes = observed.reshape(slots, CY, CX, CZ).transpose(1, 0, 2, 3).reshape(CY, slots * CX, CZ)
    estimate = deblur_tile(planes, spread_taps, order)
    both = jnp.stack([observed[halo_tiles].reshape(CY, CX, CZ), estimate])
    both = jnp.concatenate([both[..., : CZ // 2], both[..., CZ // 2 :][..., ::-1]], axis=-1).transpose(0, 2, 1, 3)
    stacked, estimate = both[0], both[1]
    return (stacked[None], estimate[None])


def solution(mesh):
    placed = (P(None, None, "sta"), P("grid", "sta"), P("grid", None, "sta"), P())
    return jax.shard_map(
        per_device,
        mesh=mesh,
        in_specs=placed,
        out_specs=(P("grid", None, None, None), P("grid", None, None, None)),
        check_vma=False,
    )
```

```python
import math

import jax
import jax.numpy as jnp
from jax import lax
from jax.sharding import PartitionSpec as P
from jax.experimental import pallas as pl
from jax.experimental.pallas import tpu as pltpu

STATIONS = 6144
FREQS = 64
F0 = 600
NT = 6000
TAPS = 17
HALF = 8
ITERS = 4
CX = 32
CY = 8
CZ = 128


TWO_PI = 2.0 * math.pi
BACKGROUND = 0.05


def with_halo(array, sides, width):
    for axis, dim in sides:
        size, length = (lax.axis_size(axis), array.shape[dim])
        up = [(i, (i + 1) % size) for i in range(size - 1)]
        down = [(j, i) for i, j in up]
        last = lax.slice_in_dim(array, length - width, length, axis=dim)
        leading = lax.slice_in_dim(array, 0, width, axis=dim)
        before = lax.ppermute(last, axis, up)
        after = lax.ppermute(leading, axis, down)
        array = jnp.concatenate([before, array, after], axis=dim)
    return array


def align_rows(spectra, lag_row):
    bins = F0 + jnp.arange(FREQS, dtype=jnp.int32)
    cycles = bins[:, None] * lag_row[None, :] % NT
    turned = cycles.astype(jnp.float32) * (TWO_PI / NT)
    cosine = jnp.cos(turned)
    sine = jnp.sin(turned)
    real_in = spectra[:, 0, :].astype(jnp.float32)
    imag_in = spectra[:, 1, :].astype(jnp.float32)
    real_out = real_in * cosine + imag_in * sine
    imag_out = imag_in * cosine - real_in * sine
    return jnp.stack([real_out, imag_out], axis=1).astype(jnp.bfloat16)


def beam_freq(freq, aligned_row, slow_rows):
    omega = (F0 + freq).astype(jnp.float32) * (TWO_PI / NT)
    slow = slow_rows.astype(jnp.float32)
    x_coord = jnp.arange(CX, dtype=jnp.float32) - (CX - 1) / 2.0
    y_coord = jnp.arange(CY, dtype=jnp.float32) - (CY - 1) / 2.0
    z_coord = jnp.arange(CZ, dtype=jnp.float32) - (CZ - 1) / 2.0
    phase_x = (omega * slow[0])[None, :] * x_coord[:, None]
    phase_y = (omega * slow[1])[None, :] * y_coord[:, None]
    phase = phase_x[:, None, :] + phase_y[None, :, :]
    cosine = jnp.cos(phase)
    sine = jnp.sin(phase)
    real_in = aligned_row[0].astype(jnp.float32)[None, None, :]
    imag_in = aligned_row[1].astype(jnp.float32)[None, None, :]
    front_real = (real_in * cosine + imag_in * sine).astype(jnp.bfloat16).reshape(CX * CY, -1)
    front_imag = (imag_in * cosine - real_in * sine).astype(jnp.bfloat16).reshape(CX * CY, -1)
    left_side = jnp.concatenate([front_real, front_imag], axis=1)
    phase_z = (omega * slow[2])[:, None] * z_coord[None, :]
    depth_real = jnp.cos(phase_z).astype(jnp.bfloat16)
    depth_imag = jnp.sin(phase_z).astype(jnp.bfloat16)
    upper_rows = jnp.concatenate([depth_real, -depth_imag], axis=1)
    lower_rows = jnp.concatenate([depth_imag, depth_real], axis=1)
    right_side = jnp.concatenate([upper_rows, lower_rows], axis=0)
    return jnp.dot(left_side, right_side, preferred_element_type=jnp.float32)


CHUNK = 256


def exp_neg(angle):
    return jnp.cos(angle), -jnp.sin(angle)


def exchange_inputs(spec_ref, lag_ref, slow_ref, spec_in, lag_in, slow_in, local_sem, send_sem, recv_sem, then):
    count = spec_in.shape[0]
    me = lax.axis_index("sta")
    tile = lax.axis_index("grid")
    mesh_ids = pl.DeviceIdType.MESH
    barrier = pltpu.get_barrier_semaphore()
    for shift in range(1, count):
        peer = lax.rem(me + shift, count)
        pl.semaphore_signal(barrier, inc=1, device_id=(tile, peer), device_id_type=mesh_ids)
    pl.semaphore_wait(barrier, count - 1)
    pairs = ((spec_ref, spec_in), (lag_ref, lag_in), (slow_ref, slow_in))
    local = []
    for kind, (source, target) in enumerate(pairs):
        own = source.at[me] if kind == 0 else source
        copy = pltpu.make_async_copy(own, target.at[me], local_sem.at[kind])
        copy.start()
        local.append(copy)
    sends = []
    for shift in range(1, count):
        peer = lax.rem(me + shift, count)
        for kind, (source, target) in enumerate(pairs):
            part = source.at[peer] if kind == 0 else source
            copy = pltpu.make_async_remote_copy(
                src_ref=part,
                dst_ref=target.at[me],
                send_sem=send_sem.at[kind, shift],
                recv_sem=recv_sem.at[kind, me],
                device_id=(tile, peer),
                device_id_type=mesh_ids,
            )
            copy.start()
            sends.append(copy)
    then()
    for copy in local:
        copy.wait()
    for copy in sends:
        copy.wait_send()
    for shift in range(1, count):
        source_id = lax.rem(me + count - shift, count)
        for kind, (source, target) in enumerate(pairs):
            part = source.at[source_id] if kind == 0 else source
            pltpu.make_async_remote_copy(
                src_ref=part,
                dst_ref=target.at[source_id],
                send_sem=send_sem.at[kind, shift],
                recv_sem=recv_sem.at[kind, source_id],
                device_id=(tile, source_id),
                device_id_type=mesh_ids,
            ).wait_recv()


def align_block(spec, lag, slow, source, real_ref, imag_ref, turn_ref):
    bins, block = spec.shape[1], spec.shape[2]
    first_bin = lax.axis_index("sta") * bins
    bin_rows = (F0 + first_bin + lax.broadcasted_iota(jnp.int32, (bins, block), 0)).astype(jnp.float32)
    cols = pl.ds(pl.multiple_of(source * block, 128), block)
    product = bin_rows * lag.astype(jnp.float32)
    whole = jnp.floor(product * (1.0 / NT))
    left = product - whole * NT
    left = jnp.where(left < 0.0, left + NT, left)
    left = jnp.where(left >= NT, left - NT, left)
    turned = left * (TWO_PI / NT)
    cosine = jnp.cos(turned)
    sine = jnp.sin(turned)
    real_in = spec[0].astype(jnp.float32)
    imag_in = spec[1].astype(jnp.float32)
    real_ref[:, cols] = (real_in * cosine + imag_in * sine).astype(jnp.bfloat16).astype(jnp.float32)
    imag_ref[:, cols] = (imag_in * cosine - real_in * sine).astype(jnp.bfloat16).astype(jnp.float32)
    turn_ref[:, cols] = slow.astype(jnp.float32)


def complex_times(left, right):
    return left[0] * right[0] - left[1] * right[1], left[0] * right[1] + left[1] * right[0]


def factor_rows(turn_x, turn_y, turn_z, rows8, rows16):
    return (
        exp_neg(turn_x * (rows8 - 3.5)),
        exp_neg(turn_x * (8.0 * (rows8 - 1.5))),
        exp_neg(turn_y * (rows8 - 3.5)),
        exp_neg(turn_z * (rows16 - 7.5)),
        exp_neg(turn_z * (16.0 * (rows8 - 3.5))),
    )


def beam_kernel(spec_ref, lag_ref, slow_ref, power_ref, spec_in, lag_in, slow_in, local_sem, send_sem, recv_sem,
                real_ref, imag_ref, turn_ref, acc_ref, left_ref, right_ref):
    count, bins, block = spec_in.shape[0], spec_in.shape[2], spec_in.shape[3]
    me = lax.axis_index("sta")
    first_bin = me * bins
    width = CHUNK
    per_block = block // width
    half_z = CZ // 2
    rows8 = lax.broadcasted_iota(jnp.int32, (8, width), 0).astype(jnp.float32)
    rows16 = lax.broadcasted_iota(jnp.int32, (16, width), 0).astype(jnp.float32)
    omega0 = (F0 + first_bin).astype(jnp.float32) * (TWO_PI / NT)
    step = TWO_PI / NT
    acc_ref[...] = jnp.zeros_like(acc_ref)

    def per_chunk(k, carry):
        source = lax.rem(me + k // per_block, count)
        cols = pl.ds(pl.multiple_of(source * block + lax.rem(k, per_block) * width, 128), width)
        slow_x = turn_ref[0:1, cols]
        slow_y = turn_ref[1:2, cols]
        slow_z = turn_ref[2:3, cols]
        start = factor_rows(omega0 * slow_x, omega0 * slow_y, omega0 * slow_z, rows8, rows16)
        ratio = factor_rows(step * slow_x, step * slow_y, step * slow_z, rows8, rows16)

        def per_bin(f, state):
            (a_r, a_i), (b_r, b_i), (y_r, y_i), (c_r, c_i), (d_r, d_i) = state
            real_in = real_ref[pl.ds(f, 1), cols]
            imag_in = imag_ref[pl.ds(f, 1), cols]
            q_r = real_in * y_r - imag_in * y_i
            q_i = real_in * y_i + imag_in * y_r
            near = [complex_times((b_r[m : m + 1], b_i[m : m + 1]), (a_r, a_i)) for m in range(CX // 16)]
            cells = CX * CY
            for y in range(CY):
                qq_r, qq_i = q_r[y : y + 1], q_i[y : y + 1]
                lo_r, lo_i, hi_r, hi_i = [], [], [], []
                for x_r, x_i in near:
                    t1, t2 = qq_r * x_r, qq_i * x_i
                    t3, t4 = qq_r * x_i, qq_i * x_r
                    lo_r.append(t1 - t2)
                    lo_i.append(t3 + t4)
                    hi_r.append(t1 + t2)
                    hi_i.append(t4 - t3)
                row = y * CX
                half = CX // 2
                left_ref[row : row + half, :] = jnp.concatenate(lo_r, axis=0).astype(jnp.bfloat16)
                left_ref[row + half : row + CX, :] = jnp.concatenate(hi_r, axis=0).astype(jnp.bfloat16)
                left_ref[cells + row : cells + row + half, :] = jnp.concatenate(lo_i, axis=0).astype(jnp.bfloat16)
                left_ref[cells + row + half : cells + row + CX, :] = jnp.concatenate(hi_i, axis=0).astype(jnp.bfloat16)
            for m in range(half_z // 16):
                z_r, z_i = complex_times((d_r[m : m + 1], d_i[m : m + 1]), (c_r, c_i))
                row = 16 * m
                right_ref[row : row + 16, :] = z_r.astype(jnp.bfloat16)
                right_ref[half_z + row : half_z + row + 16, :] = z_i.astype(jnp.bfloat16)
            acc_ref[f] += lax.dot_general(
                left_ref[...], right_ref[...], (((1,), (1,)), ((), ())), preferred_element_type=jnp.float32
            )
            return tuple(complex_times(now, turn) for now, turn in zip(state, ratio))

        lax.fori_loop(0, bins, per_bin, start)
        return carry

    def own_block():
        align_block(spec_ref[me], lag_ref[...], slow_ref[...], me, real_ref, imag_ref, turn_ref)
        lax.fori_loop(0, per_block, per_chunk, 0)

    exchange_inputs(spec_ref, lag_ref, slow_ref, spec_in, lag_in, slow_in, local_sem, send_sem, recv_sem, own_block)

    def align_other(shift, carry):
        source = lax.rem(me + shift, count)
        align_block(spec_in[source], lag_in[source], slow_in[source], source, real_ref, imag_ref, turn_ref)
        return carry

    lax.fori_loop(1, count, align_other, 0)
    lax.fori_loop(per_block, count * per_block, per_chunk, 0)
    cells = CX * CY
    low = jnp.zeros((cells, half_z), jnp.float32)
    high = jnp.zeros((cells, half_z), jnp.float32)
    for f in range(bins):
        sums = acc_ref[f]
        u, w = sums[:cells, :half_z], sums[:cells, half_z:]
        x, v = sums[cells:, :half_z], sums[cells:, half_z:]
        low = low + ((u - v) * (u - v) + (w + x) * (w + x))
        high = high + ((u + v) * (u + v) + (x - w) * (x - w))
    power_ref[:, :half_z] = low
    power_ref[:, half_z:] = high


def beam_power(spec_send, lag_row, slow_rows):
    count = spec_send.shape[0]
    bins, block = spec_send.shape[2], spec_send.shape[3]
    width = CHUNK
    stations = count * block
    vmem = pl.BlockSpec(memory_space=pltpu.VMEM)
    return pl.pallas_call(
        beam_kernel,
        out_shape=jax.ShapeDtypeStruct((CX * CY, CZ), jnp.float32),
        in_specs=[vmem, vmem, vmem],
        out_specs=vmem,
        scratch_shapes=[
            pltpu.VMEM((count,) + spec_send.shape[1:], jnp.bfloat16),
            pltpu.VMEM((count,) + lag_row.shape, jnp.int32),
            pltpu.VMEM((count,) + slow_rows.shape, jnp.bfloat16),
            pltpu.SemaphoreType.DMA((3,)),
            pltpu.SemaphoreType.DMA((3, count)),
            pltpu.SemaphoreType.DMA((3, count)),
            pltpu.VMEM((bins, stations), jnp.float32),
            pltpu.VMEM((bins, stations), jnp.float32),
            pltpu.VMEM((slow_rows.shape[0], stations), jnp.float32),
            pltpu.VMEM((bins, 2 * CX * CY, CZ), jnp.float32),
            pltpu.VMEM((2 * CX * CY, width), jnp.bfloat16),
            pltpu.VMEM((CZ, width), jnp.bfloat16),
        ],
        compiler_params=pltpu.CompilerParams(collective_id=1, has_side_effects=True),
    )(spec_send, lag_row, slow_rows)


def share_kernel(part_ref, out_ref, pieces, send_rs, recv_rs, send_ag, recv_ag, local_sem):
    count = pieces.shape[0]
    slots = out_ref.shape[0]
    reach = slots // 2
    rows = pieces.shape[1]
    me = lax.axis_index("sta")
    tile = lax.axis_index("grid")
    tiles = lax.axis_size("grid")
    mesh_ids = pl.DeviceIdType.MESH
    barrier = pltpu.get_barrier_semaphore()
    for shift in range(1, count):
        pl.semaphore_signal(barrier, inc=1, device_id=(tile, lax.rem(me + shift, count)), device_id_type=mesh_ids)
    neighbours = jnp.int32(0)
    for k in range(-reach, reach + 1):
        if k == 0:
            continue
        there = (tile + k >= 0) & (tile + k < tiles)
        neighbours = neighbours + there.astype(jnp.int32)

        @pl.when(there)
        def _():
            for peer in range(count):
                pl.semaphore_signal(barrier, inc=1, device_id=(tile + k, peer), device_id_type=mesh_ids)

    pl.semaphore_wait(barrier, count - 1 + count * neighbours)
    own = pltpu.make_async_copy(part_ref.at[pl.ds(pl.multiple_of(me * rows, 8), rows)], pieces.at[me], local_sem.at[0])
    own.start()
    sends = []
    for shift in range(1, count):
        peer = lax.rem(me + shift, count)
        copy = pltpu.make_async_remote_copy(
            src_ref=part_ref.at[pl.ds(pl.multiple_of(peer * rows, 8), rows)],
            dst_ref=pieces.at[me],
            send_sem=send_rs.at[shift],
            recv_sem=recv_rs.at[me],
            device_id=(tile, peer),
            device_id_type=mesh_ids,
        )
        copy.start()
        sends.append(copy)
    own.wait()
    for copy in sends:
        copy.wait_send()
    for shift in range(1, count):
        source = lax.rem(me + count - shift, count)
        pltpu.make_async_remote_copy(
            src_ref=pieces.at[source],
            dst_ref=pieces.at[source],
            send_sem=send_rs.at[shift],
            recv_sem=recv_rs.at[source],
            device_id=(tile, source),
            device_id_type=mesh_ids,
        ).wait_recv()
    total = pieces[0]
    for source in range(1, count):
        total = total + pieces[source]
    mine = pl.ds(pl.multiple_of(me * rows, 8), rows)
    out_ref[reach, mine] = total
    block = out_ref.at[reach, mine]

    def gather_copy(k, peer, slot):
        return pltpu.make_async_remote_copy(
            src_ref=block,
            dst_ref=out_ref.at[slot, mine],
            send_sem=send_ag.at[slot, peer],
            recv_sem=recv_ag.at[slot, me],
            device_id=(tile + k, peer),
            device_id_type=mesh_ids,
        )

    peers = []
    for shift in range(1, count):
        copy = gather_copy(0, lax.rem(me + shift, count), reach)
        copy.start()
        peers.append(copy)
    for k in range(-reach, reach + 1):
        if k == 0:
            continue
        there = (tile + k >= 0) & (tile + k < tiles)

        @pl.when(there)
        def _():
            for peer in range(count):
                gather_copy(k, peer, reach - k).start()

        @pl.when(jnp.logical_not(there))
        def _():
            out_ref[reach + k] = jnp.zeros(out_ref.shape[1:], out_ref.dtype)

    for copy in peers:
        copy.wait_send()
    for shift in range(1, count):
        source = lax.rem(me + count - shift, count)
        pltpu.make_async_remote_copy(
            src_ref=block,
            dst_ref=out_ref.at[reach, pl.ds(pl.multiple_of(source * rows, 8), rows)],
            send_sem=send_ag.at[reach, source],
            recv_sem=recv_ag.at[reach, source],
            device_id=(tile, source),
            device_id_type=mesh_ids,
        ).wait_recv()
    for k in range(-reach, reach + 1):
        if k == 0:
            continue
        there = (tile + k >= 0) & (tile + k < tiles)

        @pl.when(there)
        def _():
            for peer in range(count):
                gather_copy(k, peer, reach - k).wait_send()
                pltpu.make_async_remote_copy(
                    src_ref=block,
                    dst_ref=out_ref.at[reach + k, pl.ds(peer * rows, rows)],
                    send_sem=send_ag.at[reach + k, peer],
                    recv_sem=recv_ag.at[reach + k, peer],
                    device_id=(tile + k, peer),
                    device_id_type=mesh_ids,
                ).wait_recv()


def share_power(part, reach):
    count = lax.axis_size("sta")
    rows = part.shape[0] // count
    slots = 2 * reach + 1
    return pl.pallas_call(
        share_kernel,
        out_shape=jax.ShapeDtypeStruct((slots,) + part.shape, jnp.float32),
        in_specs=[pl.BlockSpec(memory_space=pltpu.VMEM)],
        out_specs=pl.BlockSpec(memory_space=pltpu.VMEM),
        scratch_shapes=[
            pltpu.VMEM((count, rows, part.shape[1]), jnp.float32),
            pltpu.SemaphoreType.DMA((count,)),
            pltpu.SemaphoreType.DMA((count,)),
            pltpu.SemaphoreType.DMA((slots, count)),
            pltpu.SemaphoreType.DMA((slots, count)),
            pltpu.SemaphoreType.DMA((1,)),
        ],
        compiler_params=pltpu.CompilerParams(collective_id=0, has_side_effects=True),
    )(part)


def freq_beams(freq_ids, aligned_rows, slow_rows):
    return lax.map(lambda pair: beam_freq(pair[0], pair[1], slow_rows), (freq_ids, aligned_rows))


def band_matrix(taps, length):
    rows = jnp.arange(length, dtype=jnp.int32)[:, None]
    columns = jnp.arange(length + 2 * HALF, dtype=jnp.int32)[None, :]
    offset = columns - rows
    picks = jnp.arange(TAPS, dtype=jnp.int32)[:, None, None]
    return jnp.sum(jnp.where(offset[None] == picks, taps[:, None, None], 0.0), axis=0)


def blur(volume, bands):
    band_x, square_y, square_z = bands
    padded = with_halo(volume.astype(jnp.bfloat16), (("grid", 0),), HALF).astype(volume.dtype)
    along_x = jnp.einsum("ip,pyz->iyz", band_x, padded, precision=lax.Precision.HIGHEST)
    along_y = jnp.einsum("jq,xqz->xjz", square_y, along_x, precision=lax.Precision.HIGHEST)
    return jnp.einsum("xyw,kw->xyk", along_y, square_z, precision=lax.Precision.HIGHEST)


def blur_narrowing(volume, taps, square_y, square_z):
    band_x = band_matrix(taps, volume.shape[0] - 2 * HALF)
    along_x = jnp.einsum("ip,pyz->iyz", band_x, volume, precision=lax.Precision.HIGHEST)
    along_y = jnp.einsum("jq,xqz->xjz", square_y, along_x, precision=lax.Precision.HIGHEST)
    return jnp.einsum("xyw,kw->xyk", along_y, square_z, precision=lax.Precision.HIGHEST)


def deblur(observed, halo_tiles, spread_taps):
    tiles = lax.axis_size("grid")
    me = lax.axis_index("grid")
    reach = ITERS * 2 * HALF
    cut = halo_tiles * CX - reach
    observed = observed[cut : observed.shape[0] - cut]
    width = observed.shape[0]
    cell = (me - halo_tiles) * CX + cut + jnp.arange(width, dtype=jnp.int32)
    inside = (cell >= 0) & (cell < tiles * CX)
    square_y = band_matrix(spread_taps[1], CY)[:, HALF : HALF + CY]
    square_z = band_matrix(spread_taps[2], CZ)[:, HALF : HALF + CZ]
    estimate = jnp.where(inside[:, None, None], observed, 0.0)
    for sweep in range(ITERS):
        low = 2 * HALF * sweep + HALF
        blurred = blur_narrowing(estimate, spread_taps[0], square_y, square_z)
        ratio = jnp.where(
            inside[low : width - low, None, None], observed[low : width - low] / blurred, 0.0
        )
        estimate = estimate[2 * HALF : estimate.shape[0] - 2 * HALF] * blur_narrowing(
            ratio, spread_taps[0], square_y, square_z
        )
    return estimate


def deblur_kernel(taps_ref, obs_ref, kx_ref, kz_ref, out_ref):
    tiles = lax.axis_size("grid")
    me = lax.axis_index("grid")
    planes, width, depth = obs_ref.shape
    halo_tiles = (width - CX) // (2 * CX)
    highest = lax.Precision.HIGHEST

    def inside(low, size):
        cell = (me - halo_tiles) * CX + low + lax.broadcasted_iota(jnp.int32, (size, depth), 0)
        return (cell >= 0) & (cell < tiles * CX)

    def blur(volume):
        size_in = volume[0].shape[0]
        size_out = size_in - 2 * HALF
        band = kx_ref[0:size_out, 0:size_in]
        along_x = [jnp.dot(band, plane, precision=highest, preferred_element_type=jnp.float32) for plane in volume]
        along_y = []
        for y in range(planes):
            total = None
            for q in range(planes):
                term = taps_ref[1, q - y + HALF] * along_x[q]
                total = term if total is None else total + term
            along_y.append(total)
        joined = jnp.concatenate(along_y, axis=0)
        along_z = jnp.dot(joined, kz_ref[...], precision=highest, preferred_element_type=jnp.float32)
        return [along_z[y * size_out : (y + 1) * size_out] for y in range(planes)]

    observed = [obs_ref[y] for y in range(planes)]
    mask = inside(0, width)
    estimate = [jnp.where(mask, plane, 0.0) for plane in observed]
    for sweep in range(ITERS):
        low = 2 * HALF * sweep + HALF
        blurred = blur(estimate)
        size = blurred[0].shape[0]
        mask = inside(low, size)
        ratio = [jnp.where(mask, observed[y][low : low + size] / blurred[y], 0.0) for y in range(planes)]
        spread = blur(ratio)
        estimate = [estimate[y][2 * HALF : 2 * HALF + spread[y].shape[0]] * spread[y] for y in range(planes)]
    for y in range(planes):
        out_ref[y] = estimate[y]


def deblur_tile(observed, spread_taps, order):
    planes, width, depth = observed.shape
    band_x = band_matrix(spread_taps[0], width - 2 * HALF)
    square_z = band_matrix(spread_taps[2], CZ)[:, HALF : HALF + CZ]
    band_z = square_z[order][:, order].T
    vmem = pl.BlockSpec(memory_space=pltpu.VMEM)
    return pl.pallas_call(
        deblur_kernel,
        out_shape=jax.ShapeDtypeStruct((planes, CX, depth), jnp.float32),
        in_specs=[pl.BlockSpec(memory_space=pltpu.SMEM), vmem, vmem, vmem],
        out_specs=vmem,
    )(spread_taps, observed, band_x, band_z)


def per_device(spectra, lag_samples, slowness, spread_taps):
    groups = lax.axis_size("sta")
    own_count = FREQS // groups
    first_bin = lax.axis_index("sta") * own_count
    block = spectra.shape[2]
    spec_send = spectra.reshape(groups, own_count, 2, block).transpose(0, 2, 1, 3)
    local_power = beam_power(spec_send, lag_samples, slowness[0])
    halo_tiles = -(-(ITERS * 2 * HALF) // CX)
    summed = share_power(local_power, halo_tiles)
    order = jnp.concatenate([jnp.arange(CZ // 2), jnp.arange(CZ - 1, CZ // 2 - 1, -1)])
    observed = summed / (FREQS * STATIONS) + BACKGROUND
    slots = observed.shape[0]
    observed = observed.reshape(slots, CY, CX, CZ)
    observed = jnp.concatenate([observed[:, :, : CX // 2], observed[:, :, CX // 2 :][:, :, ::-1]], axis=2)
    planes = observed.transpose(1, 0, 2, 3).reshape(CY, slots * CX, CZ)
    estimate = deblur_tile(planes, spread_taps, order)
    both = jnp.stack([observed[halo_tiles], estimate])
    both = jnp.concatenate([both[..., : CZ // 2], both[..., CZ // 2 :][..., ::-1]], axis=-1).transpose(0, 2, 1, 3)
    stacked, estimate = both[0], both[1]
    return (stacked[None], estimate[None])


def solution(mesh):
    placed = (P(None, None, "sta"), P("grid", "sta"), P("grid", None, "sta"), P())
    return jax.shard_map(
        per_device,
        mesh=mesh,
        in_specs=placed,
        out_specs=(P("grid", None, None, None), P("grid", None, None, None)),
        check_vma=False,
    )
```

```python
import math

import jax
import jax.numpy as jnp
from jax import lax
from jax.sharding import PartitionSpec as P
from jax.experimental import pallas as pl
from jax.experimental.pallas import tpu as pltpu

STATIONS = 6144
FREQS = 64
F0 = 600
NT = 6000
TAPS = 17
HALF = 8
ITERS = 4
CX = 32
CY = 8
CZ = 128


TWO_PI = 2.0 * math.pi
BACKGROUND = 0.05


def with_halo(array, sides, width):
    for axis, dim in sides:
        size, length = (lax.axis_size(axis), array.shape[dim])
        up = [(i, (i + 1) % size) for i in range(size - 1)]
        down = [(j, i) for i, j in up]
        last = lax.slice_in_dim(array, length - width, length, axis=dim)
        leading = lax.slice_in_dim(array, 0, width, axis=dim)
        before = lax.ppermute(last, axis, up)
        after = lax.ppermute(leading, axis, down)
        array = jnp.concatenate([before, array, after], axis=dim)
    return array


def align_rows(spectra, lag_row):
    bins = F0 + jnp.arange(FREQS, dtype=jnp.int32)
    cycles = bins[:, None] * lag_row[None, :] % NT
    turned = cycles.astype(jnp.float32) * (TWO_PI / NT)
    cosine = jnp.cos(turned)
    sine = jnp.sin(turned)
    real_in = spectra[:, 0, :].astype(jnp.float32)
    imag_in = spectra[:, 1, :].astype(jnp.float32)
    real_out = real_in * cosine + imag_in * sine
    imag_out = imag_in * cosine - real_in * sine
    return jnp.stack([real_out, imag_out], axis=1).astype(jnp.bfloat16)


def beam_freq(freq, aligned_row, slow_rows):
    omega = (F0 + freq).astype(jnp.float32) * (TWO_PI / NT)
    slow = slow_rows.astype(jnp.float32)
    x_coord = jnp.arange(CX, dtype=jnp.float32) - (CX - 1) / 2.0
    y_coord = jnp.arange(CY, dtype=jnp.float32) - (CY - 1) / 2.0
    z_coord = jnp.arange(CZ, dtype=jnp.float32) - (CZ - 1) / 2.0
    phase_x = (omega * slow[0])[None, :] * x_coord[:, None]
    phase_y = (omega * slow[1])[None, :] * y_coord[:, None]
    phase = phase_x[:, None, :] + phase_y[None, :, :]
    cosine = jnp.cos(phase)
    sine = jnp.sin(phase)
    real_in = aligned_row[0].astype(jnp.float32)[None, None, :]
    imag_in = aligned_row[1].astype(jnp.float32)[None, None, :]
    front_real = (real_in * cosine + imag_in * sine).astype(jnp.bfloat16).reshape(CX * CY, -1)
    front_imag = (imag_in * cosine - real_in * sine).astype(jnp.bfloat16).reshape(CX * CY, -1)
    left_side = jnp.concatenate([front_real, front_imag], axis=1)
    phase_z = (omega * slow[2])[:, None] * z_coord[None, :]
    depth_real = jnp.cos(phase_z).astype(jnp.bfloat16)
    depth_imag = jnp.sin(phase_z).astype(jnp.bfloat16)
    upper_rows = jnp.concatenate([depth_real, -depth_imag], axis=1)
    lower_rows = jnp.concatenate([depth_imag, depth_real], axis=1)
    right_side = jnp.concatenate([upper_rows, lower_rows], axis=0)
    return jnp.dot(left_side, right_side, preferred_element_type=jnp.float32)


CHUNK = 256


def exp_neg(angle):
    return jnp.cos(angle), -jnp.sin(angle)


def exchange_inputs(spec_ref, lag_ref, slow_ref, spec_in, lag_in, slow_in, local_sem, send_sem, recv_sem, then):
    count = spec_in.shape[0]
    me = lax.axis_index("sta")
    tile = lax.axis_index("grid")
    mesh_ids = pl.DeviceIdType.MESH
    barrier = pltpu.get_barrier_semaphore()
    for shift in range(1, count):
        peer = lax.rem(me + shift, count)
        pl.semaphore_signal(barrier, inc=1, device_id=(tile, peer), device_id_type=mesh_ids)
    pl.semaphore_wait(barrier, count - 1)
    pairs = ((spec_ref, spec_in), (lag_ref, lag_in), (slow_ref, slow_in))
    local = []
    for kind, (source, target) in enumerate(pairs):
        own = source.at[me] if kind == 0 else source
        copy = pltpu.make_async_copy(own, target.at[me], local_sem.at[kind])
        copy.start()
        local.append(copy)
    sends = []
    for shift in range(1, count):
        peer = lax.rem(me + shift, count)
        for kind, (source, target) in enumerate(pairs):
            part = source.at[peer] if kind == 0 else source
            copy = pltpu.make_async_remote_copy(
                src_ref=part,
                dst_ref=target.at[me],
                send_sem=send_sem.at[kind, shift],
                recv_sem=recv_sem.at[kind, me],
                device_id=(tile, peer),
                device_id_type=mesh_ids,
            )
            copy.start()
            sends.append(copy)
    then()
    for copy in local:
        copy.wait()
    for copy in sends:
        copy.wait_send()
    for shift in range(1, count):
        source_id = lax.rem(me + count - shift, count)
        for kind, (source, target) in enumerate(pairs):
            part = source.at[source_id] if kind == 0 else source
            pltpu.make_async_remote_copy(
                src_ref=part,
                dst_ref=target.at[source_id],
                send_sem=send_sem.at[kind, shift],
                recv_sem=recv_sem.at[kind, source_id],
                device_id=(tile, source_id),
                device_id_type=mesh_ids,
            ).wait_recv()


def align_block(spec, lag, slow, source, real_ref, imag_ref, turn_ref):
    bins, block = spec.shape[1], spec.shape[2]
    first_bin = lax.axis_index("sta") * bins
    bin_rows = (F0 + first_bin + lax.broadcasted_iota(jnp.int32, (bins, block), 0)).astype(jnp.float32)
    cols = pl.ds(pl.multiple_of(source * block, 128), block)
    product = bin_rows * lag.astype(jnp.float32)
    whole = jnp.floor(product * (1.0 / NT))
    left = product - whole * NT
    left = jnp.where(left < 0.0, left + NT, left)
    left = jnp.where(left >= NT, left - NT, left)
    turned = left * (TWO_PI / NT)
    cosine = jnp.cos(turned)
    sine = jnp.sin(turned)
    real_in = spec[0].astype(jnp.float32)
    imag_in = spec[1].astype(jnp.float32)
    real_ref[:, cols] = (real_in * cosine + imag_in * sine).astype(jnp.bfloat16).astype(jnp.float32)
    imag_ref[:, cols] = (imag_in * cosine - real_in * sine).astype(jnp.bfloat16).astype(jnp.float32)
    turn_ref[:, cols] = slow.astype(jnp.float32)


def complex_times(left, right):
    return left[0] * right[0] - left[1] * right[1], left[0] * right[1] + left[1] * right[0]


def factor_rows(turn_x, turn_y, turn_z, rows8, rows16):
    return (
        exp_neg(turn_x * (rows8 - 3.5)),
        exp_neg(turn_x * (8.0 * (rows8 - 1.5))),
        exp_neg(turn_y * (rows8 - 3.5)),
        exp_neg(turn_z * (rows16 - 7.5)),
        exp_neg(turn_z * (16.0 * (rows8 - 3.5))),
    )


def beam_kernel(spec_ref, lag_ref, slow_ref, power_ref, spec_in, lag_in, slow_in, local_sem, send_sem, recv_sem,
                real_ref, imag_ref, turn_ref, acc_ref, left_ref, right_ref):
    count, bins, block = spec_in.shape[0], spec_in.shape[2], spec_in.shape[3]
    me = lax.axis_index("sta")
    first_bin = me * bins
    width = CHUNK
    per_block = block // width
    half_z = CZ // 2
    rows8 = lax.broadcasted_iota(jnp.int32, (8, width), 0).astype(jnp.float32)
    rows16 = lax.broadcasted_iota(jnp.int32, (16, width), 0).astype(jnp.float32)
    omega0 = (F0 + first_bin).astype(jnp.float32) * (TWO_PI / NT)
    step = TWO_PI / NT
    acc_ref[...] = jnp.zeros_like(acc_ref)

    def per_chunk(k, carry):
        source = lax.rem(me + k // per_block, count)
        cols = pl.ds(pl.multiple_of(source * block + lax.rem(k, per_block) * width, 128), width)
        slow_x = turn_ref[0:1, cols]
        slow_y = turn_ref[1:2, cols]
        slow_z = turn_ref[2:3, cols]
        start = factor_rows(omega0 * slow_x, omega0 * slow_y, omega0 * slow_z, rows8, rows16)
        ratio = factor_rows(step * slow_x, step * slow_y, step * slow_z, rows8, rows16)

        def per_bin(f, state):
            (a_r, a_i), (b_r, b_i), (y_r, y_i), (c_r, c_i), (d_r, d_i) = state
            real_in = real_ref[pl.ds(f, 1), cols]
            imag_in = imag_ref[pl.ds(f, 1), cols]
            q_r = real_in * y_r - imag_in * y_i
            q_i = real_in * y_i + imag_in * y_r
            near = [complex_times((b_r[m : m + 1], b_i[m : m + 1]), (a_r, a_i)) for m in range(CX // 16)]
            cells = CX * CY
            for y in range(CY):
                qq_r, qq_i = q_r[y : y + 1], q_i[y : y + 1]
                lo_r, lo_i, hi_r, hi_i = [], [], [], []
                for x_r, x_i in near:
                    t1, t2 = qq_r * x_r, qq_i * x_i
                    t3, t4 = qq_r * x_i, qq_i * x_r
                    lo_r.append(t1 - t2)
                    lo_i.append(t3 + t4)
                    hi_r.append(t1 + t2)
                    hi_i.append(t4 - t3)
                row = y * CX
                half = CX // 2
                left_ref[row : row + half, :] = jnp.concatenate(lo_r, axis=0).astype(jnp.bfloat16)
                left_ref[row + half : row + CX, :] = jnp.concatenate(hi_r, axis=0).astype(jnp.bfloat16)
                left_ref[cells + row : cells + row + half, :] = jnp.concatenate(lo_i, axis=0).astype(jnp.bfloat16)
                left_ref[cells + row + half : cells + row + CX, :] = jnp.concatenate(hi_i, axis=0).astype(jnp.bfloat16)
            for m in range(half_z // 16):
                z_r, z_i = complex_times((d_r[m : m + 1], d_i[m : m + 1]), (c_r, c_i))
                row = 16 * m
                right_ref[row : row + 16, :] = z_r.astype(jnp.bfloat16)
                right_ref[half_z + row : half_z + row + 16, :] = z_i.astype(jnp.bfloat16)
            acc_ref[f] += lax.dot_general(
                left_ref[...], right_ref[...], (((1,), (1,)), ((), ())), preferred_element_type=jnp.float32
            )
            return tuple(complex_times(now, turn) for now, turn in zip(state, ratio))

        lax.fori_loop(0, bins, per_bin, start)
        return carry

    def own_block():
        align_block(spec_ref[me], lag_ref[...], slow_ref[...], me, real_ref, imag_ref, turn_ref)
        lax.fori_loop(0, per_block, per_chunk, 0)

    exchange_inputs(spec_ref, lag_ref, slow_ref, spec_in, lag_in, slow_in, local_sem, send_sem, recv_sem, own_block)

    def align_other(shift, carry):
        source = lax.rem(me + shift, count)
        align_block(spec_in[source], lag_in[source], slow_in[source], source, real_ref, imag_ref, turn_ref)
        return carry

    lax.fori_loop(1, count, align_other, 0)
    lax.fori_loop(per_block, count * per_block, per_chunk, 0)
    cells = CX * CY
    low = jnp.zeros((cells, half_z), jnp.float32)
    high = jnp.zeros((cells, half_z), jnp.float32)
    for f in range(bins):
        sums = acc_ref[f]
        u, w = sums[:cells, :half_z], sums[:cells, half_z:]
        x, v = sums[cells:, :half_z], sums[cells:, half_z:]
        low = low + ((u - v) * (u - v) + (w + x) * (w + x))
        high = high + ((u + v) * (u + v) + (x - w) * (x - w))
    power_ref[:, :half_z] = low
    power_ref[:, half_z:] = high


def beam_power(spec_send, lag_row, slow_rows):
    count = spec_send.shape[0]
    bins, block = spec_send.shape[2], spec_send.shape[3]
    width = CHUNK
    stations = count * block
    vmem = pl.BlockSpec(memory_space=pltpu.VMEM)
    return pl.pallas_call(
        beam_kernel,
        out_shape=jax.ShapeDtypeStruct((CX * CY, CZ), jnp.float32),
        in_specs=[vmem, vmem, vmem],
        out_specs=vmem,
        scratch_shapes=[
            pltpu.VMEM((count,) + spec_send.shape[1:], jnp.bfloat16),
            pltpu.VMEM((count,) + lag_row.shape, jnp.int32),
            pltpu.VMEM((count,) + slow_rows.shape, jnp.bfloat16),
            pltpu.SemaphoreType.DMA((3,)),
            pltpu.SemaphoreType.DMA((3, count)),
            pltpu.SemaphoreType.DMA((3, count)),
            pltpu.VMEM((bins, stations), jnp.float32),
            pltpu.VMEM((bins, stations), jnp.float32),
            pltpu.VMEM((slow_rows.shape[0], stations), jnp.float32),
            pltpu.VMEM((bins, 2 * CX * CY, CZ), jnp.float32),
            pltpu.VMEM((2 * CX * CY, width), jnp.bfloat16),
            pltpu.VMEM((CZ, width), jnp.bfloat16),
        ],
        compiler_params=pltpu.CompilerParams(collective_id=1, has_side_effects=True),
    )(spec_send, lag_row, slow_rows)


def share_kernel(part_ref, out_ref, pieces, send_rs, recv_rs, send_ag, recv_ag, local_sem):
    count = pieces.shape[0]
    slots = out_ref.shape[0]
    reach = slots // 2
    rows = pieces.shape[1]
    me = lax.axis_index("sta")
    tile = lax.axis_index("grid")
    tiles = lax.axis_size("grid")
    mesh_ids = pl.DeviceIdType.MESH
    barrier = pltpu.get_barrier_semaphore()
    for shift in range(1, count):
        pl.semaphore_signal(barrier, inc=1, device_id=(tile, lax.rem(me + shift, count)), device_id_type=mesh_ids)
    neighbours = jnp.int32(0)
    for k in range(-reach, reach + 1):
        if k == 0:
            continue
        there = (tile + k >= 0) & (tile + k < tiles)
        neighbours = neighbours + there.astype(jnp.int32)

        @pl.when(there)
        def _():
            pl.semaphore_signal(barrier, inc=1, device_id=(tile + k, me), device_id_type=mesh_ids)

    pl.semaphore_wait(barrier, count - 1 + neighbours)
    own = pltpu.make_async_copy(part_ref.at[pl.ds(pl.multiple_of(me * rows, 8), rows)], pieces.at[me], local_sem.at[0])
    own.start()
    sends = []
    for shift in range(1, count):
        peer = lax.rem(me + shift, count)
        copy = pltpu.make_async_remote_copy(
            src_ref=part_ref.at[pl.ds(pl.multiple_of(peer * rows, 8), rows)],
            dst_ref=pieces.at[me],
            send_sem=send_rs.at[shift],
            recv_sem=recv_rs.at[me],
            device_id=(tile, peer),
            device_id_type=mesh_ids,
        )
        copy.start()
        sends.append(copy)
    own.wait()
    for copy in sends:
        copy.wait_send()
    for shift in range(1, count):
        source = lax.rem(me + count - shift, count)
        pltpu.make_async_remote_copy(
            src_ref=pieces.at[source],
            dst_ref=pieces.at[source],
            send_sem=send_rs.at[shift],
            recv_sem=recv_rs.at[source],
            device_id=(tile, source),
            device_id_type=mesh_ids,
        ).wait_recv()
    total = pieces[0]
    for source in range(1, count):
        total = total + pieces[source]
    mine = pl.ds(pl.multiple_of(me * rows, 8), rows)
    out_ref[reach, mine] = total
    block = out_ref.at[reach, mine]

    def gather_copy(k, peer, slot):
        return pltpu.make_async_remote_copy(
            src_ref=block,
            dst_ref=out_ref.at[slot, mine],
            send_sem=send_ag.at[slot, peer],
            recv_sem=recv_ag.at[slot, me],
            device_id=(tile + k, peer),
            device_id_type=mesh_ids,
        )

    peers = []
    for shift in range(1, count):
        copy = gather_copy(0, lax.rem(me + shift, count), reach)
        copy.start()
        peers.append(copy)
    for k in range(-reach, reach + 1):
        if k == 0:
            continue

        @pl.when(jnp.logical_not((tile + k >= 0) & (tile + k < tiles)))
        def _():
            out_ref[reach + k] = jnp.zeros(out_ref.shape[1:], out_ref.dtype)

    for copy in peers:
        copy.wait_send()
    for shift in range(1, count):
        source = lax.rem(me + count - shift, count)
        pltpu.make_async_remote_copy(
            src_ref=block,
            dst_ref=out_ref.at[reach, pl.ds(pl.multiple_of(source * rows, 8), rows)],
            send_sem=send_ag.at[reach, source],
            recv_sem=recv_ag.at[reach, source],
            device_id=(tile, source),
            device_id_type=mesh_ids,
        ).wait_recv()

    def halo_copy(k):
        return pltpu.make_async_remote_copy(
            src_ref=out_ref.at[reach],
            dst_ref=out_ref.at[reach - k],
            send_sem=send_ag.at[reach - k, me],
            recv_sem=recv_ag.at[reach - k, me],
            device_id=(tile + k, me),
            device_id_type=mesh_ids,
        )

    for k in range(-reach, reach + 1):
        if k == 0:
            continue

        @pl.when((tile + k >= 0) & (tile + k < tiles))
        def _():
            halo_copy(k).start()

    for k in range(-reach, reach + 1):
        if k == 0:
            continue

        @pl.when((tile + k >= 0) & (tile + k < tiles))
        def _():
            halo_copy(k).wait_send()
            pltpu.make_async_remote_copy(
                src_ref=out_ref.at[reach],
                dst_ref=out_ref.at[reach + k],
                send_sem=send_ag.at[reach + k, me],
                recv_sem=recv_ag.at[reach + k, me],
                device_id=(tile + k, me),
                device_id_type=mesh_ids,
            ).wait_recv()


def share_power(part, reach):
    count = lax.axis_size("sta")
    rows = part.shape[0] // count
    slots = 2 * reach + 1
    return pl.pallas_call(
        share_kernel,
        out_shape=jax.ShapeDtypeStruct((slots,) + part.shape, jnp.float32),
        in_specs=[pl.BlockSpec(memory_space=pltpu.VMEM)],
        out_specs=pl.BlockSpec(memory_space=pltpu.VMEM),
        scratch_shapes=[
            pltpu.VMEM((count, rows, part.shape[1]), jnp.float32),
            pltpu.SemaphoreType.DMA((count,)),
            pltpu.SemaphoreType.DMA((count,)),
            pltpu.SemaphoreType.DMA((slots, count)),
            pltpu.SemaphoreType.DMA((slots, count)),
            pltpu.SemaphoreType.DMA((1,)),
        ],
        compiler_params=pltpu.CompilerParams(collective_id=0, has_side_effects=True),
    )(part)


def freq_beams(freq_ids, aligned_rows, slow_rows):
    return lax.map(lambda pair: beam_freq(pair[0], pair[1], slow_rows), (freq_ids, aligned_rows))


def band_matrix(taps, length):
    rows = jnp.arange(length, dtype=jnp.int32)[:, None]
    columns = jnp.arange(length + 2 * HALF, dtype=jnp.int32)[None, :]
    offset = columns - rows
    picks = jnp.arange(TAPS, dtype=jnp.int32)[:, None, None]
    return jnp.sum(jnp.where(offset[None] == picks, taps[:, None, None], 0.0), axis=0)


def blur(volume, bands):
    band_x, square_y, square_z = bands
    padded = with_halo(volume.astype(jnp.bfloat16), (("grid", 0),), HALF).astype(volume.dtype)
    along_x = jnp.einsum("ip,pyz->iyz", band_x, padded, precision=lax.Precision.HIGHEST)
    along_y = jnp.einsum("jq,xqz->xjz", square_y, along_x, precision=lax.Precision.HIGHEST)
    return jnp.einsum("xyw,kw->xyk", along_y, square_z, precision=lax.Precision.HIGHEST)


def blur_narrowing(volume, taps, square_y, square_z):
    band_x = band_matrix(taps, volume.shape[0] - 2 * HALF)
    along_x = jnp.einsum("ip,pyz->iyz", band_x, volume, precision=lax.Precision.HIGHEST)
    along_y = jnp.einsum("jq,xqz->xjz", square_y, along_x, precision=lax.Precision.HIGHEST)
    return jnp.einsum("xyw,kw->xyk", along_y, square_z, precision=lax.Precision.HIGHEST)


def deblur(observed, halo_tiles, spread_taps):
    tiles = lax.axis_size("grid")
    me = lax.axis_index("grid")
    reach = ITERS * 2 * HALF
    cut = halo_tiles * CX - reach
    observed = observed[cut : observed.shape[0] - cut]
    width = observed.shape[0]
    cell = (me - halo_tiles) * CX + cut + jnp.arange(width, dtype=jnp.int32)
    inside = (cell >= 0) & (cell < tiles * CX)
    square_y = band_matrix(spread_taps[1], CY)[:, HALF : HALF + CY]
    square_z = band_matrix(spread_taps[2], CZ)[:, HALF : HALF + CZ]
    estimate = jnp.where(inside[:, None, None], observed, 0.0)
    for sweep in range(ITERS):
        low = 2 * HALF * sweep + HALF
        blurred = blur_narrowing(estimate, spread_taps[0], square_y, square_z)
        ratio = jnp.where(
            inside[low : width - low, None, None], observed[low : width - low] / blurred, 0.0
        )
        estimate = estimate[2 * HALF : estimate.shape[0] - 2 * HALF] * blur_narrowing(
            ratio, spread_taps[0], square_y, square_z
        )
    return estimate


def deblur_kernel(taps_ref, obs_ref, kx_ref, kz_ref, out_ref):
    tiles = lax.axis_size("grid")
    me = lax.axis_index("grid")
    planes, width, depth = obs_ref.shape
    halo_tiles = (width - CX) // (2 * CX)
    highest = lax.Precision.HIGHEST

    def inside(low, size):
        cell = (me - halo_tiles) * CX + low + lax.broadcasted_iota(jnp.int32, (size, depth), 0)
        return (cell >= 0) & (cell < tiles * CX)

    def blur(volume):
        size_in = volume[0].shape[0]
        size_out = size_in - 2 * HALF
        band = kx_ref[0:size_out, 0:size_in]
        along_x = [jnp.dot(band, plane, precision=highest, preferred_element_type=jnp.float32) for plane in volume]
        along_y = []
        for y in range(planes):
            total = None
            for q in range(planes):
                term = taps_ref[1, q - y + HALF] * along_x[q]
                total = term if total is None else total + term
            along_y.append(total)
        joined = jnp.concatenate(along_y, axis=0)
        along_z = jnp.dot(joined, kz_ref[...], precision=highest, preferred_element_type=jnp.float32)
        return [along_z[y * size_out : (y + 1) * size_out] for y in range(planes)]

    observed = [obs_ref[y] for y in range(planes)]
    mask = inside(0, width)
    estimate = [jnp.where(mask, plane, 0.0) for plane in observed]
    for sweep in range(ITERS):
        low = 2 * HALF * sweep + HALF
        blurred = blur(estimate)
        size = blurred[0].shape[0]
        mask = inside(low, size)
        ratio = [jnp.where(mask, observed[y][low : low + size] / blurred[y], 0.0) for y in range(planes)]
        spread = blur(ratio)
        estimate = [estimate[y][2 * HALF : 2 * HALF + spread[y].shape[0]] * spread[y] for y in range(planes)]
    for y in range(planes):
        out_ref[y] = estimate[y]


def deblur_tile(observed, spread_taps, order):
    planes, width, depth = observed.shape
    band_x = band_matrix(spread_taps[0], width - 2 * HALF)
    square_z = band_matrix(spread_taps[2], CZ)[:, HALF : HALF + CZ]
    band_z = square_z[order][:, order].T
    vmem = pl.BlockSpec(memory_space=pltpu.VMEM)
    return pl.pallas_call(
        deblur_kernel,
        out_shape=jax.ShapeDtypeStruct((planes, CX, depth), jnp.float32),
        in_specs=[pl.BlockSpec(memory_space=pltpu.SMEM), vmem, vmem, vmem],
        out_specs=vmem,
    )(spread_taps, observed, band_x, band_z)


def per_device(spectra, lag_samples, slowness, spread_taps):
    groups = lax.axis_size("sta")
    own_count = FREQS // groups
    first_bin = lax.axis_index("sta") * own_count
    block = spectra.shape[2]
    spec_send = spectra.reshape(groups, own_count, 2, block).transpose(0, 2, 1, 3)
    local_power = beam_power(spec_send, lag_samples, slowness[0])
    halo_tiles = -(-(ITERS * 2 * HALF) // CX)
    summed = share_power(local_power, halo_tiles)
    order = jnp.concatenate([jnp.arange(CZ // 2), jnp.arange(CZ - 1, CZ // 2 - 1, -1)])
    observed = summed / (FREQS * STATIONS) + BACKGROUND
    slots = observed.shape[0]
    observed = observed.reshape(slots, CY, CX, CZ)
    observed = jnp.concatenate([observed[:, :, : CX // 2], observed[:, :, CX // 2 :][:, :, ::-1]], axis=2)
    planes = observed.transpose(1, 0, 2, 3).reshape(CY, slots * CX, CZ)
    estimate = deblur_tile(planes, spread_taps, order)
    both = jnp.stack([observed[halo_tiles], estimate])
    both = jnp.concatenate([both[..., : CZ // 2], both[..., CZ // 2 :][..., ::-1]], axis=-1).transpose(0, 2, 1, 3)
    stacked, estimate = both[0], both[1]
    return (stacked[None], estimate[None])


def solution(mesh):
    placed = (P(None, None, "sta"), P("grid", "sta"), P("grid", None, "sta"), P())
    return jax.shard_map(
        per_device,
        mesh=mesh,
        in_specs=placed,
        out_specs=(P("grid", None, None, None), P("grid", None, None, None)),
        check_vma=False,
    )
```

```python
import math

import jax
import jax.numpy as jnp
from jax import lax
from jax.sharding import PartitionSpec as P
from jax.experimental import pallas as pl
from jax.experimental.pallas import tpu as pltpu

STATIONS = 6144
FREQS = 64
F0 = 600
NT = 6000
TAPS = 17
HALF = 8
ITERS = 4
CX = 32
CY = 8
CZ = 128


TWO_PI = 2.0 * math.pi
BACKGROUND = 0.05


def with_halo(array, sides, width):
    for axis, dim in sides:
        size, length = (lax.axis_size(axis), array.shape[dim])
        up = [(i, (i + 1) % size) for i in range(size - 1)]
        down = [(j, i) for i, j in up]
        last = lax.slice_in_dim(array, length - width, length, axis=dim)
        leading = lax.slice_in_dim(array, 0, width, axis=dim)
        before = lax.ppermute(last, axis, up)
        after = lax.ppermute(leading, axis, down)
        array = jnp.concatenate([before, array, after], axis=dim)
    return array


def align_rows(spectra, lag_row):
    bins = F0 + jnp.arange(FREQS, dtype=jnp.int32)
    cycles = bins[:, None] * lag_row[None, :] % NT
    turned = cycles.astype(jnp.float32) * (TWO_PI / NT)
    cosine = jnp.cos(turned)
    sine = jnp.sin(turned)
    real_in = spectra[:, 0, :].astype(jnp.float32)
    imag_in = spectra[:, 1, :].astype(jnp.float32)
    real_out = real_in * cosine + imag_in * sine
    imag_out = imag_in * cosine - real_in * sine
    return jnp.stack([real_out, imag_out], axis=1).astype(jnp.bfloat16)


def beam_freq(freq, aligned_row, slow_rows):
    omega = (F0 + freq).astype(jnp.float32) * (TWO_PI / NT)
    slow = slow_rows.astype(jnp.float32)
    x_coord = jnp.arange(CX, dtype=jnp.float32) - (CX - 1) / 2.0
    y_coord = jnp.arange(CY, dtype=jnp.float32) - (CY - 1) / 2.0
    z_coord = jnp.arange(CZ, dtype=jnp.float32) - (CZ - 1) / 2.0
    phase_x = (omega * slow[0])[None, :] * x_coord[:, None]
    phase_y = (omega * slow[1])[None, :] * y_coord[:, None]
    phase = phase_x[:, None, :] + phase_y[None, :, :]
    cosine = jnp.cos(phase)
    sine = jnp.sin(phase)
    real_in = aligned_row[0].astype(jnp.float32)[None, None, :]
    imag_in = aligned_row[1].astype(jnp.float32)[None, None, :]
    front_real = (real_in * cosine + imag_in * sine).astype(jnp.bfloat16).reshape(CX * CY, -1)
    front_imag = (imag_in * cosine - real_in * sine).astype(jnp.bfloat16).reshape(CX * CY, -1)
    left_side = jnp.concatenate([front_real, front_imag], axis=1)
    phase_z = (omega * slow[2])[:, None] * z_coord[None, :]
    depth_real = jnp.cos(phase_z).astype(jnp.bfloat16)
    depth_imag = jnp.sin(phase_z).astype(jnp.bfloat16)
    upper_rows = jnp.concatenate([depth_real, -depth_imag], axis=1)
    lower_rows = jnp.concatenate([depth_imag, depth_real], axis=1)
    right_side = jnp.concatenate([upper_rows, lower_rows], axis=0)
    return jnp.dot(left_side, right_side, preferred_element_type=jnp.float32)


CHUNK = 256


def exp_neg(angle):
    return jnp.cos(angle), -jnp.sin(angle)


def exchange_inputs(spec_ref, lag_ref, slow_ref, spec_in, lag_in, slow_in, local_sem, send_sem, recv_sem, then):
    count = spec_in.shape[0]
    me = lax.axis_index("sta")
    tile = lax.axis_index("grid")
    mesh_ids = pl.DeviceIdType.MESH
    barrier = pltpu.get_barrier_semaphore()
    for shift in range(1, count):
        peer = lax.rem(me + shift, count)
        pl.semaphore_signal(barrier, inc=1, device_id=(tile, peer), device_id_type=mesh_ids)
    pl.semaphore_wait(barrier, count - 1)
    pairs = ((spec_ref, spec_in), (lag_ref, lag_in), (slow_ref, slow_in))
    local = []
    for kind, (source, target) in enumerate(pairs):
        own = source.at[me] if kind == 0 else source
        copy = pltpu.make_async_copy(own, target.at[me], local_sem.at[kind])
        copy.start()
        local.append(copy)
    sends = []
    for shift in range(1, count):
        peer = lax.rem(me + shift, count)
        for kind, (source, target) in enumerate(pairs):
            part = source.at[peer] if kind == 0 else source
            copy = pltpu.make_async_remote_copy(
                src_ref=part,
                dst_ref=target.at[me],
                send_sem=send_sem.at[kind, shift],
                recv_sem=recv_sem.at[kind, me],
                device_id=(tile, peer),
                device_id_type=mesh_ids,
            )
            copy.start()
            sends.append(copy)
    then()
    for copy in local:
        copy.wait()
    for copy in sends:
        copy.wait_send()
    for shift in range(1, count):
        source_id = lax.rem(me + count - shift, count)
        for kind, (source, target) in enumerate(pairs):
            part = source.at[source_id] if kind == 0 else source
            pltpu.make_async_remote_copy(
                src_ref=part,
                dst_ref=target.at[source_id],
                send_sem=send_sem.at[kind, shift],
                recv_sem=recv_sem.at[kind, source_id],
                device_id=(tile, source_id),
                device_id_type=mesh_ids,
            ).wait_recv()


def align_block(spec, lag, slow, source, real_ref, imag_ref, turn_ref):
    bins, block = spec.shape[1], spec.shape[2]
    first_bin = lax.axis_index("sta") * bins
    bin_rows = (F0 + first_bin + lax.broadcasted_iota(jnp.int32, (bins, block), 0)).astype(jnp.float32)
    cols = pl.ds(pl.multiple_of(source * block, 128), block)
    product = bin_rows * lag.astype(jnp.float32)
    whole = jnp.floor(product * (1.0 / NT))
    left = product - whole * NT
    left = jnp.where(left < 0.0, left + NT, left)
    left = jnp.where(left >= NT, left - NT, left)
    turned = left * (TWO_PI / NT)
    cosine = jnp.cos(turned)
    sine = jnp.sin(turned)
    real_in = spec[0].astype(jnp.float32)
    imag_in = spec[1].astype(jnp.float32)
    real_ref[:, cols] = (real_in * cosine + imag_in * sine).astype(jnp.bfloat16).astype(jnp.float32)
    imag_ref[:, cols] = (imag_in * cosine - real_in * sine).astype(jnp.bfloat16).astype(jnp.float32)
    turn_ref[:, cols] = slow.astype(jnp.float32)


def complex_times(left, right):
    return left[0] * right[0] - left[1] * right[1], left[0] * right[1] + left[1] * right[0]


def factor_rows(turn_x, turn_y, turn_z, rows8, rows16):
    return (
        exp_neg(turn_x * (rows8 - 3.5)),
        exp_neg(turn_x * (8.0 * (rows8 - 1.5))),
        exp_neg(turn_y * (rows8 - 3.5)),
        exp_neg(turn_z * (rows16 - 7.5)),
        exp_neg(turn_z * (16.0 * (rows8 - 3.5))),
    )


def beam_kernel(spec_ref, lag_ref, slow_ref, power_ref, spec_in, lag_in, slow_in, local_sem, send_sem, recv_sem,
                real_ref, imag_ref, turn_ref, acc_ref, left_ref, right_ref):
    count, bins, block = spec_in.shape[0], spec_in.shape[2], spec_in.shape[3]
    me = lax.axis_index("sta")
    first_bin = me * bins
    width = CHUNK
    per_block = block // width
    half_z = CZ // 2
    rows8 = lax.broadcasted_iota(jnp.int32, (8, width), 0).astype(jnp.float32)
    rows16 = lax.broadcasted_iota(jnp.int32, (16, width), 0).astype(jnp.float32)
    omega0 = (F0 + first_bin).astype(jnp.float32) * (TWO_PI / NT)
    step = TWO_PI / NT
    acc_ref[...] = jnp.zeros_like(acc_ref)

    def per_chunk(k, carry):
        source = lax.rem(me + k // per_block, count)
        cols = pl.ds(pl.multiple_of(source * block + lax.rem(k, per_block) * width, 128), width)
        slow_x = turn_ref[0:1, cols]
        slow_y = turn_ref[1:2, cols]
        slow_z = turn_ref[2:3, cols]
        start = factor_rows(omega0 * slow_x, omega0 * slow_y, omega0 * slow_z, rows8, rows16)
        ratio = factor_rows(step * slow_x, step * slow_y, step * slow_z, rows8, rows16)

        def per_bin(f, state):
            (a_r, a_i), (b_r, b_i), (y_r, y_i), (c_r, c_i), (d_r, d_i) = state
            real_in = real_ref[pl.ds(f, 1), cols]
            imag_in = imag_ref[pl.ds(f, 1), cols]
            q_r = real_in * y_r - imag_in * y_i
            q_i = real_in * y_i + imag_in * y_r
            near = [complex_times((b_r[m : m + 1], b_i[m : m + 1]), (a_r, a_i)) for m in range(CX // 16)]
            cells = CX * CY
            for y in range(CY):
                qq_r, qq_i = q_r[y : y + 1], q_i[y : y + 1]
                lo_r, lo_i, hi_r, hi_i = [], [], [], []
                for x_r, x_i in near:
                    t1, t2 = qq_r * x_r, qq_i * x_i
                    t3, t4 = qq_r * x_i, qq_i * x_r
                    lo_r.append(t1 - t2)
                    lo_i.append(t3 + t4)
                    hi_r.append(t1 + t2)
                    hi_i.append(t4 - t3)
                row = y * CX
                half = CX // 2
                left_ref[row : row + half, :] = jnp.concatenate(lo_r, axis=0).astype(jnp.bfloat16)
                left_ref[row + half : row + CX, :] = jnp.concatenate(hi_r, axis=0).astype(jnp.bfloat16)
                left_ref[cells + row : cells + row + half, :] = jnp.concatenate(lo_i, axis=0).astype(jnp.bfloat16)
                left_ref[cells + row + half : cells + row + CX, :] = jnp.concatenate(hi_i, axis=0).astype(jnp.bfloat16)
            for m in range(half_z // 16):
                z_r, z_i = complex_times((d_r[m : m + 1], d_i[m : m + 1]), (c_r, c_i))
                row = 16 * m
                right_ref[row : row + 16, :] = z_r.astype(jnp.bfloat16)
                right_ref[half_z + row : half_z + row + 16, :] = z_i.astype(jnp.bfloat16)
            acc_ref[f] += lax.dot_general(
                left_ref[...], right_ref[...], (((1,), (1,)), ((), ())), preferred_element_type=jnp.float32
            )
            return tuple(complex_times(now, turn) for now, turn in zip(state, ratio))

        lax.fori_loop(0, bins, per_bin, start)
        return carry

    def own_block():
        align_block(spec_ref[me], lag_ref[...], slow_ref[...], me, real_ref, imag_ref, turn_ref)
        lax.fori_loop(0, per_block, per_chunk, 0)

    exchange_inputs(spec_ref, lag_ref, slow_ref, spec_in, lag_in, slow_in, local_sem, send_sem, recv_sem, own_block)

    def align_other(shift, carry):
        source = lax.rem(me + shift, count)
        align_block(spec_in[source], lag_in[source], slow_in[source], source, real_ref, imag_ref, turn_ref)
        return carry

    lax.fori_loop(1, count, align_other, 0)
    lax.fori_loop(per_block, count * per_block, per_chunk, 0)
    cells = CX * CY
    low = jnp.zeros((cells, half_z), jnp.float32)
    high = jnp.zeros((cells, half_z), jnp.float32)
    for f in range(bins):
        sums = acc_ref[f]
        u, w = sums[:cells, :half_z], sums[:cells, half_z:]
        x, v = sums[cells:, :half_z], sums[cells:, half_z:]
        low = low + ((u - v) * (u - v) + (w + x) * (w + x))
        high = high + ((u + v) * (u + v) + (x - w) * (x - w))
    power_ref[:, :half_z] = low
    power_ref[:, half_z:] = high


def beam_power(spec_send, lag_row, slow_rows):
    count = spec_send.shape[0]
    bins, block = spec_send.shape[2], spec_send.shape[3]
    width = CHUNK
    stations = count * block
    vmem = pl.BlockSpec(memory_space=pltpu.VMEM)
    return pl.pallas_call(
        beam_kernel,
        out_shape=jax.ShapeDtypeStruct((CX * CY, CZ), jnp.float32),
        in_specs=[vmem, vmem, vmem],
        out_specs=vmem,
        scratch_shapes=[
            pltpu.VMEM((count,) + spec_send.shape[1:], jnp.bfloat16),
            pltpu.VMEM((count,) + lag_row.shape, jnp.int32),
            pltpu.VMEM((count,) + slow_rows.shape, jnp.bfloat16),
            pltpu.SemaphoreType.DMA((3,)),
            pltpu.SemaphoreType.DMA((3, count)),
            pltpu.SemaphoreType.DMA((3, count)),
            pltpu.VMEM((bins, stations), jnp.float32),
            pltpu.VMEM((bins, stations), jnp.float32),
            pltpu.VMEM((slow_rows.shape[0], stations), jnp.float32),
            pltpu.VMEM((bins, 2 * CX * CY, CZ), jnp.float32),
            pltpu.VMEM((2 * CX * CY, width), jnp.bfloat16),
            pltpu.VMEM((CZ, width), jnp.bfloat16),
        ],
        compiler_params=pltpu.CompilerParams(collective_id=1, has_side_effects=True),
    )(spec_send, lag_row, slow_rows)


def share_kernel(part_ref, out_ref, pieces, send_rs, recv_rs, send_ag, recv_ag, local_sem):
    count = pieces.shape[0]
    slots = out_ref.shape[0]
    reach = slots // 2
    rows = pieces.shape[1]
    me = lax.axis_index("sta")
    tile = lax.axis_index("grid")
    tiles = lax.axis_size("grid")
    mesh_ids = pl.DeviceIdType.MESH
    barrier = pltpu.get_barrier_semaphore()
    for shift in range(1, count):
        pl.semaphore_signal(barrier, inc=1, device_id=(tile, lax.rem(me + shift, count)), device_id_type=mesh_ids)
    neighbours = jnp.int32(0)
    for k in range(-reach, reach + 1):
        if k == 0:
            continue
        there = (tile + k >= 0) & (tile + k < tiles)
        neighbours = neighbours + there.astype(jnp.int32)

        @pl.when(there)
        def _():
            pl.semaphore_signal(barrier, inc=1, device_id=(tile + k, me), device_id_type=mesh_ids)

    pl.semaphore_wait(barrier, count - 1 + neighbours)
    own = pltpu.make_async_copy(part_ref.at[pl.ds(pl.multiple_of(me * rows, 8), rows)], pieces.at[me], local_sem.at[0])
    own.start()
    sends = []
    for shift in range(1, count):
        peer = lax.rem(me + shift, count)
        copy = pltpu.make_async_remote_copy(
            src_ref=part_ref.at[pl.ds(pl.multiple_of(peer * rows, 8), rows)],
            dst_ref=pieces.at[me],
            send_sem=send_rs.at[shift],
            recv_sem=recv_rs.at[me],
            device_id=(tile, peer),
            device_id_type=mesh_ids,
        )
        copy.start()
        sends.append(copy)
    own.wait()
    for copy in sends:
        copy.wait_send()
    for shift in range(1, count):
        source = lax.rem(me + count - shift, count)
        pltpu.make_async_remote_copy(
            src_ref=pieces.at[source],
            dst_ref=pieces.at[source],
            send_sem=send_rs.at[shift],
            recv_sem=recv_rs.at[source],
            device_id=(tile, source),
            device_id_type=mesh_ids,
        ).wait_recv()
    total = pieces[0]
    for source in range(1, count):
        total = total + pieces[source]
    mine = pl.ds(pl.multiple_of(me * rows, 8), rows)
    out_ref[reach, mine] = total
    block = out_ref.at[reach, mine]

    def gather_copy(k, peer, slot):
        return pltpu.make_async_remote_copy(
            src_ref=block,
            dst_ref=out_ref.at[slot, mine],
            send_sem=send_ag.at[slot, peer],
            recv_sem=recv_ag.at[slot, me],
            device_id=(tile + k, peer),
            device_id_type=mesh_ids,
        )

    peers = []
    for shift in range(1, count):
        copy = gather_copy(0, lax.rem(me + shift, count), reach)
        copy.start()
        peers.append(copy)
    for k in range(-reach, reach + 1):
        if k == 0:
            continue

        @pl.when(jnp.logical_not((tile + k >= 0) & (tile + k < tiles)))
        def _():
            out_ref[reach + k] = jnp.zeros(out_ref.shape[1:], out_ref.dtype)

    for copy in peers:
        copy.wait_send()
    for shift in range(1, count):
        source = lax.rem(me + count - shift, count)
        pltpu.make_async_remote_copy(
            src_ref=block,
            dst_ref=out_ref.at[reach, pl.ds(pl.multiple_of(source * rows, 8), rows)],
            send_sem=send_ag.at[reach, source],
            recv_sem=recv_ag.at[reach, source],
            device_id=(tile, source),
            device_id_type=mesh_ids,
        ).wait_recv()

    def halo_copy(k):
        return pltpu.make_async_remote_copy(
            src_ref=out_ref.at[reach],
            dst_ref=out_ref.at[reach - k],
            send_sem=send_ag.at[reach - k, me],
            recv_sem=recv_ag.at[reach - k, me],
            device_id=(tile + k, me),
            device_id_type=mesh_ids,
        )

    for k in range(-reach, reach + 1):
        if k == 0:
            continue

        @pl.when((tile + k >= 0) & (tile + k < tiles))
        def _():
            halo_copy(k).start()

    for k in range(-reach, reach + 1):
        if k == 0:
            continue

        @pl.when((tile + k >= 0) & (tile + k < tiles))
        def _():
            halo_copy(k).wait_send()
            pltpu.make_async_remote_copy(
                src_ref=out_ref.at[reach],
                dst_ref=out_ref.at[reach + k],
                send_sem=send_ag.at[reach + k, me],
                recv_sem=recv_ag.at[reach + k, me],
                device_id=(tile + k, me),
                device_id_type=mesh_ids,
            ).wait_recv()


def share_power(part, reach):
    count = lax.axis_size("sta")
    rows = part.shape[0] // count
    slots = 2 * reach + 1
    return pl.pallas_call(
        share_kernel,
        out_shape=jax.ShapeDtypeStruct((slots,) + part.shape, jnp.float32),
        in_specs=[pl.BlockSpec(memory_space=pltpu.VMEM)],
        out_specs=pl.BlockSpec(memory_space=pltpu.VMEM),
        scratch_shapes=[
            pltpu.VMEM((count, rows, part.shape[1]), jnp.float32),
            pltpu.SemaphoreType.DMA((count,)),
            pltpu.SemaphoreType.DMA((count,)),
            pltpu.SemaphoreType.DMA((slots, count)),
            pltpu.SemaphoreType.DMA((slots, count)),
            pltpu.SemaphoreType.DMA((1,)),
        ],
        compiler_params=pltpu.CompilerParams(collective_id=0, has_side_effects=True),
    )(part)


def freq_beams(freq_ids, aligned_rows, slow_rows):
    return lax.map(lambda pair: beam_freq(pair[0], pair[1], slow_rows), (freq_ids, aligned_rows))


def band_matrix(taps, length):
    rows = jnp.arange(length, dtype=jnp.int32)[:, None]
    columns = jnp.arange(length + 2 * HALF, dtype=jnp.int32)[None, :]
    offset = columns - rows
    picks = jnp.arange(TAPS, dtype=jnp.int32)[:, None, None]
    return jnp.sum(jnp.where(offset[None] == picks, taps[:, None, None], 0.0), axis=0)


def blur(volume, bands):
    band_x, square_y, square_z = bands
    padded = with_halo(volume.astype(jnp.bfloat16), (("grid", 0),), HALF).astype(volume.dtype)
    along_x = jnp.einsum("ip,pyz->iyz", band_x, padded, precision=lax.Precision.HIGHEST)
    along_y = jnp.einsum("jq,xqz->xjz", square_y, along_x, precision=lax.Precision.HIGHEST)
    return jnp.einsum("xyw,kw->xyk", along_y, square_z, precision=lax.Precision.HIGHEST)


def blur_narrowing(volume, taps, square_y, square_z):
    band_x = band_matrix(taps, volume.shape[0] - 2 * HALF)
    along_x = jnp.einsum("ip,pyz->iyz", band_x, volume, precision=lax.Precision.HIGHEST)
    along_y = jnp.einsum("jq,xqz->xjz", square_y, along_x, precision=lax.Precision.HIGHEST)
    return jnp.einsum("xyw,kw->xyk", along_y, square_z, precision=lax.Precision.HIGHEST)


def deblur(observed, halo_tiles, spread_taps):
    tiles = lax.axis_size("grid")
    me = lax.axis_index("grid")
    reach = ITERS * 2 * HALF
    cut = halo_tiles * CX - reach
    observed = observed[cut : observed.shape[0] - cut]
    width = observed.shape[0]
    cell = (me - halo_tiles) * CX + cut + jnp.arange(width, dtype=jnp.int32)
    inside = (cell >= 0) & (cell < tiles * CX)
    square_y = band_matrix(spread_taps[1], CY)[:, HALF : HALF + CY]
    square_z = band_matrix(spread_taps[2], CZ)[:, HALF : HALF + CZ]
    estimate = jnp.where(inside[:, None, None], observed, 0.0)
    for sweep in range(ITERS):
        low = 2 * HALF * sweep + HALF
        blurred = blur_narrowing(estimate, spread_taps[0], square_y, square_z)
        ratio = jnp.where(
            inside[low : width - low, None, None], observed[low : width - low] / blurred, 0.0
        )
        estimate = estimate[2 * HALF : estimate.shape[0] - 2 * HALF] * blur_narrowing(
            ratio, spread_taps[0], square_y, square_z
        )
    return estimate


def band_of(taps_ref, axis, rows, cols):
    offset = cols - rows + HALF
    band = jnp.zeros(offset.shape, jnp.float32)
    for tap in range(TAPS):
        band = jnp.where(offset == tap, taps_ref[axis, tap], band)
    return band


def mirror(index, length):
    return jnp.where(index < length // 2, index, 3 * (length // 2) - 1 - index)


def deblur_kernel(taps_ref, obs_ref, out_ref, kx_ref, kz_ref):
    tiles = lax.axis_size("grid")
    me = lax.axis_index("grid")
    planes, width, depth = obs_ref.shape
    shape_x = kx_ref.shape
    kx_ref[...] = band_of(
        taps_ref, 0, lax.broadcasted_iota(jnp.int32, shape_x, 0) + HALF, lax.broadcasted_iota(jnp.int32, shape_x, 1)
    )
    shape_z = kz_ref.shape
    kz_ref[...] = band_of(
        taps_ref,
        2,
        mirror(lax.broadcasted_iota(jnp.int32, shape_z, 1), depth),
        mirror(lax.broadcasted_iota(jnp.int32, shape_z, 0), depth),
    )
    halo_tiles = (width - CX) // (2 * CX)
    highest = lax.Precision.HIGHEST

    def inside(low, size):
        cell = (me - halo_tiles) * CX + low + lax.broadcasted_iota(jnp.int32, (size, depth), 0)
        return (cell >= 0) & (cell < tiles * CX)

    def blur(volume):
        size_in = volume[0].shape[0]
        size_out = size_in - 2 * HALF
        band = kx_ref[0:size_out, 0:size_in]
        along_x = [jnp.dot(band, plane, precision=highest, preferred_element_type=jnp.float32) for plane in volume]
        along_y = []
        for y in range(planes):
            total = None
            for q in range(planes):
                term = taps_ref[1, q - y + HALF] * along_x[q]
                total = term if total is None else total + term
            along_y.append(total)
        joined = jnp.concatenate(along_y, axis=0)
        along_z = jnp.dot(joined, kz_ref[...], precision=highest, preferred_element_type=jnp.float32)
        return [along_z[y * size_out : (y + 1) * size_out] for y in range(planes)]

    observed = [obs_ref[y] for y in range(planes)]
    mask = inside(0, width)
    estimate = [jnp.where(mask, plane, 0.0) for plane in observed]
    for sweep in range(ITERS):
        low = 2 * HALF * sweep + HALF
        blurred = blur(estimate)
        size = blurred[0].shape[0]
        mask = inside(low, size)
        ratio = [jnp.where(mask, observed[y][low : low + size] / blurred[y], 0.0) for y in range(planes)]
        spread = blur(ratio)
        estimate = [estimate[y][2 * HALF : 2 * HALF + spread[y].shape[0]] * spread[y] for y in range(planes)]
    for y in range(planes):
        out_ref[y] = estimate[y]


def deblur_tile(observed, spread_taps):
    planes, width, depth = observed.shape
    vmem = pl.BlockSpec(memory_space=pltpu.VMEM)
    return pl.pallas_call(
        deblur_kernel,
        out_shape=jax.ShapeDtypeStruct((planes, CX, depth), jnp.float32),
        in_specs=[pl.BlockSpec(memory_space=pltpu.SMEM), vmem],
        out_specs=vmem,
        scratch_shapes=[
            pltpu.VMEM((width - 2 * HALF, width), jnp.float32),
            pltpu.VMEM((depth, depth), jnp.float32),
        ],
    )(spread_taps, observed)


def per_device(spectra, lag_samples, slowness, spread_taps):
    groups = lax.axis_size("sta")
    own_count = FREQS // groups
    first_bin = lax.axis_index("sta") * own_count
    block = spectra.shape[2]
    spec_send = spectra.reshape(groups, own_count, 2, block).transpose(0, 2, 1, 3)
    local_power = beam_power(spec_send, lag_samples, slowness[0])
    halo_tiles = -(-(ITERS * 2 * HALF) // CX)
    summed = share_power(local_power, halo_tiles)
    observed = summed / (FREQS * STATIONS) + BACKGROUND
    slots = observed.shape[0]
    observed = observed.reshape(slots, CY, CX, CZ)
    observed = jnp.concatenate([observed[:, :, : CX // 2], observed[:, :, CX // 2 :][:, :, ::-1]], axis=2)
    planes = observed.transpose(1, 0, 2, 3).reshape(CY, slots * CX, CZ)
    estimate = deblur_tile(planes, spread_taps)
    both = jnp.stack([observed[halo_tiles], estimate])
    both = jnp.concatenate([both[..., : CZ // 2], both[..., CZ // 2 :][..., ::-1]], axis=-1).transpose(0, 2, 1, 3)
    stacked, estimate = both[0], both[1]
    return (stacked[None], estimate[None])


def solution(mesh):
    placed = (P(None, None, "sta"), P("grid", "sta"), P("grid", None, "sta"), P())
    return jax.shard_map(
        per_device,
        mesh=mesh,
        in_specs=placed,
        out_specs=(P("grid", None, None, None), P("grid", None, None, None)),
        check_vma=False,
    )
```

```python
import math

import jax
import jax.numpy as jnp
from jax import lax
from jax.sharding import PartitionSpec as P
from jax.experimental import pallas as pl
from jax.experimental.pallas import tpu as pltpu

STATIONS = 6144
FREQS = 64
F0 = 600
NT = 6000
TAPS = 17
HALF = 8
ITERS = 4
CX = 32
CY = 8
CZ = 128


TWO_PI = 2.0 * math.pi
BACKGROUND = 0.05


def with_halo(array, sides, width):
    for axis, dim in sides:
        size, length = (lax.axis_size(axis), array.shape[dim])
        up = [(i, (i + 1) % size) for i in range(size - 1)]
        down = [(j, i) for i, j in up]
        last = lax.slice_in_dim(array, length - width, length, axis=dim)
        leading = lax.slice_in_dim(array, 0, width, axis=dim)
        before = lax.ppermute(last, axis, up)
        after = lax.ppermute(leading, axis, down)
        array = jnp.concatenate([before, array, after], axis=dim)
    return array


def align_rows(spectra, lag_row):
    bins = F0 + jnp.arange(FREQS, dtype=jnp.int32)
    cycles = bins[:, None] * lag_row[None, :] % NT
    turned = cycles.astype(jnp.float32) * (TWO_PI / NT)
    cosine = jnp.cos(turned)
    sine = jnp.sin(turned)
    real_in = spectra[:, 0, :].astype(jnp.float32)
    imag_in = spectra[:, 1, :].astype(jnp.float32)
    real_out = real_in * cosine + imag_in * sine
    imag_out = imag_in * cosine - real_in * sine
    return jnp.stack([real_out, imag_out], axis=1).astype(jnp.bfloat16)


def beam_freq(freq, aligned_row, slow_rows):
    omega = (F0 + freq).astype(jnp.float32) * (TWO_PI / NT)
    slow = slow_rows.astype(jnp.float32)
    x_coord = jnp.arange(CX, dtype=jnp.float32) - (CX - 1) / 2.0
    y_coord = jnp.arange(CY, dtype=jnp.float32) - (CY - 1) / 2.0
    z_coord = jnp.arange(CZ, dtype=jnp.float32) - (CZ - 1) / 2.0
    phase_x = (omega * slow[0])[None, :] * x_coord[:, None]
    phase_y = (omega * slow[1])[None, :] * y_coord[:, None]
    phase = phase_x[:, None, :] + phase_y[None, :, :]
    cosine = jnp.cos(phase)
    sine = jnp.sin(phase)
    real_in = aligned_row[0].astype(jnp.float32)[None, None, :]
    imag_in = aligned_row[1].astype(jnp.float32)[None, None, :]
    front_real = (real_in * cosine + imag_in * sine).astype(jnp.bfloat16).reshape(CX * CY, -1)
    front_imag = (imag_in * cosine - real_in * sine).astype(jnp.bfloat16).reshape(CX * CY, -1)
    left_side = jnp.concatenate([front_real, front_imag], axis=1)
    phase_z = (omega * slow[2])[:, None] * z_coord[None, :]
    depth_real = jnp.cos(phase_z).astype(jnp.bfloat16)
    depth_imag = jnp.sin(phase_z).astype(jnp.bfloat16)
    upper_rows = jnp.concatenate([depth_real, -depth_imag], axis=1)
    lower_rows = jnp.concatenate([depth_imag, depth_real], axis=1)
    right_side = jnp.concatenate([upper_rows, lower_rows], axis=0)
    return jnp.dot(left_side, right_side, preferred_element_type=jnp.float32)


CHUNK = 256


def exp_neg(angle):
    return jnp.cos(angle), -jnp.sin(angle)


def enter_barrier(count, reach):
    me = lax.axis_index("sta")
    tile = lax.axis_index("grid")
    tiles = lax.axis_size("grid")
    mesh_ids = pl.DeviceIdType.MESH
    barrier = pltpu.get_barrier_semaphore()
    for shift in range(1, count):
        pl.semaphore_signal(barrier, inc=1, device_id=(tile, lax.rem(me + shift, count)), device_id_type=mesh_ids)
    neighbours = jnp.int32(0)
    for k in range(-reach, reach + 1):
        if k == 0:
            continue
        there = (tile + k >= 0) & (tile + k < tiles)
        neighbours = neighbours + there.astype(jnp.int32)

        @pl.when(there)
        def _():
            pl.semaphore_signal(barrier, inc=1, device_id=(tile + k, me), device_id_type=mesh_ids)

    pl.semaphore_wait(barrier, count - 1 + neighbours)


def exchange_inputs(spec_ref, lag_ref, slow_ref, spec_in, lag_in, slow_in, local_sem, send_sem, recv_sem, then, reach):
    count = spec_in.shape[0]
    me = lax.axis_index("sta")
    tile = lax.axis_index("grid")
    mesh_ids = pl.DeviceIdType.MESH
    enter_barrier(count, reach)
    pairs = ((spec_ref, spec_in), (lag_ref, lag_in), (slow_ref, slow_in))
    local = []
    for kind, (source, target) in enumerate(pairs):
        own = source.at[me] if kind == 0 else source
        copy = pltpu.make_async_copy(own, target.at[me], local_sem.at[kind])
        copy.start()
        local.append(copy)
    sends = []
    for shift in range(1, count):
        peer = lax.rem(me + shift, count)
        for kind, (source, target) in enumerate(pairs):
            part = source.at[peer] if kind == 0 else source
            copy = pltpu.make_async_remote_copy(
                src_ref=part,
                dst_ref=target.at[me],
                send_sem=send_sem.at[kind, shift],
                recv_sem=recv_sem.at[kind, me],
                device_id=(tile, peer),
                device_id_type=mesh_ids,
            )
            copy.start()
            sends.append(copy)
    then()
    for copy in local:
        copy.wait()
    for copy in sends:
        copy.wait_send()
    for shift in range(1, count):
        source_id = lax.rem(me + count - shift, count)
        for kind, (source, target) in enumerate(pairs):
            part = source.at[source_id] if kind == 0 else source
            pltpu.make_async_remote_copy(
                src_ref=part,
                dst_ref=target.at[source_id],
                send_sem=send_sem.at[kind, shift],
                recv_sem=recv_sem.at[kind, source_id],
                device_id=(tile, source_id),
                device_id_type=mesh_ids,
            ).wait_recv()


def align_block(spec, lag, slow, source, real_ref, imag_ref, turn_ref):
    bins, block = spec.shape[1], spec.shape[2]
    first_bin = lax.axis_index("sta") * bins
    bin_rows = (F0 + first_bin + lax.broadcasted_iota(jnp.int32, (bins, block), 0)).astype(jnp.float32)
    cols = pl.ds(pl.multiple_of(source * block, 128), block)
    product = bin_rows * lag.astype(jnp.float32)
    whole = jnp.floor(product * (1.0 / NT))
    left = product - whole * NT
    left = jnp.where(left < 0.0, left + NT, left)
    left = jnp.where(left >= NT, left - NT, left)
    turned = left * (TWO_PI / NT)
    cosine = jnp.cos(turned)
    sine = jnp.sin(turned)
    real_in = spec[0].astype(jnp.float32)
    imag_in = spec[1].astype(jnp.float32)
    real_ref[:, cols] = (real_in * cosine + imag_in * sine).astype(jnp.bfloat16).astype(jnp.float32)
    imag_ref[:, cols] = (imag_in * cosine - real_in * sine).astype(jnp.bfloat16).astype(jnp.float32)
    turn_ref[:, cols] = slow.astype(jnp.float32)


def complex_times(left, right):
    return left[0] * right[0] - left[1] * right[1], left[0] * right[1] + left[1] * right[0]


def factor_rows(turn_x, turn_y, turn_z, rows8, rows16):
    return (
        exp_neg(turn_x * (rows8 - 3.5)),
        exp_neg(turn_x * (8.0 * (rows8 - 1.5))),
        exp_neg(turn_y * (rows8 - 3.5)),
        exp_neg(turn_z * (rows16 - 7.5)),
        exp_neg(turn_z * (16.0 * (rows8 - 3.5))),
    )


def beam_kernel(spec_ref, lag_ref, slow_ref, out_ref, spec_in, lag_in, slow_in, local_sem, send_sem, recv_sem,
                real_ref, imag_ref, turn_ref, acc_ref, left_ref, right_ref, power_ref, pieces, send_rs, recv_rs,
                send_ag, recv_ag, share_sem):
    count, bins, block = spec_in.shape[0], spec_in.shape[2], spec_in.shape[3]
    me = lax.axis_index("sta")
    first_bin = me * bins
    width = CHUNK
    per_block = block // width
    half_z = CZ // 2
    rows8 = lax.broadcasted_iota(jnp.int32, (8, width), 0).astype(jnp.float32)
    rows16 = lax.broadcasted_iota(jnp.int32, (16, width), 0).astype(jnp.float32)
    omega0 = (F0 + first_bin).astype(jnp.float32) * (TWO_PI / NT)
    step = TWO_PI / NT
    acc_ref[...] = jnp.zeros_like(acc_ref)

    def per_chunk(k, carry):
        source = lax.rem(me + k // per_block, count)
        cols = pl.ds(pl.multiple_of(source * block + lax.rem(k, per_block) * width, 128), width)
        slow_x = turn_ref[0:1, cols]
        slow_y = turn_ref[1:2, cols]
        slow_z = turn_ref[2:3, cols]
        start = factor_rows(omega0 * slow_x, omega0 * slow_y, omega0 * slow_z, rows8, rows16)
        ratio = factor_rows(step * slow_x, step * slow_y, step * slow_z, rows8, rows16)

        def per_bin(f, state):
            (a_r, a_i), (b_r, b_i), (y_r, y_i), (c_r, c_i), (d_r, d_i) = state
            real_in = real_ref[pl.ds(f, 1), cols]
            imag_in = imag_ref[pl.ds(f, 1), cols]
            q_r = real_in * y_r - imag_in * y_i
            q_i = real_in * y_i + imag_in * y_r
            near = [complex_times((b_r[m : m + 1], b_i[m : m + 1]), (a_r, a_i)) for m in range(CX // 16)]
            cells = CX * CY
            for y in range(CY):
                qq_r, qq_i = q_r[y : y + 1], q_i[y : y + 1]
                lo_r, lo_i, hi_r, hi_i = [], [], [], []
                for x_r, x_i in near:
                    t1, t2 = qq_r * x_r, qq_i * x_i
                    t3, t4 = qq_r * x_i, qq_i * x_r
                    lo_r.append(t1 - t2)
                    lo_i.append(t3 + t4)
                    hi_r.append(t1 + t2)
                    hi_i.append(t4 - t3)
                row = y * CX
                half = CX // 2
                left_ref[row : row + half, :] = jnp.concatenate(lo_r, axis=0).astype(jnp.bfloat16)
                left_ref[row + half : row + CX, :] = jnp.concatenate(hi_r, axis=0).astype(jnp.bfloat16)
                left_ref[cells + row : cells + row + half, :] = jnp.concatenate(lo_i, axis=0).astype(jnp.bfloat16)
                left_ref[cells + row + half : cells + row + CX, :] = jnp.concatenate(hi_i, axis=0).astype(jnp.bfloat16)
            for m in range(half_z // 16):
                z_r, z_i = complex_times((d_r[m : m + 1], d_i[m : m + 1]), (c_r, c_i))
                row = 16 * m
                right_ref[row : row + 16, :] = z_r.astype(jnp.bfloat16)
                right_ref[half_z + row : half_z + row + 16, :] = z_i.astype(jnp.bfloat16)
            acc_ref[f] += lax.dot_general(
                left_ref[...], right_ref[...], (((1,), (1,)), ((), ())), preferred_element_type=jnp.float32
            )
            return tuple(complex_times(now, turn) for now, turn in zip(state, ratio))

        lax.fori_loop(0, bins, per_bin, start)
        return carry

    def own_block():
        align_block(spec_ref[me], lag_ref[...], slow_ref[...], me, real_ref, imag_ref, turn_ref)
        lax.fori_loop(0, per_block, per_chunk, 0)

    exchange_inputs(
        spec_ref, lag_ref, slow_ref, spec_in, lag_in, slow_in, local_sem, send_sem, recv_sem, own_block, out_ref.shape[0] // 2
    )

    def align_other(shift, carry):
        source = lax.rem(me + shift, count)
        align_block(spec_in[source], lag_in[source], slow_in[source], source, real_ref, imag_ref, turn_ref)
        return carry

    lax.fori_loop(1, count, align_other, 0)
    lax.fori_loop(per_block, count * per_block, per_chunk, 0)
    cells = CX * CY
    low = jnp.zeros((cells, half_z), jnp.float32)
    high = jnp.zeros((cells, half_z), jnp.float32)
    for f in range(bins):
        sums = acc_ref[f]
        u, w = sums[:cells, :half_z], sums[:cells, half_z:]
        x, v = sums[cells:, :half_z], sums[cells:, half_z:]
        low = low + ((u - v) * (u - v) + (w + x) * (w + x))
        high = high + ((u + v) * (u + v) + (x - w) * (x - w))
    power_ref[:, :half_z] = low
    power_ref[:, half_z:] = high
    share_kernel(power_ref, out_ref, pieces, send_rs, recv_rs, send_ag, recv_ag, share_sem)


def beam_power(spec_send, lag_row, slow_rows, reach):
    count = spec_send.shape[0]
    slots = 2 * reach + 1
    cells = CX * CY
    bins, block = spec_send.shape[2], spec_send.shape[3]
    width = CHUNK
    stations = count * block
    vmem = pl.BlockSpec(memory_space=pltpu.VMEM)
    return pl.pallas_call(
        beam_kernel,
        out_shape=jax.ShapeDtypeStruct((slots, cells, CZ), jnp.float32),
        in_specs=[vmem, vmem, vmem],
        out_specs=vmem,
        scratch_shapes=[
            pltpu.VMEM((count,) + spec_send.shape[1:], jnp.bfloat16),
            pltpu.VMEM((count,) + lag_row.shape, jnp.int32),
            pltpu.VMEM((count,) + slow_rows.shape, jnp.bfloat16),
            pltpu.SemaphoreType.DMA((3,)),
            pltpu.SemaphoreType.DMA((3, count)),
            pltpu.SemaphoreType.DMA((3, count)),
            pltpu.VMEM((bins, stations), jnp.float32),
            pltpu.VMEM((bins, stations), jnp.float32),
            pltpu.VMEM((slow_rows.shape[0], stations), jnp.float32),
            pltpu.VMEM((bins, 2 * CX * CY, CZ), jnp.float32),
            pltpu.VMEM((2 * CX * CY, width), jnp.bfloat16),
            pltpu.VMEM((CZ, width), jnp.bfloat16),
            pltpu.VMEM((cells, CZ), jnp.float32),
            pltpu.VMEM((count, cells // count, CZ), jnp.float32),
            pltpu.SemaphoreType.DMA((count,)),
            pltpu.SemaphoreType.DMA((count,)),
            pltpu.SemaphoreType.DMA((slots, count)),
            pltpu.SemaphoreType.DMA((slots, count)),
            pltpu.SemaphoreType.DMA((1,)),
        ],
        compiler_params=pltpu.CompilerParams(collective_id=1, has_side_effects=True),
    )(spec_send, lag_row, slow_rows)


def share_kernel(part_ref, out_ref, pieces, send_rs, recv_rs, send_ag, recv_ag, local_sem):
    count = pieces.shape[0]
    slots = out_ref.shape[0]
    reach = slots // 2
    rows = pieces.shape[1]
    me = lax.axis_index("sta")
    tile = lax.axis_index("grid")
    tiles = lax.axis_size("grid")
    mesh_ids = pl.DeviceIdType.MESH
    own = pltpu.make_async_copy(part_ref.at[pl.ds(pl.multiple_of(me * rows, 8), rows)], pieces.at[me], local_sem.at[0])
    own.start()
    sends = []
    for shift in range(1, count):
        peer = lax.rem(me + shift, count)
        copy = pltpu.make_async_remote_copy(
            src_ref=part_ref.at[pl.ds(pl.multiple_of(peer * rows, 8), rows)],
            dst_ref=pieces.at[me],
            send_sem=send_rs.at[shift],
            recv_sem=recv_rs.at[me],
            device_id=(tile, peer),
            device_id_type=mesh_ids,
        )
        copy.start()
        sends.append(copy)
    own.wait()
    for copy in sends:
        copy.wait_send()
    for shift in range(1, count):
        source = lax.rem(me + count - shift, count)
        pltpu.make_async_remote_copy(
            src_ref=pieces.at[source],
            dst_ref=pieces.at[source],
            send_sem=send_rs.at[shift],
            recv_sem=recv_rs.at[source],
            device_id=(tile, source),
            device_id_type=mesh_ids,
        ).wait_recv()
    total = pieces[0]
    for source in range(1, count):
        total = total + pieces[source]
    mine = pl.ds(pl.multiple_of(me * rows, 8), rows)
    out_ref[reach, mine] = total
    block = out_ref.at[reach, mine]

    def gather_copy(k, peer, slot):
        return pltpu.make_async_remote_copy(
            src_ref=block,
            dst_ref=out_ref.at[slot, mine],
            send_sem=send_ag.at[slot, peer],
            recv_sem=recv_ag.at[slot, me],
            device_id=(tile + k, peer),
            device_id_type=mesh_ids,
        )

    peers = []
    for shift in range(1, count):
        copy = gather_copy(0, lax.rem(me + shift, count), reach)
        copy.start()
        peers.append(copy)
    for k in range(-reach, reach + 1):
        if k == 0:
            continue

        @pl.when(jnp.logical_not((tile + k >= 0) & (tile + k < tiles)))
        def _():
            out_ref[reach + k] = jnp.zeros(out_ref.shape[1:], out_ref.dtype)

    for copy in peers:
        copy.wait_send()
    for shift in range(1, count):
        source = lax.rem(me + count - shift, count)
        pltpu.make_async_remote_copy(
            src_ref=block,
            dst_ref=out_ref.at[reach, pl.ds(pl.multiple_of(source * rows, 8), rows)],
            send_sem=send_ag.at[reach, source],
            recv_sem=recv_ag.at[reach, source],
            device_id=(tile, source),
            device_id_type=mesh_ids,
        ).wait_recv()

    def halo_copy(k):
        return pltpu.make_async_remote_copy(
            src_ref=out_ref.at[reach],
            dst_ref=out_ref.at[reach - k],
            send_sem=send_ag.at[reach - k, me],
            recv_sem=recv_ag.at[reach - k, me],
            device_id=(tile + k, me),
            device_id_type=mesh_ids,
        )

    for k in range(-reach, reach + 1):
        if k == 0:
            continue

        @pl.when((tile + k >= 0) & (tile + k < tiles))
        def _():
            halo_copy(k).start()

    for k in range(-reach, reach + 1):
        if k == 0:
            continue

        @pl.when((tile + k >= 0) & (tile + k < tiles))
        def _():
            halo_copy(k).wait_send()
            pltpu.make_async_remote_copy(
                src_ref=out_ref.at[reach],
                dst_ref=out_ref.at[reach + k],
                send_sem=send_ag.at[reach + k, me],
                recv_sem=recv_ag.at[reach + k, me],
                device_id=(tile + k, me),
                device_id_type=mesh_ids,
            ).wait_recv()


def share_power(part, reach):
    count = lax.axis_size("sta")
    rows = part.shape[0] // count
    slots = 2 * reach + 1
    return pl.pallas_call(
        share_kernel,
        out_shape=jax.ShapeDtypeStruct((slots,) + part.shape, jnp.float32),
        in_specs=[pl.BlockSpec(memory_space=pltpu.VMEM)],
        out_specs=pl.BlockSpec(memory_space=pltpu.VMEM),
        scratch_shapes=[
            pltpu.VMEM((count, rows, part.shape[1]), jnp.float32),
            pltpu.SemaphoreType.DMA((count,)),
            pltpu.SemaphoreType.DMA((count,)),
            pltpu.SemaphoreType.DMA((slots, count)),
            pltpu.SemaphoreType.DMA((slots, count)),
            pltpu.SemaphoreType.DMA((1,)),
        ],
        compiler_params=pltpu.CompilerParams(collective_id=0, has_side_effects=True),
    )(part)


def freq_beams(freq_ids, aligned_rows, slow_rows):
    return lax.map(lambda pair: beam_freq(pair[0], pair[1], slow_rows), (freq_ids, aligned_rows))


def band_matrix(taps, length):
    rows = jnp.arange(length, dtype=jnp.int32)[:, None]
    columns = jnp.arange(length + 2 * HALF, dtype=jnp.int32)[None, :]
    offset = columns - rows
    picks = jnp.arange(TAPS, dtype=jnp.int32)[:, None, None]
    return jnp.sum(jnp.where(offset[None] == picks, taps[:, None, None], 0.0), axis=0)


def blur(volume, bands):
    band_x, square_y, square_z = bands
    padded = with_halo(volume.astype(jnp.bfloat16), (("grid", 0),), HALF).astype(volume.dtype)
    along_x = jnp.einsum("ip,pyz->iyz", band_x, padded, precision=lax.Precision.HIGHEST)
    along_y = jnp.einsum("jq,xqz->xjz", square_y, along_x, precision=lax.Precision.HIGHEST)
    return jnp.einsum("xyw,kw->xyk", along_y, square_z, precision=lax.Precision.HIGHEST)


def blur_narrowing(volume, taps, square_y, square_z):
    band_x = band_matrix(taps, volume.shape[0] - 2 * HALF)
    along_x = jnp.einsum("ip,pyz->iyz", band_x, volume, precision=lax.Precision.HIGHEST)
    along_y = jnp.einsum("jq,xqz->xjz", square_y, along_x, precision=lax.Precision.HIGHEST)
    return jnp.einsum("xyw,kw->xyk", along_y, square_z, precision=lax.Precision.HIGHEST)


def deblur(observed, halo_tiles, spread_taps):
    tiles = lax.axis_size("grid")
    me = lax.axis_index("grid")
    reach = ITERS * 2 * HALF
    cut = halo_tiles * CX - reach
    observed = observed[cut : observed.shape[0] - cut]
    width = observed.shape[0]
    cell = (me - halo_tiles) * CX + cut + jnp.arange(width, dtype=jnp.int32)
    inside = (cell >= 0) & (cell < tiles * CX)
    square_y = band_matrix(spread_taps[1], CY)[:, HALF : HALF + CY]
    square_z = band_matrix(spread_taps[2], CZ)[:, HALF : HALF + CZ]
    estimate = jnp.where(inside[:, None, None], observed, 0.0)
    for sweep in range(ITERS):
        low = 2 * HALF * sweep + HALF
        blurred = blur_narrowing(estimate, spread_taps[0], square_y, square_z)
        ratio = jnp.where(
            inside[low : width - low, None, None], observed[low : width - low] / blurred, 0.0
        )
        estimate = estimate[2 * HALF : estimate.shape[0] - 2 * HALF] * blur_narrowing(
            ratio, spread_taps[0], square_y, square_z
        )
    return estimate


def band_of(taps_ref, axis, rows, cols):
    offset = cols - rows + HALF
    band = jnp.zeros(offset.shape, jnp.float32)
    for tap in range(TAPS):
        band = jnp.where(offset == tap, taps_ref[axis, tap], band)
    return band


def mirror(index, length):
    return jnp.where(index < length // 2, index, 3 * (length // 2) - 1 - index)


def deblur_kernel(taps_ref, obs_ref, out_ref, kx_ref, kz_ref):
    tiles = lax.axis_size("grid")
    me = lax.axis_index("grid")
    planes, width, depth = obs_ref.shape
    shape_x = kx_ref.shape
    kx_ref[...] = band_of(
        taps_ref, 0, lax.broadcasted_iota(jnp.int32, shape_x, 0) + HALF, lax.broadcasted_iota(jnp.int32, shape_x, 1)
    )
    shape_z = kz_ref.shape
    kz_ref[...] = band_of(
        taps_ref,
        2,
        mirror(lax.broadcasted_iota(jnp.int32, shape_z, 1), depth),
        mirror(lax.broadcasted_iota(jnp.int32, shape_z, 0), depth),
    )
    halo_tiles = (width - CX) // (2 * CX)
    highest = lax.Precision.HIGHEST

    def inside(low, size):
        cell = (me - halo_tiles) * CX + low + lax.broadcasted_iota(jnp.int32, (size, depth), 0)
        return (cell >= 0) & (cell < tiles * CX)

    def blur(volume):
        size_in = volume[0].shape[0]
        size_out = size_in - 2 * HALF
        band = kx_ref[0:size_out, 0:size_in]
        along_x = [jnp.dot(band, plane, precision=highest, preferred_element_type=jnp.float32) for plane in volume]
        along_y = []
        for y in range(planes):
            total = None
            for q in range(planes):
                term = taps_ref[1, q - y + HALF] * along_x[q]
                total = term if total is None else total + term
            along_y.append(total)
        joined = jnp.concatenate(along_y, axis=0)
        along_z = jnp.dot(joined, kz_ref[...], precision=highest, preferred_element_type=jnp.float32)
        return [along_z[y * size_out : (y + 1) * size_out] for y in range(planes)]

    observed = [obs_ref[y] for y in range(planes)]
    mask = inside(0, width)
    estimate = [jnp.where(mask, plane, 0.0) for plane in observed]
    for sweep in range(ITERS):
        low = 2 * HALF * sweep + HALF
        blurred = blur(estimate)
        size = blurred[0].shape[0]
        mask = inside(low, size)
        ratio = [jnp.where(mask, observed[y][low : low + size] / blurred[y], 0.0) for y in range(planes)]
        spread = blur(ratio)
        estimate = [estimate[y][2 * HALF : 2 * HALF + spread[y].shape[0]] * spread[y] for y in range(planes)]
    for y in range(planes):
        out_ref[y] = estimate[y]


def deblur_tile(observed, spread_taps):
    planes, width, depth = observed.shape
    vmem = pl.BlockSpec(memory_space=pltpu.VMEM)
    return pl.pallas_call(
        deblur_kernel,
        out_shape=jax.ShapeDtypeStruct((planes, CX, depth), jnp.float32),
        in_specs=[pl.BlockSpec(memory_space=pltpu.SMEM), vmem],
        out_specs=vmem,
        scratch_shapes=[
            pltpu.VMEM((width - 2 * HALF, width), jnp.float32),
            pltpu.VMEM((depth, depth), jnp.float32),
        ],
    )(spread_taps, observed)


def per_device(spectra, lag_samples, slowness, spread_taps):
    groups = lax.axis_size("sta")
    own_count = FREQS // groups
    first_bin = lax.axis_index("sta") * own_count
    block = spectra.shape[2]
    spec_send = spectra.reshape(groups, own_count, 2, block).transpose(0, 2, 1, 3)
    halo_tiles = -(-(ITERS * 2 * HALF) // CX)
    summed = beam_power(spec_send, lag_samples, slowness[0], halo_tiles)
    observed = summed / (FREQS * STATIONS) + BACKGROUND
    slots = observed.shape[0]
    observed = observed.reshape(slots, CY, CX, CZ)
    observed = jnp.concatenate([observed[:, :, : CX // 2], observed[:, :, CX // 2 :][:, :, ::-1]], axis=2)
    planes = observed.transpose(1, 0, 2, 3).reshape(CY, slots * CX, CZ)
    estimate = deblur_tile(planes, spread_taps)
    both = jnp.stack([observed[halo_tiles], estimate])
    both = jnp.concatenate([both[..., : CZ // 2], both[..., CZ // 2 :][..., ::-1]], axis=-1).transpose(0, 2, 1, 3)
    stacked, estimate = both[0], both[1]
    return (stacked[None], estimate[None])


def solution(mesh):
    placed = (P(None, None, "sta"), P("grid", "sta"), P("grid", None, "sta"), P())
    return jax.shard_map(
        per_device,
        mesh=mesh,
        in_specs=placed,
        out_specs=(P("grid", None, None, None), P("grid", None, None, None)),
        check_vma=False,
    )
```

```python
import math

import jax
import jax.numpy as jnp
from jax import lax
from jax.sharding import PartitionSpec as P
from jax.experimental import pallas as pl
from jax.experimental.pallas import tpu as pltpu

STATIONS = 6144
FREQS = 64
F0 = 600
NT = 6000
TAPS = 17
HALF = 8
ITERS = 4
CX = 32
CY = 8
CZ = 128


TWO_PI = 2.0 * math.pi
BACKGROUND = 0.05


def with_halo(array, sides, width):
    for axis, dim in sides:
        size, length = (lax.axis_size(axis), array.shape[dim])
        up = [(i, (i + 1) % size) for i in range(size - 1)]
        down = [(j, i) for i, j in up]
        last = lax.slice_in_dim(array, length - width, length, axis=dim)
        leading = lax.slice_in_dim(array, 0, width, axis=dim)
        before = lax.ppermute(last, axis, up)
        after = lax.ppermute(leading, axis, down)
        array = jnp.concatenate([before, array, after], axis=dim)
    return array


def align_rows(spectra, lag_row):
    bins = F0 + jnp.arange(FREQS, dtype=jnp.int32)
    cycles = bins[:, None] * lag_row[None, :] % NT
    turned = cycles.astype(jnp.float32) * (TWO_PI / NT)
    cosine = jnp.cos(turned)
    sine = jnp.sin(turned)
    real_in = spectra[:, 0, :].astype(jnp.float32)
    imag_in = spectra[:, 1, :].astype(jnp.float32)
    real_out = real_in * cosine + imag_in * sine
    imag_out = imag_in * cosine - real_in * sine
    return jnp.stack([real_out, imag_out], axis=1).astype(jnp.bfloat16)


def beam_freq(freq, aligned_row, slow_rows):
    omega = (F0 + freq).astype(jnp.float32) * (TWO_PI / NT)
    slow = slow_rows.astype(jnp.float32)
    x_coord = jnp.arange(CX, dtype=jnp.float32) - (CX - 1) / 2.0
    y_coord = jnp.arange(CY, dtype=jnp.float32) - (CY - 1) / 2.0
    z_coord = jnp.arange(CZ, dtype=jnp.float32) - (CZ - 1) / 2.0
    phase_x = (omega * slow[0])[None, :] * x_coord[:, None]
    phase_y = (omega * slow[1])[None, :] * y_coord[:, None]
    phase = phase_x[:, None, :] + phase_y[None, :, :]
    cosine = jnp.cos(phase)
    sine = jnp.sin(phase)
    real_in = aligned_row[0].astype(jnp.float32)[None, None, :]
    imag_in = aligned_row[1].astype(jnp.float32)[None, None, :]
    front_real = (real_in * cosine + imag_in * sine).astype(jnp.bfloat16).reshape(CX * CY, -1)
    front_imag = (imag_in * cosine - real_in * sine).astype(jnp.bfloat16).reshape(CX * CY, -1)
    left_side = jnp.concatenate([front_real, front_imag], axis=1)
    phase_z = (omega * slow[2])[:, None] * z_coord[None, :]
    depth_real = jnp.cos(phase_z).astype(jnp.bfloat16)
    depth_imag = jnp.sin(phase_z).astype(jnp.bfloat16)
    upper_rows = jnp.concatenate([depth_real, -depth_imag], axis=1)
    lower_rows = jnp.concatenate([depth_imag, depth_real], axis=1)
    right_side = jnp.concatenate([upper_rows, lower_rows], axis=0)
    return jnp.dot(left_side, right_side, preferred_element_type=jnp.float32)


CHUNK = 256


def exp_neg(angle):
    return jnp.cos(angle), -jnp.sin(angle)


def enter_barrier(count, reach):
    me = lax.axis_index("sta")
    tile = lax.axis_index("grid")
    tiles = lax.axis_size("grid")
    mesh_ids = pl.DeviceIdType.MESH
    barrier = pltpu.get_barrier_semaphore()
    for shift in range(1, count):
        pl.semaphore_signal(barrier, inc=1, device_id=(tile, lax.rem(me + shift, count)), device_id_type=mesh_ids)
    neighbours = jnp.int32(0)
    for k in range(-reach, reach + 1):
        if k == 0:
            continue
        there = (tile + k >= 0) & (tile + k < tiles)
        neighbours = neighbours + there.astype(jnp.int32)

        @pl.when(there)
        def _():
            pl.semaphore_signal(barrier, inc=1, device_id=(tile + k, me), device_id_type=mesh_ids)

    pl.semaphore_wait(barrier, count - 1 + neighbours)


def exchange_inputs(spec_ref, lag_ref, slow_ref, spec_in, lag_in, slow_in, local_sem, send_sem, recv_sem, then, reach):
    count = spec_in.shape[0]
    me = lax.axis_index("sta")
    tile = lax.axis_index("grid")
    mesh_ids = pl.DeviceIdType.MESH
    enter_barrier(count, reach)
    pairs = ((spec_ref, spec_in), (lag_ref, lag_in), (slow_ref, slow_in))
    local = []
    for kind, (source, target) in enumerate(pairs):
        own = source.at[me] if kind == 0 else source
        copy = pltpu.make_async_copy(own, target.at[me], local_sem.at[kind])
        copy.start()
        local.append(copy)
    sends = []
    for shift in range(1, count):
        peer = lax.rem(me + shift, count)
        for kind, (source, target) in enumerate(pairs):
            part = source.at[peer] if kind == 0 else source
            copy = pltpu.make_async_remote_copy(
                src_ref=part,
                dst_ref=target.at[me],
                send_sem=send_sem.at[kind, shift],
                recv_sem=recv_sem.at[kind, me],
                device_id=(tile, peer),
                device_id_type=mesh_ids,
            )
            copy.start()
            sends.append(copy)
    then()
    for copy in local:
        copy.wait()
    for copy in sends:
        copy.wait_send()
    for shift in range(1, count):
        source_id = lax.rem(me + count - shift, count)
        for kind, (source, target) in enumerate(pairs):
            part = source.at[source_id] if kind == 0 else source
            pltpu.make_async_remote_copy(
                src_ref=part,
                dst_ref=target.at[source_id],
                send_sem=send_sem.at[kind, shift],
                recv_sem=recv_sem.at[kind, source_id],
                device_id=(tile, source_id),
                device_id_type=mesh_ids,
            ).wait_recv()


def align_block(spec, lag, slow, source, real_ref, imag_ref, turn_ref):
    bins, block = spec.shape[1], spec.shape[2]
    first_bin = lax.axis_index("sta") * bins
    bin_rows = (F0 + first_bin + lax.broadcasted_iota(jnp.int32, (bins, block), 0)).astype(jnp.float32)
    cols = pl.ds(pl.multiple_of(source * block, 128), block)
    product = bin_rows * lag.astype(jnp.float32)
    whole = jnp.floor(product * (1.0 / NT))
    left = product - whole * NT
    left = jnp.where(left < 0.0, left + NT, left)
    left = jnp.where(left >= NT, left - NT, left)
    turned = left * (TWO_PI / NT)
    cosine = jnp.cos(turned)
    sine = jnp.sin(turned)
    real_in = spec[0].astype(jnp.float32)
    imag_in = spec[1].astype(jnp.float32)
    real_ref[:, cols] = (real_in * cosine + imag_in * sine).astype(jnp.bfloat16).astype(jnp.float32)
    imag_ref[:, cols] = (imag_in * cosine - real_in * sine).astype(jnp.bfloat16).astype(jnp.float32)
    turn_ref[:, cols] = slow.astype(jnp.float32)


def complex_times(left, right):
    return left[0] * right[0] - left[1] * right[1], left[0] * right[1] + left[1] * right[0]


def factor_rows(turn_x, turn_y, turn_z, rows8, rows16):
    return (
        exp_neg(turn_x * (rows8 - 3.5)),
        exp_neg(turn_x * (8.0 * (rows8 - 1.5))),
        exp_neg(turn_y * (rows8 - 3.5)),
        exp_neg(turn_z * (rows16 - 7.5)),
        exp_neg(turn_z * (16.0 * (rows8 - 3.5))),
    )


def beam_kernel(spec_ref, lag_ref, slow_ref, out_ref, spec_in, lag_in, slow_in, local_sem, send_sem, recv_sem,
                real_ref, imag_ref, turn_ref, acc_ref, left_ref, right_ref, power_ref, pieces, send_rs, recv_rs,
                send_ag, recv_ag, share_sem):
    count, bins, block = spec_in.shape[0], spec_in.shape[2], spec_in.shape[3]
    me = lax.axis_index("sta")
    first_bin = me * bins
    width = CHUNK
    per_block = block // width
    half_z = CZ // 2
    rows8 = lax.broadcasted_iota(jnp.int32, (8, width), 0).astype(jnp.float32)
    rows16 = lax.broadcasted_iota(jnp.int32, (16, width), 0).astype(jnp.float32)
    omega0 = (F0 + first_bin).astype(jnp.float32) * (TWO_PI / NT)
    step = TWO_PI / NT
    acc_ref[...] = jnp.zeros_like(acc_ref)

    def per_chunk(k, carry):
        source = lax.rem(me + k // per_block, count)
        cols = pl.ds(pl.multiple_of(source * block + lax.rem(k, per_block) * width, 128), width)
        slow_x = turn_ref[0:1, cols]
        slow_y = turn_ref[1:2, cols]
        slow_z = turn_ref[2:3, cols]
        start = factor_rows(omega0 * slow_x, omega0 * slow_y, omega0 * slow_z, rows8, rows16)
        ratio = factor_rows(step * slow_x, step * slow_y, step * slow_z, rows8, rows16)

        def per_bin(f, state):
            (a_r, a_i), (b_r, b_i), (y_r, y_i), (c_r, c_i), (d_r, d_i) = state
            real_in = real_ref[pl.ds(f, 1), cols]
            imag_in = imag_ref[pl.ds(f, 1), cols]
            q_r = real_in * y_r - imag_in * y_i
            q_i = real_in * y_i + imag_in * y_r
            near = [complex_times((b_r[m : m + 1], b_i[m : m + 1]), (a_r, a_i)) for m in range(CX // 16)]
            cells = CX * CY
            for y in range(CY):
                qq_r, qq_i = q_r[y : y + 1], q_i[y : y + 1]
                lo_r, lo_i, hi_r, hi_i = [], [], [], []
                for x_r, x_i in near:
                    t1, t2 = qq_r * x_r, qq_i * x_i
                    t3, t4 = qq_r * x_i, qq_i * x_r
                    lo_r.append(t1 - t2)
                    lo_i.append(t3 + t4)
                    hi_r.append(t1 + t2)
                    hi_i.append(t4 - t3)
                row = y * CX
                half = CX // 2
                left_ref[row : row + half, :] = jnp.concatenate(lo_r, axis=0).astype(jnp.bfloat16)
                left_ref[row + half : row + CX, :] = jnp.concatenate(hi_r, axis=0).astype(jnp.bfloat16)
                left_ref[cells + row : cells + row + half, :] = jnp.concatenate(lo_i, axis=0).astype(jnp.bfloat16)
                left_ref[cells + row + half : cells + row + CX, :] = jnp.concatenate(hi_i, axis=0).astype(jnp.bfloat16)
            for m in range(half_z // 16):
                z_r, z_i = complex_times((d_r[m : m + 1], d_i[m : m + 1]), (c_r, c_i))
                row = 16 * m
                right_ref[row : row + 16, :] = z_r.astype(jnp.bfloat16)
                right_ref[half_z + row : half_z + row + 16, :] = z_i.astype(jnp.bfloat16)
            acc_ref[f] += lax.dot_general(
                left_ref[...], right_ref[...], (((1,), (1,)), ((), ())), preferred_element_type=jnp.float32
            )
            return tuple(complex_times(now, turn) for now, turn in zip(state, ratio))

        lax.fori_loop(0, bins, per_bin, start)
        return carry

    def own_block():
        align_block(spec_ref[me], lag_ref[...], slow_ref[...], me, real_ref, imag_ref, turn_ref)
        lax.fori_loop(0, per_block, per_chunk, 0)

    exchange_inputs(
        spec_ref, lag_ref, slow_ref, spec_in, lag_in, slow_in, local_sem, send_sem, recv_sem, own_block, out_ref.shape[0] // 2
    )

    def align_other(shift, carry):
        source = lax.rem(me + shift, count)
        align_block(spec_in[source], lag_in[source], slow_in[source], source, real_ref, imag_ref, turn_ref)
        return carry

    lax.fori_loop(1, count, align_other, 0)
    lax.fori_loop(per_block, count * per_block, per_chunk, 0)
    cells = CX * CY
    low = jnp.zeros((cells, half_z), jnp.float32)
    high = jnp.zeros((cells, half_z), jnp.float32)
    for f in range(bins):
        sums = acc_ref[f]
        u, w = sums[:cells, :half_z], sums[:cells, half_z:]
        x, v = sums[cells:, :half_z], sums[cells:, half_z:]
        low = low + ((u - v) * (u - v) + (w + x) * (w + x))
        high = high + ((u + v) * (u + v) + (x - w) * (x - w))
    power_ref[:, :half_z] = low
    power_ref[:, half_z:] = high
    share_kernel(power_ref, out_ref, pieces, send_rs, recv_rs, send_ag, recv_ag, share_sem)


def beam_power(spec_send, lag_row, slow_rows, reach):
    count = spec_send.shape[0]
    slots = 2 * reach + 1
    cells = CX * CY
    bins, block = spec_send.shape[2], spec_send.shape[3]
    width = CHUNK
    stations = count * block
    vmem = pl.BlockSpec(memory_space=pltpu.VMEM)
    return pl.pallas_call(
        beam_kernel,
        out_shape=jax.ShapeDtypeStruct((slots, cells, CZ), jnp.float32),
        in_specs=[vmem, vmem, vmem],
        out_specs=vmem,
        scratch_shapes=[
            pltpu.VMEM((count,) + spec_send.shape[1:], jnp.bfloat16),
            pltpu.VMEM((count,) + lag_row.shape, jnp.int32),
            pltpu.VMEM((count,) + slow_rows.shape, jnp.bfloat16),
            pltpu.SemaphoreType.DMA((3,)),
            pltpu.SemaphoreType.DMA((3, count)),
            pltpu.SemaphoreType.DMA((3, count)),
            pltpu.VMEM((bins, stations), jnp.float32),
            pltpu.VMEM((bins, stations), jnp.float32),
            pltpu.VMEM((slow_rows.shape[0], stations), jnp.float32),
            pltpu.VMEM((bins, 2 * CX * CY, CZ), jnp.float32),
            pltpu.VMEM((2 * CX * CY, width), jnp.bfloat16),
            pltpu.VMEM((CZ, width), jnp.bfloat16),
            pltpu.VMEM((cells, CZ), jnp.float32),
            pltpu.VMEM((count, cells // count, CZ), jnp.float32),
            pltpu.SemaphoreType.DMA((count,)),
            pltpu.SemaphoreType.DMA((count,)),
            pltpu.SemaphoreType.DMA((slots, count)),
            pltpu.SemaphoreType.DMA((slots, count)),
            pltpu.SemaphoreType.DMA((1,)),
        ],
        compiler_params=pltpu.CompilerParams(collective_id=1, has_side_effects=True),
    )(spec_send, lag_row, slow_rows)


def share_kernel(part_ref, out_ref, pieces, send_rs, recv_rs, send_ag, recv_ag, local_sem):
    count = pieces.shape[0]
    slots = out_ref.shape[0]
    reach = slots // 2
    rows = pieces.shape[1]
    me = lax.axis_index("sta")
    tile = lax.axis_index("grid")
    tiles = lax.axis_size("grid")
    mesh_ids = pl.DeviceIdType.MESH
    own = pltpu.make_async_copy(part_ref.at[pl.ds(pl.multiple_of(me * rows, 8), rows)], pieces.at[me], local_sem.at[0])
    own.start()
    sends = []
    for shift in range(1, count):
        peer = lax.rem(me + shift, count)
        copy = pltpu.make_async_remote_copy(
            src_ref=part_ref.at[pl.ds(pl.multiple_of(peer * rows, 8), rows)],
            dst_ref=pieces.at[me],
            send_sem=send_rs.at[shift],
            recv_sem=recv_rs.at[me],
            device_id=(tile, peer),
            device_id_type=mesh_ids,
        )
        copy.start()
        sends.append(copy)
    own.wait()
    for copy in sends:
        copy.wait_send()
    for shift in range(1, count):
        source = lax.rem(me + count - shift, count)
        pltpu.make_async_remote_copy(
            src_ref=pieces.at[source],
            dst_ref=pieces.at[source],
            send_sem=send_rs.at[shift],
            recv_sem=recv_rs.at[source],
            device_id=(tile, source),
            device_id_type=mesh_ids,
        ).wait_recv()
    total = pieces[0]
    for source in range(1, count):
        total = total + pieces[source]
    mine = pl.ds(pl.multiple_of(me * rows, 8), rows)
    out_ref[reach, mine] = total
    block = out_ref.at[reach, mine]

    def gather_copy(k, peer, slot):
        return pltpu.make_async_remote_copy(
            src_ref=block,
            dst_ref=out_ref.at[slot, mine],
            send_sem=send_ag.at[slot, peer],
            recv_sem=recv_ag.at[slot, me],
            device_id=(tile + k, peer),
            device_id_type=mesh_ids,
        )

    peers = []
    for shift in range(1, count):
        copy = gather_copy(0, lax.rem(me + shift, count), reach)
        copy.start()
        peers.append(copy)
    for k in range(-reach, reach + 1):
        if k == 0:
            continue

        @pl.when(jnp.logical_not((tile + k >= 0) & (tile + k < tiles)))
        def _():
            out_ref[reach + k] = jnp.zeros(out_ref.shape[1:], out_ref.dtype)

    for copy in peers:
        copy.wait_send()
    for shift in range(1, count):
        source = lax.rem(me + count - shift, count)
        pltpu.make_async_remote_copy(
            src_ref=block,
            dst_ref=out_ref.at[reach, pl.ds(pl.multiple_of(source * rows, 8), rows)],
            send_sem=send_ag.at[reach, source],
            recv_sem=recv_ag.at[reach, source],
            device_id=(tile, source),
            device_id_type=mesh_ids,
        ).wait_recv()

    def halo_copy(k):
        return pltpu.make_async_remote_copy(
            src_ref=out_ref.at[reach],
            dst_ref=out_ref.at[reach - k],
            send_sem=send_ag.at[reach - k, me],
            recv_sem=recv_ag.at[reach - k, me],
            device_id=(tile + k, me),
            device_id_type=mesh_ids,
        )

    for k in range(-reach, reach + 1):
        if k == 0:
            continue

        @pl.when((tile + k >= 0) & (tile + k < tiles))
        def _():
            halo_copy(k).start()

    for k in range(-reach, reach + 1):
        if k == 0:
            continue

        @pl.when((tile + k >= 0) & (tile + k < tiles))
        def _():
            halo_copy(k).wait_send()
            pltpu.make_async_remote_copy(
                src_ref=out_ref.at[reach],
                dst_ref=out_ref.at[reach + k],
                send_sem=send_ag.at[reach + k, me],
                recv_sem=recv_ag.at[reach + k, me],
                device_id=(tile + k, me),
                device_id_type=mesh_ids,
            ).wait_recv()


def share_power(part, reach):
    count = lax.axis_size("sta")
    rows = part.shape[0] // count
    slots = 2 * reach + 1
    return pl.pallas_call(
        share_kernel,
        out_shape=jax.ShapeDtypeStruct((slots,) + part.shape, jnp.float32),
        in_specs=[pl.BlockSpec(memory_space=pltpu.VMEM)],
        out_specs=pl.BlockSpec(memory_space=pltpu.VMEM),
        scratch_shapes=[
            pltpu.VMEM((count, rows, part.shape[1]), jnp.float32),
            pltpu.SemaphoreType.DMA((count,)),
            pltpu.SemaphoreType.DMA((count,)),
            pltpu.SemaphoreType.DMA((slots, count)),
            pltpu.SemaphoreType.DMA((slots, count)),
            pltpu.SemaphoreType.DMA((1,)),
        ],
        compiler_params=pltpu.CompilerParams(collective_id=0, has_side_effects=True),
    )(part)


def freq_beams(freq_ids, aligned_rows, slow_rows):
    return lax.map(lambda pair: beam_freq(pair[0], pair[1], slow_rows), (freq_ids, aligned_rows))


def band_matrix(taps, length):
    rows = jnp.arange(length, dtype=jnp.int32)[:, None]
    columns = jnp.arange(length + 2 * HALF, dtype=jnp.int32)[None, :]
    offset = columns - rows
    picks = jnp.arange(TAPS, dtype=jnp.int32)[:, None, None]
    return jnp.sum(jnp.where(offset[None] == picks, taps[:, None, None], 0.0), axis=0)


def blur(volume, bands):
    band_x, square_y, square_z = bands
    padded = with_halo(volume.astype(jnp.bfloat16), (("grid", 0),), HALF).astype(volume.dtype)
    along_x = jnp.einsum("ip,pyz->iyz", band_x, padded, precision=lax.Precision.HIGHEST)
    along_y = jnp.einsum("jq,xqz->xjz", square_y, along_x, precision=lax.Precision.HIGHEST)
    return jnp.einsum("xyw,kw->xyk", along_y, square_z, precision=lax.Precision.HIGHEST)


def blur_narrowing(volume, taps, square_y, square_z):
    band_x = band_matrix(taps, volume.shape[0] - 2 * HALF)
    along_x = jnp.einsum("ip,pyz->iyz", band_x, volume, precision=lax.Precision.HIGHEST)
    along_y = jnp.einsum("jq,xqz->xjz", square_y, along_x, precision=lax.Precision.HIGHEST)
    return jnp.einsum("xyw,kw->xyk", along_y, square_z, precision=lax.Precision.HIGHEST)


def deblur(observed, halo_tiles, spread_taps):
    tiles = lax.axis_size("grid")
    me = lax.axis_index("grid")
    reach = ITERS * 2 * HALF
    cut = halo_tiles * CX - reach
    observed = observed[cut : observed.shape[0] - cut]
    width = observed.shape[0]
    cell = (me - halo_tiles) * CX + cut + jnp.arange(width, dtype=jnp.int32)
    inside = (cell >= 0) & (cell < tiles * CX)
    square_y = band_matrix(spread_taps[1], CY)[:, HALF : HALF + CY]
    square_z = band_matrix(spread_taps[2], CZ)[:, HALF : HALF + CZ]
    estimate = jnp.where(inside[:, None, None], observed, 0.0)
    for sweep in range(ITERS):
        low = 2 * HALF * sweep + HALF
        blurred = blur_narrowing(estimate, spread_taps[0], square_y, square_z)
        ratio = jnp.where(
            inside[low : width - low, None, None], observed[low : width - low] / blurred, 0.0
        )
        estimate = estimate[2 * HALF : estimate.shape[0] - 2 * HALF] * blur_narrowing(
            ratio, spread_taps[0], square_y, square_z
        )
    return estimate


def band_of(taps_ref, axis, rows, cols):
    offset = cols - rows + HALF
    band = jnp.zeros(offset.shape, jnp.float32)
    for tap in range(TAPS):
        band = jnp.where(offset == tap, taps_ref[axis, tap], band)
    return band


def mirror(index, length):
    return jnp.where(index < length // 2, index, 3 * (length // 2) - 1 - index)


def deblur_kernel(taps_ref, obs_ref, out_ref, kx_ref, kz_ref):
    tiles = lax.axis_size("grid")
    me = lax.axis_index("grid")
    planes, width, depth = obs_ref.shape
    shape_x = kx_ref.shape
    kx_ref[...] = band_of(
        taps_ref, 0, lax.broadcasted_iota(jnp.int32, shape_x, 0) + HALF, lax.broadcasted_iota(jnp.int32, shape_x, 1)
    )
    shape_z = kz_ref.shape
    kz_ref[...] = band_of(
        taps_ref,
        2,
        mirror(lax.broadcasted_iota(jnp.int32, shape_z, 1), depth),
        mirror(lax.broadcasted_iota(jnp.int32, shape_z, 0), depth),
    )
    halo_tiles = (width - CX) // (2 * CX)
    highest = lax.Precision.HIGHEST

    def inside(low, size):
        cell = (me - halo_tiles) * CX + low + lax.broadcasted_iota(jnp.int32, (size, depth), 0)
        return (cell >= 0) & (cell < tiles * CX)

    lanes = planes * depth

    def blur(volume):
        size_in = volume.shape[0]
        size_out = size_in - 2 * HALF
        band = kx_ref[0:size_out, 0:size_in]
        along_x = jnp.dot(band, volume, precision=highest, preferred_element_type=jnp.float32)
        along_y = []
        for y in range(planes):
            total = None
            for q in range(planes):
                term = taps_ref[1, q - y + HALF] * along_x[:, q * depth : (q + 1) * depth]
                total = term if total is None else total + term
            along_y.append(total)
        joined = jnp.concatenate(along_y, axis=0)
        along_z = jnp.dot(joined, kz_ref[...], precision=highest, preferred_element_type=jnp.float32)
        return jnp.concatenate([along_z[y * size_out : (y + 1) * size_out] for y in range(planes)], axis=1)

    def inside_wide(low, size):
        cell = (me - halo_tiles) * CX + low + lax.broadcasted_iota(jnp.int32, (size, lanes), 0)
        return (cell >= 0) & (cell < tiles * CX)

    observed = jnp.concatenate([obs_ref[y] for y in range(planes)], axis=1)
    estimate = jnp.where(inside_wide(0, width), observed, 0.0)
    for sweep in range(ITERS):
        low = 2 * HALF * sweep + HALF
        blurred = blur(estimate)
        size = blurred.shape[0]
        ratio = jnp.where(inside_wide(low, size), observed[low : low + size] / blurred, 0.0)
        spread = blur(ratio)
        estimate = estimate[2 * HALF : 2 * HALF + spread.shape[0]] * spread
    for y in range(planes):
        out_ref[y] = estimate[:, y * depth : (y + 1) * depth]


def deblur_tile(observed, spread_taps):
    planes, width, depth = observed.shape
    vmem = pl.BlockSpec(memory_space=pltpu.VMEM)
    return pl.pallas_call(
        deblur_kernel,
        out_shape=jax.ShapeDtypeStruct((planes, CX, depth), jnp.float32),
        in_specs=[pl.BlockSpec(memory_space=pltpu.SMEM), vmem],
        out_specs=vmem,
        scratch_shapes=[
            pltpu.VMEM((width - 2 * HALF, width), jnp.float32),
            pltpu.VMEM((depth, depth), jnp.float32),
        ],
    )(spread_taps, observed)


def per_device(spectra, lag_samples, slowness, spread_taps):
    groups = lax.axis_size("sta")
    own_count = FREQS // groups
    first_bin = lax.axis_index("sta") * own_count
    block = spectra.shape[2]
    spec_send = spectra.reshape(groups, own_count, 2, block).transpose(0, 2, 1, 3)
    halo_tiles = -(-(ITERS * 2 * HALF) // CX)
    summed = beam_power(spec_send, lag_samples, slowness[0], halo_tiles)
    observed = summed / (FREQS * STATIONS) + BACKGROUND
    slots = observed.shape[0]
    observed = observed.reshape(slots, CY, CX, CZ)
    observed = jnp.concatenate([observed[:, :, : CX // 2], observed[:, :, CX // 2 :][:, :, ::-1]], axis=2)
    planes = observed.transpose(1, 0, 2, 3).reshape(CY, slots * CX, CZ)
    estimate = deblur_tile(planes, spread_taps)
    both = jnp.stack([observed[halo_tiles], estimate])
    both = jnp.concatenate([both[..., : CZ // 2], both[..., CZ // 2 :][..., ::-1]], axis=-1).transpose(0, 2, 1, 3)
    stacked, estimate = both[0], both[1]
    return (stacked[None], estimate[None])


def solution(mesh):
    placed = (P(None, None, "sta"), P("grid", "sta"), P("grid", None, "sta"), P())
    return jax.shard_map(
        per_device,
        mesh=mesh,
        in_specs=placed,
        out_specs=(P("grid", None, None, None), P("grid", None, None, None)),
        check_vma=False,
    )
```

```python
import math

import jax
import jax.numpy as jnp
from jax import lax
from jax.sharding import PartitionSpec as P
from jax.experimental import pallas as pl
from jax.experimental.pallas import tpu as pltpu

STATIONS = 6144
FREQS = 64
F0 = 600
NT = 6000
TAPS = 17
HALF = 8
ITERS = 4
CX = 32
CY = 8
CZ = 128


TWO_PI = 2.0 * math.pi
BACKGROUND = 0.05


def with_halo(array, sides, width):
    for axis, dim in sides:
        size, length = (lax.axis_size(axis), array.shape[dim])
        up = [(i, (i + 1) % size) for i in range(size - 1)]
        down = [(j, i) for i, j in up]
        last = lax.slice_in_dim(array, length - width, length, axis=dim)
        leading = lax.slice_in_dim(array, 0, width, axis=dim)
        before = lax.ppermute(last, axis, up)
        after = lax.ppermute(leading, axis, down)
        array = jnp.concatenate([before, array, after], axis=dim)
    return array


def align_rows(spectra, lag_row):
    bins = F0 + jnp.arange(FREQS, dtype=jnp.int32)
    cycles = bins[:, None] * lag_row[None, :] % NT
    turned = cycles.astype(jnp.float32) * (TWO_PI / NT)
    cosine = jnp.cos(turned)
    sine = jnp.sin(turned)
    real_in = spectra[:, 0, :].astype(jnp.float32)
    imag_in = spectra[:, 1, :].astype(jnp.float32)
    real_out = real_in * cosine + imag_in * sine
    imag_out = imag_in * cosine - real_in * sine
    return jnp.stack([real_out, imag_out], axis=1).astype(jnp.bfloat16)


def beam_freq(freq, aligned_row, slow_rows):
    omega = (F0 + freq).astype(jnp.float32) * (TWO_PI / NT)
    slow = slow_rows.astype(jnp.float32)
    x_coord = jnp.arange(CX, dtype=jnp.float32) - (CX - 1) / 2.0
    y_coord = jnp.arange(CY, dtype=jnp.float32) - (CY - 1) / 2.0
    z_coord = jnp.arange(CZ, dtype=jnp.float32) - (CZ - 1) / 2.0
    phase_x = (omega * slow[0])[None, :] * x_coord[:, None]
    phase_y = (omega * slow[1])[None, :] * y_coord[:, None]
    phase = phase_x[:, None, :] + phase_y[None, :, :]
    cosine = jnp.cos(phase)
    sine = jnp.sin(phase)
    real_in = aligned_row[0].astype(jnp.float32)[None, None, :]
    imag_in = aligned_row[1].astype(jnp.float32)[None, None, :]
    front_real = (real_in * cosine + imag_in * sine).astype(jnp.bfloat16).reshape(CX * CY, -1)
    front_imag = (imag_in * cosine - real_in * sine).astype(jnp.bfloat16).reshape(CX * CY, -1)
    left_side = jnp.concatenate([front_real, front_imag], axis=1)
    phase_z = (omega * slow[2])[:, None] * z_coord[None, :]
    depth_real = jnp.cos(phase_z).astype(jnp.bfloat16)
    depth_imag = jnp.sin(phase_z).astype(jnp.bfloat16)
    upper_rows = jnp.concatenate([depth_real, -depth_imag], axis=1)
    lower_rows = jnp.concatenate([depth_imag, depth_real], axis=1)
    right_side = jnp.concatenate([upper_rows, lower_rows], axis=0)
    return jnp.dot(left_side, right_side, preferred_element_type=jnp.float32)


CHUNK = 384


def exp_neg(angle):
    return jnp.cos(angle), -jnp.sin(angle)


def enter_barrier(count, reach):
    me = lax.axis_index("sta")
    tile = lax.axis_index("grid")
    tiles = lax.axis_size("grid")
    mesh_ids = pl.DeviceIdType.MESH
    barrier = pltpu.get_barrier_semaphore()
    for shift in range(1, count):
        pl.semaphore_signal(barrier, inc=1, device_id=(tile, lax.rem(me + shift, count)), device_id_type=mesh_ids)
    neighbours = jnp.int32(0)
    for k in range(-reach, reach + 1):
        if k == 0:
            continue
        there = (tile + k >= 0) & (tile + k < tiles)
        neighbours = neighbours + there.astype(jnp.int32)

        @pl.when(there)
        def _():
            pl.semaphore_signal(barrier, inc=1, device_id=(tile + k, me), device_id_type=mesh_ids)

    pl.semaphore_wait(barrier, count - 1 + neighbours)


def exchange_inputs(spec_ref, lag_ref, slow_ref, spec_in, lag_in, slow_in, local_sem, send_sem, recv_sem, then, reach):
    count = spec_in.shape[0]
    me = lax.axis_index("sta")
    tile = lax.axis_index("grid")
    mesh_ids = pl.DeviceIdType.MESH
    enter_barrier(count, reach)
    pairs = ((spec_ref, spec_in), (lag_ref, lag_in), (slow_ref, slow_in))
    local = []
    for kind, (source, target) in enumerate(pairs):
        own = source.at[me] if kind == 0 else source
        copy = pltpu.make_async_copy(own, target.at[me], local_sem.at[kind])
        copy.start()
        local.append(copy)
    sends = []
    for shift in range(1, count):
        peer = lax.rem(me + shift, count)
        for kind, (source, target) in enumerate(pairs):
            part = source.at[peer] if kind == 0 else source
            copy = pltpu.make_async_remote_copy(
                src_ref=part,
                dst_ref=target.at[me],
                send_sem=send_sem.at[kind, shift],
                recv_sem=recv_sem.at[kind, me],
                device_id=(tile, peer),
                device_id_type=mesh_ids,
            )
            copy.start()
            sends.append(copy)
    then()
    for copy in local:
        copy.wait()
    for copy in sends:
        copy.wait_send()
    for shift in range(1, count):
        source_id = lax.rem(me + count - shift, count)
        for kind, (source, target) in enumerate(pairs):
            part = source.at[source_id] if kind == 0 else source
            pltpu.make_async_remote_copy(
                src_ref=part,
                dst_ref=target.at[source_id],
                send_sem=send_sem.at[kind, shift],
                recv_sem=recv_sem.at[kind, source_id],
                device_id=(tile, source_id),
                device_id_type=mesh_ids,
            ).wait_recv()


def align_block(spec, lag, slow, source, real_ref, imag_ref, turn_ref):
    bins, block = spec.shape[1], spec.shape[2]
    first_bin = lax.axis_index("sta") * bins
    bin_rows = (F0 + first_bin + lax.broadcasted_iota(jnp.int32, (bins, block), 0)).astype(jnp.float32)
    cols = pl.ds(pl.multiple_of(source * block, 128), block)
    product = bin_rows * lag.astype(jnp.float32)
    whole = jnp.floor(product * (1.0 / NT))
    left = product - whole * NT
    left = jnp.where(left < 0.0, left + NT, left)
    left = jnp.where(left >= NT, left - NT, left)
    turned = left * (TWO_PI / NT)
    cosine = jnp.cos(turned)
    sine = jnp.sin(turned)
    real_in = spec[0].astype(jnp.float32)
    imag_in = spec[1].astype(jnp.float32)
    real_ref[:, cols] = (real_in * cosine + imag_in * sine).astype(jnp.bfloat16).astype(jnp.float32)
    imag_ref[:, cols] = (imag_in * cosine - real_in * sine).astype(jnp.bfloat16).astype(jnp.float32)
    turn_ref[:, cols] = slow.astype(jnp.float32)


def complex_times(left, right):
    return left[0] * right[0] - left[1] * right[1], left[0] * right[1] + left[1] * right[0]


def factor_rows(turn_x, turn_y, turn_z, rows8, rows16):
    return (
        exp_neg(turn_x * (rows8 - 3.5)),
        exp_neg(turn_x * (8.0 * (rows8 - 1.5))),
        exp_neg(turn_y * (rows8 - 3.5)),
        exp_neg(turn_z * (rows16 - 7.5)),
        exp_neg(turn_z * (16.0 * (rows8 - 3.5))),
    )


def beam_kernel(spec_ref, lag_ref, slow_ref, out_ref, spec_in, lag_in, slow_in, local_sem, send_sem, recv_sem,
                real_ref, imag_ref, turn_ref, acc_ref, left_ref, right_ref, power_ref, pieces, send_rs, recv_rs,
                send_ag, recv_ag, share_sem):
    count, bins, block = spec_in.shape[0], spec_in.shape[2], spec_in.shape[3]
    me = lax.axis_index("sta")
    first_bin = me * bins
    width = CHUNK
    per_block = block // width
    half_z = CZ // 2
    rows8 = lax.broadcasted_iota(jnp.int32, (8, width), 0).astype(jnp.float32)
    rows16 = lax.broadcasted_iota(jnp.int32, (16, width), 0).astype(jnp.float32)
    omega0 = (F0 + first_bin).astype(jnp.float32) * (TWO_PI / NT)
    step = TWO_PI / NT
    acc_ref[...] = jnp.zeros_like(acc_ref)

    def per_chunk(k, carry):
        source = lax.rem(me + k // per_block, count)
        cols = pl.ds(pl.multiple_of(source * block + lax.rem(k, per_block) * width, 128), width)
        slow_x = turn_ref[0:1, cols]
        slow_y = turn_ref[1:2, cols]
        slow_z = turn_ref[2:3, cols]
        start = factor_rows(omega0 * slow_x, omega0 * slow_y, omega0 * slow_z, rows8, rows16)
        ratio = factor_rows(step * slow_x, step * slow_y, step * slow_z, rows8, rows16)

        def per_bin(f, state):
            (a_r, a_i), (b_r, b_i), (y_r, y_i), (c_r, c_i), (d_r, d_i) = state
            real_in = real_ref[pl.ds(f, 1), cols]
            imag_in = imag_ref[pl.ds(f, 1), cols]
            q_r = real_in * y_r - imag_in * y_i
            q_i = real_in * y_i + imag_in * y_r
            near = [complex_times((b_r[m : m + 1], b_i[m : m + 1]), (a_r, a_i)) for m in range(CX // 16)]
            cells = CX * CY
            for y in range(CY):
                qq_r, qq_i = q_r[y : y + 1], q_i[y : y + 1]
                lo_r, lo_i, hi_r, hi_i = [], [], [], []
                for x_r, x_i in near:
                    t1, t2 = qq_r * x_r, qq_i * x_i
                    t3, t4 = qq_r * x_i, qq_i * x_r
                    lo_r.append(t1 - t2)
                    lo_i.append(t3 + t4)
                    hi_r.append(t1 + t2)
                    hi_i.append(t4 - t3)
                row = y * CX
                half = CX // 2
                left_ref[row : row + half, :] = jnp.concatenate(lo_r, axis=0).astype(jnp.bfloat16)
                left_ref[row + half : row + CX, :] = jnp.concatenate(hi_r, axis=0).astype(jnp.bfloat16)
                left_ref[cells + row : cells + row + half, :] = jnp.concatenate(lo_i, axis=0).astype(jnp.bfloat16)
                left_ref[cells + row + half : cells + row + CX, :] = jnp.concatenate(hi_i, axis=0).astype(jnp.bfloat16)
            for m in range(half_z // 16):
                z_r, z_i = complex_times((d_r[m : m + 1], d_i[m : m + 1]), (c_r, c_i))
                row = 16 * m
                right_ref[row : row + 16, :] = z_r.astype(jnp.bfloat16)
                right_ref[half_z + row : half_z + row + 16, :] = z_i.astype(jnp.bfloat16)
            acc_ref[f] += lax.dot_general(
                left_ref[...], right_ref[...], (((1,), (1,)), ((), ())), preferred_element_type=jnp.float32
            )
            return tuple(complex_times(now, turn) for now, turn in zip(state, ratio))

        lax.fori_loop(0, bins, per_bin, start)
        return carry

    def own_block():
        align_block(spec_ref[me], lag_ref[...], slow_ref[...], me, real_ref, imag_ref, turn_ref)
        lax.fori_loop(0, per_block, per_chunk, 0)

    exchange_inputs(
        spec_ref, lag_ref, slow_ref, spec_in, lag_in, slow_in, local_sem, send_sem, recv_sem, own_block, out_ref.shape[0] // 2
    )

    def align_other(shift, carry):
        source = lax.rem(me + shift, count)
        align_block(spec_in[source], lag_in[source], slow_in[source], source, real_ref, imag_ref, turn_ref)
        return carry

    lax.fori_loop(1, count, align_other, 0)
    lax.fori_loop(per_block, count * per_block, per_chunk, 0)
    cells = CX * CY
    low = jnp.zeros((cells, half_z), jnp.float32)
    high = jnp.zeros((cells, half_z), jnp.float32)
    for f in range(bins):
        sums = acc_ref[f]
        u, w = sums[:cells, :half_z], sums[:cells, half_z:]
        x, v = sums[cells:, :half_z], sums[cells:, half_z:]
        low = low + ((u - v) * (u - v) + (w + x) * (w + x))
        high = high + ((u + v) * (u + v) + (x - w) * (x - w))
    power_ref[:, :half_z] = low
    power_ref[:, half_z:] = high
    share_kernel(power_ref, out_ref, pieces, send_rs, recv_rs, send_ag, recv_ag, share_sem)


def beam_power(spec_send, lag_row, slow_rows, reach):
    count = spec_send.shape[0]
    slots = 2 * reach + 1
    cells = CX * CY
    bins, block = spec_send.shape[2], spec_send.shape[3]
    width = CHUNK
    stations = count * block
    vmem = pl.BlockSpec(memory_space=pltpu.VMEM)
    return pl.pallas_call(
        beam_kernel,
        out_shape=jax.ShapeDtypeStruct((slots, cells, CZ), jnp.float32),
        in_specs=[vmem, vmem, vmem],
        out_specs=vmem,
        scratch_shapes=[
            pltpu.VMEM((count,) + spec_send.shape[1:], jnp.bfloat16),
            pltpu.VMEM((count,) + lag_row.shape, jnp.int32),
            pltpu.VMEM((count,) + slow_rows.shape, jnp.bfloat16),
            pltpu.SemaphoreType.DMA((3,)),
            pltpu.SemaphoreType.DMA((3, count)),
            pltpu.SemaphoreType.DMA((3, count)),
            pltpu.VMEM((bins, stations), jnp.float32),
            pltpu.VMEM((bins, stations), jnp.float32),
            pltpu.VMEM((slow_rows.shape[0], stations), jnp.float32),
            pltpu.VMEM((bins, 2 * CX * CY, CZ), jnp.float32),
            pltpu.VMEM((2 * CX * CY, width), jnp.bfloat16),
            pltpu.VMEM((CZ, width), jnp.bfloat16),
            pltpu.VMEM((cells, CZ), jnp.float32),
            pltpu.VMEM((count, cells // count, CZ), jnp.float32),
            pltpu.SemaphoreType.DMA((count,)),
            pltpu.SemaphoreType.DMA((count,)),
            pltpu.SemaphoreType.DMA((slots, count)),
            pltpu.SemaphoreType.DMA((slots, count)),
            pltpu.SemaphoreType.DMA((1,)),
        ],
        compiler_params=pltpu.CompilerParams(collective_id=1, has_side_effects=True),
    )(spec_send, lag_row, slow_rows)


def share_kernel(part_ref, out_ref, pieces, send_rs, recv_rs, send_ag, recv_ag, local_sem):
    count = pieces.shape[0]
    slots = out_ref.shape[0]
    reach = slots // 2
    rows = pieces.shape[1]
    me = lax.axis_index("sta")
    tile = lax.axis_index("grid")
    tiles = lax.axis_size("grid")
    mesh_ids = pl.DeviceIdType.MESH
    own = pltpu.make_async_copy(part_ref.at[pl.ds(pl.multiple_of(me * rows, 8), rows)], pieces.at[me], local_sem.at[0])
    own.start()
    sends = []
    for shift in range(1, count):
        peer = lax.rem(me + shift, count)
        copy = pltpu.make_async_remote_copy(
            src_ref=part_ref.at[pl.ds(pl.multiple_of(peer * rows, 8), rows)],
            dst_ref=pieces.at[me],
            send_sem=send_rs.at[shift],
            recv_sem=recv_rs.at[me],
            device_id=(tile, peer),
            device_id_type=mesh_ids,
        )
        copy.start()
        sends.append(copy)
    own.wait()
    for copy in sends:
        copy.wait_send()
    for shift in range(1, count):
        source = lax.rem(me + count - shift, count)
        pltpu.make_async_remote_copy(
            src_ref=pieces.at[source],
            dst_ref=pieces.at[source],
            send_sem=send_rs.at[shift],
            recv_sem=recv_rs.at[source],
            device_id=(tile, source),
            device_id_type=mesh_ids,
        ).wait_recv()
    total = pieces[0]
    for source in range(1, count):
        total = total + pieces[source]
    mine = pl.ds(pl.multiple_of(me * rows, 8), rows)
    out_ref[reach, mine] = total
    block = out_ref.at[reach, mine]

    def gather_copy(k, peer, slot):
        return pltpu.make_async_remote_copy(
            src_ref=block,
            dst_ref=out_ref.at[slot, mine],
            send_sem=send_ag.at[slot, peer],
            recv_sem=recv_ag.at[slot, me],
            device_id=(tile + k, peer),
            device_id_type=mesh_ids,
        )

    peers = []
    for shift in range(1, count):
        copy = gather_copy(0, lax.rem(me + shift, count), reach)
        copy.start()
        peers.append(copy)
    for k in range(-reach, reach + 1):
        if k == 0:
            continue

        @pl.when(jnp.logical_not((tile + k >= 0) & (tile + k < tiles)))
        def _():
            out_ref[reach + k] = jnp.zeros(out_ref.shape[1:], out_ref.dtype)

    for copy in peers:
        copy.wait_send()
    for shift in range(1, count):
        source = lax.rem(me + count - shift, count)
        pltpu.make_async_remote_copy(
            src_ref=block,
            dst_ref=out_ref.at[reach, pl.ds(pl.multiple_of(source * rows, 8), rows)],
            send_sem=send_ag.at[reach, source],
            recv_sem=recv_ag.at[reach, source],
            device_id=(tile, source),
            device_id_type=mesh_ids,
        ).wait_recv()

    def halo_copy(k):
        return pltpu.make_async_remote_copy(
            src_ref=out_ref.at[reach],
            dst_ref=out_ref.at[reach - k],
            send_sem=send_ag.at[reach - k, me],
            recv_sem=recv_ag.at[reach - k, me],
            device_id=(tile + k, me),
            device_id_type=mesh_ids,
        )

    for k in range(-reach, reach + 1):
        if k == 0:
            continue

        @pl.when((tile + k >= 0) & (tile + k < tiles))
        def _():
            halo_copy(k).start()

    for k in range(-reach, reach + 1):
        if k == 0:
            continue

        @pl.when((tile + k >= 0) & (tile + k < tiles))
        def _():
            halo_copy(k).wait_send()
            pltpu.make_async_remote_copy(
                src_ref=out_ref.at[reach],
                dst_ref=out_ref.at[reach + k],
                send_sem=send_ag.at[reach + k, me],
                recv_sem=recv_ag.at[reach + k, me],
                device_id=(tile + k, me),
                device_id_type=mesh_ids,
            ).wait_recv()


def share_power(part, reach):
    count = lax.axis_size("sta")
    rows = part.shape[0] // count
    slots = 2 * reach + 1
    return pl.pallas_call(
        share_kernel,
        out_shape=jax.ShapeDtypeStruct((slots,) + part.shape, jnp.float32),
        in_specs=[pl.BlockSpec(memory_space=pltpu.VMEM)],
        out_specs=pl.BlockSpec(memory_space=pltpu.VMEM),
        scratch_shapes=[
            pltpu.VMEM((count, rows, part.shape[1]), jnp.float32),
            pltpu.SemaphoreType.DMA((count,)),
            pltpu.SemaphoreType.DMA((count,)),
            pltpu.SemaphoreType.DMA((slots, count)),
            pltpu.SemaphoreType.DMA((slots, count)),
            pltpu.SemaphoreType.DMA((1,)),
        ],
        compiler_params=pltpu.CompilerParams(collective_id=0, has_side_effects=True),
    )(part)


def freq_beams(freq_ids, aligned_rows, slow_rows):
    return lax.map(lambda pair: beam_freq(pair[0], pair[1], slow_rows), (freq_ids, aligned_rows))


def band_matrix(taps, length):
    rows = jnp.arange(length, dtype=jnp.int32)[:, None]
    columns = jnp.arange(length + 2 * HALF, dtype=jnp.int32)[None, :]
    offset = columns - rows
    picks = jnp.arange(TAPS, dtype=jnp.int32)[:, None, None]
    return jnp.sum(jnp.where(offset[None] == picks, taps[:, None, None], 0.0), axis=0)


def blur(volume, bands):
    band_x, square_y, square_z = bands
    padded = with_halo(volume.astype(jnp.bfloat16), (("grid", 0),), HALF).astype(volume.dtype)
    along_x = jnp.einsum("ip,pyz->iyz", band_x, padded, precision=lax.Precision.HIGHEST)
    along_y = jnp.einsum("jq,xqz->xjz", square_y, along_x, precision=lax.Precision.HIGHEST)
    return jnp.einsum("xyw,kw->xyk", along_y, square_z, precision=lax.Precision.HIGHEST)


def blur_narrowing(volume, taps, square_y, square_z):
    band_x = band_matrix(taps, volume.shape[0] - 2 * HALF)
    along_x = jnp.einsum("ip,pyz->iyz", band_x, volume, precision=lax.Precision.HIGHEST)
    along_y = jnp.einsum("jq,xqz->xjz", square_y, along_x, precision=lax.Precision.HIGHEST)
    return jnp.einsum("xyw,kw->xyk", along_y, square_z, precision=lax.Precision.HIGHEST)


def deblur(observed, halo_tiles, spread_taps):
    tiles = lax.axis_size("grid")
    me = lax.axis_index("grid")
    reach = ITERS * 2 * HALF
    cut = halo_tiles * CX - reach
    observed = observed[cut : observed.shape[0] - cut]
    width = observed.shape[0]
    cell = (me - halo_tiles) * CX + cut + jnp.arange(width, dtype=jnp.int32)
    inside = (cell >= 0) & (cell < tiles * CX)
    square_y = band_matrix(spread_taps[1], CY)[:, HALF : HALF + CY]
    square_z = band_matrix(spread_taps[2], CZ)[:, HALF : HALF + CZ]
    estimate = jnp.where(inside[:, None, None], observed, 0.0)
    for sweep in range(ITERS):
        low = 2 * HALF * sweep + HALF
        blurred = blur_narrowing(estimate, spread_taps[0], square_y, square_z)
        ratio = jnp.where(
            inside[low : width - low, None, None], observed[low : width - low] / blurred, 0.0
        )
        estimate = estimate[2 * HALF : estimate.shape[0] - 2 * HALF] * blur_narrowing(
            ratio, spread_taps[0], square_y, square_z
        )
    return estimate


def band_of(taps_ref, axis, rows, cols):
    offset = cols - rows + HALF
    band = jnp.zeros(offset.shape, jnp.float32)
    for tap in range(TAPS):
        band = jnp.where(offset == tap, taps_ref[axis, tap], band)
    return band


def mirror(index, length):
    return jnp.where(index < length // 2, index, 3 * (length // 2) - 1 - index)


def deblur_kernel(taps_ref, obs_ref, out_ref, kx_ref, kz_ref):
    tiles = lax.axis_size("grid")
    me = lax.axis_index("grid")
    planes, width, depth = obs_ref.shape
    shape_x = kx_ref.shape
    kx_ref[...] = band_of(
        taps_ref, 0, lax.broadcasted_iota(jnp.int32, shape_x, 0) + HALF, lax.broadcasted_iota(jnp.int32, shape_x, 1)
    )
    shape_z = kz_ref.shape
    kz_ref[...] = band_of(
        taps_ref,
        2,
        mirror(lax.broadcasted_iota(jnp.int32, shape_z, 1), depth),
        mirror(lax.broadcasted_iota(jnp.int32, shape_z, 0), depth),
    )
    halo_tiles = (width - CX) // (2 * CX)
    highest = lax.Precision.HIGHEST

    def inside(low, size):
        cell = (me - halo_tiles) * CX + low + lax.broadcasted_iota(jnp.int32, (size, depth), 0)
        return (cell >= 0) & (cell < tiles * CX)

    lanes = planes * depth

    def blur(volume):
        size_in = volume.shape[0]
        size_out = size_in - 2 * HALF
        band = kx_ref[0:size_out, 0:size_in]
        along_x = jnp.dot(band, volume, precision=highest, preferred_element_type=jnp.float32)
        along_y = []
        for y in range(planes):
            total = None
            for q in range(planes):
                term = taps_ref[1, q - y + HALF] * along_x[:, q * depth : (q + 1) * depth]
                total = term if total is None else total + term
            along_y.append(total)
        joined = jnp.concatenate(along_y, axis=0)
        along_z = jnp.dot(joined, kz_ref[...], precision=highest, preferred_element_type=jnp.float32)
        return jnp.concatenate([along_z[y * size_out : (y + 1) * size_out] for y in range(planes)], axis=1)

    def inside_wide(low, size):
        cell = (me - halo_tiles) * CX + low + lax.broadcasted_iota(jnp.int32, (size, lanes), 0)
        return (cell >= 0) & (cell < tiles * CX)

    observed = jnp.concatenate([obs_ref[y] for y in range(planes)], axis=1)
    estimate = jnp.where(inside_wide(0, width), observed, 0.0)
    for sweep in range(ITERS):
        low = 2 * HALF * sweep + HALF
        blurred = blur(estimate)
        size = blurred.shape[0]
        ratio = jnp.where(inside_wide(low, size), observed[low : low + size] / blurred, 0.0)
        spread = blur(ratio)
        estimate = estimate[2 * HALF : 2 * HALF + spread.shape[0]] * spread
    for y in range(planes):
        out_ref[y] = estimate[:, y * depth : (y + 1) * depth]


def deblur_tile(observed, spread_taps):
    planes, width, depth = observed.shape
    vmem = pl.BlockSpec(memory_space=pltpu.VMEM)
    return pl.pallas_call(
        deblur_kernel,
        out_shape=jax.ShapeDtypeStruct((planes, CX, depth), jnp.float32),
        in_specs=[pl.BlockSpec(memory_space=pltpu.SMEM), vmem],
        out_specs=vmem,
        scratch_shapes=[
            pltpu.VMEM((width - 2 * HALF, width), jnp.float32),
            pltpu.VMEM((depth, depth), jnp.float32),
        ],
    )(spread_taps, observed)


def per_device(spectra, lag_samples, slowness, spread_taps):
    groups = lax.axis_size("sta")
    own_count = FREQS // groups
    first_bin = lax.axis_index("sta") * own_count
    block = spectra.shape[2]
    spec_send = spectra.reshape(groups, own_count, 2, block).transpose(0, 2, 1, 3)
    halo_tiles = -(-(ITERS * 2 * HALF) // CX)
    summed = beam_power(spec_send, lag_samples, slowness[0], halo_tiles)
    observed = summed / (FREQS * STATIONS) + BACKGROUND
    slots = observed.shape[0]
    observed = observed.reshape(slots, CY, CX, CZ)
    observed = jnp.concatenate([observed[:, :, : CX // 2], observed[:, :, CX // 2 :][:, :, ::-1]], axis=2)
    planes = observed.transpose(1, 0, 2, 3).reshape(CY, slots * CX, CZ)
    estimate = deblur_tile(planes, spread_taps)
    both = jnp.stack([observed[halo_tiles], estimate])
    both = jnp.concatenate([both[..., : CZ // 2], both[..., CZ // 2 :][..., ::-1]], axis=-1).transpose(0, 2, 1, 3)
    stacked, estimate = both[0], both[1]
    return (stacked[None], estimate[None])


def solution(mesh):
    placed = (P(None, None, "sta"), P("grid", "sta"), P("grid", None, "sta"), P())
    return jax.shard_map(
        per_device,
        mesh=mesh,
        in_specs=placed,
        out_specs=(P("grid", None, None, None), P("grid", None, None, None)),
        check_vma=False,
    )
```

```python
import math

import jax
import jax.numpy as jnp
from jax import lax
from jax.sharding import PartitionSpec as P
from jax.experimental import pallas as pl
from jax.experimental.pallas import tpu as pltpu

STATIONS = 6144
FREQS = 64
F0 = 600
NT = 6000
TAPS = 17
HALF = 8
ITERS = 4
CX = 32
CY = 8
CZ = 128


TWO_PI = 2.0 * math.pi
BACKGROUND = 0.05


def with_halo(array, sides, width):
    for axis, dim in sides:
        size, length = (lax.axis_size(axis), array.shape[dim])
        up = [(i, (i + 1) % size) for i in range(size - 1)]
        down = [(j, i) for i, j in up]
        last = lax.slice_in_dim(array, length - width, length, axis=dim)
        leading = lax.slice_in_dim(array, 0, width, axis=dim)
        before = lax.ppermute(last, axis, up)
        after = lax.ppermute(leading, axis, down)
        array = jnp.concatenate([before, array, after], axis=dim)
    return array


def align_rows(spectra, lag_row):
    bins = F0 + jnp.arange(FREQS, dtype=jnp.int32)
    cycles = bins[:, None] * lag_row[None, :] % NT
    turned = cycles.astype(jnp.float32) * (TWO_PI / NT)
    cosine = jnp.cos(turned)
    sine = jnp.sin(turned)
    real_in = spectra[:, 0, :].astype(jnp.float32)
    imag_in = spectra[:, 1, :].astype(jnp.float32)
    real_out = real_in * cosine + imag_in * sine
    imag_out = imag_in * cosine - real_in * sine
    return jnp.stack([real_out, imag_out], axis=1).astype(jnp.bfloat16)


def beam_freq(freq, aligned_row, slow_rows):
    omega = (F0 + freq).astype(jnp.float32) * (TWO_PI / NT)
    slow = slow_rows.astype(jnp.float32)
    x_coord = jnp.arange(CX, dtype=jnp.float32) - (CX - 1) / 2.0
    y_coord = jnp.arange(CY, dtype=jnp.float32) - (CY - 1) / 2.0
    z_coord = jnp.arange(CZ, dtype=jnp.float32) - (CZ - 1) / 2.0
    phase_x = (omega * slow[0])[None, :] * x_coord[:, None]
    phase_y = (omega * slow[1])[None, :] * y_coord[:, None]
    phase = phase_x[:, None, :] + phase_y[None, :, :]
    cosine = jnp.cos(phase)
    sine = jnp.sin(phase)
    real_in = aligned_row[0].astype(jnp.float32)[None, None, :]
    imag_in = aligned_row[1].astype(jnp.float32)[None, None, :]
    front_real = (real_in * cosine + imag_in * sine).astype(jnp.bfloat16).reshape(CX * CY, -1)
    front_imag = (imag_in * cosine - real_in * sine).astype(jnp.bfloat16).reshape(CX * CY, -1)
    left_side = jnp.concatenate([front_real, front_imag], axis=1)
    phase_z = (omega * slow[2])[:, None] * z_coord[None, :]
    depth_real = jnp.cos(phase_z).astype(jnp.bfloat16)
    depth_imag = jnp.sin(phase_z).astype(jnp.bfloat16)
    upper_rows = jnp.concatenate([depth_real, -depth_imag], axis=1)
    lower_rows = jnp.concatenate([depth_imag, depth_real], axis=1)
    right_side = jnp.concatenate([upper_rows, lower_rows], axis=0)
    return jnp.dot(left_side, right_side, preferred_element_type=jnp.float32)


CHUNK = 768


def exp_neg(angle):
    return jnp.cos(angle), -jnp.sin(angle)


def enter_barrier(count, reach):
    me = lax.axis_index("sta")
    tile = lax.axis_index("grid")
    tiles = lax.axis_size("grid")
    mesh_ids = pl.DeviceIdType.MESH
    barrier = pltpu.get_barrier_semaphore()
    for shift in range(1, count):
        pl.semaphore_signal(barrier, inc=1, device_id=(tile, lax.rem(me + shift, count)), device_id_type=mesh_ids)
    neighbours = jnp.int32(0)
    for k in range(-reach, reach + 1):
        if k == 0:
            continue
        there = (tile + k >= 0) & (tile + k < tiles)
        neighbours = neighbours + there.astype(jnp.int32)

        @pl.when(there)
        def _():
            pl.semaphore_signal(barrier, inc=1, device_id=(tile + k, me), device_id_type=mesh_ids)

    pl.semaphore_wait(barrier, count - 1 + neighbours)


def exchange_inputs(spec_ref, lag_ref, slow_ref, spec_in, lag_in, slow_in, local_sem, send_sem, recv_sem, then, reach):
    count = spec_in.shape[0]
    me = lax.axis_index("sta")
    tile = lax.axis_index("grid")
    mesh_ids = pl.DeviceIdType.MESH
    enter_barrier(count, reach)
    pairs = ((spec_ref, spec_in), (lag_ref, lag_in), (slow_ref, slow_in))
    local = []
    for kind, (source, target) in enumerate(pairs):
        own = source.at[me] if kind == 0 else source
        copy = pltpu.make_async_copy(own, target.at[me], local_sem.at[kind])
        copy.start()
        local.append(copy)
    sends = []
    for shift in range(1, count):
        peer = lax.rem(me + shift, count)
        for kind, (source, target) in enumerate(pairs):
            part = source.at[peer] if kind == 0 else source
            copy = pltpu.make_async_remote_copy(
                src_ref=part,
                dst_ref=target.at[me],
                send_sem=send_sem.at[kind, shift],
                recv_sem=recv_sem.at[kind, me],
                device_id=(tile, peer),
                device_id_type=mesh_ids,
            )
            copy.start()
            sends.append(copy)
    then()
    for copy in local:
        copy.wait()
    for copy in sends:
        copy.wait_send()
    for shift in range(1, count):
        source_id = lax.rem(me + count - shift, count)
        for kind, (source, target) in enumerate(pairs):
            part = source.at[source_id] if kind == 0 else source
            pltpu.make_async_remote_copy(
                src_ref=part,
                dst_ref=target.at[source_id],
                send_sem=send_sem.at[kind, shift],
                recv_sem=recv_sem.at[kind, source_id],
                device_id=(tile, source_id),
                device_id_type=mesh_ids,
            ).wait_recv()


def align_block(spec, lag, slow, source, real_ref, imag_ref, turn_ref):
    bins, block = spec.shape[1], spec.shape[2]
    first_bin = lax.axis_index("sta") * bins
    bin_rows = (F0 + first_bin + lax.broadcasted_iota(jnp.int32, (bins, block), 0)).astype(jnp.float32)
    cols = pl.ds(pl.multiple_of(source * block, 128), block)
    product = bin_rows * lag.astype(jnp.float32)
    whole = jnp.floor(product * (1.0 / NT))
    left = product - whole * NT
    left = jnp.where(left < 0.0, left + NT, left)
    left = jnp.where(left >= NT, left - NT, left)
    turned = left * (TWO_PI / NT)
    cosine = jnp.cos(turned)
    sine = jnp.sin(turned)
    real_in = spec[0].astype(jnp.float32)
    imag_in = spec[1].astype(jnp.float32)
    real_ref[:, cols] = (real_in * cosine + imag_in * sine).astype(jnp.bfloat16).astype(jnp.float32)
    imag_ref[:, cols] = (imag_in * cosine - real_in * sine).astype(jnp.bfloat16).astype(jnp.float32)
    turn_ref[:, cols] = slow.astype(jnp.float32)


def complex_times(left, right):
    return left[0] * right[0] - left[1] * right[1], left[0] * right[1] + left[1] * right[0]


def factor_rows(turn_x, turn_y, turn_z, rows8, rows16):
    return (
        exp_neg(turn_x * (rows8 - 3.5)),
        exp_neg(turn_x * (8.0 * (rows8 - 1.5))),
        exp_neg(turn_y * (rows8 - 3.5)),
        exp_neg(turn_z * (rows16 - 7.5)),
        exp_neg(turn_z * (16.0 * (rows8 - 3.5))),
    )


def beam_kernel(spec_ref, lag_ref, slow_ref, out_ref, spec_in, lag_in, slow_in, local_sem, send_sem, recv_sem,
                real_ref, imag_ref, turn_ref, acc_ref, left_ref, right_ref, power_ref, pieces, send_rs, recv_rs,
                send_ag, recv_ag, share_sem):
    count, bins, block = spec_in.shape[0], spec_in.shape[2], spec_in.shape[3]
    me = lax.axis_index("sta")
    first_bin = me * bins
    width = CHUNK
    per_block = block // width
    half_z = CZ // 2
    rows8 = lax.broadcasted_iota(jnp.int32, (8, width), 0).astype(jnp.float32)
    rows16 = lax.broadcasted_iota(jnp.int32, (16, width), 0).astype(jnp.float32)
    omega0 = (F0 + first_bin).astype(jnp.float32) * (TWO_PI / NT)
    step = TWO_PI / NT
    acc_ref[...] = jnp.zeros_like(acc_ref)

    def per_chunk(k, carry):
        source = lax.rem(me + k // per_block, count)
        cols = pl.ds(pl.multiple_of(source * block + lax.rem(k, per_block) * width, 128), width)
        slow_x = turn_ref[0:1, cols]
        slow_y = turn_ref[1:2, cols]
        slow_z = turn_ref[2:3, cols]
        start = factor_rows(omega0 * slow_x, omega0 * slow_y, omega0 * slow_z, rows8, rows16)
        ratio = factor_rows(step * slow_x, step * slow_y, step * slow_z, rows8, rows16)

        def per_bin(f, state):
            (a_r, a_i), (b_r, b_i), (y_r, y_i), (c_r, c_i), (d_r, d_i) = state
            real_in = real_ref[pl.ds(f, 1), cols]
            imag_in = imag_ref[pl.ds(f, 1), cols]
            q_r = real_in * y_r - imag_in * y_i
            q_i = real_in * y_i + imag_in * y_r
            near = [complex_times((b_r[m : m + 1], b_i[m : m + 1]), (a_r, a_i)) for m in range(CX // 16)]
            cells = CX * CY
            for y in range(CY):
                qq_r, qq_i = q_r[y : y + 1], q_i[y : y + 1]
                lo_r, lo_i, hi_r, hi_i = [], [], [], []
                for x_r, x_i in near:
                    t1, t2 = qq_r * x_r, qq_i * x_i
                    t3, t4 = qq_r * x_i, qq_i * x_r
                    lo_r.append(t1 - t2)
                    lo_i.append(t3 + t4)
                    hi_r.append(t1 + t2)
                    hi_i.append(t4 - t3)
                row = y * CX
                half = CX // 2
                left_ref[row : row + half, :] = jnp.concatenate(lo_r, axis=0).astype(jnp.bfloat16)
                left_ref[row + half : row + CX, :] = jnp.concatenate(hi_r, axis=0).astype(jnp.bfloat16)
                left_ref[cells + row : cells + row + half, :] = jnp.concatenate(lo_i, axis=0).astype(jnp.bfloat16)
                left_ref[cells + row + half : cells + row + CX, :] = jnp.concatenate(hi_i, axis=0).astype(jnp.bfloat16)
            for m in range(half_z // 16):
                z_r, z_i = complex_times((d_r[m : m + 1], d_i[m : m + 1]), (c_r, c_i))
                row = 16 * m
                right_ref[row : row + 16, :] = z_r.astype(jnp.bfloat16)
                right_ref[half_z + row : half_z + row + 16, :] = z_i.astype(jnp.bfloat16)
            acc_ref[f] += lax.dot_general(
                left_ref[...], right_ref[...], (((1,), (1,)), ((), ())), preferred_element_type=jnp.float32
            )
            return tuple(complex_times(now, turn) for now, turn in zip(state, ratio))

        lax.fori_loop(0, bins, per_bin, start)
        return carry

    def own_block():
        align_block(spec_ref[me], lag_ref[...], slow_ref[...], me, real_ref, imag_ref, turn_ref)
        lax.fori_loop(0, per_block, per_chunk, 0)

    exchange_inputs(
        spec_ref, lag_ref, slow_ref, spec_in, lag_in, slow_in, local_sem, send_sem, recv_sem, own_block, out_ref.shape[0] // 2
    )

    def align_other(shift, carry):
        source = lax.rem(me + shift, count)
        align_block(spec_in[source], lag_in[source], slow_in[source], source, real_ref, imag_ref, turn_ref)
        return carry

    lax.fori_loop(1, count, align_other, 0)
    lax.fori_loop(per_block, count * per_block, per_chunk, 0)
    cells = CX * CY
    low = jnp.zeros((cells, half_z), jnp.float32)
    high = jnp.zeros((cells, half_z), jnp.float32)
    for f in range(bins):
        sums = acc_ref[f]
        u, w = sums[:cells, :half_z], sums[:cells, half_z:]
        x, v = sums[cells:, :half_z], sums[cells:, half_z:]
        low = low + ((u - v) * (u - v) + (w + x) * (w + x))
        high = high + ((u + v) * (u + v) + (x - w) * (x - w))
    power_ref[:, :half_z] = low
    power_ref[:, half_z:] = high
    share_kernel(power_ref, out_ref, pieces, send_rs, recv_rs, send_ag, recv_ag, share_sem)


def beam_power(spec_send, lag_row, slow_rows, reach):
    count = spec_send.shape[0]
    slots = 2 * reach + 1
    cells = CX * CY
    bins, block = spec_send.shape[2], spec_send.shape[3]
    width = CHUNK
    stations = count * block
    vmem = pl.BlockSpec(memory_space=pltpu.VMEM)
    return pl.pallas_call(
        beam_kernel,
        out_shape=jax.ShapeDtypeStruct((slots, cells, CZ), jnp.float32),
        in_specs=[vmem, vmem, vmem],
        out_specs=vmem,
        scratch_shapes=[
            pltpu.VMEM((count,) + spec_send.shape[1:], jnp.bfloat16),
            pltpu.VMEM((count,) + lag_row.shape, jnp.int32),
            pltpu.VMEM((count,) + slow_rows.shape, jnp.bfloat16),
            pltpu.SemaphoreType.DMA((3,)),
            pltpu.SemaphoreType.DMA((3, count)),
            pltpu.SemaphoreType.DMA((3, count)),
            pltpu.VMEM((bins, stations), jnp.float32),
            pltpu.VMEM((bins, stations), jnp.float32),
            pltpu.VMEM((slow_rows.shape[0], stations), jnp.float32),
            pltpu.VMEM((bins, 2 * CX * CY, CZ), jnp.float32),
            pltpu.VMEM((2 * CX * CY, width), jnp.bfloat16),
            pltpu.VMEM((CZ, width), jnp.bfloat16),
            pltpu.VMEM((cells, CZ), jnp.float32),
            pltpu.VMEM((count, cells // count, CZ), jnp.float32),
            pltpu.SemaphoreType.DMA((count,)),
            pltpu.SemaphoreType.DMA((count,)),
            pltpu.SemaphoreType.DMA((slots, count)),
            pltpu.SemaphoreType.DMA((slots, count)),
            pltpu.SemaphoreType.DMA((1,)),
        ],
        compiler_params=pltpu.CompilerParams(collective_id=1, has_side_effects=True),
    )(spec_send, lag_row, slow_rows)


def share_kernel(part_ref, out_ref, pieces, send_rs, recv_rs, send_ag, recv_ag, local_sem):
    count = pieces.shape[0]
    slots = out_ref.shape[0]
    reach = slots // 2
    rows = pieces.shape[1]
    me = lax.axis_index("sta")
    tile = lax.axis_index("grid")
    tiles = lax.axis_size("grid")
    mesh_ids = pl.DeviceIdType.MESH
    own = pltpu.make_async_copy(part_ref.at[pl.ds(pl.multiple_of(me * rows, 8), rows)], pieces.at[me], local_sem.at[0])
    own.start()
    sends = []
    for shift in range(1, count):
        peer = lax.rem(me + shift, count)
        copy = pltpu.make_async_remote_copy(
            src_ref=part_ref.at[pl.ds(pl.multiple_of(peer * rows, 8), rows)],
            dst_ref=pieces.at[me],
            send_sem=send_rs.at[shift],
            recv_sem=recv_rs.at[me],
            device_id=(tile, peer),
            device_id_type=mesh_ids,
        )
        copy.start()
        sends.append(copy)
    own.wait()
    for copy in sends:
        copy.wait_send()
    for shift in range(1, count):
        source = lax.rem(me + count - shift, count)
        pltpu.make_async_remote_copy(
            src_ref=pieces.at[source],
            dst_ref=pieces.at[source],
            send_sem=send_rs.at[shift],
            recv_sem=recv_rs.at[source],
            device_id=(tile, source),
            device_id_type=mesh_ids,
        ).wait_recv()
    total = pieces[0]
    for source in range(1, count):
        total = total + pieces[source]
    mine = pl.ds(pl.multiple_of(me * rows, 8), rows)
    out_ref[reach, mine] = total
    block = out_ref.at[reach, mine]

    def gather_copy(k, peer, slot):
        return pltpu.make_async_remote_copy(
            src_ref=block,
            dst_ref=out_ref.at[slot, mine],
            send_sem=send_ag.at[slot, peer],
            recv_sem=recv_ag.at[slot, me],
            device_id=(tile + k, peer),
            device_id_type=mesh_ids,
        )

    peers = []
    for shift in range(1, count):
        copy = gather_copy(0, lax.rem(me + shift, count), reach)
        copy.start()
        peers.append(copy)
    for k in range(-reach, reach + 1):
        if k == 0:
            continue

        @pl.when(jnp.logical_not((tile + k >= 0) & (tile + k < tiles)))
        def _():
            out_ref[reach + k] = jnp.zeros(out_ref.shape[1:], out_ref.dtype)

    for copy in peers:
        copy.wait_send()
    for shift in range(1, count):
        source = lax.rem(me + count - shift, count)
        pltpu.make_async_remote_copy(
            src_ref=block,
            dst_ref=out_ref.at[reach, pl.ds(pl.multiple_of(source * rows, 8), rows)],
            send_sem=send_ag.at[reach, source],
            recv_sem=recv_ag.at[reach, source],
            device_id=(tile, source),
            device_id_type=mesh_ids,
        ).wait_recv()

    def halo_copy(k):
        return pltpu.make_async_remote_copy(
            src_ref=out_ref.at[reach],
            dst_ref=out_ref.at[reach - k],
            send_sem=send_ag.at[reach - k, me],
            recv_sem=recv_ag.at[reach - k, me],
            device_id=(tile + k, me),
            device_id_type=mesh_ids,
        )

    for k in range(-reach, reach + 1):
        if k == 0:
            continue

        @pl.when((tile + k >= 0) & (tile + k < tiles))
        def _():
            halo_copy(k).start()

    for k in range(-reach, reach + 1):
        if k == 0:
            continue

        @pl.when((tile + k >= 0) & (tile + k < tiles))
        def _():
            halo_copy(k).wait_send()
            pltpu.make_async_remote_copy(
                src_ref=out_ref.at[reach],
                dst_ref=out_ref.at[reach + k],
                send_sem=send_ag.at[reach + k, me],
                recv_sem=recv_ag.at[reach + k, me],
                device_id=(tile + k, me),
                device_id_type=mesh_ids,
            ).wait_recv()


def share_power(part, reach):
    count = lax.axis_size("sta")
    rows = part.shape[0] // count
    slots = 2 * reach + 1
    return pl.pallas_call(
        share_kernel,
        out_shape=jax.ShapeDtypeStruct((slots,) + part.shape, jnp.float32),
        in_specs=[pl.BlockSpec(memory_space=pltpu.VMEM)],
        out_specs=pl.BlockSpec(memory_space=pltpu.VMEM),
        scratch_shapes=[
            pltpu.VMEM((count, rows, part.shape[1]), jnp.float32),
            pltpu.SemaphoreType.DMA((count,)),
            pltpu.SemaphoreType.DMA((count,)),
            pltpu.SemaphoreType.DMA((slots, count)),
            pltpu.SemaphoreType.DMA((slots, count)),
            pltpu.SemaphoreType.DMA((1,)),
        ],
        compiler_params=pltpu.CompilerParams(collective_id=0, has_side_effects=True),
    )(part)


def freq_beams(freq_ids, aligned_rows, slow_rows):
    return lax.map(lambda pair: beam_freq(pair[0], pair[1], slow_rows), (freq_ids, aligned_rows))


def band_matrix(taps, length):
    rows = jnp.arange(length, dtype=jnp.int32)[:, None]
    columns = jnp.arange(length + 2 * HALF, dtype=jnp.int32)[None, :]
    offset = columns - rows
    picks = jnp.arange(TAPS, dtype=jnp.int32)[:, None, None]
    return jnp.sum(jnp.where(offset[None] == picks, taps[:, None, None], 0.0), axis=0)


def blur(volume, bands):
    band_x, square_y, square_z = bands
    padded = with_halo(volume.astype(jnp.bfloat16), (("grid", 0),), HALF).astype(volume.dtype)
    along_x = jnp.einsum("ip,pyz->iyz", band_x, padded, precision=lax.Precision.HIGHEST)
    along_y = jnp.einsum("jq,xqz->xjz", square_y, along_x, precision=lax.Precision.HIGHEST)
    return jnp.einsum("xyw,kw->xyk", along_y, square_z, precision=lax.Precision.HIGHEST)


def blur_narrowing(volume, taps, square_y, square_z):
    band_x = band_matrix(taps, volume.shape[0] - 2 * HALF)
    along_x = jnp.einsum("ip,pyz->iyz", band_x, volume, precision=lax.Precision.HIGHEST)
    along_y = jnp.einsum("jq,xqz->xjz", square_y, along_x, precision=lax.Precision.HIGHEST)
    return jnp.einsum("xyw,kw->xyk", along_y, square_z, precision=lax.Precision.HIGHEST)


def deblur(observed, halo_tiles, spread_taps):
    tiles = lax.axis_size("grid")
    me = lax.axis_index("grid")
    reach = ITERS * 2 * HALF
    cut = halo_tiles * CX - reach
    observed = observed[cut : observed.shape[0] - cut]
    width = observed.shape[0]
    cell = (me - halo_tiles) * CX + cut + jnp.arange(width, dtype=jnp.int32)
    inside = (cell >= 0) & (cell < tiles * CX)
    square_y = band_matrix(spread_taps[1], CY)[:, HALF : HALF + CY]
    square_z = band_matrix(spread_taps[2], CZ)[:, HALF : HALF + CZ]
    estimate = jnp.where(inside[:, None, None], observed, 0.0)
    for sweep in range(ITERS):
        low = 2 * HALF * sweep + HALF
        blurred = blur_narrowing(estimate, spread_taps[0], square_y, square_z)
        ratio = jnp.where(
            inside[low : width - low, None, None], observed[low : width - low] / blurred, 0.0
        )
        estimate = estimate[2 * HALF : estimate.shape[0] - 2 * HALF] * blur_narrowing(
            ratio, spread_taps[0], square_y, square_z
        )
    return estimate


def band_of(taps_ref, axis, rows, cols):
    offset = cols - rows + HALF
    band = jnp.zeros(offset.shape, jnp.float32)
    for tap in range(TAPS):
        band = jnp.where(offset == tap, taps_ref[axis, tap], band)
    return band


def mirror(index, length):
    return jnp.where(index < length // 2, index, 3 * (length // 2) - 1 - index)


def deblur_kernel(taps_ref, obs_ref, out_ref, kx_ref, kz_ref):
    tiles = lax.axis_size("grid")
    me = lax.axis_index("grid")
    planes, width, depth = obs_ref.shape
    shape_x = kx_ref.shape
    kx_ref[...] = band_of(
        taps_ref, 0, lax.broadcasted_iota(jnp.int32, shape_x, 0) + HALF, lax.broadcasted_iota(jnp.int32, shape_x, 1)
    )
    shape_z = kz_ref.shape
    kz_ref[...] = band_of(
        taps_ref,
        2,
        mirror(lax.broadcasted_iota(jnp.int32, shape_z, 1), depth),
        mirror(lax.broadcasted_iota(jnp.int32, shape_z, 0), depth),
    )
    halo_tiles = (width - CX) // (2 * CX)
    highest = lax.Precision.HIGHEST

    def inside(low, size):
        cell = (me - halo_tiles) * CX + low + lax.broadcasted_iota(jnp.int32, (size, depth), 0)
        return (cell >= 0) & (cell < tiles * CX)

    lanes = planes * depth

    def blur(volume):
        size_in = volume.shape[0]
        size_out = size_in - 2 * HALF
        band = kx_ref[0:size_out, 0:size_in]
        along_x = jnp.dot(band, volume, precision=highest, preferred_element_type=jnp.float32)
        along_y = []
        for y in range(planes):
            total = None
            for q in range(planes):
                term = taps_ref[1, q - y + HALF] * along_x[:, q * depth : (q + 1) * depth]
                total = term if total is None else total + term
            along_y.append(total)
        joined = jnp.concatenate(along_y, axis=0)
        along_z = jnp.dot(joined, kz_ref[...], precision=highest, preferred_element_type=jnp.float32)
        return jnp.concatenate([along_z[y * size_out : (y + 1) * size_out] for y in range(planes)], axis=1)

    def inside_wide(low, size):
        cell = (me - halo_tiles) * CX + low + lax.broadcasted_iota(jnp.int32, (size, lanes), 0)
        return (cell >= 0) & (cell < tiles * CX)

    observed = jnp.concatenate([obs_ref[y] for y in range(planes)], axis=1)
    estimate = jnp.where(inside_wide(0, width), observed, 0.0)
    for sweep in range(ITERS):
        low = 2 * HALF * sweep + HALF
        blurred = blur(estimate)
        size = blurred.shape[0]
        ratio = jnp.where(inside_wide(low, size), observed[low : low + size] / blurred, 0.0)
        spread = blur(ratio)
        estimate = estimate[2 * HALF : 2 * HALF + spread.shape[0]] * spread
    for y in range(planes):
        out_ref[y] = estimate[:, y * depth : (y + 1) * depth]


def deblur_tile(observed, spread_taps):
    planes, width, depth = observed.shape
    vmem = pl.BlockSpec(memory_space=pltpu.VMEM)
    return pl.pallas_call(
        deblur_kernel,
        out_shape=jax.ShapeDtypeStruct((planes, CX, depth), jnp.float32),
        in_specs=[pl.BlockSpec(memory_space=pltpu.SMEM), vmem],
        out_specs=vmem,
        scratch_shapes=[
            pltpu.VMEM((width - 2 * HALF, width), jnp.float32),
            pltpu.VMEM((depth, depth), jnp.float32),
        ],
    )(spread_taps, observed)


def per_device(spectra, lag_samples, slowness, spread_taps):
    groups = lax.axis_size("sta")
    own_count = FREQS // groups
    first_bin = lax.axis_index("sta") * own_count
    block = spectra.shape[2]
    spec_send = spectra.reshape(groups, own_count, 2, block).transpose(0, 2, 1, 3)
    halo_tiles = -(-(ITERS * 2 * HALF) // CX)
    summed = beam_power(spec_send, lag_samples, slowness[0], halo_tiles)
    observed = summed / (FREQS * STATIONS) + BACKGROUND
    slots = observed.shape[0]
    observed = observed.reshape(slots, CY, CX, CZ)
    observed = jnp.concatenate([observed[:, :, : CX // 2], observed[:, :, CX // 2 :][:, :, ::-1]], axis=2)
    planes = observed.transpose(1, 0, 2, 3).reshape(CY, slots * CX, CZ)
    estimate = deblur_tile(planes, spread_taps)
    both = jnp.stack([observed[halo_tiles], estimate])
    both = jnp.concatenate([both[..., : CZ // 2], both[..., CZ // 2 :][..., ::-1]], axis=-1).transpose(0, 2, 1, 3)
    stacked, estimate = both[0], both[1]
    return (stacked[None], estimate[None])


def solution(mesh):
    placed = (P(None, None, "sta"), P("grid", "sta"), P("grid", None, "sta"), P())
    return jax.shard_map(
        per_device,
        mesh=mesh,
        in_specs=placed,
        out_specs=(P("grid", None, None, None), P("grid", None, None, None)),
        check_vma=False,
    )
```

```python
import math

import jax
import jax.numpy as jnp
from jax import lax
from jax.sharding import PartitionSpec as P
from jax.experimental import pallas as pl
from jax.experimental.pallas import tpu as pltpu

STATIONS = 6144
FREQS = 64
F0 = 600
NT = 6000
TAPS = 17
HALF = 8
ITERS = 4
CX = 32
CY = 8
CZ = 128


TWO_PI = 2.0 * math.pi
BACKGROUND = 0.05


def with_halo(array, sides, width):
    for axis, dim in sides:
        size, length = (lax.axis_size(axis), array.shape[dim])
        up = [(i, (i + 1) % size) for i in range(size - 1)]
        down = [(j, i) for i, j in up]
        last = lax.slice_in_dim(array, length - width, length, axis=dim)
        leading = lax.slice_in_dim(array, 0, width, axis=dim)
        before = lax.ppermute(last, axis, up)
        after = lax.ppermute(leading, axis, down)
        array = jnp.concatenate([before, array, after], axis=dim)
    return array


def align_rows(spectra, lag_row):
    bins = F0 + jnp.arange(FREQS, dtype=jnp.int32)
    cycles = bins[:, None] * lag_row[None, :] % NT
    turned = cycles.astype(jnp.float32) * (TWO_PI / NT)
    cosine = jnp.cos(turned)
    sine = jnp.sin(turned)
    real_in = spectra[:, 0, :].astype(jnp.float32)
    imag_in = spectra[:, 1, :].astype(jnp.float32)
    real_out = real_in * cosine + imag_in * sine
    imag_out = imag_in * cosine - real_in * sine
    return jnp.stack([real_out, imag_out], axis=1).astype(jnp.bfloat16)


def beam_freq(freq, aligned_row, slow_rows):
    omega = (F0 + freq).astype(jnp.float32) * (TWO_PI / NT)
    slow = slow_rows.astype(jnp.float32)
    x_coord = jnp.arange(CX, dtype=jnp.float32) - (CX - 1) / 2.0
    y_coord = jnp.arange(CY, dtype=jnp.float32) - (CY - 1) / 2.0
    z_coord = jnp.arange(CZ, dtype=jnp.float32) - (CZ - 1) / 2.0
    phase_x = (omega * slow[0])[None, :] * x_coord[:, None]
    phase_y = (omega * slow[1])[None, :] * y_coord[:, None]
    phase = phase_x[:, None, :] + phase_y[None, :, :]
    cosine = jnp.cos(phase)
    sine = jnp.sin(phase)
    real_in = aligned_row[0].astype(jnp.float32)[None, None, :]
    imag_in = aligned_row[1].astype(jnp.float32)[None, None, :]
    front_real = (real_in * cosine + imag_in * sine).astype(jnp.bfloat16).reshape(CX * CY, -1)
    front_imag = (imag_in * cosine - real_in * sine).astype(jnp.bfloat16).reshape(CX * CY, -1)
    left_side = jnp.concatenate([front_real, front_imag], axis=1)
    phase_z = (omega * slow[2])[:, None] * z_coord[None, :]
    depth_real = jnp.cos(phase_z).astype(jnp.bfloat16)
    depth_imag = jnp.sin(phase_z).astype(jnp.bfloat16)
    upper_rows = jnp.concatenate([depth_real, -depth_imag], axis=1)
    lower_rows = jnp.concatenate([depth_imag, depth_real], axis=1)
    right_side = jnp.concatenate([upper_rows, lower_rows], axis=0)
    return jnp.dot(left_side, right_side, preferred_element_type=jnp.float32)


CHUNK = 768


def exp_neg(angle):
    return jnp.cos(angle), -jnp.sin(angle)


def enter_barrier(count, reach):
    me = lax.axis_index("sta")
    tile = lax.axis_index("grid")
    tiles = lax.axis_size("grid")
    mesh_ids = pl.DeviceIdType.MESH
    barrier = pltpu.get_barrier_semaphore()
    for shift in range(1, count):
        pl.semaphore_signal(barrier, inc=1, device_id=(tile, lax.rem(me + shift, count)), device_id_type=mesh_ids)
    neighbours = jnp.int32(0)
    for k in range(-reach, reach + 1):
        if k == 0:
            continue
        there = (tile + k >= 0) & (tile + k < tiles)
        neighbours = neighbours + there.astype(jnp.int32)

        @pl.when(there)
        def _():
            pl.semaphore_signal(barrier, inc=1, device_id=(tile + k, me), device_id_type=mesh_ids)

    pl.semaphore_wait(barrier, count - 1 + neighbours)


def exchange_inputs(spec_ref, lag_ref, slow_ref, spec_in, lag_in, slow_in, local_sem, send_sem, recv_sem, then, reach):
    count = spec_in.shape[0]
    me = lax.axis_index("sta")
    tile = lax.axis_index("grid")
    mesh_ids = pl.DeviceIdType.MESH
    enter_barrier(count, reach)
    pairs = ((spec_ref, spec_in), (lag_ref, lag_in), (slow_ref, slow_in))
    local = []
    for kind, (source, target) in enumerate(pairs):
        own = source.at[me] if kind == 0 else source
        copy = pltpu.make_async_copy(own, target.at[me], local_sem.at[kind])
        copy.start()
        local.append(copy)
    sends = []
    for shift in range(1, count):
        peer = lax.rem(me + shift, count)
        for kind, (source, target) in enumerate(pairs):
            part = source.at[peer] if kind == 0 else source
            copy = pltpu.make_async_remote_copy(
                src_ref=part,
                dst_ref=target.at[me],
                send_sem=send_sem.at[kind, shift],
                recv_sem=recv_sem.at[kind, me],
                device_id=(tile, peer),
                device_id_type=mesh_ids,
            )
            copy.start()
            sends.append(copy)
    then()
    for copy in local:
        copy.wait()
    for copy in sends:
        copy.wait_send()
    for shift in range(1, count):
        source_id = lax.rem(me + count - shift, count)
        for kind, (source, target) in enumerate(pairs):
            part = source.at[source_id] if kind == 0 else source
            pltpu.make_async_remote_copy(
                src_ref=part,
                dst_ref=target.at[source_id],
                send_sem=send_sem.at[kind, shift],
                recv_sem=recv_sem.at[kind, source_id],
                device_id=(tile, source_id),
                device_id_type=mesh_ids,
            ).wait_recv()


def align_block(spec, lag, slow, source, real_ref, imag_ref, turn_ref):
    bins, block = spec.shape[1], spec.shape[2]
    first_bin = lax.axis_index("sta") * bins
    bin_rows = (F0 + first_bin + lax.broadcasted_iota(jnp.int32, (bins, block), 0)).astype(jnp.float32)
    cols = pl.ds(pl.multiple_of(source * block, 128), block)
    product = bin_rows * lag.astype(jnp.float32)
    whole = jnp.floor(product * (1.0 / NT))
    left = product - whole * NT
    left = jnp.where(left < 0.0, left + NT, left)
    left = jnp.where(left >= NT, left - NT, left)
    turned = left * (TWO_PI / NT)
    cosine = jnp.cos(turned)
    sine = jnp.sin(turned)
    real_in = spec[0].astype(jnp.float32)
    imag_in = spec[1].astype(jnp.float32)
    real_ref[:, cols] = (real_in * cosine + imag_in * sine).astype(jnp.bfloat16).astype(jnp.float32)
    imag_ref[:, cols] = (imag_in * cosine - real_in * sine).astype(jnp.bfloat16).astype(jnp.float32)
    turn_ref[:, cols] = slow.astype(jnp.float32)


def complex_times(left, right):
    return left[0] * right[0] - left[1] * right[1], left[0] * right[1] + left[1] * right[0]


def factor_rows(turn_x, turn_y, turn_z, rows8, rows16):
    return (
        exp_neg(turn_x * (rows8 - 3.5)),
        exp_neg(turn_x * (8.0 * (rows8 - 1.5))),
        exp_neg(turn_y * (rows8 - 3.5)),
        exp_neg(turn_z * (rows16 - 7.5)),
        exp_neg(turn_z * (16.0 * (rows8 - 3.5))),
    )


def beam_kernel(spec_ref, lag_ref, slow_ref, out_ref, spec_in, lag_in, slow_in, local_sem, send_sem, recv_sem,
                real_ref, imag_ref, turn_ref, acc_ref, left_ref, right_ref, power_ref, pieces, send_rs, recv_rs,
                send_ag, recv_ag, share_sem):
    count, bins, block = spec_in.shape[0], spec_in.shape[2], spec_in.shape[3]
    me = lax.axis_index("sta")
    first_bin = me * bins
    width = CHUNK
    per_block = block // width
    half_z = CZ // 2
    rows8 = lax.broadcasted_iota(jnp.int32, (8, width), 0).astype(jnp.float32)
    rows16 = lax.broadcasted_iota(jnp.int32, (16, width), 0).astype(jnp.float32)
    omega0 = (F0 + first_bin).astype(jnp.float32) * (TWO_PI / NT)
    step = TWO_PI / NT
    acc_ref[...] = jnp.zeros_like(acc_ref)

    def per_chunk(k, carry):
        source = lax.rem(me + k // per_block, count)
        cols = pl.ds(pl.multiple_of(source * block + lax.rem(k, per_block) * width, 128), width)
        slow_x = turn_ref[0:1, cols]
        slow_y = turn_ref[1:2, cols]
        slow_z = turn_ref[2:3, cols]
        start = factor_rows(omega0 * slow_x, omega0 * slow_y, omega0 * slow_z, rows8, rows16)
        ratio = factor_rows(step * slow_x, step * slow_y, step * slow_z, rows8, rows16)

        def per_bin(f, state):
            (a_r, a_i), (b_r, b_i), (y_r, y_i), (c_r, c_i), (d_r, d_i) = state
            real_in = real_ref[pl.ds(f, 1), cols]
            imag_in = imag_ref[pl.ds(f, 1), cols]
            q_r = real_in * y_r - imag_in * y_i
            q_i = real_in * y_i + imag_in * y_r
            near = [complex_times((b_r[m : m + 1], b_i[m : m + 1]), (a_r, a_i)) for m in range(CX // 16)]
            cells = CX * CY
            for y in range(CY):
                qq_r, qq_i = q_r[y : y + 1], q_i[y : y + 1]
                lo_r, lo_i, hi_r, hi_i = [], [], [], []
                for x_r, x_i in near:
                    t1, t2 = qq_r * x_r, qq_i * x_i
                    t3, t4 = qq_r * x_i, qq_i * x_r
                    lo_r.append(t1 - t2)
                    lo_i.append(t3 + t4)
                    hi_r.append(t1 + t2)
                    hi_i.append(t4 - t3)
                row = y * CX
                half = CX // 2
                left_ref[row : row + half, :] = jnp.concatenate(lo_r, axis=0).astype(jnp.bfloat16)
                left_ref[row + half : row + CX, :] = jnp.concatenate(hi_r, axis=0).astype(jnp.bfloat16)
                left_ref[cells + row : cells + row + half, :] = jnp.concatenate(lo_i, axis=0).astype(jnp.bfloat16)
                left_ref[cells + row + half : cells + row + CX, :] = jnp.concatenate(hi_i, axis=0).astype(jnp.bfloat16)
            for m in range(half_z // 16):
                z_r, z_i = complex_times((d_r[m : m + 1], d_i[m : m + 1]), (c_r, c_i))
                row = 16 * m
                right_ref[row : row + 16, :] = z_r.astype(jnp.bfloat16)
                right_ref[half_z + row : half_z + row + 16, :] = z_i.astype(jnp.bfloat16)
            acc_ref[f] += lax.dot_general(
                left_ref[...], right_ref[...], (((1,), (1,)), ((), ())), preferred_element_type=jnp.float32
            )
            return tuple(complex_times(now, turn) for now, turn in zip(state, ratio))

        lax.fori_loop(0, bins, per_bin, start, unroll=2)
        return carry

    def own_block():
        align_block(spec_ref[me], lag_ref[...], slow_ref[...], me, real_ref, imag_ref, turn_ref)
        lax.fori_loop(0, per_block, per_chunk, 0)

    exchange_inputs(
        spec_ref, lag_ref, slow_ref, spec_in, lag_in, slow_in, local_sem, send_sem, recv_sem, own_block, out_ref.shape[0] // 2
    )

    def align_other(shift, carry):
        source = lax.rem(me + shift, count)
        align_block(spec_in[source], lag_in[source], slow_in[source], source, real_ref, imag_ref, turn_ref)
        return carry

    lax.fori_loop(1, count, align_other, 0)
    lax.fori_loop(per_block, count * per_block, per_chunk, 0)
    cells = CX * CY
    low = jnp.zeros((cells, half_z), jnp.float32)
    high = jnp.zeros((cells, half_z), jnp.float32)
    for f in range(bins):
        sums = acc_ref[f]
        u, w = sums[:cells, :half_z], sums[:cells, half_z:]
        x, v = sums[cells:, :half_z], sums[cells:, half_z:]
        low = low + ((u - v) * (u - v) + (w + x) * (w + x))
        high = high + ((u + v) * (u + v) + (x - w) * (x - w))
    power_ref[:, :half_z] = low
    power_ref[:, half_z:] = high
    share_kernel(power_ref, out_ref, pieces, send_rs, recv_rs, send_ag, recv_ag, share_sem)


def beam_power(spec_send, lag_row, slow_rows, reach):
    count = spec_send.shape[0]
    slots = 2 * reach + 1
    cells = CX * CY
    bins, block = spec_send.shape[2], spec_send.shape[3]
    width = CHUNK
    stations = count * block
    vmem = pl.BlockSpec(memory_space=pltpu.VMEM)
    return pl.pallas_call(
        beam_kernel,
        out_shape=jax.ShapeDtypeStruct((slots, cells, CZ), jnp.float32),
        in_specs=[vmem, vmem, vmem],
        out_specs=vmem,
        scratch_shapes=[
            pltpu.VMEM((count,) + spec_send.shape[1:], jnp.bfloat16),
            pltpu.VMEM((count,) + lag_row.shape, jnp.int32),
            pltpu.VMEM((count,) + slow_rows.shape, jnp.bfloat16),
            pltpu.SemaphoreType.DMA((3,)),
            pltpu.SemaphoreType.DMA((3, count)),
            pltpu.SemaphoreType.DMA((3, count)),
            pltpu.VMEM((bins, stations), jnp.float32),
            pltpu.VMEM((bins, stations), jnp.float32),
            pltpu.VMEM((slow_rows.shape[0], stations), jnp.float32),
            pltpu.VMEM((bins, 2 * CX * CY, CZ), jnp.float32),
            pltpu.VMEM((2 * CX * CY, width), jnp.bfloat16),
            pltpu.VMEM((CZ, width), jnp.bfloat16),
            pltpu.VMEM((cells, CZ), jnp.float32),
            pltpu.VMEM((count, cells // count, CZ), jnp.float32),
            pltpu.SemaphoreType.DMA((count,)),
            pltpu.SemaphoreType.DMA((count,)),
            pltpu.SemaphoreType.DMA((slots, count)),
            pltpu.SemaphoreType.DMA((slots, count)),
            pltpu.SemaphoreType.DMA((1,)),
        ],
        compiler_params=pltpu.CompilerParams(collective_id=1, has_side_effects=True),
    )(spec_send, lag_row, slow_rows)


def share_kernel(part_ref, out_ref, pieces, send_rs, recv_rs, send_ag, recv_ag, local_sem):
    count = pieces.shape[0]
    slots = out_ref.shape[0]
    reach = slots // 2
    rows = pieces.shape[1]
    me = lax.axis_index("sta")
    tile = lax.axis_index("grid")
    tiles = lax.axis_size("grid")
    mesh_ids = pl.DeviceIdType.MESH
    own = pltpu.make_async_copy(part_ref.at[pl.ds(pl.multiple_of(me * rows, 8), rows)], pieces.at[me], local_sem.at[0])
    own.start()
    sends = []
    for shift in range(1, count):
        peer = lax.rem(me + shift, count)
        copy = pltpu.make_async_remote_copy(
            src_ref=part_ref.at[pl.ds(pl.multiple_of(peer * rows, 8), rows)],
            dst_ref=pieces.at[me],
            send_sem=send_rs.at[shift],
            recv_sem=recv_rs.at[me],
            device_id=(tile, peer),
            device_id_type=mesh_ids,
        )
        copy.start()
        sends.append(copy)
    own.wait()
    for copy in sends:
        copy.wait_send()
    for shift in range(1, count):
        source = lax.rem(me + count - shift, count)
        pltpu.make_async_remote_copy(
            src_ref=pieces.at[source],
            dst_ref=pieces.at[source],
            send_sem=send_rs.at[shift],
            recv_sem=recv_rs.at[source],
            device_id=(tile, source),
            device_id_type=mesh_ids,
        ).wait_recv()
    total = pieces[0]
    for source in range(1, count):
        total = total + pieces[source]
    mine = pl.ds(pl.multiple_of(me * rows, 8), rows)
    out_ref[reach, mine] = total
    block = out_ref.at[reach, mine]

    def gather_copy(k, peer, slot):
        return pltpu.make_async_remote_copy(
            src_ref=block,
            dst_ref=out_ref.at[slot, mine],
            send_sem=send_ag.at[slot, peer],
            recv_sem=recv_ag.at[slot, me],
            device_id=(tile + k, peer),
            device_id_type=mesh_ids,
        )

    peers = []
    for shift in range(1, count):
        copy = gather_copy(0, lax.rem(me + shift, count), reach)
        copy.start()
        peers.append(copy)
    for k in range(-reach, reach + 1):
        if k == 0:
            continue

        @pl.when(jnp.logical_not((tile + k >= 0) & (tile + k < tiles)))
        def _():
            out_ref[reach + k] = jnp.zeros(out_ref.shape[1:], out_ref.dtype)

    for copy in peers:
        copy.wait_send()
    for shift in range(1, count):
        source = lax.rem(me + count - shift, count)
        pltpu.make_async_remote_copy(
            src_ref=block,
            dst_ref=out_ref.at[reach, pl.ds(pl.multiple_of(source * rows, 8), rows)],
            send_sem=send_ag.at[reach, source],
            recv_sem=recv_ag.at[reach, source],
            device_id=(tile, source),
            device_id_type=mesh_ids,
        ).wait_recv()

    def halo_copy(k):
        return pltpu.make_async_remote_copy(
            src_ref=out_ref.at[reach],
            dst_ref=out_ref.at[reach - k],
            send_sem=send_ag.at[reach - k, me],
            recv_sem=recv_ag.at[reach - k, me],
            device_id=(tile + k, me),
            device_id_type=mesh_ids,
        )

    for k in range(-reach, reach + 1):
        if k == 0:
            continue

        @pl.when((tile + k >= 0) & (tile + k < tiles))
        def _():
            halo_copy(k).start()

    for k in range(-reach, reach + 1):
        if k == 0:
            continue

        @pl.when((tile + k >= 0) & (tile + k < tiles))
        def _():
            halo_copy(k).wait_send()
            pltpu.make_async_remote_copy(
                src_ref=out_ref.at[reach],
                dst_ref=out_ref.at[reach + k],
                send_sem=send_ag.at[reach + k, me],
                recv_sem=recv_ag.at[reach + k, me],
                device_id=(tile + k, me),
                device_id_type=mesh_ids,
            ).wait_recv()


def share_power(part, reach):
    count = lax.axis_size("sta")
    rows = part.shape[0] // count
    slots = 2 * reach + 1
    return pl.pallas_call(
        share_kernel,
        out_shape=jax.ShapeDtypeStruct((slots,) + part.shape, jnp.float32),
        in_specs=[pl.BlockSpec(memory_space=pltpu.VMEM)],
        out_specs=pl.BlockSpec(memory_space=pltpu.VMEM),
        scratch_shapes=[
            pltpu.VMEM((count, rows, part.shape[1]), jnp.float32),
            pltpu.SemaphoreType.DMA((count,)),
            pltpu.SemaphoreType.DMA((count,)),
            pltpu.SemaphoreType.DMA((slots, count)),
            pltpu.SemaphoreType.DMA((slots, count)),
            pltpu.SemaphoreType.DMA((1,)),
        ],
        compiler_params=pltpu.CompilerParams(collective_id=0, has_side_effects=True),
    )(part)


def freq_beams(freq_ids, aligned_rows, slow_rows):
    return lax.map(lambda pair: beam_freq(pair[0], pair[1], slow_rows), (freq_ids, aligned_rows))


def band_matrix(taps, length):
    rows = jnp.arange(length, dtype=jnp.int32)[:, None]
    columns = jnp.arange(length + 2 * HALF, dtype=jnp.int32)[None, :]
    offset = columns - rows
    picks = jnp.arange(TAPS, dtype=jnp.int32)[:, None, None]
    return jnp.sum(jnp.where(offset[None] == picks, taps[:, None, None], 0.0), axis=0)


def blur(volume, bands):
    band_x, square_y, square_z = bands
    padded = with_halo(volume.astype(jnp.bfloat16), (("grid", 0),), HALF).astype(volume.dtype)
    along_x = jnp.einsum("ip,pyz->iyz", band_x, padded, precision=lax.Precision.HIGHEST)
    along_y = jnp.einsum("jq,xqz->xjz", square_y, along_x, precision=lax.Precision.HIGHEST)
    return jnp.einsum("xyw,kw->xyk", along_y, square_z, precision=lax.Precision.HIGHEST)


def blur_narrowing(volume, taps, square_y, square_z):
    band_x = band_matrix(taps, volume.shape[0] - 2 * HALF)
    along_x = jnp.einsum("ip,pyz->iyz", band_x, volume, precision=lax.Precision.HIGHEST)
    along_y = jnp.einsum("jq,xqz->xjz", square_y, along_x, precision=lax.Precision.HIGHEST)
    return jnp.einsum("xyw,kw->xyk", along_y, square_z, precision=lax.Precision.HIGHEST)


def deblur(observed, halo_tiles, spread_taps):
    tiles = lax.axis_size("grid")
    me = lax.axis_index("grid")
    reach = ITERS * 2 * HALF
    cut = halo_tiles * CX - reach
    observed = observed[cut : observed.shape[0] - cut]
    width = observed.shape[0]
    cell = (me - halo_tiles) * CX + cut + jnp.arange(width, dtype=jnp.int32)
    inside = (cell >= 0) & (cell < tiles * CX)
    square_y = band_matrix(spread_taps[1], CY)[:, HALF : HALF + CY]
    square_z = band_matrix(spread_taps[2], CZ)[:, HALF : HALF + CZ]
    estimate = jnp.where(inside[:, None, None], observed, 0.0)
    for sweep in range(ITERS):
        low = 2 * HALF * sweep + HALF
        blurred = blur_narrowing(estimate, spread_taps[0], square_y, square_z)
        ratio = jnp.where(
            inside[low : width - low, None, None], observed[low : width - low] / blurred, 0.0
        )
        estimate = estimate[2 * HALF : estimate.shape[0] - 2 * HALF] * blur_narrowing(
            ratio, spread_taps[0], square_y, square_z
        )
    return estimate


def band_of(taps_ref, axis, rows, cols):
    offset = cols - rows + HALF
    band = jnp.zeros(offset.shape, jnp.float32)
    for tap in range(TAPS):
        band = jnp.where(offset == tap, taps_ref[axis, tap], band)
    return band


def mirror(index, length):
    return jnp.where(index < length // 2, index, 3 * (length // 2) - 1 - index)


def deblur_kernel(taps_ref, obs_ref, out_ref, kx_ref, kz_ref):
    tiles = lax.axis_size("grid")
    me = lax.axis_index("grid")
    planes, width, depth = obs_ref.shape
    shape_x = kx_ref.shape
    kx_ref[...] = band_of(
        taps_ref, 0, lax.broadcasted_iota(jnp.int32, shape_x, 0) + HALF, lax.broadcasted_iota(jnp.int32, shape_x, 1)
    )
    shape_z = kz_ref.shape
    kz_ref[...] = band_of(
        taps_ref,
        2,
        mirror(lax.broadcasted_iota(jnp.int32, shape_z, 1), depth),
        mirror(lax.broadcasted_iota(jnp.int32, shape_z, 0), depth),
    )
    halo_tiles = (width - CX) // (2 * CX)
    highest = lax.Precision.HIGHEST

    def inside(low, size):
        cell = (me - halo_tiles) * CX + low + lax.broadcasted_iota(jnp.int32, (size, depth), 0)
        return (cell >= 0) & (cell < tiles * CX)

    lanes = planes * depth

    def blur(volume):
        size_in = volume.shape[0]
        size_out = size_in - 2 * HALF
        band = kx_ref[0:size_out, 0:size_in]
        along_x = jnp.dot(band, volume, precision=highest, preferred_element_type=jnp.float32)
        along_y = []
        for y in range(planes):
            total = None
            for q in range(planes):
                term = taps_ref[1, q - y + HALF] * along_x[:, q * depth : (q + 1) * depth]
                total = term if total is None else total + term
            along_y.append(total)
        joined = jnp.concatenate(along_y, axis=0)
        along_z = jnp.dot(joined, kz_ref[...], precision=highest, preferred_element_type=jnp.float32)
        return jnp.concatenate([along_z[y * size_out : (y + 1) * size_out] for y in range(planes)], axis=1)

    def inside_wide(low, size):
        cell = (me - halo_tiles) * CX + low + lax.broadcasted_iota(jnp.int32, (size, lanes), 0)
        return (cell >= 0) & (cell < tiles * CX)

    observed = jnp.concatenate([obs_ref[y] for y in range(planes)], axis=1)
    estimate = jnp.where(inside_wide(0, width), observed, 0.0)
    for sweep in range(ITERS):
        low = 2 * HALF * sweep + HALF
        blurred = blur(estimate)
        size = blurred.shape[0]
        ratio = jnp.where(inside_wide(low, size), observed[low : low + size] / blurred, 0.0)
        spread = blur(ratio)
        estimate = estimate[2 * HALF : 2 * HALF + spread.shape[0]] * spread
    for y in range(planes):
        out_ref[y] = estimate[:, y * depth : (y + 1) * depth]


def deblur_tile(observed, spread_taps):
    planes, width, depth = observed.shape
    vmem = pl.BlockSpec(memory_space=pltpu.VMEM)
    return pl.pallas_call(
        deblur_kernel,
        out_shape=jax.ShapeDtypeStruct((planes, CX, depth), jnp.float32),
        in_specs=[pl.BlockSpec(memory_space=pltpu.SMEM), vmem],
        out_specs=vmem,
        scratch_shapes=[
            pltpu.VMEM((width - 2 * HALF, width), jnp.float32),
            pltpu.VMEM((depth, depth), jnp.float32),
        ],
    )(spread_taps, observed)


def per_device(spectra, lag_samples, slowness, spread_taps):
    groups = lax.axis_size("sta")
    own_count = FREQS // groups
    first_bin = lax.axis_index("sta") * own_count
    block = spectra.shape[2]
    spec_send = spectra.reshape(groups, own_count, 2, block).transpose(0, 2, 1, 3)
    halo_tiles = -(-(ITERS * 2 * HALF) // CX)
    summed = beam_power(spec_send, lag_samples, slowness[0], halo_tiles)
    observed = summed / (FREQS * STATIONS) + BACKGROUND
    slots = observed.shape[0]
    observed = observed.reshape(slots, CY, CX, CZ)
    observed = jnp.concatenate([observed[:, :, : CX // 2], observed[:, :, CX // 2 :][:, :, ::-1]], axis=2)
    planes = observed.transpose(1, 0, 2, 3).reshape(CY, slots * CX, CZ)
    estimate = deblur_tile(planes, spread_taps)
    both = jnp.stack([observed[halo_tiles], estimate])
    both = jnp.concatenate([both[..., : CZ // 2], both[..., CZ // 2 :][..., ::-1]], axis=-1).transpose(0, 2, 1, 3)
    stacked, estimate = both[0], both[1]
    return (stacked[None], estimate[None])


def solution(mesh):
    placed = (P(None, None, "sta"), P("grid", "sta"), P("grid", None, "sta"), P())
    return jax.shard_map(
        per_device,
        mesh=mesh,
        in_specs=placed,
        out_specs=(P("grid", None, None, None), P("grid", None, None, None)),
        check_vma=False,
    )
```

```python
import math

import jax
import jax.numpy as jnp
from jax import lax
from jax.sharding import PartitionSpec as P
from jax.experimental import pallas as pl
from jax.experimental.pallas import tpu as pltpu

STATIONS = 6144
FREQS = 64
F0 = 600
NT = 6000
TAPS = 17
HALF = 8
ITERS = 4
CX = 32
CY = 8
CZ = 128


TWO_PI = 2.0 * math.pi
BACKGROUND = 0.05


def with_halo(array, sides, width):
    for axis, dim in sides:
        size, length = (lax.axis_size(axis), array.shape[dim])
        up = [(i, (i + 1) % size) for i in range(size - 1)]
        down = [(j, i) for i, j in up]
        last = lax.slice_in_dim(array, length - width, length, axis=dim)
        leading = lax.slice_in_dim(array, 0, width, axis=dim)
        before = lax.ppermute(last, axis, up)
        after = lax.ppermute(leading, axis, down)
        array = jnp.concatenate([before, array, after], axis=dim)
    return array


def align_rows(spectra, lag_row):
    bins = F0 + jnp.arange(FREQS, dtype=jnp.int32)
    cycles = bins[:, None] * lag_row[None, :] % NT
    turned = cycles.astype(jnp.float32) * (TWO_PI / NT)
    cosine = jnp.cos(turned)
    sine = jnp.sin(turned)
    real_in = spectra[:, 0, :].astype(jnp.float32)
    imag_in = spectra[:, 1, :].astype(jnp.float32)
    real_out = real_in * cosine + imag_in * sine
    imag_out = imag_in * cosine - real_in * sine
    return jnp.stack([real_out, imag_out], axis=1).astype(jnp.bfloat16)


def beam_freq(freq, aligned_row, slow_rows):
    omega = (F0 + freq).astype(jnp.float32) * (TWO_PI / NT)
    slow = slow_rows.astype(jnp.float32)
    x_coord = jnp.arange(CX, dtype=jnp.float32) - (CX - 1) / 2.0
    y_coord = jnp.arange(CY, dtype=jnp.float32) - (CY - 1) / 2.0
    z_coord = jnp.arange(CZ, dtype=jnp.float32) - (CZ - 1) / 2.0
    phase_x = (omega * slow[0])[None, :] * x_coord[:, None]
    phase_y = (omega * slow[1])[None, :] * y_coord[:, None]
    phase = phase_x[:, None, :] + phase_y[None, :, :]
    cosine = jnp.cos(phase)
    sine = jnp.sin(phase)
    real_in = aligned_row[0].astype(jnp.float32)[None, None, :]
    imag_in = aligned_row[1].astype(jnp.float32)[None, None, :]
    front_real = (real_in * cosine + imag_in * sine).astype(jnp.bfloat16).reshape(CX * CY, -1)
    front_imag = (imag_in * cosine - real_in * sine).astype(jnp.bfloat16).reshape(CX * CY, -1)
    left_side = jnp.concatenate([front_real, front_imag], axis=1)
    phase_z = (omega * slow[2])[:, None] * z_coord[None, :]
    depth_real = jnp.cos(phase_z).astype(jnp.bfloat16)
    depth_imag = jnp.sin(phase_z).astype(jnp.bfloat16)
    upper_rows = jnp.concatenate([depth_real, -depth_imag], axis=1)
    lower_rows = jnp.concatenate([depth_imag, depth_real], axis=1)
    right_side = jnp.concatenate([upper_rows, lower_rows], axis=0)
    return jnp.dot(left_side, right_side, preferred_element_type=jnp.float32)


CHUNK = 768


def exp_neg(angle):
    return jnp.cos(angle), -jnp.sin(angle)


def enter_barrier(count, reach):
    me = lax.axis_index("sta")
    tile = lax.axis_index("grid")
    tiles = lax.axis_size("grid")
    mesh_ids = pl.DeviceIdType.MESH
    barrier = pltpu.get_barrier_semaphore()
    for shift in range(1, count):
        pl.semaphore_signal(barrier, inc=1, device_id=(tile, lax.rem(me + shift, count)), device_id_type=mesh_ids)
    neighbours = jnp.int32(0)
    for k in range(-reach, reach + 1):
        if k == 0:
            continue
        there = (tile + k >= 0) & (tile + k < tiles)
        neighbours = neighbours + there.astype(jnp.int32)

        @pl.when(there)
        def _():
            pl.semaphore_signal(barrier, inc=1, device_id=(tile + k, me), device_id_type=mesh_ids)

    pl.semaphore_wait(barrier, count - 1 + neighbours)


def exchange_inputs(spec_ref, lag_ref, slow_ref, spec_in, lag_in, slow_in, local_sem, send_sem, recv_sem, then, reach):
    count = spec_in.shape[0]
    me = lax.axis_index("sta")
    tile = lax.axis_index("grid")
    mesh_ids = pl.DeviceIdType.MESH
    enter_barrier(count, reach)
    pairs = ((spec_ref, spec_in), (lag_ref, lag_in), (slow_ref, slow_in))
    local = []
    for kind, (source, target) in enumerate(pairs):
        own = source.at[me] if kind == 0 else source
        copy = pltpu.make_async_copy(own, target.at[me], local_sem.at[kind])
        copy.start()
        local.append(copy)
    sends = []
    for shift in range(1, count):
        peer = lax.rem(me + shift, count)
        for kind, (source, target) in enumerate(pairs):
            part = source.at[peer] if kind == 0 else source
            copy = pltpu.make_async_remote_copy(
                src_ref=part,
                dst_ref=target.at[me],
                send_sem=send_sem.at[kind, shift],
                recv_sem=recv_sem.at[kind, me],
                device_id=(tile, peer),
                device_id_type=mesh_ids,
            )
            copy.start()
            sends.append(copy)
    then()
    for copy in local:
        copy.wait()
    for copy in sends:
        copy.wait_send()
    for shift in range(1, count):
        source_id = lax.rem(me + count - shift, count)
        for kind, (source, target) in enumerate(pairs):
            part = source.at[source_id] if kind == 0 else source
            pltpu.make_async_remote_copy(
                src_ref=part,
                dst_ref=target.at[source_id],
                send_sem=send_sem.at[kind, shift],
                recv_sem=recv_sem.at[kind, source_id],
                device_id=(tile, source_id),
                device_id_type=mesh_ids,
            ).wait_recv()


def align_block(spec, lag, slow, source, real_ref, imag_ref, turn_ref):
    bins, block = spec.shape[1], spec.shape[2]
    first_bin = lax.axis_index("sta") * bins
    bin_rows = (F0 + first_bin + lax.broadcasted_iota(jnp.int32, (bins, block), 0)).astype(jnp.float32)
    cols = pl.ds(pl.multiple_of(source * block, 128), block)
    product = bin_rows * lag.astype(jnp.float32)
    whole = jnp.floor(product * (1.0 / NT))
    left = product - whole * NT
    left = jnp.where(left < 0.0, left + NT, left)
    left = jnp.where(left >= NT, left - NT, left)
    turned = left * (TWO_PI / NT)
    cosine = jnp.cos(turned)
    sine = jnp.sin(turned)
    real_in = spec[0].astype(jnp.float32)
    imag_in = spec[1].astype(jnp.float32)
    real_ref[:, cols] = (real_in * cosine + imag_in * sine).astype(jnp.bfloat16).astype(jnp.float32)
    imag_ref[:, cols] = (imag_in * cosine - real_in * sine).astype(jnp.bfloat16).astype(jnp.float32)
    turn_ref[:, cols] = slow.astype(jnp.float32)


def complex_times(left, right):
    return left[0] * right[0] - left[1] * right[1], left[0] * right[1] + left[1] * right[0]


def factor_rows(turn_x, turn_y, turn_z, rows8, rows16):
    return (
        exp_neg(turn_x * (rows8 - 3.5)),
        exp_neg(turn_x * (8.0 * (rows8 - 1.5))),
        exp_neg(turn_y * (rows8 - 3.5)),
        exp_neg(turn_z * (rows16 - 7.5)),
        exp_neg(turn_z * (16.0 * (rows8 - 3.5))),
    )


def beam_kernel(spec_ref, lag_ref, slow_ref, out_ref, spec_in, lag_in, slow_in, local_sem, send_sem, recv_sem,
                real_ref, imag_ref, turn_ref, acc_ref, left_ref, right_ref, power_ref, pieces, send_rs, recv_rs,
                send_ag, recv_ag, share_sem):
    count, bins, block = spec_in.shape[0], spec_in.shape[2], spec_in.shape[3]
    me = lax.axis_index("sta")
    first_bin = me * bins
    width = CHUNK
    per_block = block // width
    half_z = CZ // 2
    rows8 = lax.broadcasted_iota(jnp.int32, (8, width), 0).astype(jnp.float32)
    rows16 = lax.broadcasted_iota(jnp.int32, (16, width), 0).astype(jnp.float32)
    omega0 = (F0 + first_bin).astype(jnp.float32) * (TWO_PI / NT)
    step = TWO_PI / NT
    acc_ref[...] = jnp.zeros_like(acc_ref)

    def per_chunk(k, carry):
        source = lax.rem(me + k // per_block, count)
        cols = pl.ds(pl.multiple_of(source * block + lax.rem(k, per_block) * width, 128), width)
        slow_x = turn_ref[0:1, cols]
        slow_y = turn_ref[1:2, cols]
        slow_z = turn_ref[2:3, cols]
        start = factor_rows(omega0 * slow_x, omega0 * slow_y, omega0 * slow_z, rows8, rows16)
        ratio = factor_rows(step * slow_x, step * slow_y, step * slow_z, rows8, rows16)

        def per_bin(f, state):
            (a_r, a_i), (b_r, b_i), (y_r, y_i), (c_r, c_i), (d_r, d_i) = state
            real_in = real_ref[pl.ds(f, 1), cols]
            imag_in = imag_ref[pl.ds(f, 1), cols]
            q_r = real_in * y_r - imag_in * y_i
            q_i = real_in * y_i + imag_in * y_r
            near = [complex_times((b_r[m : m + 1], b_i[m : m + 1]), (a_r, a_i)) for m in range(CX // 16)]
            cells = CX * CY
            for y in range(CY):
                qq_r, qq_i = q_r[y : y + 1], q_i[y : y + 1]
                lo_r, lo_i, hi_r, hi_i = [], [], [], []
                for x_r, x_i in near:
                    t1, t2 = qq_r * x_r, qq_i * x_i
                    t3, t4 = qq_r * x_i, qq_i * x_r
                    lo_r.append(t1 - t2)
                    lo_i.append(t3 + t4)
                    hi_r.append(t1 + t2)
                    hi_i.append(t4 - t3)
                row = y * CX
                half = CX // 2
                left_ref[row : row + half, :] = jnp.concatenate(lo_r, axis=0).astype(jnp.bfloat16)
                left_ref[row + half : row + CX, :] = jnp.concatenate(hi_r, axis=0).astype(jnp.bfloat16)
                left_ref[cells + row : cells + row + half, :] = jnp.concatenate(lo_i, axis=0).astype(jnp.bfloat16)
                left_ref[cells + row + half : cells + row + CX, :] = jnp.concatenate(hi_i, axis=0).astype(jnp.bfloat16)
            for m in range(half_z // 16):
                z_r, z_i = complex_times((d_r[m : m + 1], d_i[m : m + 1]), (c_r, c_i))
                row = 16 * m
                right_ref[row : row + 16, :] = z_r.astype(jnp.bfloat16)
                right_ref[half_z + row : half_z + row + 16, :] = z_i.astype(jnp.bfloat16)
            acc_ref[f] += lax.dot_general(
                left_ref[...], right_ref[...], (((1,), (1,)), ((), ())), preferred_element_type=jnp.float32
            )
            return tuple(complex_times(now, turn) for now, turn in zip(state, ratio))

        lax.fori_loop(0, bins, per_bin, start, unroll=4)
        return carry

    def own_block():
        align_block(spec_ref[me], lag_ref[...], slow_ref[...], me, real_ref, imag_ref, turn_ref)
        lax.fori_loop(0, per_block, per_chunk, 0)

    exchange_inputs(
        spec_ref, lag_ref, slow_ref, spec_in, lag_in, slow_in, local_sem, send_sem, recv_sem, own_block, out_ref.shape[0] // 2
    )

    def align_other(shift, carry):
        source = lax.rem(me + shift, count)
        align_block(spec_in[source], lag_in[source], slow_in[source], source, real_ref, imag_ref, turn_ref)
        return carry

    lax.fori_loop(1, count, align_other, 0)
    lax.fori_loop(per_block, count * per_block, per_chunk, 0)
    cells = CX * CY
    low = jnp.zeros((cells, half_z), jnp.float32)
    high = jnp.zeros((cells, half_z), jnp.float32)
    for f in range(bins):
        sums = acc_ref[f]
        u, w = sums[:cells, :half_z], sums[:cells, half_z:]
        x, v = sums[cells:, :half_z], sums[cells:, half_z:]
        low = low + ((u - v) * (u - v) + (w + x) * (w + x))
        high = high + ((u + v) * (u + v) + (x - w) * (x - w))
    power_ref[:, :half_z] = low
    power_ref[:, half_z:] = high
    share_kernel(power_ref, out_ref, pieces, send_rs, recv_rs, send_ag, recv_ag, share_sem)


def beam_power(spec_send, lag_row, slow_rows, reach):
    count = spec_send.shape[0]
    slots = 2 * reach + 1
    cells = CX * CY
    bins, block = spec_send.shape[2], spec_send.shape[3]
    width = CHUNK
    stations = count * block
    vmem = pl.BlockSpec(memory_space=pltpu.VMEM)
    return pl.pallas_call(
        beam_kernel,
        out_shape=jax.ShapeDtypeStruct((slots, cells, CZ), jnp.float32),
        in_specs=[vmem, vmem, vmem],
        out_specs=vmem,
        scratch_shapes=[
            pltpu.VMEM((count,) + spec_send.shape[1:], jnp.bfloat16),
            pltpu.VMEM((count,) + lag_row.shape, jnp.int32),
            pltpu.VMEM((count,) + slow_rows.shape, jnp.bfloat16),
            pltpu.SemaphoreType.DMA((3,)),
            pltpu.SemaphoreType.DMA((3, count)),
            pltpu.SemaphoreType.DMA((3, count)),
            pltpu.VMEM((bins, stations), jnp.float32),
            pltpu.VMEM((bins, stations), jnp.float32),
            pltpu.VMEM((slow_rows.shape[0], stations), jnp.float32),
            pltpu.VMEM((bins, 2 * CX * CY, CZ), jnp.float32),
            pltpu.VMEM((2 * CX * CY, width), jnp.bfloat16),
            pltpu.VMEM((CZ, width), jnp.bfloat16),
            pltpu.VMEM((cells, CZ), jnp.float32),
            pltpu.VMEM((count, cells // count, CZ), jnp.float32),
            pltpu.SemaphoreType.DMA((count,)),
            pltpu.SemaphoreType.DMA((count,)),
            pltpu.SemaphoreType.DMA((slots, count)),
            pltpu.SemaphoreType.DMA((slots, count)),
            pltpu.SemaphoreType.DMA((1,)),
        ],
        compiler_params=pltpu.CompilerParams(collective_id=1, has_side_effects=True),
    )(spec_send, lag_row, slow_rows)


def share_kernel(part_ref, out_ref, pieces, send_rs, recv_rs, send_ag, recv_ag, local_sem):
    count = pieces.shape[0]
    slots = out_ref.shape[0]
    reach = slots // 2
    rows = pieces.shape[1]
    me = lax.axis_index("sta")
    tile = lax.axis_index("grid")
    tiles = lax.axis_size("grid")
    mesh_ids = pl.DeviceIdType.MESH
    own = pltpu.make_async_copy(part_ref.at[pl.ds(pl.multiple_of(me * rows, 8), rows)], pieces.at[me], local_sem.at[0])
    own.start()
    sends = []
    for shift in range(1, count):
        peer = lax.rem(me + shift, count)
        copy = pltpu.make_async_remote_copy(
            src_ref=part_ref.at[pl.ds(pl.multiple_of(peer * rows, 8), rows)],
            dst_ref=pieces.at[me],
            send_sem=send_rs.at[shift],
            recv_sem=recv_rs.at[me],
            device_id=(tile, peer),
            device_id_type=mesh_ids,
        )
        copy.start()
        sends.append(copy)
    own.wait()
    for copy in sends:
        copy.wait_send()
    for shift in range(1, count):
        source = lax.rem(me + count - shift, count)
        pltpu.make_async_remote_copy(
            src_ref=pieces.at[source],
            dst_ref=pieces.at[source],
            send_sem=send_rs.at[shift],
            recv_sem=recv_rs.at[source],
            device_id=(tile, source),
            device_id_type=mesh_ids,
        ).wait_recv()
    total = pieces[0]
    for source in range(1, count):
        total = total + pieces[source]
    mine = pl.ds(pl.multiple_of(me * rows, 8), rows)
    out_ref[reach, mine] = total
    block = out_ref.at[reach, mine]

    def gather_copy(k, peer, slot):
        return pltpu.make_async_remote_copy(
            src_ref=block,
            dst_ref=out_ref.at[slot, mine],
            send_sem=send_ag.at[slot, peer],
            recv_sem=recv_ag.at[slot, me],
            device_id=(tile + k, peer),
            device_id_type=mesh_ids,
        )

    peers = []
    for shift in range(1, count):
        copy = gather_copy(0, lax.rem(me + shift, count), reach)
        copy.start()
        peers.append(copy)
    for k in range(-reach, reach + 1):
        if k == 0:
            continue

        @pl.when(jnp.logical_not((tile + k >= 0) & (tile + k < tiles)))
        def _():
            out_ref[reach + k] = jnp.zeros(out_ref.shape[1:], out_ref.dtype)

    for copy in peers:
        copy.wait_send()
    for shift in range(1, count):
        source = lax.rem(me + count - shift, count)
        pltpu.make_async_remote_copy(
            src_ref=block,
            dst_ref=out_ref.at[reach, pl.ds(pl.multiple_of(source * rows, 8), rows)],
            send_sem=send_ag.at[reach, source],
            recv_sem=recv_ag.at[reach, source],
            device_id=(tile, source),
            device_id_type=mesh_ids,
        ).wait_recv()

    def halo_copy(k):
        return pltpu.make_async_remote_copy(
            src_ref=out_ref.at[reach],
            dst_ref=out_ref.at[reach - k],
            send_sem=send_ag.at[reach - k, me],
            recv_sem=recv_ag.at[reach - k, me],
            device_id=(tile + k, me),
            device_id_type=mesh_ids,
        )

    for k in range(-reach, reach + 1):
        if k == 0:
            continue

        @pl.when((tile + k >= 0) & (tile + k < tiles))
        def _():
            halo_copy(k).start()

    for k in range(-reach, reach + 1):
        if k == 0:
            continue

        @pl.when((tile + k >= 0) & (tile + k < tiles))
        def _():
            halo_copy(k).wait_send()
            pltpu.make_async_remote_copy(
                src_ref=out_ref.at[reach],
                dst_ref=out_ref.at[reach + k],
                send_sem=send_ag.at[reach + k, me],
                recv_sem=recv_ag.at[reach + k, me],
                device_id=(tile + k, me),
                device_id_type=mesh_ids,
            ).wait_recv()


def share_power(part, reach):
    count = lax.axis_size("sta")
    rows = part.shape[0] // count
    slots = 2 * reach + 1
    return pl.pallas_call(
        share_kernel,
        out_shape=jax.ShapeDtypeStruct((slots,) + part.shape, jnp.float32),
        in_specs=[pl.BlockSpec(memory_space=pltpu.VMEM)],
        out_specs=pl.BlockSpec(memory_space=pltpu.VMEM),
        scratch_shapes=[
            pltpu.VMEM((count, rows, part.shape[1]), jnp.float32),
            pltpu.SemaphoreType.DMA((count,)),
            pltpu.SemaphoreType.DMA((count,)),
            pltpu.SemaphoreType.DMA((slots, count)),
            pltpu.SemaphoreType.DMA((slots, count)),
            pltpu.SemaphoreType.DMA((1,)),
        ],
        compiler_params=pltpu.CompilerParams(collective_id=0, has_side_effects=True),
    )(part)


def freq_beams(freq_ids, aligned_rows, slow_rows):
    return lax.map(lambda pair: beam_freq(pair[0], pair[1], slow_rows), (freq_ids, aligned_rows))


def band_matrix(taps, length):
    rows = jnp.arange(length, dtype=jnp.int32)[:, None]
    columns = jnp.arange(length + 2 * HALF, dtype=jnp.int32)[None, :]
    offset = columns - rows
    picks = jnp.arange(TAPS, dtype=jnp.int32)[:, None, None]
    return jnp.sum(jnp.where(offset[None] == picks, taps[:, None, None], 0.0), axis=0)


def blur(volume, bands):
    band_x, square_y, square_z = bands
    padded = with_halo(volume.astype(jnp.bfloat16), (("grid", 0),), HALF).astype(volume.dtype)
    along_x = jnp.einsum("ip,pyz->iyz", band_x, padded, precision=lax.Precision.HIGHEST)
    along_y = jnp.einsum("jq,xqz->xjz", square_y, along_x, precision=lax.Precision.HIGHEST)
    return jnp.einsum("xyw,kw->xyk", along_y, square_z, precision=lax.Precision.HIGHEST)


def blur_narrowing(volume, taps, square_y, square_z):
    band_x = band_matrix(taps, volume.shape[0] - 2 * HALF)
    along_x = jnp.einsum("ip,pyz->iyz", band_x, volume, precision=lax.Precision.HIGHEST)
    along_y = jnp.einsum("jq,xqz->xjz", square_y, along_x, precision=lax.Precision.HIGHEST)
    return jnp.einsum("xyw,kw->xyk", along_y, square_z, precision=lax.Precision.HIGHEST)


def deblur(observed, halo_tiles, spread_taps):
    tiles = lax.axis_size("grid")
    me = lax.axis_index("grid")
    reach = ITERS * 2 * HALF
    cut = halo_tiles * CX - reach
    observed = observed[cut : observed.shape[0] - cut]
    width = observed.shape[0]
    cell = (me - halo_tiles) * CX + cut + jnp.arange(width, dtype=jnp.int32)
    inside = (cell >= 0) & (cell < tiles * CX)
    square_y = band_matrix(spread_taps[1], CY)[:, HALF : HALF + CY]
    square_z = band_matrix(spread_taps[2], CZ)[:, HALF : HALF + CZ]
    estimate = jnp.where(inside[:, None, None], observed, 0.0)
    for sweep in range(ITERS):
        low = 2 * HALF * sweep + HALF
        blurred = blur_narrowing(estimate, spread_taps[0], square_y, square_z)
        ratio = jnp.where(
            inside[low : width - low, None, None], observed[low : width - low] / blurred, 0.0
        )
        estimate = estimate[2 * HALF : estimate.shape[0] - 2 * HALF] * blur_narrowing(
            ratio, spread_taps[0], square_y, square_z
        )
    return estimate


def band_of(taps_ref, axis, rows, cols):
    offset = cols - rows + HALF
    band = jnp.zeros(offset.shape, jnp.float32)
    for tap in range(TAPS):
        band = jnp.where(offset == tap, taps_ref[axis, tap], band)
    return band


def mirror(index, length):
    return jnp.where(index < length // 2, index, 3 * (length // 2) - 1 - index)


def deblur_kernel(taps_ref, obs_ref, out_ref, kx_ref, kz_ref):
    tiles = lax.axis_size("grid")
    me = lax.axis_index("grid")
    planes, width, depth = obs_ref.shape
    shape_x = kx_ref.shape
    kx_ref[...] = band_of(
        taps_ref, 0, lax.broadcasted_iota(jnp.int32, shape_x, 0) + HALF, lax.broadcasted_iota(jnp.int32, shape_x, 1)
    )
    shape_z = kz_ref.shape
    kz_ref[...] = band_of(
        taps_ref,
        2,
        mirror(lax.broadcasted_iota(jnp.int32, shape_z, 1), depth),
        mirror(lax.broadcasted_iota(jnp.int32, shape_z, 0), depth),
    )
    halo_tiles = (width - CX) // (2 * CX)
    highest = lax.Precision.HIGHEST

    def inside(low, size):
        cell = (me - halo_tiles) * CX + low + lax.broadcasted_iota(jnp.int32, (size, depth), 0)
        return (cell >= 0) & (cell < tiles * CX)

    lanes = planes * depth

    def blur(volume):
        size_in = volume.shape[0]
        size_out = size_in - 2 * HALF
        band = kx_ref[0:size_out, 0:size_in]
        along_x = jnp.dot(band, volume, precision=highest, preferred_element_type=jnp.float32)
        along_y = []
        for y in range(planes):
            total = None
            for q in range(planes):
                term = taps_ref[1, q - y + HALF] * along_x[:, q * depth : (q + 1) * depth]
                total = term if total is None else total + term
            along_y.append(total)
        joined = jnp.concatenate(along_y, axis=0)
        along_z = jnp.dot(joined, kz_ref[...], precision=highest, preferred_element_type=jnp.float32)
        return jnp.concatenate([along_z[y * size_out : (y + 1) * size_out] for y in range(planes)], axis=1)

    def inside_wide(low, size):
        cell = (me - halo_tiles) * CX + low + lax.broadcasted_iota(jnp.int32, (size, lanes), 0)
        return (cell >= 0) & (cell < tiles * CX)

    observed = jnp.concatenate([obs_ref[y] for y in range(planes)], axis=1)
    estimate = jnp.where(inside_wide(0, width), observed, 0.0)
    for sweep in range(ITERS):
        low = 2 * HALF * sweep + HALF
        blurred = blur(estimate)
        size = blurred.shape[0]
        ratio = jnp.where(inside_wide(low, size), observed[low : low + size] / blurred, 0.0)
        spread = blur(ratio)
        estimate = estimate[2 * HALF : 2 * HALF + spread.shape[0]] * spread
    for y in range(planes):
        out_ref[y] = estimate[:, y * depth : (y + 1) * depth]


def deblur_tile(observed, spread_taps):
    planes, width, depth = observed.shape
    vmem = pl.BlockSpec(memory_space=pltpu.VMEM)
    return pl.pallas_call(
        deblur_kernel,
        out_shape=jax.ShapeDtypeStruct((planes, CX, depth), jnp.float32),
        in_specs=[pl.BlockSpec(memory_space=pltpu.SMEM), vmem],
        out_specs=vmem,
        scratch_shapes=[
            pltpu.VMEM((width - 2 * HALF, width), jnp.float32),
            pltpu.VMEM((depth, depth), jnp.float32),
        ],
    )(spread_taps, observed)


def per_device(spectra, lag_samples, slowness, spread_taps):
    groups = lax.axis_size("sta")
    own_count = FREQS // groups
    first_bin = lax.axis_index("sta") * own_count
    block = spectra.shape[2]
    spec_send = spectra.reshape(groups, own_count, 2, block).transpose(0, 2, 1, 3)
    halo_tiles = -(-(ITERS * 2 * HALF) // CX)
    summed = beam_power(spec_send, lag_samples, slowness[0], halo_tiles)
    observed = summed / (FREQS * STATIONS) + BACKGROUND
    slots = observed.shape[0]
    observed = observed.reshape(slots, CY, CX, CZ)
    observed = jnp.concatenate([observed[:, :, : CX // 2], observed[:, :, CX // 2 :][:, :, ::-1]], axis=2)
    planes = observed.transpose(1, 0, 2, 3).reshape(CY, slots * CX, CZ)
    estimate = deblur_tile(planes, spread_taps)
    both = jnp.stack([observed[halo_tiles], estimate])
    both = jnp.concatenate([both[..., : CZ // 2], both[..., CZ // 2 :][..., ::-1]], axis=-1).transpose(0, 2, 1, 3)
    stacked, estimate = both[0], both[1]
    return (stacked[None], estimate[None])


def solution(mesh):
    placed = (P(None, None, "sta"), P("grid", "sta"), P("grid", None, "sta"), P())
    return jax.shard_map(
        per_device,
        mesh=mesh,
        in_specs=placed,
        out_specs=(P("grid", None, None, None), P("grid", None, None, None)),
        check_vma=False,
    )
```

```python
import math

import jax
import jax.numpy as jnp
from jax import lax
from jax.sharding import PartitionSpec as P
from jax.experimental import pallas as pl
from jax.experimental.pallas import tpu as pltpu

STATIONS = 6144
FREQS = 64
F0 = 600
NT = 6000
TAPS = 17
HALF = 8
ITERS = 4
CX = 32
CY = 8
CZ = 128


TWO_PI = 2.0 * math.pi
BACKGROUND = 0.05


def with_halo(array, sides, width):
    for axis, dim in sides:
        size, length = (lax.axis_size(axis), array.shape[dim])
        up = [(i, (i + 1) % size) for i in range(size - 1)]
        down = [(j, i) for i, j in up]
        last = lax.slice_in_dim(array, length - width, length, axis=dim)
        leading = lax.slice_in_dim(array, 0, width, axis=dim)
        before = lax.ppermute(last, axis, up)
        after = lax.ppermute(leading, axis, down)
        array = jnp.concatenate([before, array, after], axis=dim)
    return array


def align_rows(spectra, lag_row):
    bins = F0 + jnp.arange(FREQS, dtype=jnp.int32)
    cycles = bins[:, None] * lag_row[None, :] % NT
    turned = cycles.astype(jnp.float32) * (TWO_PI / NT)
    cosine = jnp.cos(turned)
    sine = jnp.sin(turned)
    real_in = spectra[:, 0, :].astype(jnp.float32)
    imag_in = spectra[:, 1, :].astype(jnp.float32)
    real_out = real_in * cosine + imag_in * sine
    imag_out = imag_in * cosine - real_in * sine
    return jnp.stack([real_out, imag_out], axis=1).astype(jnp.bfloat16)


def beam_freq(freq, aligned_row, slow_rows):
    omega = (F0 + freq).astype(jnp.float32) * (TWO_PI / NT)
    slow = slow_rows.astype(jnp.float32)
    x_coord = jnp.arange(CX, dtype=jnp.float32) - (CX - 1) / 2.0
    y_coord = jnp.arange(CY, dtype=jnp.float32) - (CY - 1) / 2.0
    z_coord = jnp.arange(CZ, dtype=jnp.float32) - (CZ - 1) / 2.0
    phase_x = (omega * slow[0])[None, :] * x_coord[:, None]
    phase_y = (omega * slow[1])[None, :] * y_coord[:, None]
    phase = phase_x[:, None, :] + phase_y[None, :, :]
    cosine = jnp.cos(phase)
    sine = jnp.sin(phase)
    real_in = aligned_row[0].astype(jnp.float32)[None, None, :]
    imag_in = aligned_row[1].astype(jnp.float32)[None, None, :]
    front_real = (real_in * cosine + imag_in * sine).astype(jnp.bfloat16).reshape(CX * CY, -1)
    front_imag = (imag_in * cosine - real_in * sine).astype(jnp.bfloat16).reshape(CX * CY, -1)
    left_side = jnp.concatenate([front_real, front_imag], axis=1)
    phase_z = (omega * slow[2])[:, None] * z_coord[None, :]
    depth_real = jnp.cos(phase_z).astype(jnp.bfloat16)
    depth_imag = jnp.sin(phase_z).astype(jnp.bfloat16)
    upper_rows = jnp.concatenate([depth_real, -depth_imag], axis=1)
    lower_rows = jnp.concatenate([depth_imag, depth_real], axis=1)
    right_side = jnp.concatenate([upper_rows, lower_rows], axis=0)
    return jnp.dot(left_side, right_side, preferred_element_type=jnp.float32)


CHUNK = 768


def exp_neg(angle):
    return jnp.cos(angle), -jnp.sin(angle)


def enter_barrier(count, reach):
    me = lax.axis_index("sta")
    tile = lax.axis_index("grid")
    tiles = lax.axis_size("grid")
    mesh_ids = pl.DeviceIdType.MESH
    barrier = pltpu.get_barrier_semaphore()
    for shift in range(1, count):
        pl.semaphore_signal(barrier, inc=1, device_id=(tile, lax.rem(me + shift, count)), device_id_type=mesh_ids)
    neighbours = jnp.int32(0)
    for k in range(-reach, reach + 1):
        if k == 0:
            continue
        there = (tile + k >= 0) & (tile + k < tiles)
        neighbours = neighbours + there.astype(jnp.int32)

        @pl.when(there)
        def _():
            pl.semaphore_signal(barrier, inc=1, device_id=(tile + k, me), device_id_type=mesh_ids)

    pl.semaphore_wait(barrier, count - 1 + neighbours)


def exchange_inputs(spec_ref, lag_ref, slow_ref, spec_in, lag_in, slow_in, local_sem, send_sem, recv_sem, then, reach):
    count = spec_in.shape[0]
    me = lax.axis_index("sta")
    tile = lax.axis_index("grid")
    mesh_ids = pl.DeviceIdType.MESH
    enter_barrier(count, reach)
    pairs = ((spec_ref, spec_in), (lag_ref, lag_in), (slow_ref, slow_in))
    local = []
    for kind, (source, target) in enumerate(pairs):
        own = source.at[me] if kind == 0 else source
        copy = pltpu.make_async_copy(own, target.at[me], local_sem.at[kind])
        copy.start()
        local.append(copy)
    sends = []
    for shift in range(1, count):
        peer = lax.rem(me + shift, count)
        for kind, (source, target) in enumerate(pairs):
            part = source.at[peer] if kind == 0 else source
            copy = pltpu.make_async_remote_copy(
                src_ref=part,
                dst_ref=target.at[me],
                send_sem=send_sem.at[kind, shift],
                recv_sem=recv_sem.at[kind, me],
                device_id=(tile, peer),
                device_id_type=mesh_ids,
            )
            copy.start()
            sends.append(copy)
    then()
    for copy in local:
        copy.wait()
    for copy in sends:
        copy.wait_send()
    for shift in range(1, count):
        source_id = lax.rem(me + count - shift, count)
        for kind, (source, target) in enumerate(pairs):
            part = source.at[source_id] if kind == 0 else source
            pltpu.make_async_remote_copy(
                src_ref=part,
                dst_ref=target.at[source_id],
                send_sem=send_sem.at[kind, shift],
                recv_sem=recv_sem.at[kind, source_id],
                device_id=(tile, source_id),
                device_id_type=mesh_ids,
            ).wait_recv()


def align_block(spec, lag, slow, source, real_ref, imag_ref, turn_ref):
    bins, block = spec.shape[1], spec.shape[2]
    first_bin = lax.axis_index("sta") * bins
    bin_rows = (F0 + first_bin + lax.broadcasted_iota(jnp.int32, (bins, block), 0)).astype(jnp.float32)
    cols = pl.ds(pl.multiple_of(source * block, 128), block)
    product = bin_rows * lag.astype(jnp.float32)
    whole = jnp.floor(product * (1.0 / NT))
    left = product - whole * NT
    left = jnp.where(left < 0.0, left + NT, left)
    left = jnp.where(left >= NT, left - NT, left)
    turned = left * (TWO_PI / NT)
    cosine = jnp.cos(turned)
    sine = jnp.sin(turned)
    real_in = spec[0].astype(jnp.float32)
    imag_in = spec[1].astype(jnp.float32)
    real_ref[:, cols] = (real_in * cosine + imag_in * sine).astype(jnp.bfloat16).astype(jnp.float32)
    imag_ref[:, cols] = (imag_in * cosine - real_in * sine).astype(jnp.bfloat16).astype(jnp.float32)
    turn_ref[:, cols] = slow.astype(jnp.float32)


def complex_times(left, right):
    return left[0] * right[0] - left[1] * right[1], left[0] * right[1] + left[1] * right[0]


def factor_rows(turn_x, turn_y, turn_z, rows8, rows16):
    return (
        exp_neg(turn_x * (rows8 - 3.5)),
        exp_neg(turn_x * (8.0 * (rows8 - 1.5))),
        exp_neg(turn_y * (rows8 - 3.5)),
        exp_neg(turn_z * (rows16 - 7.5)),
        exp_neg(turn_z * (16.0 * (rows8 - 3.5))),
    )


def beam_kernel(spec_ref, lag_ref, slow_ref, out_ref, spec_in, lag_in, slow_in, local_sem, send_sem, recv_sem,
                real_ref, imag_ref, turn_ref, acc_ref, left_ref, right_ref, power_ref, pieces, send_rs, recv_rs,
                send_ag, recv_ag, share_sem):
    count, bins, block = spec_in.shape[0], spec_in.shape[2], spec_in.shape[3]
    me = lax.axis_index("sta")
    first_bin = me * bins
    width = CHUNK
    per_block = block // width
    half_z = CZ // 2
    rows8 = lax.broadcasted_iota(jnp.int32, (8, width), 0).astype(jnp.float32)
    rows16 = lax.broadcasted_iota(jnp.int32, (16, width), 0).astype(jnp.float32)
    omega0 = (F0 + first_bin).astype(jnp.float32) * (TWO_PI / NT)
    step = TWO_PI / NT
    acc_ref[...] = jnp.zeros_like(acc_ref)

    def per_chunk(k, carry):
        source = lax.rem(me + k // per_block, count)
        cols = pl.ds(pl.multiple_of(source * block + lax.rem(k, per_block) * width, 128), width)
        slow_x = turn_ref[0:1, cols]
        slow_y = turn_ref[1:2, cols]
        slow_z = turn_ref[2:3, cols]
        start = factor_rows(omega0 * slow_x, omega0 * slow_y, omega0 * slow_z, rows8, rows16)
        ratio = factor_rows(step * slow_x, step * slow_y, step * slow_z, rows8, rows16)

        def per_bin(f, state):
            (a_r, a_i), (b_r, b_i), (y_r, y_i), (c_r, c_i), (d_r, d_i) = state
            real_in = real_ref[pl.ds(f, 1), cols]
            imag_in = imag_ref[pl.ds(f, 1), cols]
            q_r = real_in * y_r - imag_in * y_i
            q_i = real_in * y_i + imag_in * y_r
            near = [complex_times((b_r[m : m + 1], b_i[m : m + 1]), (a_r, a_i)) for m in range(CX // 16)]
            cells = CX * CY
            for y in range(CY):
                qq_r, qq_i = q_r[y : y + 1], q_i[y : y + 1]
                lo_r, lo_i, hi_r, hi_i = [], [], [], []
                for x_r, x_i in near:
                    t1, t2 = qq_r * x_r, qq_i * x_i
                    t3, t4 = qq_r * x_i, qq_i * x_r
                    lo_r.append(t1 - t2)
                    lo_i.append(t3 + t4)
                    hi_r.append(t1 + t2)
                    hi_i.append(t4 - t3)
                row = y * CX
                half = CX // 2
                left_ref[row : row + half, :] = jnp.concatenate(lo_r, axis=0).astype(jnp.bfloat16)
                left_ref[row + half : row + CX, :] = jnp.concatenate(hi_r, axis=0).astype(jnp.bfloat16)
                left_ref[cells + row : cells + row + half, :] = jnp.concatenate(lo_i, axis=0).astype(jnp.bfloat16)
                left_ref[cells + row + half : cells + row + CX, :] = jnp.concatenate(hi_i, axis=0).astype(jnp.bfloat16)
            for m in range(half_z // 16):
                z_r, z_i = complex_times((d_r[m : m + 1], d_i[m : m + 1]), (c_r, c_i))
                row = 16 * m
                right_ref[row : row + 16, :] = z_r.astype(jnp.bfloat16)
                right_ref[half_z + row : half_z + row + 16, :] = z_i.astype(jnp.bfloat16)
            acc_ref[f] += lax.dot_general(
                left_ref[...], right_ref[...], (((1,), (1,)), ((), ())), preferred_element_type=jnp.float32
            )
            return tuple(complex_times(now, turn) for now, turn in zip(state, ratio))

        lax.fori_loop(0, bins, per_bin, start, unroll=4)
        return carry

    def own_block():
        align_block(spec_ref[me], lag_ref[...], slow_ref[...], me, real_ref, imag_ref, turn_ref)
        lax.fori_loop(0, per_block, per_chunk, 0)

    exchange_inputs(
        spec_ref, lag_ref, slow_ref, spec_in, lag_in, slow_in, local_sem, send_sem, recv_sem, own_block, out_ref.shape[0] // 2
    )

    def align_other(shift, carry):
        source = lax.rem(me + shift, count)
        align_block(spec_in[source], lag_in[source], slow_in[source], source, real_ref, imag_ref, turn_ref)
        return carry

    lax.fori_loop(1, count, align_other, 0, unroll=True)
    lax.fori_loop(per_block, count * per_block, per_chunk, 0)
    cells = CX * CY
    low = jnp.zeros((cells, half_z), jnp.float32)
    high = jnp.zeros((cells, half_z), jnp.float32)
    for f in range(bins):
        sums = acc_ref[f]
        u, w = sums[:cells, :half_z], sums[:cells, half_z:]
        x, v = sums[cells:, :half_z], sums[cells:, half_z:]
        low = low + ((u - v) * (u - v) + (w + x) * (w + x))
        high = high + ((u + v) * (u + v) + (x - w) * (x - w))
    power_ref[:, :half_z] = low
    power_ref[:, half_z:] = high
    share_kernel(power_ref, out_ref, pieces, send_rs, recv_rs, send_ag, recv_ag, share_sem)


def beam_power(spec_send, lag_row, slow_rows, reach):
    count = spec_send.shape[0]
    slots = 2 * reach + 1
    cells = CX * CY
    bins, block = spec_send.shape[2], spec_send.shape[3]
    width = CHUNK
    stations = count * block
    vmem = pl.BlockSpec(memory_space=pltpu.VMEM)
    return pl.pallas_call(
        beam_kernel,
        out_shape=jax.ShapeDtypeStruct((slots, cells, CZ), jnp.float32),
        in_specs=[vmem, vmem, vmem],
        out_specs=vmem,
        scratch_shapes=[
            pltpu.VMEM((count,) + spec_send.shape[1:], jnp.bfloat16),
            pltpu.VMEM((count,) + lag_row.shape, jnp.int32),
            pltpu.VMEM((count,) + slow_rows.shape, jnp.bfloat16),
            pltpu.SemaphoreType.DMA((3,)),
            pltpu.SemaphoreType.DMA((3, count)),
            pltpu.SemaphoreType.DMA((3, count)),
            pltpu.VMEM((bins, stations), jnp.float32),
            pltpu.VMEM((bins, stations), jnp.float32),
            pltpu.VMEM((slow_rows.shape[0], stations), jnp.float32),
            pltpu.VMEM((bins, 2 * CX * CY, CZ), jnp.float32),
            pltpu.VMEM((2 * CX * CY, width), jnp.bfloat16),
            pltpu.VMEM((CZ, width), jnp.bfloat16),
            pltpu.VMEM((cells, CZ), jnp.float32),
            pltpu.VMEM((count, cells // count, CZ), jnp.float32),
            pltpu.SemaphoreType.DMA((count,)),
            pltpu.SemaphoreType.DMA((count,)),
            pltpu.SemaphoreType.DMA((slots, count)),
            pltpu.SemaphoreType.DMA((slots, count)),
            pltpu.SemaphoreType.DMA((1,)),
        ],
        compiler_params=pltpu.CompilerParams(collective_id=1, has_side_effects=True),
    )(spec_send, lag_row, slow_rows)


def share_kernel(part_ref, out_ref, pieces, send_rs, recv_rs, send_ag, recv_ag, local_sem):
    count = pieces.shape[0]
    slots = out_ref.shape[0]
    reach = slots // 2
    rows = pieces.shape[1]
    me = lax.axis_index("sta")
    tile = lax.axis_index("grid")
    tiles = lax.axis_size("grid")
    mesh_ids = pl.DeviceIdType.MESH
    own = pltpu.make_async_copy(part_ref.at[pl.ds(pl.multiple_of(me * rows, 8), rows)], pieces.at[me], local_sem.at[0])
    own.start()
    sends = []
    for shift in range(1, count):
        peer = lax.rem(me + shift, count)
        copy = pltpu.make_async_remote_copy(
            src_ref=part_ref.at[pl.ds(pl.multiple_of(peer * rows, 8), rows)],
            dst_ref=pieces.at[me],
            send_sem=send_rs.at[shift],
            recv_sem=recv_rs.at[me],
            device_id=(tile, peer),
            device_id_type=mesh_ids,
        )
        copy.start()
        sends.append(copy)
    own.wait()
    for copy in sends:
        copy.wait_send()
    for shift in range(1, count):
        source = lax.rem(me + count - shift, count)
        pltpu.make_async_remote_copy(
            src_ref=pieces.at[source],
            dst_ref=pieces.at[source],
            send_sem=send_rs.at[shift],
            recv_sem=recv_rs.at[source],
            device_id=(tile, source),
            device_id_type=mesh_ids,
        ).wait_recv()
    total = pieces[0]
    for source in range(1, count):
        total = total + pieces[source]
    mine = pl.ds(pl.multiple_of(me * rows, 8), rows)
    out_ref[reach, mine] = total
    block = out_ref.at[reach, mine]

    def gather_copy(k, peer, slot):
        return pltpu.make_async_remote_copy(
            src_ref=block,
            dst_ref=out_ref.at[slot, mine],
            send_sem=send_ag.at[slot, peer],
            recv_sem=recv_ag.at[slot, me],
            device_id=(tile + k, peer),
            device_id_type=mesh_ids,
        )

    peers = []
    for shift in range(1, count):
        copy = gather_copy(0, lax.rem(me + shift, count), reach)
        copy.start()
        peers.append(copy)
    for k in range(-reach, reach + 1):
        if k == 0:
            continue

        @pl.when(jnp.logical_not((tile + k >= 0) & (tile + k < tiles)))
        def _():
            out_ref[reach + k] = jnp.zeros(out_ref.shape[1:], out_ref.dtype)

    for copy in peers:
        copy.wait_send()
    for shift in range(1, count):
        source = lax.rem(me + count - shift, count)
        pltpu.make_async_remote_copy(
            src_ref=block,
            dst_ref=out_ref.at[reach, pl.ds(pl.multiple_of(source * rows, 8), rows)],
            send_sem=send_ag.at[reach, source],
            recv_sem=recv_ag.at[reach, source],
            device_id=(tile, source),
            device_id_type=mesh_ids,
        ).wait_recv()

    def halo_copy(k):
        return pltpu.make_async_remote_copy(
            src_ref=out_ref.at[reach],
            dst_ref=out_ref.at[reach - k],
            send_sem=send_ag.at[reach - k, me],
            recv_sem=recv_ag.at[reach - k, me],
            device_id=(tile + k, me),
            device_id_type=mesh_ids,
        )

    for k in range(-reach, reach + 1):
        if k == 0:
            continue

        @pl.when((tile + k >= 0) & (tile + k < tiles))
        def _():
            halo_copy(k).start()

    for k in range(-reach, reach + 1):
        if k == 0:
            continue

        @pl.when((tile + k >= 0) & (tile + k < tiles))
        def _():
            halo_copy(k).wait_send()
            pltpu.make_async_remote_copy(
                src_ref=out_ref.at[reach],
                dst_ref=out_ref.at[reach + k],
                send_sem=send_ag.at[reach + k, me],
                recv_sem=recv_ag.at[reach + k, me],
                device_id=(tile + k, me),
                device_id_type=mesh_ids,
            ).wait_recv()


def share_power(part, reach):
    count = lax.axis_size("sta")
    rows = part.shape[0] // count
    slots = 2 * reach + 1
    return pl.pallas_call(
        share_kernel,
        out_shape=jax.ShapeDtypeStruct((slots,) + part.shape, jnp.float32),
        in_specs=[pl.BlockSpec(memory_space=pltpu.VMEM)],
        out_specs=pl.BlockSpec(memory_space=pltpu.VMEM),
        scratch_shapes=[
            pltpu.VMEM((count, rows, part.shape[1]), jnp.float32),
            pltpu.SemaphoreType.DMA((count,)),
            pltpu.SemaphoreType.DMA((count,)),
            pltpu.SemaphoreType.DMA((slots, count)),
            pltpu.SemaphoreType.DMA((slots, count)),
            pltpu.SemaphoreType.DMA((1,)),
        ],
        compiler_params=pltpu.CompilerParams(collective_id=0, has_side_effects=True),
    )(part)


def freq_beams(freq_ids, aligned_rows, slow_rows):
    return lax.map(lambda pair: beam_freq(pair[0], pair[1], slow_rows), (freq_ids, aligned_rows))


def band_matrix(taps, length):
    rows = jnp.arange(length, dtype=jnp.int32)[:, None]
    columns = jnp.arange(length + 2 * HALF, dtype=jnp.int32)[None, :]
    offset = columns - rows
    picks = jnp.arange(TAPS, dtype=jnp.int32)[:, None, None]
    return jnp.sum(jnp.where(offset[None] == picks, taps[:, None, None], 0.0), axis=0)


def blur(volume, bands):
    band_x, square_y, square_z = bands
    padded = with_halo(volume.astype(jnp.bfloat16), (("grid", 0),), HALF).astype(volume.dtype)
    along_x = jnp.einsum("ip,pyz->iyz", band_x, padded, precision=lax.Precision.HIGHEST)
    along_y = jnp.einsum("jq,xqz->xjz", square_y, along_x, precision=lax.Precision.HIGHEST)
    return jnp.einsum("xyw,kw->xyk", along_y, square_z, precision=lax.Precision.HIGHEST)


def blur_narrowing(volume, taps, square_y, square_z):
    band_x = band_matrix(taps, volume.shape[0] - 2 * HALF)
    along_x = jnp.einsum("ip,pyz->iyz", band_x, volume, precision=lax.Precision.HIGHEST)
    along_y = jnp.einsum("jq,xqz->xjz", square_y, along_x, precision=lax.Precision.HIGHEST)
    return jnp.einsum("xyw,kw->xyk", along_y, square_z, precision=lax.Precision.HIGHEST)


def deblur(observed, halo_tiles, spread_taps):
    tiles = lax.axis_size("grid")
    me = lax.axis_index("grid")
    reach = ITERS * 2 * HALF
    cut = halo_tiles * CX - reach
    observed = observed[cut : observed.shape[0] - cut]
    width = observed.shape[0]
    cell = (me - halo_tiles) * CX + cut + jnp.arange(width, dtype=jnp.int32)
    inside = (cell >= 0) & (cell < tiles * CX)
    square_y = band_matrix(spread_taps[1], CY)[:, HALF : HALF + CY]
    square_z = band_matrix(spread_taps[2], CZ)[:, HALF : HALF + CZ]
    estimate = jnp.where(inside[:, None, None], observed, 0.0)
    for sweep in range(ITERS):
        low = 2 * HALF * sweep + HALF
        blurred = blur_narrowing(estimate, spread_taps[0], square_y, square_z)
        ratio = jnp.where(
            inside[low : width - low, None, None], observed[low : width - low] / blurred, 0.0
        )
        estimate = estimate[2 * HALF : estimate.shape[0] - 2 * HALF] * blur_narrowing(
            ratio, spread_taps[0], square_y, square_z
        )
    return estimate


def band_of(taps_ref, axis, rows, cols):
    offset = cols - rows + HALF
    band = jnp.zeros(offset.shape, jnp.float32)
    for tap in range(TAPS):
        band = jnp.where(offset == tap, taps_ref[axis, tap], band)
    return band


def mirror(index, length):
    return jnp.where(index < length // 2, index, 3 * (length // 2) - 1 - index)


def deblur_kernel(taps_ref, obs_ref, out_ref, kx_ref, kz_ref):
    tiles = lax.axis_size("grid")
    me = lax.axis_index("grid")
    planes, width, depth = obs_ref.shape
    shape_x = kx_ref.shape
    kx_ref[...] = band_of(
        taps_ref, 0, lax.broadcasted_iota(jnp.int32, shape_x, 0) + HALF, lax.broadcasted_iota(jnp.int32, shape_x, 1)
    )
    shape_z = kz_ref.shape
    kz_ref[...] = band_of(
        taps_ref,
        2,
        mirror(lax.broadcasted_iota(jnp.int32, shape_z, 1), depth),
        mirror(lax.broadcasted_iota(jnp.int32, shape_z, 0), depth),
    )
    halo_tiles = (width - CX) // (2 * CX)
    highest = lax.Precision.HIGHEST

    def inside(low, size):
        cell = (me - halo_tiles) * CX + low + lax.broadcasted_iota(jnp.int32, (size, depth), 0)
        return (cell >= 0) & (cell < tiles * CX)

    lanes = planes * depth

    def blur(volume):
        size_in = volume.shape[0]
        size_out = size_in - 2 * HALF
        band = kx_ref[0:size_out, 0:size_in]
        along_x = jnp.dot(band, volume, precision=highest, preferred_element_type=jnp.float32)
        along_y = []
        for y in range(planes):
            total = None
            for q in range(planes):
                term = taps_ref[1, q - y + HALF] * along_x[:, q * depth : (q + 1) * depth]
                total = term if total is None else total + term
            along_y.append(total)
        joined = jnp.concatenate(along_y, axis=0)
        along_z = jnp.dot(joined, kz_ref[...], precision=highest, preferred_element_type=jnp.float32)
        return jnp.concatenate([along_z[y * size_out : (y + 1) * size_out] for y in range(planes)], axis=1)

    def inside_wide(low, size):
        cell = (me - halo_tiles) * CX + low + lax.broadcasted_iota(jnp.int32, (size, lanes), 0)
        return (cell >= 0) & (cell < tiles * CX)

    observed = jnp.concatenate([obs_ref[y] for y in range(planes)], axis=1)
    estimate = jnp.where(inside_wide(0, width), observed, 0.0)
    for sweep in range(ITERS):
        low = 2 * HALF * sweep + HALF
        blurred = blur(estimate)
        size = blurred.shape[0]
        ratio = jnp.where(inside_wide(low, size), observed[low : low + size] / blurred, 0.0)
        spread = blur(ratio)
        estimate = estimate[2 * HALF : 2 * HALF + spread.shape[0]] * spread
    for y in range(planes):
        out_ref[y] = estimate[:, y * depth : (y + 1) * depth]


def deblur_tile(observed, spread_taps):
    planes, width, depth = observed.shape
    vmem = pl.BlockSpec(memory_space=pltpu.VMEM)
    return pl.pallas_call(
        deblur_kernel,
        out_shape=jax.ShapeDtypeStruct((planes, CX, depth), jnp.float32),
        in_specs=[pl.BlockSpec(memory_space=pltpu.SMEM), vmem],
        out_specs=vmem,
        scratch_shapes=[
            pltpu.VMEM((width - 2 * HALF, width), jnp.float32),
            pltpu.VMEM((depth, depth), jnp.float32),
        ],
    )(spread_taps, observed)


def per_device(spectra, lag_samples, slowness, spread_taps):
    groups = lax.axis_size("sta")
    own_count = FREQS // groups
    first_bin = lax.axis_index("sta") * own_count
    block = spectra.shape[2]
    spec_send = spectra.reshape(groups, own_count, 2, block).transpose(0, 2, 1, 3)
    halo_tiles = -(-(ITERS * 2 * HALF) // CX)
    summed = beam_power(spec_send, lag_samples, slowness[0], halo_tiles)
    observed = summed / (FREQS * STATIONS) + BACKGROUND
    slots = observed.shape[0]
    observed = observed.reshape(slots, CY, CX, CZ)
    observed = jnp.concatenate([observed[:, :, : CX // 2], observed[:, :, CX // 2 :][:, :, ::-1]], axis=2)
    planes = observed.transpose(1, 0, 2, 3).reshape(CY, slots * CX, CZ)
    estimate = deblur_tile(planes, spread_taps)
    both = jnp.stack([observed[halo_tiles], estimate])
    both = jnp.concatenate([both[..., : CZ // 2], both[..., CZ // 2 :][..., ::-1]], axis=-1).transpose(0, 2, 1, 3)
    stacked, estimate = both[0], both[1]
    return (stacked[None], estimate[None])


def solution(mesh):
    placed = (P(None, None, "sta"), P("grid", "sta"), P("grid", None, "sta"), P())
    return jax.shard_map(
        per_device,
        mesh=mesh,
        in_specs=placed,
        out_specs=(P("grid", None, None, None), P("grid", None, None, None)),
        check_vma=False,
    )
```

```python
import math

import jax
import jax.numpy as jnp
from jax import lax
from jax.sharding import PartitionSpec as P
from jax.experimental import pallas as pl
from jax.experimental.pallas import tpu as pltpu

STATIONS = 6144
FREQS = 64
F0 = 600
NT = 6000
TAPS = 17
HALF = 8
ITERS = 4
CX = 32
CY = 8
CZ = 128


TWO_PI = 2.0 * math.pi
BACKGROUND = 0.05


def with_halo(array, sides, width):
    for axis, dim in sides:
        size, length = (lax.axis_size(axis), array.shape[dim])
        up = [(i, (i + 1) % size) for i in range(size - 1)]
        down = [(j, i) for i, j in up]
        last = lax.slice_in_dim(array, length - width, length, axis=dim)
        leading = lax.slice_in_dim(array, 0, width, axis=dim)
        before = lax.ppermute(last, axis, up)
        after = lax.ppermute(leading, axis, down)
        array = jnp.concatenate([before, array, after], axis=dim)
    return array


def align_rows(spectra, lag_row):
    bins = F0 + jnp.arange(FREQS, dtype=jnp.int32)
    cycles = bins[:, None] * lag_row[None, :] % NT
    turned = cycles.astype(jnp.float32) * (TWO_PI / NT)
    cosine = jnp.cos(turned)
    sine = jnp.sin(turned)
    real_in = spectra[:, 0, :].astype(jnp.float32)
    imag_in = spectra[:, 1, :].astype(jnp.float32)
    real_out = real_in * cosine + imag_in * sine
    imag_out = imag_in * cosine - real_in * sine
    return jnp.stack([real_out, imag_out], axis=1).astype(jnp.bfloat16)


def beam_freq(freq, aligned_row, slow_rows):
    omega = (F0 + freq).astype(jnp.float32) * (TWO_PI / NT)
    slow = slow_rows.astype(jnp.float32)
    x_coord = jnp.arange(CX, dtype=jnp.float32) - (CX - 1) / 2.0
    y_coord = jnp.arange(CY, dtype=jnp.float32) - (CY - 1) / 2.0
    z_coord = jnp.arange(CZ, dtype=jnp.float32) - (CZ - 1) / 2.0
    phase_x = (omega * slow[0])[None, :] * x_coord[:, None]
    phase_y = (omega * slow[1])[None, :] * y_coord[:, None]
    phase = phase_x[:, None, :] + phase_y[None, :, :]
    cosine = jnp.cos(phase)
    sine = jnp.sin(phase)
    real_in = aligned_row[0].astype(jnp.float32)[None, None, :]
    imag_in = aligned_row[1].astype(jnp.float32)[None, None, :]
    front_real = (real_in * cosine + imag_in * sine).astype(jnp.bfloat16).reshape(CX * CY, -1)
    front_imag = (imag_in * cosine - real_in * sine).astype(jnp.bfloat16).reshape(CX * CY, -1)
    left_side = jnp.concatenate([front_real, front_imag], axis=1)
    phase_z = (omega * slow[2])[:, None] * z_coord[None, :]
    depth_real = jnp.cos(phase_z).astype(jnp.bfloat16)
    depth_imag = jnp.sin(phase_z).astype(jnp.bfloat16)
    upper_rows = jnp.concatenate([depth_real, -depth_imag], axis=1)
    lower_rows = jnp.concatenate([depth_imag, depth_real], axis=1)
    right_side = jnp.concatenate([upper_rows, lower_rows], axis=0)
    return jnp.dot(left_side, right_side, preferred_element_type=jnp.float32)


CHUNK = 768


def exp_neg(angle):
    return jnp.cos(angle), -jnp.sin(angle)


def enter_barrier(count, reach):
    me = lax.axis_index("sta")
    tile = lax.axis_index("grid")
    tiles = lax.axis_size("grid")
    mesh_ids = pl.DeviceIdType.MESH
    barrier = pltpu.get_barrier_semaphore()
    for shift in range(1, count):
        pl.semaphore_signal(barrier, inc=1, device_id=(tile, lax.rem(me + shift, count)), device_id_type=mesh_ids)
    neighbours = jnp.int32(0)
    for k in range(-reach, reach + 1):
        if k == 0:
            continue
        there = (tile + k >= 0) & (tile + k < tiles)
        neighbours = neighbours + there.astype(jnp.int32)

        @pl.when(there)
        def _():
            pl.semaphore_signal(barrier, inc=1, device_id=(tile + k, me), device_id_type=mesh_ids)

    pl.semaphore_wait(barrier, count - 1 + neighbours)


def exchange_inputs(spec_ref, lag_ref, slow_ref, spec_in, lag_in, slow_in, local_sem, send_sem, recv_sem, then, reach):
    count = spec_in.shape[0]
    me = lax.axis_index("sta")
    tile = lax.axis_index("grid")
    mesh_ids = pl.DeviceIdType.MESH
    enter_barrier(count, reach)
    pairs = ((spec_ref, spec_in), (lag_ref, lag_in), (slow_ref, slow_in))
    local = []
    for kind, (source, target) in enumerate(pairs):
        own = source.at[me] if kind == 0 else source
        copy = pltpu.make_async_copy(own, target.at[me], local_sem.at[kind])
        copy.start()
        local.append(copy)
    sends = []
    for shift in range(1, count):
        peer = lax.rem(me + shift, count)
        for kind, (source, target) in enumerate(pairs):
            part = source.at[peer] if kind == 0 else source
            copy = pltpu.make_async_remote_copy(
                src_ref=part,
                dst_ref=target.at[me],
                send_sem=send_sem.at[kind, shift],
                recv_sem=recv_sem.at[kind, me],
                device_id=(tile, peer),
                device_id_type=mesh_ids,
            )
            copy.start()
            sends.append(copy)
    then()
    for copy in local:
        copy.wait()
    for copy in sends:
        copy.wait_send()
    for shift in range(1, count):
        source_id = lax.rem(me + count - shift, count)
        for kind, (source, target) in enumerate(pairs):
            part = source.at[source_id] if kind == 0 else source
            pltpu.make_async_remote_copy(
                src_ref=part,
                dst_ref=target.at[source_id],
                send_sem=send_sem.at[kind, shift],
                recv_sem=recv_sem.at[kind, source_id],
                device_id=(tile, source_id),
                device_id_type=mesh_ids,
            ).wait_recv()


def align_block(spec, lag, slow, source, real_ref, imag_ref, turn_ref):
    bins, block = spec.shape[1], spec.shape[2]
    first_bin = lax.axis_index("sta") * bins
    bin_rows = (F0 + first_bin + lax.broadcasted_iota(jnp.int32, (bins, block), 0)).astype(jnp.float32)
    cols = pl.ds(pl.multiple_of(source * block, 128), block)
    product = bin_rows * lag.astype(jnp.float32)
    whole = jnp.floor(product * (1.0 / NT))
    left = product - whole * NT
    left = jnp.where(left < 0.0, left + NT, left)
    left = jnp.where(left >= NT, left - NT, left)
    turned = left * (TWO_PI / NT)
    cosine = jnp.cos(turned)
    sine = jnp.sin(turned)
    real_in = spec[0].astype(jnp.float32)
    imag_in = spec[1].astype(jnp.float32)
    real_ref[:, cols] = (real_in * cosine + imag_in * sine).astype(jnp.bfloat16).astype(jnp.float32)
    imag_ref[:, cols] = (imag_in * cosine - real_in * sine).astype(jnp.bfloat16).astype(jnp.float32)
    turn_ref[:, cols] = slow.astype(jnp.float32)


def complex_times(left, right):
    return left[0] * right[0] - left[1] * right[1], left[0] * right[1] + left[1] * right[0]


def factor_rows(turn_x, turn_y, turn_z, rows8, rows16):
    return (
        exp_neg(turn_x * (rows8 - 3.5)),
        exp_neg(turn_x * (8.0 * (rows8 - 1.5))),
        exp_neg(turn_y * (rows8 - 3.5)),
        exp_neg(turn_z * (rows16 - 7.5)),
        exp_neg(turn_z * (16.0 * (rows8 - 3.5))),
    )


def beam_kernel(spec_ref, lag_ref, slow_ref, out_ref, spec_in, lag_in, slow_in, local_sem, send_sem, recv_sem,
                real_ref, imag_ref, turn_ref, acc_ref, left_ref, right_ref, power_ref, pieces, send_rs, recv_rs,
                send_ag, recv_ag, share_sem):
    count, bins, block = spec_in.shape[0], spec_in.shape[2], spec_in.shape[3]
    me = lax.axis_index("sta")
    first_bin = me * bins
    width = CHUNK
    per_block = block // width
    half_z = CZ // 2
    rows8 = lax.broadcasted_iota(jnp.int32, (8, width), 0).astype(jnp.float32)
    rows16 = lax.broadcasted_iota(jnp.int32, (16, width), 0).astype(jnp.float32)
    omega0 = (F0 + first_bin).astype(jnp.float32) * (TWO_PI / NT)
    step = TWO_PI / NT
    acc_ref[...] = jnp.zeros_like(acc_ref)

    def per_chunk(k, carry):
        source = lax.rem(me + k // per_block, count)
        cols = pl.ds(pl.multiple_of(source * block + lax.rem(k, per_block) * width, 128), width)
        slow_x = turn_ref[0:1, cols]
        slow_y = turn_ref[1:2, cols]
        slow_z = turn_ref[2:3, cols]
        start = factor_rows(omega0 * slow_x, omega0 * slow_y, omega0 * slow_z, rows8, rows16)
        ratio = factor_rows(step * slow_x, step * slow_y, step * slow_z, rows8, rows16)

        def per_bin(f, state):
            (a_r, a_i), (b_r, b_i), (y_r, y_i), (c_r, c_i), (d_r, d_i) = state
            real_in = real_ref[pl.ds(f, 1), cols]
            imag_in = imag_ref[pl.ds(f, 1), cols]
            q_r = real_in * y_r - imag_in * y_i
            q_i = real_in * y_i + imag_in * y_r
            near = [complex_times((b_r[m : m + 1], b_i[m : m + 1]), (a_r, a_i)) for m in range(CX // 16)]
            cells = CX * CY
            for y in range(CY):
                qq_r, qq_i = q_r[y : y + 1], q_i[y : y + 1]
                lo_r, lo_i, hi_r, hi_i = [], [], [], []
                for x_r, x_i in near:
                    t1, t2 = qq_r * x_r, qq_i * x_i
                    t3, t4 = qq_r * x_i, qq_i * x_r
                    lo_r.append(t1 - t2)
                    lo_i.append(t3 + t4)
                    hi_r.append(t1 + t2)
                    hi_i.append(t4 - t3)
                row = y * CX
                half = CX // 2
                left_ref[row : row + half, :] = jnp.concatenate(lo_r, axis=0).astype(jnp.bfloat16)
                left_ref[row + half : row + CX, :] = jnp.concatenate(hi_r, axis=0).astype(jnp.bfloat16)
                left_ref[cells + row : cells + row + half, :] = jnp.concatenate(lo_i, axis=0).astype(jnp.bfloat16)
                left_ref[cells + row + half : cells + row + CX, :] = jnp.concatenate(hi_i, axis=0).astype(jnp.bfloat16)
            for m in range(half_z // 16):
                z_r, z_i = complex_times((d_r[m : m + 1], d_i[m : m + 1]), (c_r, c_i))
                row = 16 * m
                right_ref[row : row + 16, :] = z_r.astype(jnp.bfloat16)
                right_ref[half_z + row : half_z + row + 16, :] = z_i.astype(jnp.bfloat16)
            acc_ref[f] += lax.dot_general(
                left_ref[...], right_ref[...], (((1,), (1,)), ((), ())), preferred_element_type=jnp.float32
            )
            return tuple(complex_times(now, turn) for now, turn in zip(state, ratio))

        lax.fori_loop(0, bins, per_bin, start, unroll=4)
        return carry

    def own_block():
        align_block(spec_ref[me], lag_ref[...], slow_ref[...], me, real_ref, imag_ref, turn_ref)
        lax.fori_loop(0, per_block, per_chunk, 0)

    exchange_inputs(
        spec_ref, lag_ref, slow_ref, spec_in, lag_in, slow_in, local_sem, send_sem, recv_sem, own_block, out_ref.shape[0] // 2
    )

    def align_other(shift, carry):
        source = lax.rem(me + shift, count)
        align_block(spec_in[source], lag_in[source], slow_in[source], source, real_ref, imag_ref, turn_ref)
        return carry

    lax.fori_loop(1, count, align_other, 0)
    lax.fori_loop(per_block, count * per_block, per_chunk, 0)
    cells = CX * CY
    low = jnp.zeros((cells, half_z), jnp.float32)
    high = jnp.zeros((cells, half_z), jnp.float32)
    for f in range(bins):
        sums = acc_ref[f]
        u, w = sums[:cells, :half_z], sums[:cells, half_z:]
        x, v = sums[cells:, :half_z], sums[cells:, half_z:]
        low = low + ((u - v) * (u - v) + (w + x) * (w + x))
        high = high + ((u + v) * (u + v) + (x - w) * (x - w))
    power_ref[:, :half_z] = low
    power_ref[:, half_z:] = high
    share_kernel(power_ref, out_ref, pieces, send_rs, recv_rs, send_ag, recv_ag, share_sem)


def beam_power(spec_send, lag_row, slow_rows, reach):
    count = spec_send.shape[0]
    slots = 2 * reach + 1
    cells = CX * CY
    bins, block = spec_send.shape[2], spec_send.shape[3]
    width = CHUNK
    stations = count * block
    vmem = pl.BlockSpec(memory_space=pltpu.VMEM)
    return pl.pallas_call(
        beam_kernel,
        out_shape=jax.ShapeDtypeStruct((slots, cells, CZ), jnp.float32),
        in_specs=[vmem, vmem, vmem],
        out_specs=vmem,
        scratch_shapes=[
            pltpu.VMEM((count,) + spec_send.shape[1:], jnp.bfloat16),
            pltpu.VMEM((count,) + lag_row.shape, jnp.int32),
            pltpu.VMEM((count,) + slow_rows.shape, jnp.bfloat16),
            pltpu.SemaphoreType.DMA((3,)),
            pltpu.SemaphoreType.DMA((3, count)),
            pltpu.SemaphoreType.DMA((3, count)),
            pltpu.VMEM((bins, stations), jnp.float32),
            pltpu.VMEM((bins, stations), jnp.float32),
            pltpu.VMEM((slow_rows.shape[0], stations), jnp.float32),
            pltpu.VMEM((bins, 2 * CX * CY, CZ), jnp.float32),
            pltpu.VMEM((2 * CX * CY, width), jnp.bfloat16),
            pltpu.VMEM((CZ, width), jnp.bfloat16),
            pltpu.VMEM((cells, CZ), jnp.float32),
            pltpu.VMEM((count, cells // count, CZ), jnp.float32),
            pltpu.SemaphoreType.DMA((count,)),
            pltpu.SemaphoreType.DMA((count,)),
            pltpu.SemaphoreType.DMA((slots, count)),
            pltpu.SemaphoreType.DMA((slots, count)),
            pltpu.SemaphoreType.DMA((1,)),
        ],
        compiler_params=pltpu.CompilerParams(collective_id=1, has_side_effects=True),
    )(spec_send, lag_row, slow_rows)


def share_kernel(part_ref, out_ref, pieces, send_rs, recv_rs, send_ag, recv_ag, local_sem):
    count = pieces.shape[0]
    slots = out_ref.shape[0]
    reach = slots // 2
    rows = pieces.shape[1]
    me = lax.axis_index("sta")
    tile = lax.axis_index("grid")
    tiles = lax.axis_size("grid")
    mesh_ids = pl.DeviceIdType.MESH
    own = pltpu.make_async_copy(part_ref.at[pl.ds(pl.multiple_of(me * rows, 8), rows)], pieces.at[me], local_sem.at[0])
    own.start()
    sends = []
    for shift in range(1, count):
        peer = lax.rem(me + shift, count)
        copy = pltpu.make_async_remote_copy(
            src_ref=part_ref.at[pl.ds(pl.multiple_of(peer * rows, 8), rows)],
            dst_ref=pieces.at[me],
            send_sem=send_rs.at[shift],
            recv_sem=recv_rs.at[me],
            device_id=(tile, peer),
            device_id_type=mesh_ids,
        )
        copy.start()
        sends.append(copy)
    own.wait()
    for copy in sends:
        copy.wait_send()
    for shift in range(1, count):
        source = lax.rem(me + count - shift, count)
        pltpu.make_async_remote_copy(
            src_ref=pieces.at[source],
            dst_ref=pieces.at[source],
            send_sem=send_rs.at[shift],
            recv_sem=recv_rs.at[source],
            device_id=(tile, source),
            device_id_type=mesh_ids,
        ).wait_recv()
    total = pieces[0]
    for source in range(1, count):
        total = total + pieces[source]
    mine = pl.ds(pl.multiple_of(me * rows, 8), rows)
    out_ref[reach, mine] = total
    block = out_ref.at[reach, mine]

    def gather_copy(k, peer, slot):
        return pltpu.make_async_remote_copy(
            src_ref=block,
            dst_ref=out_ref.at[slot, mine],
            send_sem=send_ag.at[slot, peer],
            recv_sem=recv_ag.at[slot, me],
            device_id=(tile + k, peer),
            device_id_type=mesh_ids,
        )

    peers = []
    for shift in range(1, count):
        copy = gather_copy(0, lax.rem(me + shift, count), reach)
        copy.start()
        peers.append(copy)
    for k in range(-reach, reach + 1):
        if k == 0:
            continue

        @pl.when(jnp.logical_not((tile + k >= 0) & (tile + k < tiles)))
        def _():
            out_ref[reach + k] = jnp.zeros(out_ref.shape[1:], out_ref.dtype)

    for copy in peers:
        copy.wait_send()
    for shift in range(1, count):
        source = lax.rem(me + count - shift, count)
        pltpu.make_async_remote_copy(
            src_ref=block,
            dst_ref=out_ref.at[reach, pl.ds(pl.multiple_of(source * rows, 8), rows)],
            send_sem=send_ag.at[reach, source],
            recv_sem=recv_ag.at[reach, source],
            device_id=(tile, source),
            device_id_type=mesh_ids,
        ).wait_recv()

    def halo_copy(k):
        return pltpu.make_async_remote_copy(
            src_ref=out_ref.at[reach],
            dst_ref=out_ref.at[reach - k],
            send_sem=send_ag.at[reach - k, me],
            recv_sem=recv_ag.at[reach - k, me],
            device_id=(tile + k, me),
            device_id_type=mesh_ids,
        )

    for k in range(-reach, reach + 1):
        if k == 0:
            continue

        @pl.when((tile + k >= 0) & (tile + k < tiles))
        def _():
            halo_copy(k).start()

    for k in range(-reach, reach + 1):
        if k == 0:
            continue

        @pl.when((tile + k >= 0) & (tile + k < tiles))
        def _():
            halo_copy(k).wait_send()
            pltpu.make_async_remote_copy(
                src_ref=out_ref.at[reach],
                dst_ref=out_ref.at[reach + k],
                send_sem=send_ag.at[reach + k, me],
                recv_sem=recv_ag.at[reach + k, me],
                device_id=(tile + k, me),
                device_id_type=mesh_ids,
            ).wait_recv()


def share_power(part, reach):
    count = lax.axis_size("sta")
    rows = part.shape[0] // count
    slots = 2 * reach + 1
    return pl.pallas_call(
        share_kernel,
        out_shape=jax.ShapeDtypeStruct((slots,) + part.shape, jnp.float32),
        in_specs=[pl.BlockSpec(memory_space=pltpu.VMEM)],
        out_specs=pl.BlockSpec(memory_space=pltpu.VMEM),
        scratch_shapes=[
            pltpu.VMEM((count, rows, part.shape[1]), jnp.float32),
            pltpu.SemaphoreType.DMA((count,)),
            pltpu.SemaphoreType.DMA((count,)),
            pltpu.SemaphoreType.DMA((slots, count)),
            pltpu.SemaphoreType.DMA((slots, count)),
            pltpu.SemaphoreType.DMA((1,)),
        ],
        compiler_params=pltpu.CompilerParams(collective_id=0, has_side_effects=True),
    )(part)


def freq_beams(freq_ids, aligned_rows, slow_rows):
    return lax.map(lambda pair: beam_freq(pair[0], pair[1], slow_rows), (freq_ids, aligned_rows))


def band_matrix(taps, length):
    rows = jnp.arange(length, dtype=jnp.int32)[:, None]
    columns = jnp.arange(length + 2 * HALF, dtype=jnp.int32)[None, :]
    offset = columns - rows
    picks = jnp.arange(TAPS, dtype=jnp.int32)[:, None, None]
    return jnp.sum(jnp.where(offset[None] == picks, taps[:, None, None], 0.0), axis=0)


def blur(volume, bands):
    band_x, square_y, square_z = bands
    padded = with_halo(volume.astype(jnp.bfloat16), (("grid", 0),), HALF).astype(volume.dtype)
    along_x = jnp.einsum("ip,pyz->iyz", band_x, padded, precision=lax.Precision.HIGHEST)
    along_y = jnp.einsum("jq,xqz->xjz", square_y, along_x, precision=lax.Precision.HIGHEST)
    return jnp.einsum("xyw,kw->xyk", along_y, square_z, precision=lax.Precision.HIGHEST)


def blur_narrowing(volume, taps, square_y, square_z):
    band_x = band_matrix(taps, volume.shape[0] - 2 * HALF)
    along_x = jnp.einsum("ip,pyz->iyz", band_x, volume, precision=lax.Precision.HIGHEST)
    along_y = jnp.einsum("jq,xqz->xjz", square_y, along_x, precision=lax.Precision.HIGHEST)
    return jnp.einsum("xyw,kw->xyk", along_y, square_z, precision=lax.Precision.HIGHEST)


def deblur(observed, halo_tiles, spread_taps):
    tiles = lax.axis_size("grid")
    me = lax.axis_index("grid")
    reach = ITERS * 2 * HALF
    cut = halo_tiles * CX - reach
    observed = observed[cut : observed.shape[0] - cut]
    width = observed.shape[0]
    cell = (me - halo_tiles) * CX + cut + jnp.arange(width, dtype=jnp.int32)
    inside = (cell >= 0) & (cell < tiles * CX)
    square_y = band_matrix(spread_taps[1], CY)[:, HALF : HALF + CY]
    square_z = band_matrix(spread_taps[2], CZ)[:, HALF : HALF + CZ]
    estimate = jnp.where(inside[:, None, None], observed, 0.0)
    for sweep in range(ITERS):
        low = 2 * HALF * sweep + HALF
        blurred = blur_narrowing(estimate, spread_taps[0], square_y, square_z)
        ratio = jnp.where(
            inside[low : width - low, None, None], observed[low : width - low] / blurred, 0.0
        )
        estimate = estimate[2 * HALF : estimate.shape[0] - 2 * HALF] * blur_narrowing(
            ratio, spread_taps[0], square_y, square_z
        )
    return estimate


def band_of(taps_ref, axis, rows, cols):
    offset = cols - rows + HALF
    band = jnp.zeros(offset.shape, jnp.float32)
    for tap in range(TAPS):
        band = jnp.where(offset == tap, taps_ref[axis, tap], band)
    return band


def mirror(index, length):
    return jnp.where(index < length // 2, index, 3 * (length // 2) - 1 - index)


def deblur_kernel(taps_ref, obs_ref, out_ref, kx_ref, kz_ref):
    tiles = lax.axis_size("grid")
    me = lax.axis_index("grid")
    planes, width, depth = obs_ref.shape
    shape_x = kx_ref.shape
    kx_ref[...] = band_of(
        taps_ref, 0, lax.broadcasted_iota(jnp.int32, shape_x, 0) + HALF, lax.broadcasted_iota(jnp.int32, shape_x, 1)
    )
    shape_z = kz_ref.shape
    kz_ref[...] = band_of(
        taps_ref,
        2,
        mirror(lax.broadcasted_iota(jnp.int32, shape_z, 1), depth),
        mirror(lax.broadcasted_iota(jnp.int32, shape_z, 0), depth),
    )
    halo_tiles = (width - CX) // (2 * CX)
    highest = lax.Precision.HIGH

    def inside(low, size):
        cell = (me - halo_tiles) * CX + low + lax.broadcasted_iota(jnp.int32, (size, depth), 0)
        return (cell >= 0) & (cell < tiles * CX)

    lanes = planes * depth

    def blur(volume):
        size_in = volume.shape[0]
        size_out = size_in - 2 * HALF
        band = kx_ref[0:size_out, 0:size_in]
        along_x = jnp.dot(band, volume, precision=highest, preferred_element_type=jnp.float32)
        along_y = []
        for y in range(planes):
            total = None
            for q in range(planes):
                term = taps_ref[1, q - y + HALF] * along_x[:, q * depth : (q + 1) * depth]
                total = term if total is None else total + term
            along_y.append(total)
        joined = jnp.concatenate(along_y, axis=0)
        along_z = jnp.dot(joined, kz_ref[...], precision=highest, preferred_element_type=jnp.float32)
        return jnp.concatenate([along_z[y * size_out : (y + 1) * size_out] for y in range(planes)], axis=1)

    def inside_wide(low, size):
        cell = (me - halo_tiles) * CX + low + lax.broadcasted_iota(jnp.int32, (size, lanes), 0)
        return (cell >= 0) & (cell < tiles * CX)

    observed = jnp.concatenate([obs_ref[y] for y in range(planes)], axis=1)
    estimate = jnp.where(inside_wide(0, width), observed, 0.0)
    for sweep in range(ITERS):
        low = 2 * HALF * sweep + HALF
        blurred = blur(estimate)
        size = blurred.shape[0]
        ratio = jnp.where(inside_wide(low, size), observed[low : low + size] / blurred, 0.0)
        spread = blur(ratio)
        estimate = estimate[2 * HALF : 2 * HALF + spread.shape[0]] * spread
    for y in range(planes):
        out_ref[y] = estimate[:, y * depth : (y + 1) * depth]


def deblur_tile(observed, spread_taps):
    planes, width, depth = observed.shape
    vmem = pl.BlockSpec(memory_space=pltpu.VMEM)
    return pl.pallas_call(
        deblur_kernel,
        out_shape=jax.ShapeDtypeStruct((planes, CX, depth), jnp.float32),
        in_specs=[pl.BlockSpec(memory_space=pltpu.SMEM), vmem],
        out_specs=vmem,
        scratch_shapes=[
            pltpu.VMEM((width - 2 * HALF, width), jnp.float32),
            pltpu.VMEM((depth, depth), jnp.float32),
        ],
    )(spread_taps, observed)


def per_device(spectra, lag_samples, slowness, spread_taps):
    groups = lax.axis_size("sta")
    own_count = FREQS // groups
    first_bin = lax.axis_index("sta") * own_count
    block = spectra.shape[2]
    spec_send = spectra.reshape(groups, own_count, 2, block).transpose(0, 2, 1, 3)
    halo_tiles = -(-(ITERS * 2 * HALF) // CX)
    summed = beam_power(spec_send, lag_samples, slowness[0], halo_tiles)
    observed = summed / (FREQS * STATIONS) + BACKGROUND
    slots = observed.shape[0]
    observed = observed.reshape(slots, CY, CX, CZ)
    observed = jnp.concatenate([observed[:, :, : CX // 2], observed[:, :, CX // 2 :][:, :, ::-1]], axis=2)
    planes = observed.transpose(1, 0, 2, 3).reshape(CY, slots * CX, CZ)
    estimate = deblur_tile(planes, spread_taps)
    both = jnp.stack([observed[halo_tiles], estimate])
    both = jnp.concatenate([both[..., : CZ // 2], both[..., CZ // 2 :][..., ::-1]], axis=-1).transpose(0, 2, 1, 3)
    stacked, estimate = both[0], both[1]
    return (stacked[None], estimate[None])


def solution(mesh):
    placed = (P(None, None, "sta"), P("grid", "sta"), P("grid", None, "sta"), P())
    return jax.shard_map(
        per_device,
        mesh=mesh,
        in_specs=placed,
        out_specs=(P("grid", None, None, None), P("grid", None, None, None)),
        check_vma=False,
    )
```

```python
import math

import jax
import jax.numpy as jnp
from jax import lax
from jax.sharding import PartitionSpec as P
from jax.experimental import pallas as pl
from jax.experimental.pallas import tpu as pltpu

STATIONS = 6144
FREQS = 64
F0 = 600
NT = 6000
TAPS = 17
HALF = 8
ITERS = 4
CX = 32
CY = 8
CZ = 128


TWO_PI = 2.0 * math.pi
BACKGROUND = 0.05


def with_halo(array, sides, width):
    for axis, dim in sides:
        size, length = (lax.axis_size(axis), array.shape[dim])
        up = [(i, (i + 1) % size) for i in range(size - 1)]
        down = [(j, i) for i, j in up]
        last = lax.slice_in_dim(array, length - width, length, axis=dim)
        leading = lax.slice_in_dim(array, 0, width, axis=dim)
        before = lax.ppermute(last, axis, up)
        after = lax.ppermute(leading, axis, down)
        array = jnp.concatenate([before, array, after], axis=dim)
    return array


def align_rows(spectra, lag_row):
    bins = F0 + jnp.arange(FREQS, dtype=jnp.int32)
    cycles = bins[:, None] * lag_row[None, :] % NT
    turned = cycles.astype(jnp.float32) * (TWO_PI / NT)
    cosine = jnp.cos(turned)
    sine = jnp.sin(turned)
    real_in = spectra[:, 0, :].astype(jnp.float32)
    imag_in = spectra[:, 1, :].astype(jnp.float32)
    real_out = real_in * cosine + imag_in * sine
    imag_out = imag_in * cosine - real_in * sine
    return jnp.stack([real_out, imag_out], axis=1).astype(jnp.bfloat16)


def beam_freq(freq, aligned_row, slow_rows):
    omega = (F0 + freq).astype(jnp.float32) * (TWO_PI / NT)
    slow = slow_rows.astype(jnp.float32)
    x_coord = jnp.arange(CX, dtype=jnp.float32) - (CX - 1) / 2.0
    y_coord = jnp.arange(CY, dtype=jnp.float32) - (CY - 1) / 2.0
    z_coord = jnp.arange(CZ, dtype=jnp.float32) - (CZ - 1) / 2.0
    phase_x = (omega * slow[0])[None, :] * x_coord[:, None]
    phase_y = (omega * slow[1])[None, :] * y_coord[:, None]
    phase = phase_x[:, None, :] + phase_y[None, :, :]
    cosine = jnp.cos(phase)
    sine = jnp.sin(phase)
    real_in = aligned_row[0].astype(jnp.float32)[None, None, :]
    imag_in = aligned_row[1].astype(jnp.float32)[None, None, :]
    front_real = (real_in * cosine + imag_in * sine).astype(jnp.bfloat16).reshape(CX * CY, -1)
    front_imag = (imag_in * cosine - real_in * sine).astype(jnp.bfloat16).reshape(CX * CY, -1)
    left_side = jnp.concatenate([front_real, front_imag], axis=1)
    phase_z = (omega * slow[2])[:, None] * z_coord[None, :]
    depth_real = jnp.cos(phase_z).astype(jnp.bfloat16)
    depth_imag = jnp.sin(phase_z).astype(jnp.bfloat16)
    upper_rows = jnp.concatenate([depth_real, -depth_imag], axis=1)
    lower_rows = jnp.concatenate([depth_imag, depth_real], axis=1)
    right_side = jnp.concatenate([upper_rows, lower_rows], axis=0)
    return jnp.dot(left_side, right_side, preferred_element_type=jnp.float32)


CHUNK = 768


def exp_neg(angle):
    return jnp.cos(angle), -jnp.sin(angle)


def enter_barrier(count, reach):
    me = lax.axis_index("sta")
    tile = lax.axis_index("grid")
    tiles = lax.axis_size("grid")
    mesh_ids = pl.DeviceIdType.MESH
    barrier = pltpu.get_barrier_semaphore()
    for shift in range(1, count):
        pl.semaphore_signal(barrier, inc=1, device_id=(tile, lax.rem(me + shift, count)), device_id_type=mesh_ids)
    neighbours = jnp.int32(0)
    for k in range(-reach, reach + 1):
        if k == 0:
            continue
        there = (tile + k >= 0) & (tile + k < tiles)
        neighbours = neighbours + there.astype(jnp.int32)

        @pl.when(there)
        def _():
            pl.semaphore_signal(barrier, inc=1, device_id=(tile + k, me), device_id_type=mesh_ids)

    pl.semaphore_wait(barrier, count - 1 + neighbours)


def exchange_inputs(spec_ref, lag_ref, slow_ref, spec_in, lag_in, slow_in, local_sem, send_sem, recv_sem, then, reach):
    count = spec_in.shape[0]
    me = lax.axis_index("sta")
    tile = lax.axis_index("grid")
    mesh_ids = pl.DeviceIdType.MESH
    enter_barrier(count, reach)
    pairs = ((spec_ref, spec_in), (lag_ref, lag_in), (slow_ref, slow_in))
    local = []
    for kind, (source, target) in enumerate(pairs):
        own = source.at[me] if kind == 0 else source
        copy = pltpu.make_async_copy(own, target.at[me], local_sem.at[kind])
        copy.start()
        local.append(copy)
    sends = []
    for shift in range(1, count):
        peer = lax.rem(me + shift, count)
        for kind, (source, target) in enumerate(pairs):
            part = source.at[peer] if kind == 0 else source
            copy = pltpu.make_async_remote_copy(
                src_ref=part,
                dst_ref=target.at[me],
                send_sem=send_sem.at[kind, shift],
                recv_sem=recv_sem.at[kind, me],
                device_id=(tile, peer),
                device_id_type=mesh_ids,
            )
            copy.start()
            sends.append(copy)
    then()
    for copy in local:
        copy.wait()
    for copy in sends:
        copy.wait_send()
    for shift in range(1, count):
        source_id = lax.rem(me + count - shift, count)
        for kind, (source, target) in enumerate(pairs):
            part = source.at[source_id] if kind == 0 else source
            pltpu.make_async_remote_copy(
                src_ref=part,
                dst_ref=target.at[source_id],
                send_sem=send_sem.at[kind, shift],
                recv_sem=recv_sem.at[kind, source_id],
                device_id=(tile, source_id),
                device_id_type=mesh_ids,
            ).wait_recv()


def align_block(spec, lag, slow, source, real_ref, imag_ref, turn_ref):
    bins, block = spec.shape[0], spec.shape[2]
    first_bin = lax.axis_index("sta") * bins
    bin_rows = (F0 + first_bin + lax.broadcasted_iota(jnp.int32, (bins, block), 0)).astype(jnp.float32)
    cols = pl.ds(pl.multiple_of(source * block, 128), block)
    product = bin_rows * lag.astype(jnp.float32)
    whole = jnp.floor(product * (1.0 / NT))
    left = product - whole * NT
    left = jnp.where(left < 0.0, left + NT, left)
    left = jnp.where(left >= NT, left - NT, left)
    turned = left * (TWO_PI / NT)
    cosine = jnp.cos(turned)
    sine = jnp.sin(turned)
    real_in = spec[:, 0, :].astype(jnp.float32)
    imag_in = spec[:, 1, :].astype(jnp.float32)
    real_ref[:, cols] = (real_in * cosine + imag_in * sine).astype(jnp.bfloat16).astype(jnp.float32)
    imag_ref[:, cols] = (imag_in * cosine - real_in * sine).astype(jnp.bfloat16).astype(jnp.float32)
    turn_ref[:, cols] = slow.astype(jnp.float32)


def complex_times(left, right):
    return left[0] * right[0] - left[1] * right[1], left[0] * right[1] + left[1] * right[0]


def factor_rows(turn_x, turn_y, turn_z, rows8, rows16):
    return (
        exp_neg(turn_x * (rows8 - 3.5)),
        exp_neg(turn_x * (8.0 * (rows8 - 1.5))),
        exp_neg(turn_y * (rows8 - 3.5)),
        exp_neg(turn_z * (rows16 - 7.5)),
        exp_neg(turn_z * (16.0 * (rows8 - 3.5))),
    )


def beam_kernel(spec_ref, lag_ref, slow_ref, out_ref, spec_in, lag_in, slow_in, local_sem, send_sem, recv_sem,
                real_ref, imag_ref, turn_ref, acc_ref, left_ref, right_ref, power_ref, pieces, send_rs, recv_rs,
                send_ag, recv_ag, share_sem):
    count, bins, block = spec_in.shape[0], spec_in.shape[1], spec_in.shape[3]
    me = lax.axis_index("sta")
    first_bin = me * bins
    width = CHUNK
    per_block = block // width
    half_z = CZ // 2
    rows8 = lax.broadcasted_iota(jnp.int32, (8, width), 0).astype(jnp.float32)
    rows16 = lax.broadcasted_iota(jnp.int32, (16, width), 0).astype(jnp.float32)
    omega0 = (F0 + first_bin).astype(jnp.float32) * (TWO_PI / NT)
    step = TWO_PI / NT
    acc_ref[...] = jnp.zeros_like(acc_ref)

    def per_chunk(k, carry):
        source = lax.rem(me + k // per_block, count)
        cols = pl.ds(pl.multiple_of(source * block + lax.rem(k, per_block) * width, 128), width)
        slow_x = turn_ref[0:1, cols]
        slow_y = turn_ref[1:2, cols]
        slow_z = turn_ref[2:3, cols]
        start = factor_rows(omega0 * slow_x, omega0 * slow_y, omega0 * slow_z, rows8, rows16)
        ratio = factor_rows(step * slow_x, step * slow_y, step * slow_z, rows8, rows16)

        def per_bin(f, state):
            (a_r, a_i), (b_r, b_i), (y_r, y_i), (c_r, c_i), (d_r, d_i) = state
            real_in = real_ref[pl.ds(f, 1), cols]
            imag_in = imag_ref[pl.ds(f, 1), cols]
            q_r = real_in * y_r - imag_in * y_i
            q_i = real_in * y_i + imag_in * y_r
            near = [complex_times((b_r[m : m + 1], b_i[m : m + 1]), (a_r, a_i)) for m in range(CX // 16)]
            cells = CX * CY
            for y in range(CY):
                qq_r, qq_i = q_r[y : y + 1], q_i[y : y + 1]
                lo_r, lo_i, hi_r, hi_i = [], [], [], []
                for x_r, x_i in near:
                    t1, t2 = qq_r * x_r, qq_i * x_i
                    t3, t4 = qq_r * x_i, qq_i * x_r
                    lo_r.append(t1 - t2)
                    lo_i.append(t3 + t4)
                    hi_r.append(t1 + t2)
                    hi_i.append(t4 - t3)
                row = y * CX
                half = CX // 2
                left_ref[row : row + half, :] = jnp.concatenate(lo_r, axis=0).astype(jnp.bfloat16)
                left_ref[row + half : row + CX, :] = jnp.concatenate(hi_r, axis=0).astype(jnp.bfloat16)
                left_ref[cells + row : cells + row + half, :] = jnp.concatenate(lo_i, axis=0).astype(jnp.bfloat16)
                left_ref[cells + row + half : cells + row + CX, :] = jnp.concatenate(hi_i, axis=0).astype(jnp.bfloat16)
            for m in range(half_z // 16):
                z_r, z_i = complex_times((d_r[m : m + 1], d_i[m : m + 1]), (c_r, c_i))
                row = 16 * m
                right_ref[row : row + 16, :] = z_r.astype(jnp.bfloat16)
                right_ref[half_z + row : half_z + row + 16, :] = z_i.astype(jnp.bfloat16)
            acc_ref[f] += lax.dot_general(
                left_ref[...], right_ref[...], (((1,), (1,)), ((), ())), preferred_element_type=jnp.float32
            )
            return tuple(complex_times(now, turn) for now, turn in zip(state, ratio))

        lax.fori_loop(0, bins, per_bin, start, unroll=4)
        return carry

    def own_block():
        align_block(spec_ref.at[me], lag_ref[...], slow_ref[...], me, real_ref, imag_ref, turn_ref)
        lax.fori_loop(0, per_block, per_chunk, 0)

    exchange_inputs(
        spec_ref, lag_ref, slow_ref, spec_in, lag_in, slow_in, local_sem, send_sem, recv_sem, own_block, out_ref.shape[0] // 2
    )

    def align_other(shift, carry):
        source = lax.rem(me + shift, count)
        align_block(spec_in.at[source], lag_in[source], slow_in[source], source, real_ref, imag_ref, turn_ref)
        return carry

    lax.fori_loop(1, count, align_other, 0)
    lax.fori_loop(per_block, count * per_block, per_chunk, 0)
    cells = CX * CY
    low = jnp.zeros((cells, half_z), jnp.float32)
    high = jnp.zeros((cells, half_z), jnp.float32)
    for f in range(bins):
        sums = acc_ref[f]
        u, w = sums[:cells, :half_z], sums[:cells, half_z:]
        x, v = sums[cells:, :half_z], sums[cells:, half_z:]
        low = low + ((u - v) * (u - v) + (w + x) * (w + x))
        high = high + ((u + v) * (u + v) + (x - w) * (x - w))
    power_ref[:, :half_z] = low
    power_ref[:, half_z:] = high
    share_kernel(power_ref, out_ref, pieces, send_rs, recv_rs, send_ag, recv_ag, share_sem)


def beam_power(spec_send, lag_row, slow_rows, reach):
    count = spec_send.shape[0]
    slots = 2 * reach + 1
    cells = CX * CY
    bins, block = spec_send.shape[1], spec_send.shape[3]
    width = CHUNK
    stations = count * block
    vmem = pl.BlockSpec(memory_space=pltpu.VMEM)
    return pl.pallas_call(
        beam_kernel,
        out_shape=jax.ShapeDtypeStruct((slots, cells, CZ), jnp.float32),
        in_specs=[vmem, vmem, vmem],
        out_specs=vmem,
        scratch_shapes=[
            pltpu.VMEM((count,) + spec_send.shape[1:], jnp.bfloat16),
            pltpu.VMEM((count,) + lag_row.shape, jnp.int32),
            pltpu.VMEM((count,) + slow_rows.shape, jnp.bfloat16),
            pltpu.SemaphoreType.DMA((3,)),
            pltpu.SemaphoreType.DMA((3, count)),
            pltpu.SemaphoreType.DMA((3, count)),
            pltpu.VMEM((bins, stations), jnp.float32),
            pltpu.VMEM((bins, stations), jnp.float32),
            pltpu.VMEM((slow_rows.shape[0], stations), jnp.float32),
            pltpu.VMEM((bins, 2 * CX * CY, CZ), jnp.float32),
            pltpu.VMEM((2 * CX * CY, width), jnp.bfloat16),
            pltpu.VMEM((CZ, width), jnp.bfloat16),
            pltpu.VMEM((cells, CZ), jnp.float32),
            pltpu.VMEM((count, cells // count, CZ), jnp.float32),
            pltpu.SemaphoreType.DMA((count,)),
            pltpu.SemaphoreType.DMA((count,)),
            pltpu.SemaphoreType.DMA((slots, count)),
            pltpu.SemaphoreType.DMA((slots, count)),
            pltpu.SemaphoreType.DMA((1,)),
        ],
        compiler_params=pltpu.CompilerParams(collective_id=1, has_side_effects=True),
    )(spec_send, lag_row, slow_rows)


def share_kernel(part_ref, out_ref, pieces, send_rs, recv_rs, send_ag, recv_ag, local_sem):
    count = pieces.shape[0]
    slots = out_ref.shape[0]
    reach = slots // 2
    rows = pieces.shape[1]
    me = lax.axis_index("sta")
    tile = lax.axis_index("grid")
    tiles = lax.axis_size("grid")
    mesh_ids = pl.DeviceIdType.MESH
    own = pltpu.make_async_copy(part_ref.at[pl.ds(pl.multiple_of(me * rows, 8), rows)], pieces.at[me], local_sem.at[0])
    own.start()
    sends = []
    for shift in range(1, count):
        peer = lax.rem(me + shift, count)
        copy = pltpu.make_async_remote_copy(
            src_ref=part_ref.at[pl.ds(pl.multiple_of(peer * rows, 8), rows)],
            dst_ref=pieces.at[me],
            send_sem=send_rs.at[shift],
            recv_sem=recv_rs.at[me],
            device_id=(tile, peer),
            device_id_type=mesh_ids,
        )
        copy.start()
        sends.append(copy)
    own.wait()
    for copy in sends:
        copy.wait_send()
    for shift in range(1, count):
        source = lax.rem(me + count - shift, count)
        pltpu.make_async_remote_copy(
            src_ref=pieces.at[source],
            dst_ref=pieces.at[source],
            send_sem=send_rs.at[shift],
            recv_sem=recv_rs.at[source],
            device_id=(tile, source),
            device_id_type=mesh_ids,
        ).wait_recv()
    total = pieces[0]
    for source in range(1, count):
        total = total + pieces[source]
    mine = pl.ds(pl.multiple_of(me * rows, 8), rows)
    out_ref[reach, mine] = total
    block = out_ref.at[reach, mine]

    def gather_copy(k, peer, slot):
        return pltpu.make_async_remote_copy(
            src_ref=block,
            dst_ref=out_ref.at[slot, mine],
            send_sem=send_ag.at[slot, peer],
            recv_sem=recv_ag.at[slot, me],
            device_id=(tile + k, peer),
            device_id_type=mesh_ids,
        )

    peers = []
    for shift in range(1, count):
        copy = gather_copy(0, lax.rem(me + shift, count), reach)
        copy.start()
        peers.append(copy)
    for k in range(-reach, reach + 1):
        if k == 0:
            continue

        @pl.when(jnp.logical_not((tile + k >= 0) & (tile + k < tiles)))
        def _():
            out_ref[reach + k] = jnp.zeros(out_ref.shape[1:], out_ref.dtype)

    for copy in peers:
        copy.wait_send()
    for shift in range(1, count):
        source = lax.rem(me + count - shift, count)
        pltpu.make_async_remote_copy(
            src_ref=block,
            dst_ref=out_ref.at[reach, pl.ds(pl.multiple_of(source * rows, 8), rows)],
            send_sem=send_ag.at[reach, source],
            recv_sem=recv_ag.at[reach, source],
            device_id=(tile, source),
            device_id_type=mesh_ids,
        ).wait_recv()

    def halo_copy(k):
        return pltpu.make_async_remote_copy(
            src_ref=out_ref.at[reach],
            dst_ref=out_ref.at[reach - k],
            send_sem=send_ag.at[reach - k, me],
            recv_sem=recv_ag.at[reach - k, me],
            device_id=(tile + k, me),
            device_id_type=mesh_ids,
        )

    for k in range(-reach, reach + 1):
        if k == 0:
            continue

        @pl.when((tile + k >= 0) & (tile + k < tiles))
        def _():
            halo_copy(k).start()

    for k in range(-reach, reach + 1):
        if k == 0:
            continue

        @pl.when((tile + k >= 0) & (tile + k < tiles))
        def _():
            halo_copy(k).wait_send()
            pltpu.make_async_remote_copy(
                src_ref=out_ref.at[reach],
                dst_ref=out_ref.at[reach + k],
                send_sem=send_ag.at[reach + k, me],
                recv_sem=recv_ag.at[reach + k, me],
                device_id=(tile + k, me),
                device_id_type=mesh_ids,
            ).wait_recv()


def share_power(part, reach):
    count = lax.axis_size("sta")
    rows = part.shape[0] // count
    slots = 2 * reach + 1
    return pl.pallas_call(
        share_kernel,
        out_shape=jax.ShapeDtypeStruct((slots,) + part.shape, jnp.float32),
        in_specs=[pl.BlockSpec(memory_space=pltpu.VMEM)],
        out_specs=pl.BlockSpec(memory_space=pltpu.VMEM),
        scratch_shapes=[
            pltpu.VMEM((count, rows, part.shape[1]), jnp.float32),
            pltpu.SemaphoreType.DMA((count,)),
            pltpu.SemaphoreType.DMA((count,)),
            pltpu.SemaphoreType.DMA((slots, count)),
            pltpu.SemaphoreType.DMA((slots, count)),
            pltpu.SemaphoreType.DMA((1,)),
        ],
        compiler_params=pltpu.CompilerParams(collective_id=0, has_side_effects=True),
    )(part)


def freq_beams(freq_ids, aligned_rows, slow_rows):
    return lax.map(lambda pair: beam_freq(pair[0], pair[1], slow_rows), (freq_ids, aligned_rows))


def band_matrix(taps, length):
    rows = jnp.arange(length, dtype=jnp.int32)[:, None]
    columns = jnp.arange(length + 2 * HALF, dtype=jnp.int32)[None, :]
    offset = columns - rows
    picks = jnp.arange(TAPS, dtype=jnp.int32)[:, None, None]
    return jnp.sum(jnp.where(offset[None] == picks, taps[:, None, None], 0.0), axis=0)


def blur(volume, bands):
    band_x, square_y, square_z = bands
    padded = with_halo(volume.astype(jnp.bfloat16), (("grid", 0),), HALF).astype(volume.dtype)
    along_x = jnp.einsum("ip,pyz->iyz", band_x, padded, precision=lax.Precision.HIGHEST)
    along_y = jnp.einsum("jq,xqz->xjz", square_y, along_x, precision=lax.Precision.HIGHEST)
    return jnp.einsum("xyw,kw->xyk", along_y, square_z, precision=lax.Precision.HIGHEST)


def blur_narrowing(volume, taps, square_y, square_z):
    band_x = band_matrix(taps, volume.shape[0] - 2 * HALF)
    along_x = jnp.einsum("ip,pyz->iyz", band_x, volume, precision=lax.Precision.HIGHEST)
    along_y = jnp.einsum("jq,xqz->xjz", square_y, along_x, precision=lax.Precision.HIGHEST)
    return jnp.einsum("xyw,kw->xyk", along_y, square_z, precision=lax.Precision.HIGHEST)


def deblur(observed, halo_tiles, spread_taps):
    tiles = lax.axis_size("grid")
    me = lax.axis_index("grid")
    reach = ITERS * 2 * HALF
    cut = halo_tiles * CX - reach
    observed = observed[cut : observed.shape[0] - cut]
    width = observed.shape[0]
    cell = (me - halo_tiles) * CX + cut + jnp.arange(width, dtype=jnp.int32)
    inside = (cell >= 0) & (cell < tiles * CX)
    square_y = band_matrix(spread_taps[1], CY)[:, HALF : HALF + CY]
    square_z = band_matrix(spread_taps[2], CZ)[:, HALF : HALF + CZ]
    estimate = jnp.where(inside[:, None, None], observed, 0.0)
    for sweep in range(ITERS):
        low = 2 * HALF * sweep + HALF
        blurred = blur_narrowing(estimate, spread_taps[0], square_y, square_z)
        ratio = jnp.where(
            inside[low : width - low, None, None], observed[low : width - low] / blurred, 0.0
        )
        estimate = estimate[2 * HALF : estimate.shape[0] - 2 * HALF] * blur_narrowing(
            ratio, spread_taps[0], square_y, square_z
        )
    return estimate


def band_of(taps_ref, axis, rows, cols):
    offset = cols - rows + HALF
    band = jnp.zeros(offset.shape, jnp.float32)
    for tap in range(TAPS):
        band = jnp.where(offset == tap, taps_ref[axis, tap], band)
    return band


def mirror(index, length):
    return jnp.where(index < length // 2, index, 3 * (length // 2) - 1 - index)


def deblur_kernel(taps_ref, obs_ref, out_ref, kx_ref, kz_ref):
    tiles = lax.axis_size("grid")
    me = lax.axis_index("grid")
    planes, width, depth = obs_ref.shape
    shape_x = kx_ref.shape
    kx_ref[...] = band_of(
        taps_ref, 0, lax.broadcasted_iota(jnp.int32, shape_x, 0) + HALF, lax.broadcasted_iota(jnp.int32, shape_x, 1)
    )
    shape_z = kz_ref.shape
    kz_ref[...] = band_of(
        taps_ref,
        2,
        mirror(lax.broadcasted_iota(jnp.int32, shape_z, 1), depth),
        mirror(lax.broadcasted_iota(jnp.int32, shape_z, 0), depth),
    )
    halo_tiles = (width - CX) // (2 * CX)
    highest = lax.Precision.HIGH

    def inside(low, size):
        cell = (me - halo_tiles) * CX + low + lax.broadcasted_iota(jnp.int32, (size, depth), 0)
        return (cell >= 0) & (cell < tiles * CX)

    lanes = planes * depth

    def blur(volume):
        size_in = volume.shape[0]
        size_out = size_in - 2 * HALF
        band = kx_ref[0:size_out, 0:size_in]
        along_x = jnp.dot(band, volume, precision=highest, preferred_element_type=jnp.float32)
        along_y = []
        for y in range(planes):
            total = None
            for q in range(planes):
                term = taps_ref[1, q - y + HALF] * along_x[:, q * depth : (q + 1) * depth]
                total = term if total is None else total + term
            along_y.append(total)
        joined = jnp.concatenate(along_y, axis=0)
        along_z = jnp.dot(joined, kz_ref[...], precision=highest, preferred_element_type=jnp.float32)
        return jnp.concatenate([along_z[y * size_out : (y + 1) * size_out] for y in range(planes)], axis=1)

    def inside_wide(low, size):
        cell = (me - halo_tiles) * CX + low + lax.broadcasted_iota(jnp.int32, (size, lanes), 0)
        return (cell >= 0) & (cell < tiles * CX)

    observed = jnp.concatenate([obs_ref[y] for y in range(planes)], axis=1)
    estimate = jnp.where(inside_wide(0, width), observed, 0.0)
    for sweep in range(ITERS):
        low = 2 * HALF * sweep + HALF
        blurred = blur(estimate)
        size = blurred.shape[0]
        ratio = jnp.where(inside_wide(low, size), observed[low : low + size] / blurred, 0.0)
        spread = blur(ratio)
        estimate = estimate[2 * HALF : 2 * HALF + spread.shape[0]] * spread
    for y in range(planes):
        out_ref[y] = estimate[:, y * depth : (y + 1) * depth]


def deblur_tile(observed, spread_taps):
    planes, width, depth = observed.shape
    vmem = pl.BlockSpec(memory_space=pltpu.VMEM)
    return pl.pallas_call(
        deblur_kernel,
        out_shape=jax.ShapeDtypeStruct((planes, CX, depth), jnp.float32),
        in_specs=[pl.BlockSpec(memory_space=pltpu.SMEM), vmem],
        out_specs=vmem,
        scratch_shapes=[
            pltpu.VMEM((width - 2 * HALF, width), jnp.float32),
            pltpu.VMEM((depth, depth), jnp.float32),
        ],
    )(spread_taps, observed)


def per_device(spectra, lag_samples, slowness, spread_taps):
    groups = lax.axis_size("sta")
    own_count = FREQS // groups
    first_bin = lax.axis_index("sta") * own_count
    block = spectra.shape[2]
    spec_send = spectra.reshape(groups, own_count, 2, block)
    halo_tiles = -(-(ITERS * 2 * HALF) // CX)
    summed = beam_power(spec_send, lag_samples, slowness[0], halo_tiles)
    observed = summed / (FREQS * STATIONS) + BACKGROUND
    slots = observed.shape[0]
    observed = observed.reshape(slots, CY, CX, CZ)
    observed = jnp.concatenate([observed[:, :, : CX // 2], observed[:, :, CX // 2 :][:, :, ::-1]], axis=2)
    planes = observed.transpose(1, 0, 2, 3).reshape(CY, slots * CX, CZ)
    estimate = deblur_tile(planes, spread_taps)
    both = jnp.stack([observed[halo_tiles], estimate])
    both = jnp.concatenate([both[..., : CZ // 2], both[..., CZ // 2 :][..., ::-1]], axis=-1).transpose(0, 2, 1, 3)
    stacked, estimate = both[0], both[1]
    return (stacked[None], estimate[None])


def solution(mesh):
    placed = (P(None, None, "sta"), P("grid", "sta"), P("grid", None, "sta"), P())
    return jax.shard_map(
        per_device,
        mesh=mesh,
        in_specs=placed,
        out_specs=(P("grid", None, None, None), P("grid", None, None, None)),
        check_vma=False,
    )
```

```python
import math

import jax
import jax.numpy as jnp
from jax import lax
from jax.sharding import PartitionSpec as P
from jax.experimental import pallas as pl
from jax.experimental.pallas import tpu as pltpu

STATIONS = 6144
FREQS = 64
F0 = 600
NT = 6000
TAPS = 17
HALF = 8
ITERS = 4
CX = 32
CY = 8
CZ = 128


TWO_PI = 2.0 * math.pi
BACKGROUND = 0.05


def with_halo(array, sides, width):
    for axis, dim in sides:
        size, length = (lax.axis_size(axis), array.shape[dim])
        up = [(i, (i + 1) % size) for i in range(size - 1)]
        down = [(j, i) for i, j in up]
        last = lax.slice_in_dim(array, length - width, length, axis=dim)
        leading = lax.slice_in_dim(array, 0, width, axis=dim)
        before = lax.ppermute(last, axis, up)
        after = lax.ppermute(leading, axis, down)
        array = jnp.concatenate([before, array, after], axis=dim)
    return array


def align_rows(spectra, lag_row):
    bins = F0 + jnp.arange(FREQS, dtype=jnp.int32)
    cycles = bins[:, None] * lag_row[None, :] % NT
    turned = cycles.astype(jnp.float32) * (TWO_PI / NT)
    cosine = jnp.cos(turned)
    sine = jnp.sin(turned)
    real_in = spectra[:, 0, :].astype(jnp.float32)
    imag_in = spectra[:, 1, :].astype(jnp.float32)
    real_out = real_in * cosine + imag_in * sine
    imag_out = imag_in * cosine - real_in * sine
    return jnp.stack([real_out, imag_out], axis=1).astype(jnp.bfloat16)


def beam_freq(freq, aligned_row, slow_rows):
    omega = (F0 + freq).astype(jnp.float32) * (TWO_PI / NT)
    slow = slow_rows.astype(jnp.float32)
    x_coord = jnp.arange(CX, dtype=jnp.float32) - (CX - 1) / 2.0
    y_coord = jnp.arange(CY, dtype=jnp.float32) - (CY - 1) / 2.0
    z_coord = jnp.arange(CZ, dtype=jnp.float32) - (CZ - 1) / 2.0
    phase_x = (omega * slow[0])[None, :] * x_coord[:, None]
    phase_y = (omega * slow[1])[None, :] * y_coord[:, None]
    phase = phase_x[:, None, :] + phase_y[None, :, :]
    cosine = jnp.cos(phase)
    sine = jnp.sin(phase)
    real_in = aligned_row[0].astype(jnp.float32)[None, None, :]
    imag_in = aligned_row[1].astype(jnp.float32)[None, None, :]
    front_real = (real_in * cosine + imag_in * sine).astype(jnp.bfloat16).reshape(CX * CY, -1)
    front_imag = (imag_in * cosine - real_in * sine).astype(jnp.bfloat16).reshape(CX * CY, -1)
    left_side = jnp.concatenate([front_real, front_imag], axis=1)
    phase_z = (omega * slow[2])[:, None] * z_coord[None, :]
    depth_real = jnp.cos(phase_z).astype(jnp.bfloat16)
    depth_imag = jnp.sin(phase_z).astype(jnp.bfloat16)
    upper_rows = jnp.concatenate([depth_real, -depth_imag], axis=1)
    lower_rows = jnp.concatenate([depth_imag, depth_real], axis=1)
    right_side = jnp.concatenate([upper_rows, lower_rows], axis=0)
    return jnp.dot(left_side, right_side, preferred_element_type=jnp.float32)


CHUNK = 768


def exp_neg(angle):
    return jnp.cos(angle), -jnp.sin(angle)


def enter_barrier(count, reach):
    me = lax.axis_index("sta")
    tile = lax.axis_index("grid")
    tiles = lax.axis_size("grid")
    mesh_ids = pl.DeviceIdType.MESH
    barrier = pltpu.get_barrier_semaphore()
    for shift in range(1, count):
        pl.semaphore_signal(barrier, inc=1, device_id=(tile, lax.rem(me + shift, count)), device_id_type=mesh_ids)
    neighbours = jnp.int32(0)
    for k in range(-reach, reach + 1):
        if k == 0:
            continue
        there = (tile + k >= 0) & (tile + k < tiles)
        neighbours = neighbours + there.astype(jnp.int32)

        @pl.when(there)
        def _():
            pl.semaphore_signal(barrier, inc=1, device_id=(tile + k, me), device_id_type=mesh_ids)

    pl.semaphore_wait(barrier, count - 1 + neighbours)


def exchange_inputs(spec_ref, lag_ref, slow_ref, spec_in, lag_in, slow_in, local_sem, send_sem, recv_sem, then, reach):
    count = spec_in.shape[0]
    me = lax.axis_index("sta")
    tile = lax.axis_index("grid")
    mesh_ids = pl.DeviceIdType.MESH
    enter_barrier(count, reach)
    pairs = ((spec_ref, spec_in), (lag_ref, lag_in), (slow_ref, slow_in))
    local = []
    for kind, (source, target) in enumerate(pairs):
        own = source.at[me] if kind == 0 else source
        copy = pltpu.make_async_copy(own, target.at[me], local_sem.at[kind])
        copy.start()
        local.append(copy)
    sends = []
    for shift in range(1, count):
        peer = lax.rem(me + shift, count)
        for kind, (source, target) in enumerate(pairs):
            part = source.at[peer] if kind == 0 else source
            copy = pltpu.make_async_remote_copy(
                src_ref=part,
                dst_ref=target.at[me],
                send_sem=send_sem.at[kind, shift],
                recv_sem=recv_sem.at[kind, me],
                device_id=(tile, peer),
                device_id_type=mesh_ids,
            )
            copy.start()
            sends.append(copy)
    then()
    for copy in local:
        copy.wait()
    for copy in sends:
        copy.wait_send()
    for shift in range(1, count):
        source_id = lax.rem(me + count - shift, count)
        for kind, (source, target) in enumerate(pairs):
            part = source.at[source_id] if kind == 0 else source
            pltpu.make_async_remote_copy(
                src_ref=part,
                dst_ref=target.at[source_id],
                send_sem=send_sem.at[kind, shift],
                recv_sem=recv_sem.at[kind, source_id],
                device_id=(tile, source_id),
                device_id_type=mesh_ids,
            ).wait_recv()


def align_block(spec, lag, slow, source, real_ref, imag_ref, turn_ref):
    bins, block = spec.shape[0], spec.shape[2]
    first_bin = lax.axis_index("sta") * bins
    bin_rows = (F0 + first_bin + lax.broadcasted_iota(jnp.int32, (bins, block), 0)).astype(jnp.float32)
    cols = pl.ds(pl.multiple_of(source * block, 128), block)
    product = bin_rows * lag.astype(jnp.float32)
    whole = jnp.floor(product * (1.0 / NT))
    left = product - whole * NT
    left = jnp.where(left < 0.0, left + NT, left)
    left = jnp.where(left >= NT, left - NT, left)
    turned = left * (TWO_PI / NT)
    cosine = jnp.cos(turned)
    sine = jnp.sin(turned)
    real_in = spec[:, 0, :].astype(jnp.float32)
    imag_in = spec[:, 1, :].astype(jnp.float32)
    real_ref[:, cols] = (real_in * cosine + imag_in * sine).astype(jnp.bfloat16).astype(jnp.float32)
    imag_ref[:, cols] = (imag_in * cosine - real_in * sine).astype(jnp.bfloat16).astype(jnp.float32)
    turn_ref[:, cols] = slow.astype(jnp.float32)


def complex_times(left, right):
    return left[0] * right[0] - left[1] * right[1], left[0] * right[1] + left[1] * right[0]


def factor_rows(turn_x, turn_y, turn_z, rows8, rows16):
    return (
        exp_neg(turn_x * (rows8 - 3.5)),
        exp_neg(turn_x * (8.0 * (rows8 - 1.5))),
        exp_neg(turn_y * (rows8 - 3.5)),
        exp_neg(turn_z * (rows16 - 7.5)),
        exp_neg(turn_z * (16.0 * (rows8 - 3.5))),
    )


def beam_kernel(spec_ref, lag_ref, slow_ref, out_ref, spec_in, lag_in, slow_in, local_sem, send_sem, recv_sem,
                real_ref, imag_ref, turn_ref, acc_ref, left_ref, right_ref, power_ref, pieces, send_rs, recv_rs,
                send_ag, recv_ag, share_sem):
    count, bins, block = spec_in.shape[0], spec_in.shape[1], spec_in.shape[3]
    me = lax.axis_index("sta")
    first_bin = me * bins
    width = CHUNK
    per_block = block // width
    half_z = CZ // 2
    rows8 = lax.broadcasted_iota(jnp.int32, (8, width), 0).astype(jnp.float32)
    rows16 = lax.broadcasted_iota(jnp.int32, (16, width), 0).astype(jnp.float32)
    omega0 = (F0 + first_bin).astype(jnp.float32) * (TWO_PI / NT)
    step = TWO_PI / NT
    acc_ref[...] = jnp.zeros_like(acc_ref)

    def per_chunk(k, carry):
        source = lax.rem(me + k // per_block, count)
        cols = pl.ds(pl.multiple_of(source * block + lax.rem(k, per_block) * width, 128), width)
        slow_x = turn_ref[0:1, cols]
        slow_y = turn_ref[1:2, cols]
        slow_z = turn_ref[2:3, cols]
        start = factor_rows(omega0 * slow_x, omega0 * slow_y, omega0 * slow_z, rows8, rows16)
        ratio = factor_rows(step * slow_x, step * slow_y, step * slow_z, rows8, rows16)

        def per_bin(f, state):
            (a_r, a_i), (b_r, b_i), (y_r, y_i), (c_r, c_i), (d_r, d_i) = state
            real_in = real_ref[pl.ds(f, 1), cols]
            imag_in = imag_ref[pl.ds(f, 1), cols]
            q_r = real_in * y_r - imag_in * y_i
            q_i = real_in * y_i + imag_in * y_r
            near = [complex_times((b_r[m : m + 1], b_i[m : m + 1]), (a_r, a_i)) for m in range(CX // 16)]
            cells = CX * CY
            for y in range(CY):
                qq_r, qq_i = q_r[y : y + 1], q_i[y : y + 1]
                lo_r, lo_i, hi_r, hi_i = [], [], [], []
                for x_r, x_i in near:
                    t1, t2 = qq_r * x_r, qq_i * x_i
                    t3, t4 = qq_r * x_i, qq_i * x_r
                    lo_r.append(t1 - t2)
                    lo_i.append(t3 + t4)
                    hi_r.append(t1 + t2)
                    hi_i.append(t4 - t3)
                row = y * CX
                half = CX // 2
                left_ref[row : row + half, :] = jnp.concatenate(lo_r, axis=0).astype(jnp.bfloat16)
                left_ref[row + half : row + CX, :] = jnp.concatenate(hi_r, axis=0).astype(jnp.bfloat16)
                left_ref[cells + row : cells + row + half, :] = jnp.concatenate(lo_i, axis=0).astype(jnp.bfloat16)
                left_ref[cells + row + half : cells + row + CX, :] = jnp.concatenate(hi_i, axis=0).astype(jnp.bfloat16)
            for m in range(half_z // 16):
                z_r, z_i = complex_times((d_r[m : m + 1], d_i[m : m + 1]), (c_r, c_i))
                row = 16 * m
                right_ref[row : row + 16, :] = z_r.astype(jnp.bfloat16)
                right_ref[half_z + row : half_z + row + 16, :] = z_i.astype(jnp.bfloat16)
            acc_ref[f] += lax.dot_general(
                left_ref[...], right_ref[...], (((1,), (1,)), ((), ())), preferred_element_type=jnp.float32
            )
            return tuple(complex_times(now, turn) for now, turn in zip(state, ratio))

        lax.fori_loop(0, bins, per_bin, start, unroll=4)
        return carry

    def own_block():
        align_block(spec_ref.at[me], lag_ref[...], slow_ref[...], me, real_ref, imag_ref, turn_ref)
        lax.fori_loop(0, per_block, per_chunk, 0)

    exchange_inputs(
        spec_ref, lag_ref, slow_ref, spec_in, lag_in, slow_in, local_sem, send_sem, recv_sem, own_block, out_ref.shape[0] // 2
    )

    def align_other(shift, carry):
        source = lax.rem(me + shift, count)
        align_block(spec_in.at[source], lag_in[source], slow_in[source], source, real_ref, imag_ref, turn_ref)
        return carry

    lax.fori_loop(1, count, align_other, 0)
    lax.fori_loop(per_block, count * per_block, per_chunk, 0)
    cells = CX * CY
    low = jnp.zeros((cells, half_z), jnp.float32)
    high = jnp.zeros((cells, half_z), jnp.float32)
    for f in range(bins):
        sums = acc_ref[f]
        u, w = sums[:cells, :half_z], sums[:cells, half_z:]
        x, v = sums[cells:, :half_z], sums[cells:, half_z:]
        low = low + ((u - v) * (u - v) + (w + x) * (w + x))
        high = high + ((u + v) * (u + v) + (x - w) * (x - w))
    power_ref[:, :half_z] = low
    power_ref[:, half_z:] = high
    share_kernel(power_ref, out_ref, pieces, send_rs, recv_rs, send_ag, recv_ag, share_sem)


def beam_power(spec_send, lag_row, slow_rows, reach):
    count = spec_send.shape[0]
    slots = 2 * reach + 1
    cells = CX * CY
    bins, block = spec_send.shape[1], spec_send.shape[3]
    width = CHUNK
    stations = count * block
    vmem = pl.BlockSpec(memory_space=pltpu.VMEM)
    return pl.pallas_call(
        beam_kernel,
        out_shape=jax.ShapeDtypeStruct((slots, cells, CZ), jnp.float32),
        in_specs=[vmem, vmem, vmem],
        out_specs=vmem,
        scratch_shapes=[
            pltpu.VMEM((count,) + spec_send.shape[1:], jnp.bfloat16),
            pltpu.VMEM((count,) + lag_row.shape, jnp.int32),
            pltpu.VMEM((count,) + slow_rows.shape, jnp.bfloat16),
            pltpu.SemaphoreType.DMA((3,)),
            pltpu.SemaphoreType.DMA((3, count)),
            pltpu.SemaphoreType.DMA((3, count)),
            pltpu.VMEM((bins, stations), jnp.float32),
            pltpu.VMEM((bins, stations), jnp.float32),
            pltpu.VMEM((slow_rows.shape[0], stations), jnp.float32),
            pltpu.VMEM((bins, 2 * CX * CY, CZ), jnp.float32),
            pltpu.VMEM((2 * CX * CY, width), jnp.bfloat16),
            pltpu.VMEM((CZ, width), jnp.bfloat16),
            pltpu.VMEM((cells, CZ), jnp.float32),
            pltpu.VMEM((count, cells // count, CZ), jnp.float32),
            pltpu.SemaphoreType.DMA((count,)),
            pltpu.SemaphoreType.DMA((count,)),
            pltpu.SemaphoreType.DMA((slots, count)),
            pltpu.SemaphoreType.DMA((slots, count)),
            pltpu.SemaphoreType.DMA((1,)),
        ],
        compiler_params=pltpu.CompilerParams(collective_id=1, has_side_effects=True),
    )(spec_send, lag_row, slow_rows)


def share_kernel(part_ref, out_ref, pieces, send_rs, recv_rs, send_ag, recv_ag, local_sem):
    count = pieces.shape[0]
    slots = out_ref.shape[0]
    reach = slots // 2
    rows = pieces.shape[1]
    me = lax.axis_index("sta")
    tile = lax.axis_index("grid")
    tiles = lax.axis_size("grid")
    mesh_ids = pl.DeviceIdType.MESH
    own = pltpu.make_async_copy(part_ref.at[pl.ds(pl.multiple_of(me * rows, 8), rows)], pieces.at[me], local_sem.at[0])
    own.start()
    sends = []
    for shift in range(1, count):
        peer = lax.rem(me + shift, count)
        copy = pltpu.make_async_remote_copy(
            src_ref=part_ref.at[pl.ds(pl.multiple_of(peer * rows, 8), rows)],
            dst_ref=pieces.at[me],
            send_sem=send_rs.at[shift],
            recv_sem=recv_rs.at[me],
            device_id=(tile, peer),
            device_id_type=mesh_ids,
        )
        copy.start()
        sends.append(copy)
    own.wait()
    for copy in sends:
        copy.wait_send()
    for shift in range(1, count):
        source = lax.rem(me + count - shift, count)
        pltpu.make_async_remote_copy(
            src_ref=pieces.at[source],
            dst_ref=pieces.at[source],
            send_sem=send_rs.at[shift],
            recv_sem=recv_rs.at[source],
            device_id=(tile, source),
            device_id_type=mesh_ids,
        ).wait_recv()
    total = pieces[0]
    for source in range(1, count):
        total = total + pieces[source]
    mine = pl.ds(pl.multiple_of(me * rows, 8), rows)
    out_ref[reach, mine] = total
    block = out_ref.at[reach, mine]

    def gather_copy(k, peer, slot):
        return pltpu.make_async_remote_copy(
            src_ref=block,
            dst_ref=out_ref.at[slot, mine],
            send_sem=send_ag.at[slot, peer],
            recv_sem=recv_ag.at[slot, me],
            device_id=(tile + k, peer),
            device_id_type=mesh_ids,
        )

    peers = []
    for shift in range(1, count):
        copy = gather_copy(0, lax.rem(me + shift, count), reach)
        copy.start()
        peers.append(copy)
    for k in range(-reach, reach + 1):
        if k == 0:
            continue

        @pl.when(jnp.logical_not((tile + k >= 0) & (tile + k < tiles)))
        def _():
            out_ref[reach + k] = jnp.zeros(out_ref.shape[1:], out_ref.dtype)

    for copy in peers:
        copy.wait_send()
    for shift in range(1, count):
        source = lax.rem(me + count - shift, count)
        pltpu.make_async_remote_copy(
            src_ref=block,
            dst_ref=out_ref.at[reach, pl.ds(pl.multiple_of(source * rows, 8), rows)],
            send_sem=send_ag.at[reach, source],
            recv_sem=recv_ag.at[reach, source],
            device_id=(tile, source),
            device_id_type=mesh_ids,
        ).wait_recv()

    def halo_copy(k):
        return pltpu.make_async_remote_copy(
            src_ref=out_ref.at[reach],
            dst_ref=out_ref.at[reach - k],
            send_sem=send_ag.at[reach - k, me],
            recv_sem=recv_ag.at[reach - k, me],
            device_id=(tile + k, me),
            device_id_type=mesh_ids,
        )

    for k in range(-reach, reach + 1):
        if k == 0:
            continue

        @pl.when((tile + k >= 0) & (tile + k < tiles))
        def _():
            halo_copy(k).start()

    for k in range(-reach, reach + 1):
        if k == 0:
            continue

        @pl.when((tile + k >= 0) & (tile + k < tiles))
        def _():
            halo_copy(k).wait_send()
            pltpu.make_async_remote_copy(
                src_ref=out_ref.at[reach],
                dst_ref=out_ref.at[reach + k],
                send_sem=send_ag.at[reach + k, me],
                recv_sem=recv_ag.at[reach + k, me],
                device_id=(tile + k, me),
                device_id_type=mesh_ids,
            ).wait_recv()


def share_power(part, reach):
    count = lax.axis_size("sta")
    rows = part.shape[0] // count
    slots = 2 * reach + 1
    return pl.pallas_call(
        share_kernel,
        out_shape=jax.ShapeDtypeStruct((slots,) + part.shape, jnp.float32),
        in_specs=[pl.BlockSpec(memory_space=pltpu.VMEM)],
        out_specs=pl.BlockSpec(memory_space=pltpu.VMEM),
        scratch_shapes=[
            pltpu.VMEM((count, rows, part.shape[1]), jnp.float32),
            pltpu.SemaphoreType.DMA((count,)),
            pltpu.SemaphoreType.DMA((count,)),
            pltpu.SemaphoreType.DMA((slots, count)),
            pltpu.SemaphoreType.DMA((slots, count)),
            pltpu.SemaphoreType.DMA((1,)),
        ],
        compiler_params=pltpu.CompilerParams(collective_id=0, has_side_effects=True),
    )(part)


def freq_beams(freq_ids, aligned_rows, slow_rows):
    return lax.map(lambda pair: beam_freq(pair[0], pair[1], slow_rows), (freq_ids, aligned_rows))


def band_matrix(taps, length):
    rows = jnp.arange(length, dtype=jnp.int32)[:, None]
    columns = jnp.arange(length + 2 * HALF, dtype=jnp.int32)[None, :]
    offset = columns - rows
    picks = jnp.arange(TAPS, dtype=jnp.int32)[:, None, None]
    return jnp.sum(jnp.where(offset[None] == picks, taps[:, None, None], 0.0), axis=0)


def blur(volume, bands):
    band_x, square_y, square_z = bands
    padded = with_halo(volume.astype(jnp.bfloat16), (("grid", 0),), HALF).astype(volume.dtype)
    along_x = jnp.einsum("ip,pyz->iyz", band_x, padded, precision=lax.Precision.HIGHEST)
    along_y = jnp.einsum("jq,xqz->xjz", square_y, along_x, precision=lax.Precision.HIGHEST)
    return jnp.einsum("xyw,kw->xyk", along_y, square_z, precision=lax.Precision.HIGHEST)


def blur_narrowing(volume, taps, square_y, square_z):
    band_x = band_matrix(taps, volume.shape[0] - 2 * HALF)
    along_x = jnp.einsum("ip,pyz->iyz", band_x, volume, precision=lax.Precision.HIGHEST)
    along_y = jnp.einsum("jq,xqz->xjz", square_y, along_x, precision=lax.Precision.HIGHEST)
    return jnp.einsum("xyw,kw->xyk", along_y, square_z, precision=lax.Precision.HIGHEST)


def deblur(observed, halo_tiles, spread_taps):
    tiles = lax.axis_size("grid")
    me = lax.axis_index("grid")
    reach = ITERS * 2 * HALF
    cut = halo_tiles * CX - reach
    observed = observed[cut : observed.shape[0] - cut]
    width = observed.shape[0]
    cell = (me - halo_tiles) * CX + cut + jnp.arange(width, dtype=jnp.int32)
    inside = (cell >= 0) & (cell < tiles * CX)
    square_y = band_matrix(spread_taps[1], CY)[:, HALF : HALF + CY]
    square_z = band_matrix(spread_taps[2], CZ)[:, HALF : HALF + CZ]
    estimate = jnp.where(inside[:, None, None], observed, 0.0)
    for sweep in range(ITERS):
        low = 2 * HALF * sweep + HALF
        blurred = blur_narrowing(estimate, spread_taps[0], square_y, square_z)
        ratio = jnp.where(
            inside[low : width - low, None, None], observed[low : width - low] / blurred, 0.0
        )
        estimate = estimate[2 * HALF : estimate.shape[0] - 2 * HALF] * blur_narrowing(
            ratio, spread_taps[0], square_y, square_z
        )
    return estimate


def band_of(taps_ref, axis, rows, cols):
    offset = cols - rows + HALF
    band = jnp.zeros(offset.shape, jnp.float32)
    for tap in range(TAPS):
        band = jnp.where(offset == tap, taps_ref[axis, tap], band)
    return band


def mirror(index, length):
    return jnp.where(index < length // 2, index, 3 * (length // 2) - 1 - index)


def deblur_kernel(taps_ref, obs_ref, out_ref, seen_ref, kx_ref, kz_ref):
    tiles = lax.axis_size("grid")
    me = lax.axis_index("grid")
    planes, width, depth = obs_ref.shape
    shape_x = kx_ref.shape
    kx_ref[...] = band_of(
        taps_ref, 0, lax.broadcasted_iota(jnp.int32, shape_x, 0) + HALF, lax.broadcasted_iota(jnp.int32, shape_x, 1)
    )
    shape_z = kz_ref.shape
    kz_ref[...] = band_of(
        taps_ref,
        2,
        mirror(lax.broadcasted_iota(jnp.int32, shape_z, 1), depth),
        mirror(lax.broadcasted_iota(jnp.int32, shape_z, 0), depth),
    )
    halo_tiles = (width - CX) // (2 * CX)
    highest = lax.Precision.HIGH

    def inside(low, size):
        cell = (me - halo_tiles) * CX + low + lax.broadcasted_iota(jnp.int32, (size, depth), 0)
        return (cell >= 0) & (cell < tiles * CX)

    lanes = planes * depth

    def blur(volume):
        size_in = volume.shape[0]
        size_out = size_in - 2 * HALF
        band = kx_ref[0:size_out, 0:size_in]
        along_x = jnp.dot(band, volume, precision=highest, preferred_element_type=jnp.float32)
        along_y = []
        for y in range(planes):
            total = None
            for q in range(planes):
                term = taps_ref[1, q - y + HALF] * along_x[:, q * depth : (q + 1) * depth]
                total = term if total is None else total + term
            along_y.append(total)
        joined = jnp.concatenate(along_y, axis=0)
        along_z = jnp.dot(joined, kz_ref[...], precision=highest, preferred_element_type=jnp.float32)
        return jnp.concatenate([along_z[y * size_out : (y + 1) * size_out] for y in range(planes)], axis=1)

    def inside_wide(low, size):
        cell = (me - halo_tiles) * CX + low + lax.broadcasted_iota(jnp.int32, (size, lanes), 0)
        return (cell >= 0) & (cell < tiles * CX)

    observed = jnp.concatenate([obs_ref[y] for y in range(planes)], axis=1)
    estimate = jnp.where(inside_wide(0, width), observed, 0.0)
    for sweep in range(ITERS):
        low = 2 * HALF * sweep + HALF
        blurred = blur(estimate)
        size = blurred.shape[0]
        ratio = jnp.where(inside_wide(low, size), observed[low : low + size] / blurred, 0.0)
        spread = blur(ratio)
        estimate = estimate[2 * HALF : 2 * HALF + spread.shape[0]] * spread
    for y in range(planes):
        out_ref[:, y, :] = estimate[:, y * depth : (y + 1) * depth]
        seen_ref[:, y, :] = obs_ref[y, halo_tiles * CX : halo_tiles * CX + CX, :]


def deblur_tile(observed, spread_taps):
    planes, width, depth = observed.shape
    vmem = pl.BlockSpec(memory_space=pltpu.VMEM)
    return pl.pallas_call(
        deblur_kernel,
        out_shape=[jax.ShapeDtypeStruct((CX, planes, depth), jnp.float32)] * 2,
        in_specs=[pl.BlockSpec(memory_space=pltpu.SMEM), vmem],
        out_specs=[vmem, vmem],
        scratch_shapes=[
            pltpu.VMEM((width - 2 * HALF, width), jnp.float32),
            pltpu.VMEM((depth, depth), jnp.float32),
        ],
    )(spread_taps, observed)


def per_device(spectra, lag_samples, slowness, spread_taps):
    groups = lax.axis_size("sta")
    own_count = FREQS // groups
    first_bin = lax.axis_index("sta") * own_count
    block = spectra.shape[2]
    spec_send = spectra.reshape(groups, own_count, 2, block)
    halo_tiles = -(-(ITERS * 2 * HALF) // CX)
    summed = beam_power(spec_send, lag_samples, slowness[0], halo_tiles)
    observed = summed / (FREQS * STATIONS) + BACKGROUND
    slots = observed.shape[0]
    observed = observed.reshape(slots, CY, CX, CZ)
    observed = jnp.concatenate([observed[:, :, : CX // 2], observed[:, :, CX // 2 :][:, :, ::-1]], axis=2)
    planes = observed.transpose(1, 0, 2, 3).reshape(CY, slots * CX, CZ)
    estimate, stacked = deblur_tile(planes, spread_taps)
    estimate = jnp.concatenate([estimate[..., : CZ // 2], estimate[..., CZ // 2 :][..., ::-1]], axis=-1)
    stacked = jnp.concatenate([stacked[..., : CZ // 2], stacked[..., CZ // 2 :][..., ::-1]], axis=-1)
    return (stacked[None], estimate[None])


def solution(mesh):
    placed = (P(None, None, "sta"), P("grid", "sta"), P("grid", None, "sta"), P())
    return jax.shard_map(
        per_device,
        mesh=mesh,
        in_specs=placed,
        out_specs=(P("grid", None, None, None), P("grid", None, None, None)),
        check_vma=False,
    )
```

```python
import math

import jax
import jax.numpy as jnp
from jax import lax
from jax.sharding import PartitionSpec as P
from jax.experimental import pallas as pl
from jax.experimental.pallas import tpu as pltpu

STATIONS = 6144
FREQS = 64
F0 = 600
NT = 6000
TAPS = 17
HALF = 8
ITERS = 4
CX = 32
CY = 8
CZ = 128


TWO_PI = 2.0 * math.pi
BACKGROUND = 0.05


def with_halo(array, sides, width):
    for axis, dim in sides:
        size, length = (lax.axis_size(axis), array.shape[dim])
        up = [(i, (i + 1) % size) for i in range(size - 1)]
        down = [(j, i) for i, j in up]
        last = lax.slice_in_dim(array, length - width, length, axis=dim)
        leading = lax.slice_in_dim(array, 0, width, axis=dim)
        before = lax.ppermute(last, axis, up)
        after = lax.ppermute(leading, axis, down)
        array = jnp.concatenate([before, array, after], axis=dim)
    return array


def align_rows(spectra, lag_row):
    bins = F0 + jnp.arange(FREQS, dtype=jnp.int32)
    cycles = bins[:, None] * lag_row[None, :] % NT
    turned = cycles.astype(jnp.float32) * (TWO_PI / NT)
    cosine = jnp.cos(turned)
    sine = jnp.sin(turned)
    real_in = spectra[:, 0, :].astype(jnp.float32)
    imag_in = spectra[:, 1, :].astype(jnp.float32)
    real_out = real_in * cosine + imag_in * sine
    imag_out = imag_in * cosine - real_in * sine
    return jnp.stack([real_out, imag_out], axis=1).astype(jnp.bfloat16)


def beam_freq(freq, aligned_row, slow_rows):
    omega = (F0 + freq).astype(jnp.float32) * (TWO_PI / NT)
    slow = slow_rows.astype(jnp.float32)
    x_coord = jnp.arange(CX, dtype=jnp.float32) - (CX - 1) / 2.0
    y_coord = jnp.arange(CY, dtype=jnp.float32) - (CY - 1) / 2.0
    z_coord = jnp.arange(CZ, dtype=jnp.float32) - (CZ - 1) / 2.0
    phase_x = (omega * slow[0])[None, :] * x_coord[:, None]
    phase_y = (omega * slow[1])[None, :] * y_coord[:, None]
    phase = phase_x[:, None, :] + phase_y[None, :, :]
    cosine = jnp.cos(phase)
    sine = jnp.sin(phase)
    real_in = aligned_row[0].astype(jnp.float32)[None, None, :]
    imag_in = aligned_row[1].astype(jnp.float32)[None, None, :]
    front_real = (real_in * cosine + imag_in * sine).astype(jnp.bfloat16).reshape(CX * CY, -1)
    front_imag = (imag_in * cosine - real_in * sine).astype(jnp.bfloat16).reshape(CX * CY, -1)
    left_side = jnp.concatenate([front_real, front_imag], axis=1)
    phase_z = (omega * slow[2])[:, None] * z_coord[None, :]
    depth_real = jnp.cos(phase_z).astype(jnp.bfloat16)
    depth_imag = jnp.sin(phase_z).astype(jnp.bfloat16)
    upper_rows = jnp.concatenate([depth_real, -depth_imag], axis=1)
    lower_rows = jnp.concatenate([depth_imag, depth_real], axis=1)
    right_side = jnp.concatenate([upper_rows, lower_rows], axis=0)
    return jnp.dot(left_side, right_side, preferred_element_type=jnp.float32)


CHUNK = 768


def exp_neg(angle):
    return jnp.cos(angle), -jnp.sin(angle)


def enter_barrier(count, reach):
    me = lax.axis_index("sta")
    tile = lax.axis_index("grid")
    tiles = lax.axis_size("grid")
    mesh_ids = pl.DeviceIdType.MESH
    barrier = pltpu.get_barrier_semaphore()
    for shift in range(1, count):
        pl.semaphore_signal(barrier, inc=1, device_id=(tile, lax.rem(me + shift, count)), device_id_type=mesh_ids)
    neighbours = jnp.int32(0)
    for k in range(-reach, reach + 1):
        if k == 0:
            continue
        there = (tile + k >= 0) & (tile + k < tiles)
        neighbours = neighbours + there.astype(jnp.int32)

        @pl.when(there)
        def _():
            pl.semaphore_signal(barrier, inc=1, device_id=(tile + k, me), device_id_type=mesh_ids)

    pl.semaphore_wait(barrier, count - 1 + neighbours)


def exchange_inputs(spec_ref, lag_ref, slow_ref, spec_in, lag_in, slow_in, local_sem, send_sem, recv_sem, then, reach):
    count = spec_in.shape[0]
    me = lax.axis_index("sta")
    tile = lax.axis_index("grid")
    mesh_ids = pl.DeviceIdType.MESH
    enter_barrier(count, reach)
    pairs = ((spec_ref, spec_in), (lag_ref, lag_in), (slow_ref, slow_in))
    local = []
    for kind, (source, target) in enumerate(pairs):
        own = source.at[me] if kind == 0 else source
        copy = pltpu.make_async_copy(own, target.at[me], local_sem.at[kind])
        copy.start()
        local.append(copy)
    sends = []
    for shift in range(1, count):
        peer = lax.rem(me + shift, count)
        for kind, (source, target) in enumerate(pairs):
            part = source.at[peer] if kind == 0 else source
            copy = pltpu.make_async_remote_copy(
                src_ref=part,
                dst_ref=target.at[me],
                send_sem=send_sem.at[kind, shift],
                recv_sem=recv_sem.at[kind, me],
                device_id=(tile, peer),
                device_id_type=mesh_ids,
            )
            copy.start()
            sends.append(copy)
    then()
    for copy in local:
        copy.wait()
    for copy in sends:
        copy.wait_send()
    for shift in range(1, count):
        source_id = lax.rem(me + count - shift, count)
        for kind, (source, target) in enumerate(pairs):
            part = source.at[source_id] if kind == 0 else source
            pltpu.make_async_remote_copy(
                src_ref=part,
                dst_ref=target.at[source_id],
                send_sem=send_sem.at[kind, shift],
                recv_sem=recv_sem.at[kind, source_id],
                device_id=(tile, source_id),
                device_id_type=mesh_ids,
            ).wait_recv()


def align_block(spec, lag, slow, source, real_ref, imag_ref, turn_ref):
    bins, block = spec.shape[0], spec.shape[2]
    first_bin = lax.axis_index("sta") * bins
    bin_rows = (F0 + first_bin + lax.broadcasted_iota(jnp.int32, (bins, block), 0)).astype(jnp.float32)
    cols = pl.ds(pl.multiple_of(source * block, 128), block)
    product = bin_rows * lag.astype(jnp.float32)
    whole = jnp.floor(product * (1.0 / NT))
    left = product - whole * NT
    left = jnp.where(left < 0.0, left + NT, left)
    left = jnp.where(left >= NT, left - NT, left)
    turned = left * (TWO_PI / NT)
    cosine = jnp.cos(turned)
    sine = jnp.sin(turned)
    real_in = spec[:, 0, :].astype(jnp.float32)
    imag_in = spec[:, 1, :].astype(jnp.float32)
    real_ref[:, cols] = (real_in * cosine + imag_in * sine).astype(jnp.bfloat16).astype(jnp.float32)
    imag_ref[:, cols] = (imag_in * cosine - real_in * sine).astype(jnp.bfloat16).astype(jnp.float32)
    turn_ref[:, cols] = slow.astype(jnp.float32)


def complex_times(left, right):
    return left[0] * right[0] - left[1] * right[1], left[0] * right[1] + left[1] * right[0]


def factor_rows(turn_x, turn_y, turn_z, rows8, rows16):
    return (
        exp_neg(turn_x * (rows8 - 3.5)),
        exp_neg(turn_x * (8.0 * (rows8 - 1.5))),
        exp_neg(turn_y * (rows8 - 3.5)),
        exp_neg(turn_z * (rows16 - 7.5)),
        exp_neg(turn_z * (16.0 * (rows8 - 3.5))),
    )


def beam_kernel(spec_ref, lag_ref, slow_ref, out_ref, spec_in, lag_in, slow_in, local_sem, send_sem, recv_sem,
                real_ref, imag_ref, turn_ref, acc_ref, left_ref, right_ref, power_ref, pieces, send_rs, recv_rs,
                send_ag, recv_ag, share_sem):
    count, bins, block = spec_in.shape[0], spec_in.shape[1], spec_in.shape[3]
    me = lax.axis_index("sta")
    first_bin = me * bins
    width = CHUNK
    per_block = block // width
    half_z = CZ // 2
    rows8 = lax.broadcasted_iota(jnp.int32, (8, width), 0).astype(jnp.float32)
    rows16 = lax.broadcasted_iota(jnp.int32, (16, width), 0).astype(jnp.float32)
    omega0 = (F0 + first_bin).astype(jnp.float32) * (TWO_PI / NT)
    step = TWO_PI / NT
    acc_ref[...] = jnp.zeros_like(acc_ref)

    def per_chunk(k, carry):
        source = lax.rem(me + k // per_block, count)
        cols = pl.ds(pl.multiple_of(source * block + lax.rem(k, per_block) * width, 128), width)
        slow_x = turn_ref[0:1, cols]
        slow_y = turn_ref[1:2, cols]
        slow_z = turn_ref[2:3, cols]
        start = factor_rows(omega0 * slow_x, omega0 * slow_y, omega0 * slow_z, rows8, rows16)
        ratio = factor_rows(step * slow_x, step * slow_y, step * slow_z, rows8, rows16)

        def per_bin(f, state):
            (a_r, a_i), (b_r, b_i), (y_r, y_i), (c_r, c_i), (d_r, d_i) = state
            real_in = real_ref[pl.ds(f, 1), cols]
            imag_in = imag_ref[pl.ds(f, 1), cols]
            q_r = real_in * y_r - imag_in * y_i
            q_i = real_in * y_i + imag_in * y_r
            near = [complex_times((b_r[m : m + 1], b_i[m : m + 1]), (a_r, a_i)) for m in range(CX // 16)]
            cells = CX * CY
            for y in range(CY):
                qq_r, qq_i = q_r[y : y + 1], q_i[y : y + 1]
                lo_r, lo_i, hi_r, hi_i = [], [], [], []
                for x_r, x_i in near:
                    t1, t2 = qq_r * x_r, qq_i * x_i
                    t3, t4 = qq_r * x_i, qq_i * x_r
                    lo_r.append(t1 - t2)
                    lo_i.append(t3 + t4)
                    hi_r.append(t1 + t2)
                    hi_i.append(t4 - t3)
                row = y * CX
                half = CX // 2
                left_ref[row : row + half, :] = jnp.concatenate(lo_r, axis=0).astype(jnp.bfloat16)
                left_ref[row + half : row + CX, :] = jnp.concatenate(hi_r, axis=0).astype(jnp.bfloat16)
                left_ref[cells + row : cells + row + half, :] = jnp.concatenate(lo_i, axis=0).astype(jnp.bfloat16)
                left_ref[cells + row + half : cells + row + CX, :] = jnp.concatenate(hi_i, axis=0).astype(jnp.bfloat16)
            for m in range(half_z // 16):
                z_r, z_i = complex_times((d_r[m : m + 1], d_i[m : m + 1]), (c_r, c_i))
                row = 16 * m
                right_ref[row : row + 16, :] = z_r.astype(jnp.bfloat16)
                right_ref[half_z + row : half_z + row + 16, :] = z_i.astype(jnp.bfloat16)
            acc_ref[f] += lax.dot_general(
                left_ref[...], right_ref[...], (((1,), (1,)), ((), ())), preferred_element_type=jnp.float32
            )
            return tuple(complex_times(now, turn) for now, turn in zip(state, ratio))

        lax.fori_loop(0, bins, per_bin, start, unroll=4)
        return carry

    def own_block():
        align_block(spec_ref.at[me], lag_ref[...], slow_ref[...], me, real_ref, imag_ref, turn_ref)
        lax.fori_loop(0, per_block, per_chunk, 0)

    exchange_inputs(
        spec_ref, lag_ref, slow_ref, spec_in, lag_in, slow_in, local_sem, send_sem, recv_sem, own_block, out_ref.shape[0] // 2
    )

    def align_other(shift, carry):
        source = lax.rem(me + shift, count)
        align_block(spec_in.at[source], lag_in[source], slow_in[source], source, real_ref, imag_ref, turn_ref)
        return carry

    lax.fori_loop(1, count, align_other, 0)
    lax.fori_loop(per_block, count * per_block, per_chunk, 0)
    cells = CX * CY
    low = jnp.zeros((cells, half_z), jnp.float32)
    high = jnp.zeros((cells, half_z), jnp.float32)
    for f in range(bins):
        sums = acc_ref[f]
        u, w = sums[:cells, :half_z], sums[:cells, half_z:]
        x, v = sums[cells:, :half_z], sums[cells:, half_z:]
        low = low + ((u - v) * (u - v) + (w + x) * (w + x))
        high = high + ((u + v) * (u + v) + (x - w) * (x - w))
    power_ref[:, :half_z] = low
    power_ref[:, half_z:] = high
    share_kernel(power_ref, out_ref, pieces, send_rs, recv_rs, send_ag, recv_ag, share_sem)


def beam_power(spec_send, lag_row, slow_rows, reach):
    count = spec_send.shape[0]
    slots = 2 * reach + 1
    cells = CX * CY
    bins, block = spec_send.shape[1], spec_send.shape[3]
    width = CHUNK
    stations = count * block
    vmem = pl.BlockSpec(memory_space=pltpu.VMEM)
    return pl.pallas_call(
        beam_kernel,
        out_shape=jax.ShapeDtypeStruct((slots, cells, CZ), jnp.float32),
        in_specs=[vmem, vmem, vmem],
        out_specs=vmem,
        scratch_shapes=[
            pltpu.VMEM((count,) + spec_send.shape[1:], jnp.bfloat16),
            pltpu.VMEM((count,) + lag_row.shape, jnp.int32),
            pltpu.VMEM((count,) + slow_rows.shape, jnp.bfloat16),
            pltpu.SemaphoreType.DMA((3,)),
            pltpu.SemaphoreType.DMA((3, count)),
            pltpu.SemaphoreType.DMA((3, count)),
            pltpu.VMEM((bins, stations), jnp.float32),
            pltpu.VMEM((bins, stations), jnp.float32),
            pltpu.VMEM((slow_rows.shape[0], stations), jnp.float32),
            pltpu.VMEM((bins, 2 * CX * CY, CZ), jnp.float32),
            pltpu.VMEM((2 * CX * CY, width), jnp.bfloat16),
            pltpu.VMEM((CZ, width), jnp.bfloat16),
            pltpu.VMEM((cells, CZ), jnp.float32),
            pltpu.VMEM((count, cells // count, CZ), jnp.float32),
            pltpu.SemaphoreType.DMA((count,)),
            pltpu.SemaphoreType.DMA((count,)),
            pltpu.SemaphoreType.DMA((slots, count)),
            pltpu.SemaphoreType.DMA((slots, count)),
            pltpu.SemaphoreType.DMA((1,)),
        ],
        compiler_params=pltpu.CompilerParams(collective_id=1, has_side_effects=True),
    )(spec_send, lag_row, slow_rows)


def share_kernel(part_ref, out_ref, pieces, send_rs, recv_rs, send_ag, recv_ag, local_sem):
    count = pieces.shape[0]
    slots = out_ref.shape[0]
    reach = slots // 2
    rows = pieces.shape[1]
    me = lax.axis_index("sta")
    tile = lax.axis_index("grid")
    tiles = lax.axis_size("grid")
    mesh_ids = pl.DeviceIdType.MESH
    own = pltpu.make_async_copy(part_ref.at[pl.ds(pl.multiple_of(me * rows, 8), rows)], pieces.at[me], local_sem.at[0])
    own.start()
    sends = []
    for shift in range(1, count):
        peer = lax.rem(me + shift, count)
        copy = pltpu.make_async_remote_copy(
            src_ref=part_ref.at[pl.ds(pl.multiple_of(peer * rows, 8), rows)],
            dst_ref=pieces.at[me],
            send_sem=send_rs.at[shift],
            recv_sem=recv_rs.at[me],
            device_id=(tile, peer),
            device_id_type=mesh_ids,
        )
        copy.start()
        sends.append(copy)
    own.wait()
    for copy in sends:
        copy.wait_send()
    for shift in range(1, count):
        source = lax.rem(me + count - shift, count)
        pltpu.make_async_remote_copy(
            src_ref=pieces.at[source],
            dst_ref=pieces.at[source],
            send_sem=send_rs.at[shift],
            recv_sem=recv_rs.at[source],
            device_id=(tile, source),
            device_id_type=mesh_ids,
        ).wait_recv()
    total = pieces[0]
    for source in range(1, count):
        total = total + pieces[source]
    mine = pl.ds(pl.multiple_of(me * rows, 8), rows)
    out_ref[reach, mine] = total
    block = out_ref.at[reach, mine]

    def gather_copy(k, peer, slot):
        return pltpu.make_async_remote_copy(
            src_ref=block,
            dst_ref=out_ref.at[slot, mine],
            send_sem=send_ag.at[slot, peer],
            recv_sem=recv_ag.at[slot, me],
            device_id=(tile + k, peer),
            device_id_type=mesh_ids,
        )

    peers = []
    for shift in range(1, count):
        copy = gather_copy(0, lax.rem(me + shift, count), reach)
        copy.start()
        peers.append(copy)
    for k in range(-reach, reach + 1):
        if k == 0:
            continue

        @pl.when(jnp.logical_not((tile + k >= 0) & (tile + k < tiles)))
        def _():
            out_ref[reach + k] = jnp.zeros(out_ref.shape[1:], out_ref.dtype)

    for copy in peers:
        copy.wait_send()
    for shift in range(1, count):
        source = lax.rem(me + count - shift, count)
        pltpu.make_async_remote_copy(
            src_ref=block,
            dst_ref=out_ref.at[reach, pl.ds(pl.multiple_of(source * rows, 8), rows)],
            send_sem=send_ag.at[reach, source],
            recv_sem=recv_ag.at[reach, source],
            device_id=(tile, source),
            device_id_type=mesh_ids,
        ).wait_recv()

    def halo_copy(k):
        return pltpu.make_async_remote_copy(
            src_ref=out_ref.at[reach],
            dst_ref=out_ref.at[reach - k],
            send_sem=send_ag.at[reach - k, me],
            recv_sem=recv_ag.at[reach - k, me],
            device_id=(tile + k, me),
            device_id_type=mesh_ids,
        )

    for k in range(-reach, reach + 1):
        if k == 0:
            continue

        @pl.when((tile + k >= 0) & (tile + k < tiles))
        def _():
            halo_copy(k).start()

    for k in range(-reach, reach + 1):
        if k == 0:
            continue

        @pl.when((tile + k >= 0) & (tile + k < tiles))
        def _():
            halo_copy(k).wait_send()
            pltpu.make_async_remote_copy(
                src_ref=out_ref.at[reach],
                dst_ref=out_ref.at[reach + k],
                send_sem=send_ag.at[reach + k, me],
                recv_sem=recv_ag.at[reach + k, me],
                device_id=(tile + k, me),
                device_id_type=mesh_ids,
            ).wait_recv()


def share_power(part, reach):
    count = lax.axis_size("sta")
    rows = part.shape[0] // count
    slots = 2 * reach + 1
    return pl.pallas_call(
        share_kernel,
        out_shape=jax.ShapeDtypeStruct((slots,) + part.shape, jnp.float32),
        in_specs=[pl.BlockSpec(memory_space=pltpu.VMEM)],
        out_specs=pl.BlockSpec(memory_space=pltpu.VMEM),
        scratch_shapes=[
            pltpu.VMEM((count, rows, part.shape[1]), jnp.float32),
            pltpu.SemaphoreType.DMA((count,)),
            pltpu.SemaphoreType.DMA((count,)),
            pltpu.SemaphoreType.DMA((slots, count)),
            pltpu.SemaphoreType.DMA((slots, count)),
            pltpu.SemaphoreType.DMA((1,)),
        ],
        compiler_params=pltpu.CompilerParams(collective_id=0, has_side_effects=True),
    )(part)


def freq_beams(freq_ids, aligned_rows, slow_rows):
    return lax.map(lambda pair: beam_freq(pair[0], pair[1], slow_rows), (freq_ids, aligned_rows))


def band_matrix(taps, length):
    rows = jnp.arange(length, dtype=jnp.int32)[:, None]
    columns = jnp.arange(length + 2 * HALF, dtype=jnp.int32)[None, :]
    offset = columns - rows
    picks = jnp.arange(TAPS, dtype=jnp.int32)[:, None, None]
    return jnp.sum(jnp.where(offset[None] == picks, taps[:, None, None], 0.0), axis=0)


def blur(volume, bands):
    band_x, square_y, square_z = bands
    padded = with_halo(volume.astype(jnp.bfloat16), (("grid", 0),), HALF).astype(volume.dtype)
    along_x = jnp.einsum("ip,pyz->iyz", band_x, padded, precision=lax.Precision.HIGHEST)
    along_y = jnp.einsum("jq,xqz->xjz", square_y, along_x, precision=lax.Precision.HIGHEST)
    return jnp.einsum("xyw,kw->xyk", along_y, square_z, precision=lax.Precision.HIGHEST)


def blur_narrowing(volume, taps, square_y, square_z):
    band_x = band_matrix(taps, volume.shape[0] - 2 * HALF)
    along_x = jnp.einsum("ip,pyz->iyz", band_x, volume, precision=lax.Precision.HIGHEST)
    along_y = jnp.einsum("jq,xqz->xjz", square_y, along_x, precision=lax.Precision.HIGHEST)
    return jnp.einsum("xyw,kw->xyk", along_y, square_z, precision=lax.Precision.HIGHEST)


def deblur(observed, halo_tiles, spread_taps):
    tiles = lax.axis_size("grid")
    me = lax.axis_index("grid")
    reach = ITERS * 2 * HALF
    cut = halo_tiles * CX - reach
    observed = observed[cut : observed.shape[0] - cut]
    width = observed.shape[0]
    cell = (me - halo_tiles) * CX + cut + jnp.arange(width, dtype=jnp.int32)
    inside = (cell >= 0) & (cell < tiles * CX)
    square_y = band_matrix(spread_taps[1], CY)[:, HALF : HALF + CY]
    square_z = band_matrix(spread_taps[2], CZ)[:, HALF : HALF + CZ]
    estimate = jnp.where(inside[:, None, None], observed, 0.0)
    for sweep in range(ITERS):
        low = 2 * HALF * sweep + HALF
        blurred = blur_narrowing(estimate, spread_taps[0], square_y, square_z)
        ratio = jnp.where(
            inside[low : width - low, None, None], observed[low : width - low] / blurred, 0.0
        )
        estimate = estimate[2 * HALF : estimate.shape[0] - 2 * HALF] * blur_narrowing(
            ratio, spread_taps[0], square_y, square_z
        )
    return estimate


def band_of(taps_ref, axis, rows, cols):
    offset = cols - rows + HALF
    band = jnp.zeros(offset.shape, jnp.float32)
    for tap in range(TAPS):
        band = jnp.where(offset == tap, taps_ref[axis, tap], band)
    return band


def mirror(index, length):
    return jnp.where(index < length // 2, index, 3 * (length // 2) - 1 - index)


def deblur_kernel(taps_ref, obs_ref, out_ref, seen_ref, kx_ref, kz_ref):
    tiles = lax.axis_size("grid")
    me = lax.axis_index("grid")
    planes, width, depth = obs_ref.shape
    shape_x = kx_ref.shape
    kx_ref[...] = band_of(
        taps_ref, 0, lax.broadcasted_iota(jnp.int32, shape_x, 0) + HALF, lax.broadcasted_iota(jnp.int32, shape_x, 1)
    )
    shape_z = kz_ref.shape
    kz_ref[...] = band_of(
        taps_ref,
        2,
        mirror(lax.broadcasted_iota(jnp.int32, shape_z, 1), depth),
        mirror(lax.broadcasted_iota(jnp.int32, shape_z, 0), depth),
    )
    halo_tiles = (width - CX) // (2 * CX)
    highest = lax.Precision.HIGH

    def inside(low, size):
        cell = (me - halo_tiles) * CX + low + lax.broadcasted_iota(jnp.int32, (size, depth), 0)
        return (cell >= 0) & (cell < tiles * CX)

    lanes = planes * depth

    def blur(volume):
        size_in = volume.shape[0]
        size_out = size_in - 2 * HALF
        band = kx_ref[0:size_out, 0:size_in]
        along_x = jnp.dot(band, volume, precision=highest, preferred_element_type=jnp.float32)
        along_y = []
        for y in range(planes):
            total = None
            for q in range(planes):
                term = taps_ref[1, q - y + HALF] * along_x[:, q * depth : (q + 1) * depth]
                total = term if total is None else total + term
            along_y.append(total)
        joined = jnp.concatenate(along_y, axis=0)
        along_z = jnp.dot(joined, kz_ref[...], precision=highest, preferred_element_type=jnp.float32)
        return jnp.concatenate([along_z[y * size_out : (y + 1) * size_out] for y in range(planes)], axis=1)

    def inside_wide(low, size):
        cell = (me - halo_tiles) * CX + low + lax.broadcasted_iota(jnp.int32, (size, lanes), 0)
        return (cell >= 0) & (cell < tiles * CX)

    observed = jnp.concatenate([obs_ref[y] for y in range(planes)], axis=1) / (FREQS * STATIONS) + BACKGROUND
    estimate = jnp.where(inside_wide(0, width), observed, 0.0)
    for sweep in range(ITERS):
        low = 2 * HALF * sweep + HALF
        blurred = blur(estimate)
        size = blurred.shape[0]
        ratio = jnp.where(inside_wide(low, size), observed[low : low + size] / blurred, 0.0)
        spread = blur(ratio)
        estimate = estimate[2 * HALF : 2 * HALF + spread.shape[0]] * spread
    for y in range(planes):
        out_ref[:, y, :] = estimate[:, y * depth : (y + 1) * depth]
        seen_ref[:, y, :] = observed[halo_tiles * CX : halo_tiles * CX + CX, y * depth : (y + 1) * depth]


def deblur_tile(observed, spread_taps):
    planes, width, depth = observed.shape
    vmem = pl.BlockSpec(memory_space=pltpu.VMEM)
    return pl.pallas_call(
        deblur_kernel,
        out_shape=[jax.ShapeDtypeStruct((CX, planes, depth), jnp.float32)] * 2,
        in_specs=[pl.BlockSpec(memory_space=pltpu.SMEM), vmem],
        out_specs=[vmem, vmem],
        scratch_shapes=[
            pltpu.VMEM((width - 2 * HALF, width), jnp.float32),
            pltpu.VMEM((depth, depth), jnp.float32),
        ],
    )(spread_taps, observed)


def per_device(spectra, lag_samples, slowness, spread_taps):
    groups = lax.axis_size("sta")
    own_count = FREQS // groups
    first_bin = lax.axis_index("sta") * own_count
    block = spectra.shape[2]
    spec_send = spectra.reshape(groups, own_count, 2, block)
    halo_tiles = -(-(ITERS * 2 * HALF) // CX)
    summed = beam_power(spec_send, lag_samples, slowness[0], halo_tiles)
    observed = summed
    slots = observed.shape[0]
    observed = observed.reshape(slots, CY, CX, CZ)
    observed = jnp.concatenate([observed[:, :, : CX // 2], observed[:, :, CX // 2 :][:, :, ::-1]], axis=2)
    planes = observed.transpose(1, 0, 2, 3).reshape(CY, slots * CX, CZ)
    estimate, stacked = deblur_tile(planes, spread_taps)
    estimate = jnp.concatenate([estimate[..., : CZ // 2], estimate[..., CZ // 2 :][..., ::-1]], axis=-1)
    stacked = jnp.concatenate([stacked[..., : CZ // 2], stacked[..., CZ // 2 :][..., ::-1]], axis=-1)
    return (stacked[None], estimate[None])


def solution(mesh):
    placed = (P(None, None, "sta"), P("grid", "sta"), P("grid", None, "sta"), P())
    return jax.shard_map(
        per_device,
        mesh=mesh,
        in_specs=placed,
        out_specs=(P("grid", None, None, None), P("grid", None, None, None)),
        check_vma=False,
    )
```

```python
import math

import jax
import jax.numpy as jnp
from jax import lax
from jax.sharding import PartitionSpec as P
from jax.experimental import pallas as pl
from jax.experimental.pallas import tpu as pltpu

STATIONS = 6144
FREQS = 64
F0 = 600
NT = 6000
TAPS = 17
HALF = 8
ITERS = 4
CX = 32
CY = 8
CZ = 128


TWO_PI = 2.0 * math.pi
BACKGROUND = 0.05


def with_halo(array, sides, width):
    for axis, dim in sides:
        size, length = (lax.axis_size(axis), array.shape[dim])
        up = [(i, (i + 1) % size) for i in range(size - 1)]
        down = [(j, i) for i, j in up]
        last = lax.slice_in_dim(array, length - width, length, axis=dim)
        leading = lax.slice_in_dim(array, 0, width, axis=dim)
        before = lax.ppermute(last, axis, up)
        after = lax.ppermute(leading, axis, down)
        array = jnp.concatenate([before, array, after], axis=dim)
    return array


def align_rows(spectra, lag_row):
    bins = F0 + jnp.arange(FREQS, dtype=jnp.int32)
    cycles = bins[:, None] * lag_row[None, :] % NT
    turned = cycles.astype(jnp.float32) * (TWO_PI / NT)
    cosine = jnp.cos(turned)
    sine = jnp.sin(turned)
    real_in = spectra[:, 0, :].astype(jnp.float32)
    imag_in = spectra[:, 1, :].astype(jnp.float32)
    real_out = real_in * cosine + imag_in * sine
    imag_out = imag_in * cosine - real_in * sine
    return jnp.stack([real_out, imag_out], axis=1).astype(jnp.bfloat16)


def beam_freq(freq, aligned_row, slow_rows):
    omega = (F0 + freq).astype(jnp.float32) * (TWO_PI / NT)
    slow = slow_rows.astype(jnp.float32)
    x_coord = jnp.arange(CX, dtype=jnp.float32) - (CX - 1) / 2.0
    y_coord = jnp.arange(CY, dtype=jnp.float32) - (CY - 1) / 2.0
    z_coord = jnp.arange(CZ, dtype=jnp.float32) - (CZ - 1) / 2.0
    phase_x = (omega * slow[0])[None, :] * x_coord[:, None]
    phase_y = (omega * slow[1])[None, :] * y_coord[:, None]
    phase = phase_x[:, None, :] + phase_y[None, :, :]
    cosine = jnp.cos(phase)
    sine = jnp.sin(phase)
    real_in = aligned_row[0].astype(jnp.float32)[None, None, :]
    imag_in = aligned_row[1].astype(jnp.float32)[None, None, :]
    front_real = (real_in * cosine + imag_in * sine).astype(jnp.bfloat16).reshape(CX * CY, -1)
    front_imag = (imag_in * cosine - real_in * sine).astype(jnp.bfloat16).reshape(CX * CY, -1)
    left_side = jnp.concatenate([front_real, front_imag], axis=1)
    phase_z = (omega * slow[2])[:, None] * z_coord[None, :]
    depth_real = jnp.cos(phase_z).astype(jnp.bfloat16)
    depth_imag = jnp.sin(phase_z).astype(jnp.bfloat16)
    upper_rows = jnp.concatenate([depth_real, -depth_imag], axis=1)
    lower_rows = jnp.concatenate([depth_imag, depth_real], axis=1)
    right_side = jnp.concatenate([upper_rows, lower_rows], axis=0)
    return jnp.dot(left_side, right_side, preferred_element_type=jnp.float32)


CHUNK = 768


def exp_neg(angle):
    return jnp.cos(angle), -jnp.sin(angle)


def enter_barrier(count, reach):
    me = lax.axis_index("sta")
    tile = lax.axis_index("grid")
    tiles = lax.axis_size("grid")
    mesh_ids = pl.DeviceIdType.MESH
    barrier = pltpu.get_barrier_semaphore()
    for shift in range(1, count):
        pl.semaphore_signal(barrier, inc=1, device_id=(tile, lax.rem(me + shift, count)), device_id_type=mesh_ids)
    neighbours = jnp.int32(0)
    for k in range(-reach, reach + 1):
        if k == 0:
            continue
        there = (tile + k >= 0) & (tile + k < tiles)
        neighbours = neighbours + there.astype(jnp.int32)

        @pl.when(there)
        def _():
            pl.semaphore_signal(barrier, inc=1, device_id=(tile + k, me), device_id_type=mesh_ids)

    pl.semaphore_wait(barrier, count - 1 + neighbours)


def exchange_inputs(spec_ref, lag_ref, slow_ref, spec_in, lag_in, slow_in, local_sem, send_sem, recv_sem, then, reach):
    count = spec_in.shape[0]
    me = lax.axis_index("sta")
    tile = lax.axis_index("grid")
    mesh_ids = pl.DeviceIdType.MESH
    enter_barrier(count, reach)
    pairs = ((spec_ref, spec_in), (lag_ref, lag_in), (slow_ref, slow_in))
    local = []
    for kind, (source, target) in enumerate(pairs):
        own = source.at[me] if kind == 0 else source
        copy = pltpu.make_async_copy(own, target.at[me], local_sem.at[kind])
        copy.start()
        local.append(copy)
    sends = []
    for shift in range(1, count):
        peer = lax.rem(me + shift, count)
        for kind, (source, target) in enumerate(pairs):
            part = source.at[peer] if kind == 0 else source
            copy = pltpu.make_async_remote_copy(
                src_ref=part,
                dst_ref=target.at[me],
                send_sem=send_sem.at[kind, shift],
                recv_sem=recv_sem.at[kind, me],
                device_id=(tile, peer),
                device_id_type=mesh_ids,
            )
            copy.start()
            sends.append(copy)
    then()
    for copy in local:
        copy.wait()
    for copy in sends:
        copy.wait_send()
    for shift in range(1, count):
        source_id = lax.rem(me + count - shift, count)
        for kind, (source, target) in enumerate(pairs):
            part = source.at[source_id] if kind == 0 else source
            pltpu.make_async_remote_copy(
                src_ref=part,
                dst_ref=target.at[source_id],
                send_sem=send_sem.at[kind, shift],
                recv_sem=recv_sem.at[kind, source_id],
                device_id=(tile, source_id),
                device_id_type=mesh_ids,
            ).wait_recv()


def align_block(spec, lag, slow, source, real_ref, imag_ref, turn_ref):
    bins, block = spec.shape[0], spec.shape[2]
    first_bin = lax.axis_index("sta") * bins
    bin_rows = (F0 + first_bin + lax.broadcasted_iota(jnp.int32, (bins, block), 0)).astype(jnp.float32)
    cols = pl.ds(pl.multiple_of(source * block, 128), block)
    product = bin_rows * lag.astype(jnp.float32)
    whole = jnp.floor(product * (1.0 / NT))
    left = product - whole * NT
    left = jnp.where(left < 0.0, left + NT, left)
    left = jnp.where(left >= NT, left - NT, left)
    turned = left * (TWO_PI / NT)
    cosine = jnp.cos(turned)
    sine = jnp.sin(turned)
    real_in = spec[:, 0, :].astype(jnp.float32)
    imag_in = spec[:, 1, :].astype(jnp.float32)
    real_ref[:, cols] = (real_in * cosine + imag_in * sine).astype(jnp.bfloat16).astype(jnp.float32)
    imag_ref[:, cols] = (imag_in * cosine - real_in * sine).astype(jnp.bfloat16).astype(jnp.float32)
    turn_ref[:, cols] = slow.astype(jnp.float32)


def complex_times(left, right):
    return left[0] * right[0] - left[1] * right[1], left[0] * right[1] + left[1] * right[0]


def factor_rows(turn_x, turn_y, turn_z, rows8, rows16):
    return (
        exp_neg(turn_x * (rows8 - 3.5)),
        exp_neg(turn_x * (8.0 * (rows8 - 1.5))),
        exp_neg(turn_y * (rows8 - 3.5)),
        exp_neg(turn_z * (rows16 - 7.5)),
        exp_neg(turn_z * (16.0 * (rows8 - 3.5))),
    )


def beam_kernel(spec_ref, lag_ref, slow_ref, out_ref, spec_in, lag_in, slow_in, local_sem, send_sem, recv_sem,
                real_ref, imag_ref, turn_ref, acc_ref, left_ref, right_ref, power_ref, pieces, send_rs, recv_rs,
                send_ag, recv_ag, share_sem):
    count, bins, block = spec_in.shape[0], spec_in.shape[1], spec_in.shape[3]
    me = lax.axis_index("sta")
    first_bin = me * bins
    width = CHUNK
    per_block = block // width
    half_z = CZ // 2
    rows8 = lax.broadcasted_iota(jnp.int32, (8, width), 0).astype(jnp.float32)
    rows16 = lax.broadcasted_iota(jnp.int32, (16, width), 0).astype(jnp.float32)
    omega0 = (F0 + first_bin).astype(jnp.float32) * (TWO_PI / NT)
    step = TWO_PI / NT

    def per_chunk(k, carry, first=False):
        source = lax.rem(me + k // per_block, count)
        cols = pl.ds(pl.multiple_of(source * block + lax.rem(k, per_block) * width, 128), width)
        slow_x = turn_ref[0:1, cols]
        slow_y = turn_ref[1:2, cols]
        slow_z = turn_ref[2:3, cols]
        start = factor_rows(omega0 * slow_x, omega0 * slow_y, omega0 * slow_z, rows8, rows16)
        ratio = factor_rows(step * slow_x, step * slow_y, step * slow_z, rows8, rows16)

        def per_bin(f, state):
            (a_r, a_i), (b_r, b_i), (y_r, y_i), (c_r, c_i), (d_r, d_i) = state
            real_in = real_ref[pl.ds(f, 1), cols]
            imag_in = imag_ref[pl.ds(f, 1), cols]
            q_r = real_in * y_r - imag_in * y_i
            q_i = real_in * y_i + imag_in * y_r
            near = [complex_times((b_r[m : m + 1], b_i[m : m + 1]), (a_r, a_i)) for m in range(CX // 16)]
            cells = CX * CY
            for y in range(CY):
                qq_r, qq_i = q_r[y : y + 1], q_i[y : y + 1]
                lo_r, lo_i, hi_r, hi_i = [], [], [], []
                for x_r, x_i in near:
                    t1, t2 = qq_r * x_r, qq_i * x_i
                    t3, t4 = qq_r * x_i, qq_i * x_r
                    lo_r.append(t1 - t2)
                    lo_i.append(t3 + t4)
                    hi_r.append(t1 + t2)
                    hi_i.append(t4 - t3)
                row = y * CX
                half = CX // 2
                left_ref[row : row + half, :] = jnp.concatenate(lo_r, axis=0).astype(jnp.bfloat16)
                left_ref[row + half : row + CX, :] = jnp.concatenate(hi_r, axis=0).astype(jnp.bfloat16)
                left_ref[cells + row : cells + row + half, :] = jnp.concatenate(lo_i, axis=0).astype(jnp.bfloat16)
                left_ref[cells + row + half : cells + row + CX, :] = jnp.concatenate(hi_i, axis=0).astype(jnp.bfloat16)
            for m in range(half_z // 16):
                z_r, z_i = complex_times((d_r[m : m + 1], d_i[m : m + 1]), (c_r, c_i))
                row = 16 * m
                right_ref[row : row + 16, :] = z_r.astype(jnp.bfloat16)
                right_ref[half_z + row : half_z + row + 16, :] = z_i.astype(jnp.bfloat16)
            product = lax.dot_general(
                left_ref[...], right_ref[...], (((1,), (1,)), ((), ())), preferred_element_type=jnp.float32
            )
            if first:
                acc_ref[f] = product
            else:
                acc_ref[f] += product
            return tuple(complex_times(now, turn) for now, turn in zip(state, ratio))

        lax.fori_loop(0, bins, per_bin, start, unroll=4)
        return carry

    def own_block():
        align_block(spec_ref.at[me], lag_ref[...], slow_ref[...], me, real_ref, imag_ref, turn_ref)
        per_chunk(0, 0, first=True)
        lax.fori_loop(1, per_block, per_chunk, 0)

    exchange_inputs(
        spec_ref, lag_ref, slow_ref, spec_in, lag_in, slow_in, local_sem, send_sem, recv_sem, own_block, out_ref.shape[0] // 2
    )

    def align_other(shift, carry):
        source = lax.rem(me + shift, count)
        align_block(spec_in.at[source], lag_in[source], slow_in[source], source, real_ref, imag_ref, turn_ref)
        return carry

    lax.fori_loop(1, count, align_other, 0)
    lax.fori_loop(per_block, count * per_block, per_chunk, 0)
    cells = CX * CY
    low = jnp.zeros((cells, half_z), jnp.float32)
    high = jnp.zeros((cells, half_z), jnp.float32)
    for f in range(bins):
        sums = acc_ref[f]
        u, w = sums[:cells, :half_z], sums[:cells, half_z:]
        x, v = sums[cells:, :half_z], sums[cells:, half_z:]
        low = low + ((u - v) * (u - v) + (w + x) * (w + x))
        high = high + ((u + v) * (u + v) + (x - w) * (x - w))
    power_ref[:, :half_z] = low
    power_ref[:, half_z:] = high
    share_kernel(power_ref, out_ref, pieces, send_rs, recv_rs, send_ag, recv_ag, share_sem)


def beam_power(spec_send, lag_row, slow_rows, reach):
    count = spec_send.shape[0]
    slots = 2 * reach + 1
    cells = CX * CY
    bins, block = spec_send.shape[1], spec_send.shape[3]
    width = CHUNK
    stations = count * block
    vmem = pl.BlockSpec(memory_space=pltpu.VMEM)
    return pl.pallas_call(
        beam_kernel,
        out_shape=jax.ShapeDtypeStruct((slots, cells, CZ), jnp.float32),
        in_specs=[vmem, vmem, vmem],
        out_specs=vmem,
        scratch_shapes=[
            pltpu.VMEM((count,) + spec_send.shape[1:], jnp.bfloat16),
            pltpu.VMEM((count,) + lag_row.shape, jnp.int32),
            pltpu.VMEM((count,) + slow_rows.shape, jnp.bfloat16),
            pltpu.SemaphoreType.DMA((3,)),
            pltpu.SemaphoreType.DMA((3, count)),
            pltpu.SemaphoreType.DMA((3, count)),
            pltpu.VMEM((bins, stations), jnp.float32),
            pltpu.VMEM((bins, stations), jnp.float32),
            pltpu.VMEM((slow_rows.shape[0], stations), jnp.float32),
            pltpu.VMEM((bins, 2 * CX * CY, CZ), jnp.float32),
            pltpu.VMEM((2 * CX * CY, width), jnp.bfloat16),
            pltpu.VMEM((CZ, width), jnp.bfloat16),
            pltpu.VMEM((cells, CZ), jnp.float32),
            pltpu.VMEM((count, cells // count, CZ), jnp.float32),
            pltpu.SemaphoreType.DMA((count,)),
            pltpu.SemaphoreType.DMA((count,)),
            pltpu.SemaphoreType.DMA((slots, count)),
            pltpu.SemaphoreType.DMA((slots, count)),
            pltpu.SemaphoreType.DMA((1,)),
        ],
        compiler_params=pltpu.CompilerParams(collective_id=1, has_side_effects=True),
    )(spec_send, lag_row, slow_rows)


def share_kernel(part_ref, out_ref, pieces, send_rs, recv_rs, send_ag, recv_ag, local_sem):
    count = pieces.shape[0]
    slots = out_ref.shape[0]
    reach = slots // 2
    rows = pieces.shape[1]
    me = lax.axis_index("sta")
    tile = lax.axis_index("grid")
    tiles = lax.axis_size("grid")
    mesh_ids = pl.DeviceIdType.MESH
    own = pltpu.make_async_copy(part_ref.at[pl.ds(pl.multiple_of(me * rows, 8), rows)], pieces.at[me], local_sem.at[0])
    own.start()
    sends = []
    for shift in range(1, count):
        peer = lax.rem(me + shift, count)
        copy = pltpu.make_async_remote_copy(
            src_ref=part_ref.at[pl.ds(pl.multiple_of(peer * rows, 8), rows)],
            dst_ref=pieces.at[me],
            send_sem=send_rs.at[shift],
            recv_sem=recv_rs.at[me],
            device_id=(tile, peer),
            device_id_type=mesh_ids,
        )
        copy.start()
        sends.append(copy)
    own.wait()
    for copy in sends:
        copy.wait_send()
    for shift in range(1, count):
        source = lax.rem(me + count - shift, count)
        pltpu.make_async_remote_copy(
            src_ref=pieces.at[source],
            dst_ref=pieces.at[source],
            send_sem=send_rs.at[shift],
            recv_sem=recv_rs.at[source],
            device_id=(tile, source),
            device_id_type=mesh_ids,
        ).wait_recv()
    total = pieces[0]
    for source in range(1, count):
        total = total + pieces[source]
    mine = pl.ds(pl.multiple_of(me * rows, 8), rows)
    out_ref[reach, mine] = total
    block = out_ref.at[reach, mine]

    def gather_copy(k, peer, slot):
        return pltpu.make_async_remote_copy(
            src_ref=block,
            dst_ref=out_ref.at[slot, mine],
            send_sem=send_ag.at[slot, peer],
            recv_sem=recv_ag.at[slot, me],
            device_id=(tile + k, peer),
            device_id_type=mesh_ids,
        )

    peers = []
    for shift in range(1, count):
        copy = gather_copy(0, lax.rem(me + shift, count), reach)
        copy.start()
        peers.append(copy)
    for k in range(-reach, reach + 1):
        if k == 0:
            continue

        @pl.when(jnp.logical_not((tile + k >= 0) & (tile + k < tiles)))
        def _():
            out_ref[reach + k] = jnp.zeros(out_ref.shape[1:], out_ref.dtype)

    for copy in peers:
        copy.wait_send()
    for shift in range(1, count):
        source = lax.rem(me + count - shift, count)
        pltpu.make_async_remote_copy(
            src_ref=block,
            dst_ref=out_ref.at[reach, pl.ds(pl.multiple_of(source * rows, 8), rows)],
            send_sem=send_ag.at[reach, source],
            recv_sem=recv_ag.at[reach, source],
            device_id=(tile, source),
            device_id_type=mesh_ids,
        ).wait_recv()

    def halo_copy(k):
        return pltpu.make_async_remote_copy(
            src_ref=out_ref.at[reach],
            dst_ref=out_ref.at[reach - k],
            send_sem=send_ag.at[reach - k, me],
            recv_sem=recv_ag.at[reach - k, me],
            device_id=(tile + k, me),
            device_id_type=mesh_ids,
        )

    for k in range(-reach, reach + 1):
        if k == 0:
            continue

        @pl.when((tile + k >= 0) & (tile + k < tiles))
        def _():
            halo_copy(k).start()

    for k in range(-reach, reach + 1):
        if k == 0:
            continue

        @pl.when((tile + k >= 0) & (tile + k < tiles))
        def _():
            halo_copy(k).wait_send()
            pltpu.make_async_remote_copy(
                src_ref=out_ref.at[reach],
                dst_ref=out_ref.at[reach + k],
                send_sem=send_ag.at[reach + k, me],
                recv_sem=recv_ag.at[reach + k, me],
                device_id=(tile + k, me),
                device_id_type=mesh_ids,
            ).wait_recv()


def share_power(part, reach):
    count = lax.axis_size("sta")
    rows = part.shape[0] // count
    slots = 2 * reach + 1
    return pl.pallas_call(
        share_kernel,
        out_shape=jax.ShapeDtypeStruct((slots,) + part.shape, jnp.float32),
        in_specs=[pl.BlockSpec(memory_space=pltpu.VMEM)],
        out_specs=pl.BlockSpec(memory_space=pltpu.VMEM),
        scratch_shapes=[
            pltpu.VMEM((count, rows, part.shape[1]), jnp.float32),
            pltpu.SemaphoreType.DMA((count,)),
            pltpu.SemaphoreType.DMA((count,)),
            pltpu.SemaphoreType.DMA((slots, count)),
            pltpu.SemaphoreType.DMA((slots, count)),
            pltpu.SemaphoreType.DMA((1,)),
        ],
        compiler_params=pltpu.CompilerParams(collective_id=0, has_side_effects=True),
    )(part)


def freq_beams(freq_ids, aligned_rows, slow_rows):
    return lax.map(lambda pair: beam_freq(pair[0], pair[1], slow_rows), (freq_ids, aligned_rows))


def band_matrix(taps, length):
    rows = jnp.arange(length, dtype=jnp.int32)[:, None]
    columns = jnp.arange(length + 2 * HALF, dtype=jnp.int32)[None, :]
    offset = columns - rows
    picks = jnp.arange(TAPS, dtype=jnp.int32)[:, None, None]
    return jnp.sum(jnp.where(offset[None] == picks, taps[:, None, None], 0.0), axis=0)


def blur(volume, bands):
    band_x, square_y, square_z = bands
    padded = with_halo(volume.astype(jnp.bfloat16), (("grid", 0),), HALF).astype(volume.dtype)
    along_x = jnp.einsum("ip,pyz->iyz", band_x, padded, precision=lax.Precision.HIGHEST)
    along_y = jnp.einsum("jq,xqz->xjz", square_y, along_x, precision=lax.Precision.HIGHEST)
    return jnp.einsum("xyw,kw->xyk", along_y, square_z, precision=lax.Precision.HIGHEST)


def blur_narrowing(volume, taps, square_y, square_z):
    band_x = band_matrix(taps, volume.shape[0] - 2 * HALF)
    along_x = jnp.einsum("ip,pyz->iyz", band_x, volume, precision=lax.Precision.HIGHEST)
    along_y = jnp.einsum("jq,xqz->xjz", square_y, along_x, precision=lax.Precision.HIGHEST)
    return jnp.einsum("xyw,kw->xyk", along_y, square_z, precision=lax.Precision.HIGHEST)


def deblur(observed, halo_tiles, spread_taps):
    tiles = lax.axis_size("grid")
    me = lax.axis_index("grid")
    reach = ITERS * 2 * HALF
    cut = halo_tiles * CX - reach
    observed = observed[cut : observed.shape[0] - cut]
    width = observed.shape[0]
    cell = (me - halo_tiles) * CX + cut + jnp.arange(width, dtype=jnp.int32)
    inside = (cell >= 0) & (cell < tiles * CX)
    square_y = band_matrix(spread_taps[1], CY)[:, HALF : HALF + CY]
    square_z = band_matrix(spread_taps[2], CZ)[:, HALF : HALF + CZ]
    estimate = jnp.where(inside[:, None, None], observed, 0.0)
    for sweep in range(ITERS):
        low = 2 * HALF * sweep + HALF
        blurred = blur_narrowing(estimate, spread_taps[0], square_y, square_z)
        ratio = jnp.where(
            inside[low : width - low, None, None], observed[low : width - low] / blurred, 0.0
        )
        estimate = estimate[2 * HALF : estimate.shape[0] - 2 * HALF] * blur_narrowing(
            ratio, spread_taps[0], square_y, square_z
        )
    return estimate


def band_of(taps_ref, axis, rows, cols):
    offset = cols - rows + HALF
    band = jnp.zeros(offset.shape, jnp.float32)
    for tap in range(TAPS):
        band = jnp.where(offset == tap, taps_ref[axis, tap], band)
    return band


def mirror(index, length):
    return jnp.where(index < length // 2, index, 3 * (length // 2) - 1 - index)


def deblur_kernel(taps_ref, obs_ref, out_ref, kx_ref, kz_ref):
    tiles = lax.axis_size("grid")
    me = lax.axis_index("grid")
    planes, width, depth = obs_ref.shape
    shape_x = kx_ref.shape
    kx_ref[...] = band_of(
        taps_ref, 0, lax.broadcasted_iota(jnp.int32, shape_x, 0) + HALF, lax.broadcasted_iota(jnp.int32, shape_x, 1)
    )
    shape_z = kz_ref.shape
    kz_ref[...] = band_of(
        taps_ref,
        2,
        mirror(lax.broadcasted_iota(jnp.int32, shape_z, 1), depth),
        mirror(lax.broadcasted_iota(jnp.int32, shape_z, 0), depth),
    )
    halo_tiles = (width - CX) // (2 * CX)
    highest = lax.Precision.HIGH

    def inside(low, size):
        cell = (me - halo_tiles) * CX + low + lax.broadcasted_iota(jnp.int32, (size, depth), 0)
        return (cell >= 0) & (cell < tiles * CX)

    lanes = planes * depth

    def blur(volume):
        size_in = volume.shape[0]
        size_out = size_in - 2 * HALF
        band = kx_ref[0:size_out, 0:size_in]
        along_x = jnp.dot(band, volume, precision=highest, preferred_element_type=jnp.float32)
        along_y = []
        for y in range(planes):
            total = None
            for q in range(planes):
                term = taps_ref[1, q - y + HALF] * along_x[:, q * depth : (q + 1) * depth]
                total = term if total is None else total + term
            along_y.append(total)
        joined = jnp.concatenate(along_y, axis=0)
        along_z = jnp.dot(joined, kz_ref[...], precision=highest, preferred_element_type=jnp.float32)
        return jnp.concatenate([along_z[y * size_out : (y + 1) * size_out] for y in range(planes)], axis=1)

    def inside_wide(low, size):
        cell = (me - halo_tiles) * CX + low + lax.broadcasted_iota(jnp.int32, (size, lanes), 0)
        return (cell >= 0) & (cell < tiles * CX)

    observed = jnp.concatenate([obs_ref[y] for y in range(planes)], axis=1)
    estimate = jnp.where(inside_wide(0, width), observed, 0.0)
    for sweep in range(ITERS):
        low = 2 * HALF * sweep + HALF
        blurred = blur(estimate)
        size = blurred.shape[0]
        ratio = jnp.where(inside_wide(low, size), observed[low : low + size] / blurred, 0.0)
        spread = blur(ratio)
        estimate = estimate[2 * HALF : 2 * HALF + spread.shape[0]] * spread
    for y in range(planes):
        out_ref[y] = estimate[:, y * depth : (y + 1) * depth]


def deblur_tile(observed, spread_taps):
    planes, width, depth = observed.shape
    vmem = pl.BlockSpec(memory_space=pltpu.VMEM)
    return pl.pallas_call(
        deblur_kernel,
        out_shape=jax.ShapeDtypeStruct((planes, CX, depth), jnp.float32),
        in_specs=[pl.BlockSpec(memory_space=pltpu.SMEM), vmem],
        out_specs=vmem,
        scratch_shapes=[
            pltpu.VMEM((width - 2 * HALF, width), jnp.float32),
            pltpu.VMEM((depth, depth), jnp.float32),
        ],
    )(spread_taps, observed)


def per_device(spectra, lag_samples, slowness, spread_taps):
    groups = lax.axis_size("sta")
    own_count = FREQS // groups
    first_bin = lax.axis_index("sta") * own_count
    block = spectra.shape[2]
    spec_send = spectra.reshape(groups, own_count, 2, block)
    halo_tiles = -(-(ITERS * 2 * HALF) // CX)
    summed = beam_power(spec_send, lag_samples, slowness[0], halo_tiles)
    observed = summed / (FREQS * STATIONS) + BACKGROUND
    slots = observed.shape[0]
    observed = observed.reshape(slots, CY, CX, CZ)
    observed = jnp.concatenate([observed[:, :, : CX // 2], observed[:, :, CX // 2 :][:, :, ::-1]], axis=2)
    planes = observed.transpose(1, 0, 2, 3).reshape(CY, slots * CX, CZ)
    estimate = deblur_tile(planes, spread_taps)
    both = jnp.stack([observed[halo_tiles], estimate])
    both = jnp.concatenate([both[..., : CZ // 2], both[..., CZ // 2 :][..., ::-1]], axis=-1).transpose(0, 2, 1, 3)
    stacked, estimate = both[0], both[1]
    return (stacked[None], estimate[None])


def solution(mesh):
    placed = (P(None, None, "sta"), P("grid", "sta"), P("grid", None, "sta"), P())
    return jax.shard_map(
        per_device,
        mesh=mesh,
        in_specs=placed,
        out_specs=(P("grid", None, None, None), P("grid", None, None, None)),
        check_vma=False,
    )
```

```python
import math

import jax
import jax.numpy as jnp
from jax import lax
from jax.sharding import PartitionSpec as P
from jax.experimental import pallas as pl
from jax.experimental.pallas import tpu as pltpu

STATIONS = 6144
FREQS = 64
F0 = 600
NT = 6000
TAPS = 17
HALF = 8
ITERS = 4
CX = 32
CY = 8
CZ = 128


TWO_PI = 2.0 * math.pi
BACKGROUND = 0.05


def with_halo(array, sides, width):
    for axis, dim in sides:
        size, length = (lax.axis_size(axis), array.shape[dim])
        up = [(i, (i + 1) % size) for i in range(size - 1)]
        down = [(j, i) for i, j in up]
        last = lax.slice_in_dim(array, length - width, length, axis=dim)
        leading = lax.slice_in_dim(array, 0, width, axis=dim)
        before = lax.ppermute(last, axis, up)
        after = lax.ppermute(leading, axis, down)
        array = jnp.concatenate([before, array, after], axis=dim)
    return array


def align_rows(spectra, lag_row):
    bins = F0 + jnp.arange(FREQS, dtype=jnp.int32)
    cycles = bins[:, None] * lag_row[None, :] % NT
    turned = cycles.astype(jnp.float32) * (TWO_PI / NT)
    cosine = jnp.cos(turned)
    sine = jnp.sin(turned)
    real_in = spectra[:, 0, :].astype(jnp.float32)
    imag_in = spectra[:, 1, :].astype(jnp.float32)
    real_out = real_in * cosine + imag_in * sine
    imag_out = imag_in * cosine - real_in * sine
    return jnp.stack([real_out, imag_out], axis=1).astype(jnp.bfloat16)


def beam_freq(freq, aligned_row, slow_rows):
    omega = (F0 + freq).astype(jnp.float32) * (TWO_PI / NT)
    slow = slow_rows.astype(jnp.float32)
    x_coord = jnp.arange(CX, dtype=jnp.float32) - (CX - 1) / 2.0
    y_coord = jnp.arange(CY, dtype=jnp.float32) - (CY - 1) / 2.0
    z_coord = jnp.arange(CZ, dtype=jnp.float32) - (CZ - 1) / 2.0
    phase_x = (omega * slow[0])[None, :] * x_coord[:, None]
    phase_y = (omega * slow[1])[None, :] * y_coord[:, None]
    phase = phase_x[:, None, :] + phase_y[None, :, :]
    cosine = jnp.cos(phase)
    sine = jnp.sin(phase)
    real_in = aligned_row[0].astype(jnp.float32)[None, None, :]
    imag_in = aligned_row[1].astype(jnp.float32)[None, None, :]
    front_real = (real_in * cosine + imag_in * sine).astype(jnp.bfloat16).reshape(CX * CY, -1)
    front_imag = (imag_in * cosine - real_in * sine).astype(jnp.bfloat16).reshape(CX * CY, -1)
    left_side = jnp.concatenate([front_real, front_imag], axis=1)
    phase_z = (omega * slow[2])[:, None] * z_coord[None, :]
    depth_real = jnp.cos(phase_z).astype(jnp.bfloat16)
    depth_imag = jnp.sin(phase_z).astype(jnp.bfloat16)
    upper_rows = jnp.concatenate([depth_real, -depth_imag], axis=1)
    lower_rows = jnp.concatenate([depth_imag, depth_real], axis=1)
    right_side = jnp.concatenate([upper_rows, lower_rows], axis=0)
    return jnp.dot(left_side, right_side, preferred_element_type=jnp.float32)


CHUNK = 768


def exp_neg(angle):
    return jnp.cos(angle), -jnp.sin(angle)


def enter_barrier(count, reach):
    me = lax.axis_index("sta")
    tile = lax.axis_index("grid")
    tiles = lax.axis_size("grid")
    mesh_ids = pl.DeviceIdType.MESH
    barrier = pltpu.get_barrier_semaphore()
    for shift in range(1, count):
        pl.semaphore_signal(barrier, inc=1, device_id=(tile, lax.rem(me + shift, count)), device_id_type=mesh_ids)
    neighbours = jnp.int32(0)
    for k in range(-reach, reach + 1):
        if k == 0:
            continue
        there = (tile + k >= 0) & (tile + k < tiles)
        neighbours = neighbours + there.astype(jnp.int32)

        @pl.when(there)
        def _():
            pl.semaphore_signal(barrier, inc=1, device_id=(tile + k, me), device_id_type=mesh_ids)

    pl.semaphore_wait(barrier, count - 1 + neighbours)


def exchange_inputs(spec_ref, lag_ref, slow_ref, spec_in, lag_in, slow_in, local_sem, send_sem, recv_sem, then, reach):
    count = spec_in.shape[0]
    me = lax.axis_index("sta")
    tile = lax.axis_index("grid")
    mesh_ids = pl.DeviceIdType.MESH
    enter_barrier(count, reach)
    pairs = ((spec_ref, spec_in), (lag_ref, lag_in), (slow_ref, slow_in))
    local = []
    for kind, (source, target) in enumerate(pairs):
        own = source.at[me] if kind == 0 else source
        copy = pltpu.make_async_copy(own, target.at[me], local_sem.at[kind])
        copy.start()
        local.append(copy)
    sends = []
    for shift in range(1, count):
        peer = lax.rem(me + shift, count)
        for kind, (source, target) in enumerate(pairs):
            part = source.at[peer] if kind == 0 else source
            copy = pltpu.make_async_remote_copy(
                src_ref=part,
                dst_ref=target.at[me],
                send_sem=send_sem.at[kind, shift],
                recv_sem=recv_sem.at[kind, me],
                device_id=(tile, peer),
                device_id_type=mesh_ids,
            )
            copy.start()
            sends.append(copy)
    then()
    for copy in local:
        copy.wait()
    for copy in sends:
        copy.wait_send()
    for shift in range(1, count):
        source_id = lax.rem(me + count - shift, count)
        for kind, (source, target) in enumerate(pairs):
            part = source.at[source_id] if kind == 0 else source
            pltpu.make_async_remote_copy(
                src_ref=part,
                dst_ref=target.at[source_id],
                send_sem=send_sem.at[kind, shift],
                recv_sem=recv_sem.at[kind, source_id],
                device_id=(tile, source_id),
                device_id_type=mesh_ids,
            ).wait_recv()


def align_block(spec, lag, slow, source, real_ref, imag_ref, turn_ref):
    bins, block = spec.shape[0], spec.shape[2]
    first_bin = lax.axis_index("sta") * bins
    bin_rows = (F0 + first_bin + lax.broadcasted_iota(jnp.int32, (bins, block), 0)).astype(jnp.float32)
    cols = pl.ds(pl.multiple_of(source * block, 128), block)
    product = bin_rows * lag.astype(jnp.float32)
    whole = jnp.floor(product * (1.0 / NT))
    left = product - whole * NT
    left = jnp.where(left < 0.0, left + NT, left)
    left = jnp.where(left >= NT, left - NT, left)
    turned = left * (TWO_PI / NT)
    cosine = jnp.cos(turned)
    sine = jnp.sin(turned)
    real_in = spec[:, 0, :].astype(jnp.float32)
    imag_in = spec[:, 1, :].astype(jnp.float32)
    real_ref[:, cols] = (real_in * cosine + imag_in * sine).astype(jnp.bfloat16).astype(jnp.float32)
    imag_ref[:, cols] = (imag_in * cosine - real_in * sine).astype(jnp.bfloat16).astype(jnp.float32)
    turn_ref[:, cols] = slow.astype(jnp.float32)


def complex_times(left, right):
    return left[0] * right[0] - left[1] * right[1], left[0] * right[1] + left[1] * right[0]


def factor_rows(turn_x, turn_y, turn_z, rows8, rows16):
    return (
        exp_neg(turn_x * (rows8 - 3.5)),
        exp_neg(turn_x * (8.0 * (rows8 - 1.5))),
        exp_neg(turn_y * (rows8 - 3.5)),
        exp_neg(turn_z * (rows16 - 7.5)),
        exp_neg(turn_z * (16.0 * (rows8 - 3.5))),
    )


def beam_kernel(spec_ref, lag_ref, slow_ref, out_ref, spec_in, lag_in, slow_in, local_sem, send_sem, recv_sem,
                real_ref, imag_ref, turn_ref, acc_ref, left_ref, right_ref, power_ref, pieces, send_rs, recv_rs,
                send_ag, recv_ag, share_sem):
    count, bins, block = spec_in.shape[0], spec_in.shape[1], spec_in.shape[3]
    me = lax.axis_index("sta")
    first_bin = me * bins
    width = CHUNK
    per_block = block // width
    half_z = CZ // 2
    rows8 = lax.broadcasted_iota(jnp.int32, (8, width), 0).astype(jnp.float32)
    rows16 = lax.broadcasted_iota(jnp.int32, (16, width), 0).astype(jnp.float32)
    omega0 = (F0 + first_bin).astype(jnp.float32) * (TWO_PI / NT)
    step = TWO_PI / NT
    acc_ref[...] = jnp.zeros_like(acc_ref)

    def per_chunk(k, carry):
        source = lax.rem(me + k // per_block, count)
        cols = pl.ds(pl.multiple_of(source * block + lax.rem(k, per_block) * width, 128), width)
        slow_x = turn_ref[0:1, cols]
        slow_y = turn_ref[1:2, cols]
        slow_z = turn_ref[2:3, cols]
        start = factor_rows(omega0 * slow_x, omega0 * slow_y, omega0 * slow_z, rows8, rows16)
        ratio = factor_rows(step * slow_x, step * slow_y, step * slow_z, rows8, rows16)

        def per_bin(f, state):
            (a_r, a_i), (b_r, b_i), (y_r, y_i), (c_r, c_i), (d_r, d_i) = state
            real_in = real_ref[pl.ds(f, 1), cols]
            imag_in = imag_ref[pl.ds(f, 1), cols]
            q_r = real_in * y_r - imag_in * y_i
            q_i = real_in * y_i + imag_in * y_r
            near = [complex_times((b_r[m : m + 1], b_i[m : m + 1]), (a_r, a_i)) for m in range(CX // 16)]
            cells = CX * CY
            for y in range(CY):
                qq_r, qq_i = q_r[y : y + 1], q_i[y : y + 1]
                lo_r, lo_i, hi_r, hi_i = [], [], [], []
                for x_r, x_i in near:
                    t1, t2 = qq_r * x_r, qq_i * x_i
                    t3, t4 = qq_r * x_i, qq_i * x_r
                    lo_r.append(t1 - t2)
                    lo_i.append(t3 + t4)
                    hi_r.append(t1 + t2)
                    hi_i.append(t4 - t3)
                row = y * CX
                half = CX // 2
                left_ref[row : row + half, :] = jnp.concatenate(lo_r, axis=0).astype(jnp.bfloat16)
                left_ref[row + half : row + CX, :] = jnp.concatenate(hi_r, axis=0).astype(jnp.bfloat16)
                left_ref[cells + row : cells + row + half, :] = jnp.concatenate(lo_i, axis=0).astype(jnp.bfloat16)
                left_ref[cells + row + half : cells + row + CX, :] = jnp.concatenate(hi_i, axis=0).astype(jnp.bfloat16)
            for m in range(half_z // 16):
                z_r, z_i = complex_times((d_r[m : m + 1], d_i[m : m + 1]), (c_r, c_i))
                row = 16 * m
                right_ref[row : row + 16, :] = z_r.astype(jnp.bfloat16)
                right_ref[half_z + row : half_z + row + 16, :] = z_i.astype(jnp.bfloat16)
            acc_ref[f] += lax.dot_general(
                left_ref[...], right_ref[...], (((1,), (1,)), ((), ())), preferred_element_type=jnp.float32
            )
            return tuple(complex_times(now, turn) for now, turn in zip(state, ratio))

        lax.fori_loop(0, bins, per_bin, start, unroll=4)
        return carry

    def own_block():
        align_block(spec_ref.at[me], lag_ref[...], slow_ref[...], me, real_ref, imag_ref, turn_ref)
        lax.fori_loop(0, per_block, per_chunk, 0)

    exchange_inputs(
        spec_ref, lag_ref, slow_ref, spec_in, lag_in, slow_in, local_sem, send_sem, recv_sem, own_block, out_ref.shape[0] // 2
    )

    def align_other(shift, carry):
        source = lax.rem(me + shift, count)
        align_block(spec_in.at[source], lag_in[source], slow_in[source], source, real_ref, imag_ref, turn_ref)
        return carry

    lax.fori_loop(1, count, align_other, 0)
    lax.fori_loop(per_block, count * per_block, per_chunk, 0, unroll=2)
    cells = CX * CY
    low = jnp.zeros((cells, half_z), jnp.float32)
    high = jnp.zeros((cells, half_z), jnp.float32)
    for f in range(bins):
        sums = acc_ref[f]
        u, w = sums[:cells, :half_z], sums[:cells, half_z:]
        x, v = sums[cells:, :half_z], sums[cells:, half_z:]
        low = low + ((u - v) * (u - v) + (w + x) * (w + x))
        high = high + ((u + v) * (u + v) + (x - w) * (x - w))
    power_ref[:, :half_z] = low
    power_ref[:, half_z:] = high
    share_kernel(power_ref, out_ref, pieces, send_rs, recv_rs, send_ag, recv_ag, share_sem)


def beam_power(spec_send, lag_row, slow_rows, reach):
    count = spec_send.shape[0]
    slots = 2 * reach + 1
    cells = CX * CY
    bins, block = spec_send.shape[1], spec_send.shape[3]
    width = CHUNK
    stations = count * block
    vmem = pl.BlockSpec(memory_space=pltpu.VMEM)
    return pl.pallas_call(
        beam_kernel,
        out_shape=jax.ShapeDtypeStruct((slots, cells, CZ), jnp.float32),
        in_specs=[vmem, vmem, vmem],
        out_specs=vmem,
        scratch_shapes=[
            pltpu.VMEM((count,) + spec_send.shape[1:], jnp.bfloat16),
            pltpu.VMEM((count,) + lag_row.shape, jnp.int32),
            pltpu.VMEM((count,) + slow_rows.shape, jnp.bfloat16),
            pltpu.SemaphoreType.DMA((3,)),
            pltpu.SemaphoreType.DMA((3, count)),
            pltpu.SemaphoreType.DMA((3, count)),
            pltpu.VMEM((bins, stations), jnp.float32),
            pltpu.VMEM((bins, stations), jnp.float32),
            pltpu.VMEM((slow_rows.shape[0], stations), jnp.float32),
            pltpu.VMEM((bins, 2 * CX * CY, CZ), jnp.float32),
            pltpu.VMEM((2 * CX * CY, width), jnp.bfloat16),
            pltpu.VMEM((CZ, width), jnp.bfloat16),
            pltpu.VMEM((cells, CZ), jnp.float32),
            pltpu.VMEM((count, cells // count, CZ), jnp.float32),
            pltpu.SemaphoreType.DMA((count,)),
            pltpu.SemaphoreType.DMA((count,)),
            pltpu.SemaphoreType.DMA((slots, count)),
            pltpu.SemaphoreType.DMA((slots, count)),
            pltpu.SemaphoreType.DMA((1,)),
        ],
        compiler_params=pltpu.CompilerParams(collective_id=1, has_side_effects=True),
    )(spec_send, lag_row, slow_rows)


def share_kernel(part_ref, out_ref, pieces, send_rs, recv_rs, send_ag, recv_ag, local_sem):
    count = pieces.shape[0]
    slots = out_ref.shape[0]
    reach = slots // 2
    rows = pieces.shape[1]
    me = lax.axis_index("sta")
    tile = lax.axis_index("grid")
    tiles = lax.axis_size("grid")
    mesh_ids = pl.DeviceIdType.MESH
    own = pltpu.make_async_copy(part_ref.at[pl.ds(pl.multiple_of(me * rows, 8), rows)], pieces.at[me], local_sem.at[0])
    own.start()
    sends = []
    for shift in range(1, count):
        peer = lax.rem(me + shift, count)
        copy = pltpu.make_async_remote_copy(
            src_ref=part_ref.at[pl.ds(pl.multiple_of(peer * rows, 8), rows)],
            dst_ref=pieces.at[me],
            send_sem=send_rs.at[shift],
            recv_sem=recv_rs.at[me],
            device_id=(tile, peer),
            device_id_type=mesh_ids,
        )
        copy.start()
        sends.append(copy)
    own.wait()
    for copy in sends:
        copy.wait_send()
    for shift in range(1, count):
        source = lax.rem(me + count - shift, count)
        pltpu.make_async_remote_copy(
            src_ref=pieces.at[source],
            dst_ref=pieces.at[source],
            send_sem=send_rs.at[shift],
            recv_sem=recv_rs.at[source],
            device_id=(tile, source),
            device_id_type=mesh_ids,
        ).wait_recv()
    total = pieces[0]
    for source in range(1, count):
        total = total + pieces[source]
    mine = pl.ds(pl.multiple_of(me * rows, 8), rows)
    out_ref[reach, mine] = total
    block = out_ref.at[reach, mine]

    def gather_copy(k, peer, slot):
        return pltpu.make_async_remote_copy(
            src_ref=block,
            dst_ref=out_ref.at[slot, mine],
            send_sem=send_ag.at[slot, peer],
            recv_sem=recv_ag.at[slot, me],
            device_id=(tile + k, peer),
            device_id_type=mesh_ids,
        )

    peers = []
    for shift in range(1, count):
        copy = gather_copy(0, lax.rem(me + shift, count), reach)
        copy.start()
        peers.append(copy)
    for k in range(-reach, reach + 1):
        if k == 0:
            continue

        @pl.when(jnp.logical_not((tile + k >= 0) & (tile + k < tiles)))
        def _():
            out_ref[reach + k] = jnp.zeros(out_ref.shape[1:], out_ref.dtype)

    for copy in peers:
        copy.wait_send()
    for shift in range(1, count):
        source = lax.rem(me + count - shift, count)
        pltpu.make_async_remote_copy(
            src_ref=block,
            dst_ref=out_ref.at[reach, pl.ds(pl.multiple_of(source * rows, 8), rows)],
            send_sem=send_ag.at[reach, source],
            recv_sem=recv_ag.at[reach, source],
            device_id=(tile, source),
            device_id_type=mesh_ids,
        ).wait_recv()

    def halo_copy(k):
        return pltpu.make_async_remote_copy(
            src_ref=out_ref.at[reach],
            dst_ref=out_ref.at[reach - k],
            send_sem=send_ag.at[reach - k, me],
            recv_sem=recv_ag.at[reach - k, me],
            device_id=(tile + k, me),
            device_id_type=mesh_ids,
        )

    for k in range(-reach, reach + 1):
        if k == 0:
            continue

        @pl.when((tile + k >= 0) & (tile + k < tiles))
        def _():
            halo_copy(k).start()

    for k in range(-reach, reach + 1):
        if k == 0:
            continue

        @pl.when((tile + k >= 0) & (tile + k < tiles))
        def _():
            halo_copy(k).wait_send()
            pltpu.make_async_remote_copy(
                src_ref=out_ref.at[reach],
                dst_ref=out_ref.at[reach + k],
                send_sem=send_ag.at[reach + k, me],
                recv_sem=recv_ag.at[reach + k, me],
                device_id=(tile + k, me),
                device_id_type=mesh_ids,
            ).wait_recv()


def share_power(part, reach):
    count = lax.axis_size("sta")
    rows = part.shape[0] // count
    slots = 2 * reach + 1
    return pl.pallas_call(
        share_kernel,
        out_shape=jax.ShapeDtypeStruct((slots,) + part.shape, jnp.float32),
        in_specs=[pl.BlockSpec(memory_space=pltpu.VMEM)],
        out_specs=pl.BlockSpec(memory_space=pltpu.VMEM),
        scratch_shapes=[
            pltpu.VMEM((count, rows, part.shape[1]), jnp.float32),
            pltpu.SemaphoreType.DMA((count,)),
            pltpu.SemaphoreType.DMA((count,)),
            pltpu.SemaphoreType.DMA((slots, count)),
            pltpu.SemaphoreType.DMA((slots, count)),
            pltpu.SemaphoreType.DMA((1,)),
        ],
        compiler_params=pltpu.CompilerParams(collective_id=0, has_side_effects=True),
    )(part)


def freq_beams(freq_ids, aligned_rows, slow_rows):
    return lax.map(lambda pair: beam_freq(pair[0], pair[1], slow_rows), (freq_ids, aligned_rows))


def band_matrix(taps, length):
    rows = jnp.arange(length, dtype=jnp.int32)[:, None]
    columns = jnp.arange(length + 2 * HALF, dtype=jnp.int32)[None, :]
    offset = columns - rows
    picks = jnp.arange(TAPS, dtype=jnp.int32)[:, None, None]
    return jnp.sum(jnp.where(offset[None] == picks, taps[:, None, None], 0.0), axis=0)


def blur(volume, bands):
    band_x, square_y, square_z = bands
    padded = with_halo(volume.astype(jnp.bfloat16), (("grid", 0),), HALF).astype(volume.dtype)
    along_x = jnp.einsum("ip,pyz->iyz", band_x, padded, precision=lax.Precision.HIGHEST)
    along_y = jnp.einsum("jq,xqz->xjz", square_y, along_x, precision=lax.Precision.HIGHEST)
    return jnp.einsum("xyw,kw->xyk", along_y, square_z, precision=lax.Precision.HIGHEST)


def blur_narrowing(volume, taps, square_y, square_z):
    band_x = band_matrix(taps, volume.shape[0] - 2 * HALF)
    along_x = jnp.einsum("ip,pyz->iyz", band_x, volume, precision=lax.Precision.HIGHEST)
    along_y = jnp.einsum("jq,xqz->xjz", square_y, along_x, precision=lax.Precision.HIGHEST)
    return jnp.einsum("xyw,kw->xyk", along_y, square_z, precision=lax.Precision.HIGHEST)


def deblur(observed, halo_tiles, spread_taps):
    tiles = lax.axis_size("grid")
    me = lax.axis_index("grid")
    reach = ITERS * 2 * HALF
    cut = halo_tiles * CX - reach
    observed = observed[cut : observed.shape[0] - cut]
    width = observed.shape[0]
    cell = (me - halo_tiles) * CX + cut + jnp.arange(width, dtype=jnp.int32)
    inside = (cell >= 0) & (cell < tiles * CX)
    square_y = band_matrix(spread_taps[1], CY)[:, HALF : HALF + CY]
    square_z = band_matrix(spread_taps[2], CZ)[:, HALF : HALF + CZ]
    estimate = jnp.where(inside[:, None, None], observed, 0.0)
    for sweep in range(ITERS):
        low = 2 * HALF * sweep + HALF
        blurred = blur_narrowing(estimate, spread_taps[0], square_y, square_z)
        ratio = jnp.where(
            inside[low : width - low, None, None], observed[low : width - low] / blurred, 0.0
        )
        estimate = estimate[2 * HALF : estimate.shape[0] - 2 * HALF] * blur_narrowing(
            ratio, spread_taps[0], square_y, square_z
        )
    return estimate


def band_of(taps_ref, axis, rows, cols):
    offset = cols - rows + HALF
    band = jnp.zeros(offset.shape, jnp.float32)
    for tap in range(TAPS):
        band = jnp.where(offset == tap, taps_ref[axis, tap], band)
    return band


def mirror(index, length):
    return jnp.where(index < length // 2, index, 3 * (length // 2) - 1 - index)


def deblur_kernel(taps_ref, obs_ref, out_ref, kx_ref, kz_ref):
    tiles = lax.axis_size("grid")
    me = lax.axis_index("grid")
    planes, width, depth = obs_ref.shape
    shape_x = kx_ref.shape
    kx_ref[...] = band_of(
        taps_ref, 0, lax.broadcasted_iota(jnp.int32, shape_x, 0) + HALF, lax.broadcasted_iota(jnp.int32, shape_x, 1)
    )
    shape_z = kz_ref.shape
    kz_ref[...] = band_of(
        taps_ref,
        2,
        mirror(lax.broadcasted_iota(jnp.int32, shape_z, 1), depth),
        mirror(lax.broadcasted_iota(jnp.int32, shape_z, 0), depth),
    )
    halo_tiles = (width - CX) // (2 * CX)
    highest = lax.Precision.HIGH

    def inside(low, size):
        cell = (me - halo_tiles) * CX + low + lax.broadcasted_iota(jnp.int32, (size, depth), 0)
        return (cell >= 0) & (cell < tiles * CX)

    lanes = planes * depth

    def blur(volume):
        size_in = volume.shape[0]
        size_out = size_in - 2 * HALF
        band = kx_ref[0:size_out, 0:size_in]
        along_x = jnp.dot(band, volume, precision=highest, preferred_element_type=jnp.float32)
        along_y = []
        for y in range(planes):
            total = None
            for q in range(planes):
                term = taps_ref[1, q - y + HALF] * along_x[:, q * depth : (q + 1) * depth]
                total = term if total is None else total + term
            along_y.append(total)
        joined = jnp.concatenate(along_y, axis=0)
        along_z = jnp.dot(joined, kz_ref[...], precision=highest, preferred_element_type=jnp.float32)
        return jnp.concatenate([along_z[y * size_out : (y + 1) * size_out] for y in range(planes)], axis=1)

    def inside_wide(low, size):
        cell = (me - halo_tiles) * CX + low + lax.broadcasted_iota(jnp.int32, (size, lanes), 0)
        return (cell >= 0) & (cell < tiles * CX)

    observed = jnp.concatenate([obs_ref[y] for y in range(planes)], axis=1)
    estimate = jnp.where(inside_wide(0, width), observed, 0.0)
    for sweep in range(ITERS):
        low = 2 * HALF * sweep + HALF
        blurred = blur(estimate)
        size = blurred.shape[0]
        ratio = jnp.where(inside_wide(low, size), observed[low : low + size] / blurred, 0.0)
        spread = blur(ratio)
        estimate = estimate[2 * HALF : 2 * HALF + spread.shape[0]] * spread
    for y in range(planes):
        out_ref[y] = estimate[:, y * depth : (y + 1) * depth]


def deblur_tile(observed, spread_taps):
    planes, width, depth = observed.shape
    vmem = pl.BlockSpec(memory_space=pltpu.VMEM)
    return pl.pallas_call(
        deblur_kernel,
        out_shape=jax.ShapeDtypeStruct((planes, CX, depth), jnp.float32),
        in_specs=[pl.BlockSpec(memory_space=pltpu.SMEM), vmem],
        out_specs=vmem,
        scratch_shapes=[
            pltpu.VMEM((width - 2 * HALF, width), jnp.float32),
            pltpu.VMEM((depth, depth), jnp.float32),
        ],
    )(spread_taps, observed)


def per_device(spectra, lag_samples, slowness, spread_taps):
    groups = lax.axis_size("sta")
    own_count = FREQS // groups
    first_bin = lax.axis_index("sta") * own_count
    block = spectra.shape[2]
    spec_send = spectra.reshape(groups, own_count, 2, block)
    halo_tiles = -(-(ITERS * 2 * HALF) // CX)
    summed = beam_power(spec_send, lag_samples, slowness[0], halo_tiles)
    observed = summed / (FREQS * STATIONS) + BACKGROUND
    slots = observed.shape[0]
    observed = observed.reshape(slots, CY, CX, CZ)
    observed = jnp.concatenate([observed[:, :, : CX // 2], observed[:, :, CX // 2 :][:, :, ::-1]], axis=2)
    planes = observed.transpose(1, 0, 2, 3).reshape(CY, slots * CX, CZ)
    estimate = deblur_tile(planes, spread_taps)
    both = jnp.stack([observed[halo_tiles], estimate])
    both = jnp.concatenate([both[..., : CZ // 2], both[..., CZ // 2 :][..., ::-1]], axis=-1).transpose(0, 2, 1, 3)
    stacked, estimate = both[0], both[1]
    return (stacked[None], estimate[None])


def solution(mesh):
    placed = (P(None, None, "sta"), P("grid", "sta"), P("grid", None, "sta"), P())
    return jax.shard_map(
        per_device,
        mesh=mesh,
        in_specs=placed,
        out_specs=(P("grid", None, None, None), P("grid", None, None, None)),
        check_vma=False,
    )
```

```python
import math

import jax
import jax.numpy as jnp
from jax import lax
from jax.sharding import PartitionSpec as P
from jax.experimental import pallas as pl
from jax.experimental.pallas import tpu as pltpu

STATIONS = 6144
FREQS = 64
F0 = 600
NT = 6000
TAPS = 17
HALF = 8
ITERS = 4
CX = 32
CY = 8
CZ = 128


TWO_PI = 2.0 * math.pi
BACKGROUND = 0.05


def with_halo(array, sides, width):
    for axis, dim in sides:
        size, length = (lax.axis_size(axis), array.shape[dim])
        up = [(i, (i + 1) % size) for i in range(size - 1)]
        down = [(j, i) for i, j in up]
        last = lax.slice_in_dim(array, length - width, length, axis=dim)
        leading = lax.slice_in_dim(array, 0, width, axis=dim)
        before = lax.ppermute(last, axis, up)
        after = lax.ppermute(leading, axis, down)
        array = jnp.concatenate([before, array, after], axis=dim)
    return array


def align_rows(spectra, lag_row):
    bins = F0 + jnp.arange(FREQS, dtype=jnp.int32)
    cycles = bins[:, None] * lag_row[None, :] % NT
    turned = cycles.astype(jnp.float32) * (TWO_PI / NT)
    cosine = jnp.cos(turned)
    sine = jnp.sin(turned)
    real_in = spectra[:, 0, :].astype(jnp.float32)
    imag_in = spectra[:, 1, :].astype(jnp.float32)
    real_out = real_in * cosine + imag_in * sine
    imag_out = imag_in * cosine - real_in * sine
    return jnp.stack([real_out, imag_out], axis=1).astype(jnp.bfloat16)


def beam_freq(freq, aligned_row, slow_rows):
    omega = (F0 + freq).astype(jnp.float32) * (TWO_PI / NT)
    slow = slow_rows.astype(jnp.float32)
    x_coord = jnp.arange(CX, dtype=jnp.float32) - (CX - 1) / 2.0
    y_coord = jnp.arange(CY, dtype=jnp.float32) - (CY - 1) / 2.0
    z_coord = jnp.arange(CZ, dtype=jnp.float32) - (CZ - 1) / 2.0
    phase_x = (omega * slow[0])[None, :] * x_coord[:, None]
    phase_y = (omega * slow[1])[None, :] * y_coord[:, None]
    phase = phase_x[:, None, :] + phase_y[None, :, :]
    cosine = jnp.cos(phase)
    sine = jnp.sin(phase)
    real_in = aligned_row[0].astype(jnp.float32)[None, None, :]
    imag_in = aligned_row[1].astype(jnp.float32)[None, None, :]
    front_real = (real_in * cosine + imag_in * sine).astype(jnp.bfloat16).reshape(CX * CY, -1)
    front_imag = (imag_in * cosine - real_in * sine).astype(jnp.bfloat16).reshape(CX * CY, -1)
    left_side = jnp.concatenate([front_real, front_imag], axis=1)
    phase_z = (omega * slow[2])[:, None] * z_coord[None, :]
    depth_real = jnp.cos(phase_z).astype(jnp.bfloat16)
    depth_imag = jnp.sin(phase_z).astype(jnp.bfloat16)
    upper_rows = jnp.concatenate([depth_real, -depth_imag], axis=1)
    lower_rows = jnp.concatenate([depth_imag, depth_real], axis=1)
    right_side = jnp.concatenate([upper_rows, lower_rows], axis=0)
    return jnp.dot(left_side, right_side, preferred_element_type=jnp.float32)


CHUNK = 768


def exp_neg(angle):
    return jnp.cos(angle), -jnp.sin(angle)


def enter_barrier(count, reach):
    me = lax.axis_index("sta")
    tile = lax.axis_index("grid")
    tiles = lax.axis_size("grid")
    mesh_ids = pl.DeviceIdType.MESH
    barrier = pltpu.get_barrier_semaphore()
    for shift in range(1, count):
        pl.semaphore_signal(barrier, inc=1, device_id=(tile, lax.rem(me + shift, count)), device_id_type=mesh_ids)
    neighbours = jnp.int32(0)
    for k in range(-reach, reach + 1):
        if k == 0:
            continue
        there = (tile + k >= 0) & (tile + k < tiles)
        neighbours = neighbours + there.astype(jnp.int32)

        @pl.when(there)
        def _():
            pl.semaphore_signal(barrier, inc=1, device_id=(tile + k, me), device_id_type=mesh_ids)

    pl.semaphore_wait(barrier, count - 1 + neighbours)


def exchange_inputs(spec_ref, lag_ref, slow_ref, spec_in, lag_in, slow_in, local_sem, send_sem, recv_sem, then, reach):
    count = spec_in.shape[0]
    me = lax.axis_index("sta")
    tile = lax.axis_index("grid")
    mesh_ids = pl.DeviceIdType.MESH
    enter_barrier(count, reach)
    pairs = ((spec_ref, spec_in), (lag_ref, lag_in), (slow_ref, slow_in))
    local = []
    for kind, (source, target) in enumerate(pairs):
        own = source.at[me] if kind == 0 else source
        copy = pltpu.make_async_copy(own, target.at[me], local_sem.at[kind])
        copy.start()
        local.append(copy)
    sends = []
    for shift in range(1, count):
        peer = lax.rem(me + shift, count)
        for kind, (source, target) in enumerate(pairs):
            part = source.at[peer] if kind == 0 else source
            copy = pltpu.make_async_remote_copy(
                src_ref=part,
                dst_ref=target.at[me],
                send_sem=send_sem.at[kind, shift],
                recv_sem=recv_sem.at[kind, me],
                device_id=(tile, peer),
                device_id_type=mesh_ids,
            )
            copy.start()
            sends.append(copy)
    then()
    for copy in local:
        copy.wait()
    for copy in sends:
        copy.wait_send()
    for shift in range(1, count):
        source_id = lax.rem(me + count - shift, count)
        for kind, (source, target) in enumerate(pairs):
            part = source.at[source_id] if kind == 0 else source
            pltpu.make_async_remote_copy(
                src_ref=part,
                dst_ref=target.at[source_id],
                send_sem=send_sem.at[kind, shift],
                recv_sem=recv_sem.at[kind, source_id],
                device_id=(tile, source_id),
                device_id_type=mesh_ids,
            ).wait_recv()


def align_block(spec, lag, slow, source, real_ref, imag_ref, turn_ref):
    bins, block = spec.shape[0], spec.shape[2]
    first_bin = lax.axis_index("sta") * bins
    bin_rows = (F0 + first_bin + lax.broadcasted_iota(jnp.int32, (bins, block), 0)).astype(jnp.float32)
    cols = pl.ds(pl.multiple_of(source * block, 128), block)
    product = bin_rows * lag.astype(jnp.float32)
    whole = jnp.floor(product * (1.0 / NT))
    left = product - whole * NT
    left = jnp.where(left < 0.0, left + NT, left)
    left = jnp.where(left >= NT, left - NT, left)
    turned = left * (TWO_PI / NT)
    cosine = jnp.cos(turned)
    sine = jnp.sin(turned)
    real_in = spec[:, 0, :].astype(jnp.float32)
    imag_in = spec[:, 1, :].astype(jnp.float32)
    real_ref[:, cols] = (real_in * cosine + imag_in * sine).astype(jnp.bfloat16).astype(jnp.float32)
    imag_ref[:, cols] = (imag_in * cosine - real_in * sine).astype(jnp.bfloat16).astype(jnp.float32)
    turn_ref[:, cols] = slow.astype(jnp.float32)


def complex_times(left, right):
    return left[0] * right[0] - left[1] * right[1], left[0] * right[1] + left[1] * right[0]


def factor_rows(turn_x, turn_y, turn_z, rows8, rows16):
    return (
        exp_neg(turn_x * (rows8 - 3.5)),
        exp_neg(turn_x * (8.0 * (rows8 - 1.5))),
        exp_neg(turn_y * (rows8 - 3.5)),
        exp_neg(turn_z * (rows16 - 7.5)),
        exp_neg(turn_z * (16.0 * (rows8 - 3.5))),
    )


def beam_kernel(spec_ref, lag_ref, slow_ref, out_ref, spec_in, lag_in, slow_in, local_sem, send_sem, recv_sem,
                real_ref, imag_ref, turn_ref, acc_ref, left_ref, right_ref, power_ref, pieces, send_rs, recv_rs,
                send_ag, recv_ag, share_sem):
    count, bins, block = spec_in.shape[0], spec_in.shape[1], spec_in.shape[3]
    me = lax.axis_index("sta")
    first_bin = me * bins
    width = CHUNK
    per_block = block // width
    half_z = CZ // 2
    rows8 = lax.broadcasted_iota(jnp.int32, (8, width), 0).astype(jnp.float32)
    rows16 = lax.broadcasted_iota(jnp.int32, (16, width), 0).astype(jnp.float32)
    omega0 = (F0 + first_bin).astype(jnp.float32) * (TWO_PI / NT)
    step = TWO_PI / NT
    acc_ref[...] = jnp.zeros_like(acc_ref)

    def per_chunk(k, carry):
        source = lax.rem(me + k // per_block, count)
        cols = pl.ds(pl.multiple_of(source * block + lax.rem(k, per_block) * width, 128), width)
        slow_x = turn_ref[0:1, cols]
        slow_y = turn_ref[1:2, cols]
        slow_z = turn_ref[2:3, cols]
        start = factor_rows(omega0 * slow_x, omega0 * slow_y, omega0 * slow_z, rows8, rows16)
        ratio = factor_rows(step * slow_x, step * slow_y, step * slow_z, rows8, rows16)

        def per_bin(f, state):
            (a_r, a_i), (b_r, b_i), (y_r, y_i), (c_r, c_i), (d_r, d_i) = state
            real_in = real_ref[pl.ds(f, 1), cols]
            imag_in = imag_ref[pl.ds(f, 1), cols]
            q_r = real_in * y_r - imag_in * y_i
            q_i = real_in * y_i + imag_in * y_r
            near = [complex_times((b_r[m : m + 1], b_i[m : m + 1]), (a_r, a_i)) for m in range(CX // 16)]
            cells = CX * CY
            for y in range(CY):
                qq_r, qq_i = q_r[y : y + 1], q_i[y : y + 1]
                lo_r, lo_i, hi_r, hi_i = [], [], [], []
                for x_r, x_i in near:
                    t1, t2 = qq_r * x_r, qq_i * x_i
                    t3, t4 = qq_r * x_i, qq_i * x_r
                    lo_r.append(t1 - t2)
                    lo_i.append(t3 + t4)
                    hi_r.append(t1 + t2)
                    hi_i.append(t4 - t3)
                row = y * CX
                half = CX // 2
                left_ref[row : row + half, :] = jnp.concatenate(lo_r, axis=0).astype(jnp.bfloat16)
                left_ref[row + half : row + CX, :] = jnp.concatenate(hi_r, axis=0).astype(jnp.bfloat16)
                left_ref[cells + row : cells + row + half, :] = jnp.concatenate(lo_i, axis=0).astype(jnp.bfloat16)
                left_ref[cells + row + half : cells + row + CX, :] = jnp.concatenate(hi_i, axis=0).astype(jnp.bfloat16)
            for m in range(half_z // 16):
                z_r, z_i = complex_times((d_r[m : m + 1], d_i[m : m + 1]), (c_r, c_i))
                row = 16 * m
                right_ref[row : row + 16, :] = z_r.astype(jnp.bfloat16)
                right_ref[half_z + row : half_z + row + 16, :] = z_i.astype(jnp.bfloat16)
            acc_ref[f] += lax.dot_general(
                left_ref[...], right_ref[...], (((1,), (1,)), ((), ())), preferred_element_type=jnp.float32
            )
            return tuple(complex_times(now, turn) for now, turn in zip(state, ratio))

        lax.fori_loop(0, bins, per_bin, start, unroll=8)
        return carry

    def own_block():
        align_block(spec_ref.at[me], lag_ref[...], slow_ref[...], me, real_ref, imag_ref, turn_ref)
        lax.fori_loop(0, per_block, per_chunk, 0)

    exchange_inputs(
        spec_ref, lag_ref, slow_ref, spec_in, lag_in, slow_in, local_sem, send_sem, recv_sem, own_block, out_ref.shape[0] // 2
    )

    def align_other(shift, carry):
        source = lax.rem(me + shift, count)
        align_block(spec_in.at[source], lag_in[source], slow_in[source], source, real_ref, imag_ref, turn_ref)
        return carry

    lax.fori_loop(1, count, align_other, 0)
    lax.fori_loop(per_block, count * per_block, per_chunk, 0)
    cells = CX * CY
    low = jnp.zeros((cells, half_z), jnp.float32)
    high = jnp.zeros((cells, half_z), jnp.float32)
    for f in range(bins):
        sums = acc_ref[f]
        u, w = sums[:cells, :half_z], sums[:cells, half_z:]
        x, v = sums[cells:, :half_z], sums[cells:, half_z:]
        low = low + ((u - v) * (u - v) + (w + x) * (w + x))
        high = high + ((u + v) * (u + v) + (x - w) * (x - w))
    power_ref[:, :half_z] = low
    power_ref[:, half_z:] = high
    share_kernel(power_ref, out_ref, pieces, send_rs, recv_rs, send_ag, recv_ag, share_sem)


def beam_power(spec_send, lag_row, slow_rows, reach):
    count = spec_send.shape[0]
    slots = 2 * reach + 1
    cells = CX * CY
    bins, block = spec_send.shape[1], spec_send.shape[3]
    width = CHUNK
    stations = count * block
    vmem = pl.BlockSpec(memory_space=pltpu.VMEM)
    return pl.pallas_call(
        beam_kernel,
        out_shape=jax.ShapeDtypeStruct((slots, cells, CZ), jnp.float32),
        in_specs=[vmem, vmem, vmem],
        out_specs=vmem,
        scratch_shapes=[
            pltpu.VMEM((count,) + spec_send.shape[1:], jnp.bfloat16),
            pltpu.VMEM((count,) + lag_row.shape, jnp.int32),
            pltpu.VMEM((count,) + slow_rows.shape, jnp.bfloat16),
            pltpu.SemaphoreType.DMA((3,)),
            pltpu.SemaphoreType.DMA((3, count)),
            pltpu.SemaphoreType.DMA((3, count)),
            pltpu.VMEM((bins, stations), jnp.float32),
            pltpu.VMEM((bins, stations), jnp.float32),
            pltpu.VMEM((slow_rows.shape[0], stations), jnp.float32),
            pltpu.VMEM((bins, 2 * CX * CY, CZ), jnp.float32),
            pltpu.VMEM((2 * CX * CY, width), jnp.bfloat16),
            pltpu.VMEM((CZ, width), jnp.bfloat16),
            pltpu.VMEM((cells, CZ), jnp.float32),
            pltpu.VMEM((count, cells // count, CZ), jnp.float32),
            pltpu.SemaphoreType.DMA((count,)),
            pltpu.SemaphoreType.DMA((count,)),
            pltpu.SemaphoreType.DMA((slots, count)),
            pltpu.SemaphoreType.DMA((slots, count)),
            pltpu.SemaphoreType.DMA((1,)),
        ],
        compiler_params=pltpu.CompilerParams(collective_id=1, has_side_effects=True),
    )(spec_send, lag_row, slow_rows)


def share_kernel(part_ref, out_ref, pieces, send_rs, recv_rs, send_ag, recv_ag, local_sem):
    count = pieces.shape[0]
    slots = out_ref.shape[0]
    reach = slots // 2
    rows = pieces.shape[1]
    me = lax.axis_index("sta")
    tile = lax.axis_index("grid")
    tiles = lax.axis_size("grid")
    mesh_ids = pl.DeviceIdType.MESH
    own = pltpu.make_async_copy(part_ref.at[pl.ds(pl.multiple_of(me * rows, 8), rows)], pieces.at[me], local_sem.at[0])
    own.start()
    sends = []
    for shift in range(1, count):
        peer = lax.rem(me + shift, count)
        copy = pltpu.make_async_remote_copy(
            src_ref=part_ref.at[pl.ds(pl.multiple_of(peer * rows, 8), rows)],
            dst_ref=pieces.at[me],
            send_sem=send_rs.at[shift],
            recv_sem=recv_rs.at[me],
            device_id=(tile, peer),
            device_id_type=mesh_ids,
        )
        copy.start()
        sends.append(copy)
    own.wait()
    for copy in sends:
        copy.wait_send()
    for shift in range(1, count):
        source = lax.rem(me + count - shift, count)
        pltpu.make_async_remote_copy(
            src_ref=pieces.at[source],
            dst_ref=pieces.at[source],
            send_sem=send_rs.at[shift],
            recv_sem=recv_rs.at[source],
            device_id=(tile, source),
            device_id_type=mesh_ids,
        ).wait_recv()
    total = pieces[0]
    for source in range(1, count):
        total = total + pieces[source]
    mine = pl.ds(pl.multiple_of(me * rows, 8), rows)
    out_ref[reach, mine] = total
    block = out_ref.at[reach, mine]

    def gather_copy(k, peer, slot):
        return pltpu.make_async_remote_copy(
            src_ref=block,
            dst_ref=out_ref.at[slot, mine],
            send_sem=send_ag.at[slot, peer],
            recv_sem=recv_ag.at[slot, me],
            device_id=(tile + k, peer),
            device_id_type=mesh_ids,
        )

    peers = []
    for shift in range(1, count):
        copy = gather_copy(0, lax.rem(me + shift, count), reach)
        copy.start()
        peers.append(copy)
    for k in range(-reach, reach + 1):
        if k == 0:
            continue

        @pl.when(jnp.logical_not((tile + k >= 0) & (tile + k < tiles)))
        def _():
            out_ref[reach + k] = jnp.zeros(out_ref.shape[1:], out_ref.dtype)

    for copy in peers:
        copy.wait_send()
    for shift in range(1, count):
        source = lax.rem(me + count - shift, count)
        pltpu.make_async_remote_copy(
            src_ref=block,
            dst_ref=out_ref.at[reach, pl.ds(pl.multiple_of(source * rows, 8), rows)],
            send_sem=send_ag.at[reach, source],
            recv_sem=recv_ag.at[reach, source],
            device_id=(tile, source),
            device_id_type=mesh_ids,
        ).wait_recv()

    def halo_copy(k):
        return pltpu.make_async_remote_copy(
            src_ref=out_ref.at[reach],
            dst_ref=out_ref.at[reach - k],
            send_sem=send_ag.at[reach - k, me],
            recv_sem=recv_ag.at[reach - k, me],
            device_id=(tile + k, me),
            device_id_type=mesh_ids,
        )

    for k in range(-reach, reach + 1):
        if k == 0:
            continue

        @pl.when((tile + k >= 0) & (tile + k < tiles))
        def _():
            halo_copy(k).start()

    for k in range(-reach, reach + 1):
        if k == 0:
            continue

        @pl.when((tile + k >= 0) & (tile + k < tiles))
        def _():
            halo_copy(k).wait_send()
            pltpu.make_async_remote_copy(
                src_ref=out_ref.at[reach],
                dst_ref=out_ref.at[reach + k],
                send_sem=send_ag.at[reach + k, me],
                recv_sem=recv_ag.at[reach + k, me],
                device_id=(tile + k, me),
                device_id_type=mesh_ids,
            ).wait_recv()


def share_power(part, reach):
    count = lax.axis_size("sta")
    rows = part.shape[0] // count
    slots = 2 * reach + 1
    return pl.pallas_call(
        share_kernel,
        out_shape=jax.ShapeDtypeStruct((slots,) + part.shape, jnp.float32),
        in_specs=[pl.BlockSpec(memory_space=pltpu.VMEM)],
        out_specs=pl.BlockSpec(memory_space=pltpu.VMEM),
        scratch_shapes=[
            pltpu.VMEM((count, rows, part.shape[1]), jnp.float32),
            pltpu.SemaphoreType.DMA((count,)),
            pltpu.SemaphoreType.DMA((count,)),
            pltpu.SemaphoreType.DMA((slots, count)),
            pltpu.SemaphoreType.DMA((slots, count)),
            pltpu.SemaphoreType.DMA((1,)),
        ],
        compiler_params=pltpu.CompilerParams(collective_id=0, has_side_effects=True),
    )(part)


def freq_beams(freq_ids, aligned_rows, slow_rows):
    return lax.map(lambda pair: beam_freq(pair[0], pair[1], slow_rows), (freq_ids, aligned_rows))


def band_matrix(taps, length):
    rows = jnp.arange(length, dtype=jnp.int32)[:, None]
    columns = jnp.arange(length + 2 * HALF, dtype=jnp.int32)[None, :]
    offset = columns - rows
    picks = jnp.arange(TAPS, dtype=jnp.int32)[:, None, None]
    return jnp.sum(jnp.where(offset[None] == picks, taps[:, None, None], 0.0), axis=0)


def blur(volume, bands):
    band_x, square_y, square_z = bands
    padded = with_halo(volume.astype(jnp.bfloat16), (("grid", 0),), HALF).astype(volume.dtype)
    along_x = jnp.einsum("ip,pyz->iyz", band_x, padded, precision=lax.Precision.HIGHEST)
    along_y = jnp.einsum("jq,xqz->xjz", square_y, along_x, precision=lax.Precision.HIGHEST)
    return jnp.einsum("xyw,kw->xyk", along_y, square_z, precision=lax.Precision.HIGHEST)


def blur_narrowing(volume, taps, square_y, square_z):
    band_x = band_matrix(taps, volume.shape[0] - 2 * HALF)
    along_x = jnp.einsum("ip,pyz->iyz", band_x, volume, precision=lax.Precision.HIGHEST)
    along_y = jnp.einsum("jq,xqz->xjz", square_y, along_x, precision=lax.Precision.HIGHEST)
    return jnp.einsum("xyw,kw->xyk", along_y, square_z, precision=lax.Precision.HIGHEST)


def deblur(observed, halo_tiles, spread_taps):
    tiles = lax.axis_size("grid")
    me = lax.axis_index("grid")
    reach = ITERS * 2 * HALF
    cut = halo_tiles * CX - reach
    observed = observed[cut : observed.shape[0] - cut]
    width = observed.shape[0]
    cell = (me - halo_tiles) * CX + cut + jnp.arange(width, dtype=jnp.int32)
    inside = (cell >= 0) & (cell < tiles * CX)
    square_y = band_matrix(spread_taps[1], CY)[:, HALF : HALF + CY]
    square_z = band_matrix(spread_taps[2], CZ)[:, HALF : HALF + CZ]
    estimate = jnp.where(inside[:, None, None], observed, 0.0)
    for sweep in range(ITERS):
        low = 2 * HALF * sweep + HALF
        blurred = blur_narrowing(estimate, spread_taps[0], square_y, square_z)
        ratio = jnp.where(
            inside[low : width - low, None, None], observed[low : width - low] / blurred, 0.0
        )
        estimate = estimate[2 * HALF : estimate.shape[0] - 2 * HALF] * blur_narrowing(
            ratio, spread_taps[0], square_y, square_z
        )
    return estimate


def band_of(taps_ref, axis, rows, cols):
    offset = cols - rows + HALF
    band = jnp.zeros(offset.shape, jnp.float32)
    for tap in range(TAPS):
        band = jnp.where(offset == tap, taps_ref[axis, tap], band)
    return band


def mirror(index, length):
    return jnp.where(index < length // 2, index, 3 * (length // 2) - 1 - index)


def deblur_kernel(taps_ref, obs_ref, out_ref, kx_ref, kz_ref):
    tiles = lax.axis_size("grid")
    me = lax.axis_index("grid")
    planes, width, depth = obs_ref.shape
    shape_x = kx_ref.shape
    kx_ref[...] = band_of(
        taps_ref, 0, lax.broadcasted_iota(jnp.int32, shape_x, 0) + HALF, lax.broadcasted_iota(jnp.int32, shape_x, 1)
    )
    shape_z = kz_ref.shape
    kz_ref[...] = band_of(
        taps_ref,
        2,
        mirror(lax.broadcasted_iota(jnp.int32, shape_z, 1), depth),
        mirror(lax.broadcasted_iota(jnp.int32, shape_z, 0), depth),
    )
    halo_tiles = (width - CX) // (2 * CX)
    highest = lax.Precision.HIGH

    def inside(low, size):
        cell = (me - halo_tiles) * CX + low + lax.broadcasted_iota(jnp.int32, (size, depth), 0)
        return (cell >= 0) & (cell < tiles * CX)

    lanes = planes * depth

    def blur(volume):
        size_in = volume.shape[0]
        size_out = size_in - 2 * HALF
        band = kx_ref[0:size_out, 0:size_in]
        along_x = jnp.dot(band, volume, precision=highest, preferred_element_type=jnp.float32)
        along_y = []
        for y in range(planes):
            total = None
            for q in range(planes):
                term = taps_ref[1, q - y + HALF] * along_x[:, q * depth : (q + 1) * depth]
                total = term if total is None else total + term
            along_y.append(total)
        joined = jnp.concatenate(along_y, axis=0)
        along_z = jnp.dot(joined, kz_ref[...], precision=highest, preferred_element_type=jnp.float32)
        return jnp.concatenate([along_z[y * size_out : (y + 1) * size_out] for y in range(planes)], axis=1)

    def inside_wide(low, size):
        cell = (me - halo_tiles) * CX + low + lax.broadcasted_iota(jnp.int32, (size, lanes), 0)
        return (cell >= 0) & (cell < tiles * CX)

    observed = jnp.concatenate([obs_ref[y] for y in range(planes)], axis=1)
    estimate = jnp.where(inside_wide(0, width), observed, 0.0)
    for sweep in range(ITERS):
        low = 2 * HALF * sweep + HALF
        blurred = blur(estimate)
        size = blurred.shape[0]
        ratio = jnp.where(inside_wide(low, size), observed[low : low + size] / blurred, 0.0)
        spread = blur(ratio)
        estimate = estimate[2 * HALF : 2 * HALF + spread.shape[0]] * spread
    for y in range(planes):
        out_ref[y] = estimate[:, y * depth : (y + 1) * depth]


def deblur_tile(observed, spread_taps):
    planes, width, depth = observed.shape
    vmem = pl.BlockSpec(memory_space=pltpu.VMEM)
    return pl.pallas_call(
        deblur_kernel,
        out_shape=jax.ShapeDtypeStruct((planes, CX, depth), jnp.float32),
        in_specs=[pl.BlockSpec(memory_space=pltpu.SMEM), vmem],
        out_specs=vmem,
        scratch_shapes=[
            pltpu.VMEM((width - 2 * HALF, width), jnp.float32),
            pltpu.VMEM((depth, depth), jnp.float32),
        ],
    )(spread_taps, observed)


def per_device(spectra, lag_samples, slowness, spread_taps):
    groups = lax.axis_size("sta")
    own_count = FREQS // groups
    first_bin = lax.axis_index("sta") * own_count
    block = spectra.shape[2]
    spec_send = spectra.reshape(groups, own_count, 2, block)
    halo_tiles = -(-(ITERS * 2 * HALF) // CX)
    summed = beam_power(spec_send, lag_samples, slowness[0], halo_tiles)
    observed = summed / (FREQS * STATIONS) + BACKGROUND
    slots = observed.shape[0]
    observed = observed.reshape(slots, CY, CX, CZ)
    observed = jnp.concatenate([observed[:, :, : CX // 2], observed[:, :, CX // 2 :][:, :, ::-1]], axis=2)
    planes = observed.transpose(1, 0, 2, 3).reshape(CY, slots * CX, CZ)
    estimate = deblur_tile(planes, spread_taps)
    both = jnp.stack([observed[halo_tiles], estimate])
    both = jnp.concatenate([both[..., : CZ // 2], both[..., CZ // 2 :][..., ::-1]], axis=-1).transpose(0, 2, 1, 3)
    stacked, estimate = both[0], both[1]
    return (stacked[None], estimate[None])


def solution(mesh):
    placed = (P(None, None, "sta"), P("grid", "sta"), P("grid", None, "sta"), P())
    return jax.shard_map(
        per_device,
        mesh=mesh,
        in_specs=placed,
        out_specs=(P("grid", None, None, None), P("grid", None, None, None)),
        check_vma=False,
    )
```

```python
import math

import jax
import jax.numpy as jnp
from jax import lax
from jax.sharding import PartitionSpec as P
from jax.experimental import pallas as pl
from jax.experimental.pallas import tpu as pltpu

STATIONS = 6144
FREQS = 64
F0 = 600
NT = 6000
TAPS = 17
HALF = 8
ITERS = 4
CX = 32
CY = 8
CZ = 128


TWO_PI = 2.0 * math.pi
BACKGROUND = 0.05


def with_halo(array, sides, width):
    for axis, dim in sides:
        size, length = (lax.axis_size(axis), array.shape[dim])
        up = [(i, (i + 1) % size) for i in range(size - 1)]
        down = [(j, i) for i, j in up]
        last = lax.slice_in_dim(array, length - width, length, axis=dim)
        leading = lax.slice_in_dim(array, 0, width, axis=dim)
        before = lax.ppermute(last, axis, up)
        after = lax.ppermute(leading, axis, down)
        array = jnp.concatenate([before, array, after], axis=dim)
    return array


def align_rows(spectra, lag_row):
    bins = F0 + jnp.arange(FREQS, dtype=jnp.int32)
    cycles = bins[:, None] * lag_row[None, :] % NT
    turned = cycles.astype(jnp.float32) * (TWO_PI / NT)
    cosine = jnp.cos(turned)
    sine = jnp.sin(turned)
    real_in = spectra[:, 0, :].astype(jnp.float32)
    imag_in = spectra[:, 1, :].astype(jnp.float32)
    real_out = real_in * cosine + imag_in * sine
    imag_out = imag_in * cosine - real_in * sine
    return jnp.stack([real_out, imag_out], axis=1).astype(jnp.bfloat16)


def beam_freq(freq, aligned_row, slow_rows):
    omega = (F0 + freq).astype(jnp.float32) * (TWO_PI / NT)
    slow = slow_rows.astype(jnp.float32)
    x_coord = jnp.arange(CX, dtype=jnp.float32) - (CX - 1) / 2.0
    y_coord = jnp.arange(CY, dtype=jnp.float32) - (CY - 1) / 2.0
    z_coord = jnp.arange(CZ, dtype=jnp.float32) - (CZ - 1) / 2.0
    phase_x = (omega * slow[0])[None, :] * x_coord[:, None]
    phase_y = (omega * slow[1])[None, :] * y_coord[:, None]
    phase = phase_x[:, None, :] + phase_y[None, :, :]
    cosine = jnp.cos(phase)
    sine = jnp.sin(phase)
    real_in = aligned_row[0].astype(jnp.float32)[None, None, :]
    imag_in = aligned_row[1].astype(jnp.float32)[None, None, :]
    front_real = (real_in * cosine + imag_in * sine).astype(jnp.bfloat16).reshape(CX * CY, -1)
    front_imag = (imag_in * cosine - real_in * sine).astype(jnp.bfloat16).reshape(CX * CY, -1)
    left_side = jnp.concatenate([front_real, front_imag], axis=1)
    phase_z = (omega * slow[2])[:, None] * z_coord[None, :]
    depth_real = jnp.cos(phase_z).astype(jnp.bfloat16)
    depth_imag = jnp.sin(phase_z).astype(jnp.bfloat16)
    upper_rows = jnp.concatenate([depth_real, -depth_imag], axis=1)
    lower_rows = jnp.concatenate([depth_imag, depth_real], axis=1)
    right_side = jnp.concatenate([upper_rows, lower_rows], axis=0)
    return jnp.dot(left_side, right_side, preferred_element_type=jnp.float32)


CHUNK = 768


def exp_neg(angle):
    return jnp.cos(angle), -jnp.sin(angle)


def enter_barrier(count, reach):
    me = lax.axis_index("sta")
    tile = lax.axis_index("grid")
    tiles = lax.axis_size("grid")
    mesh_ids = pl.DeviceIdType.MESH
    barrier = pltpu.get_barrier_semaphore()
    for shift in range(1, count):
        pl.semaphore_signal(barrier, inc=1, device_id=(tile, lax.rem(me + shift, count)), device_id_type=mesh_ids)
    neighbours = jnp.int32(0)
    for k in range(-reach, reach + 1):
        if k == 0:
            continue
        there = (tile + k >= 0) & (tile + k < tiles)
        neighbours = neighbours + there.astype(jnp.int32)

        @pl.when(there)
        def _():
            pl.semaphore_signal(barrier, inc=1, device_id=(tile + k, me), device_id_type=mesh_ids)

    pl.semaphore_wait(barrier, count - 1 + neighbours)


def exchange_inputs(spec_ref, lag_ref, slow_ref, spec_in, lag_in, slow_in, local_sem, send_sem, recv_sem, then, reach):
    count = spec_in.shape[0]
    me = lax.axis_index("sta")
    tile = lax.axis_index("grid")
    mesh_ids = pl.DeviceIdType.MESH
    enter_barrier(count, reach)
    pairs = ((spec_ref, spec_in), (lag_ref, lag_in), (slow_ref, slow_in))
    local = []
    for kind, (source, target) in enumerate(pairs):
        own = source.at[me] if kind == 0 else source
        copy = pltpu.make_async_copy(own, target.at[me], local_sem.at[kind])
        copy.start()
        local.append(copy)
    sends = []
    for shift in range(1, count):
        peer = lax.rem(me + shift, count)
        for kind, (source, target) in enumerate(pairs):
            part = source.at[peer] if kind == 0 else source
            copy = pltpu.make_async_remote_copy(
                src_ref=part,
                dst_ref=target.at[me],
                send_sem=send_sem.at[kind, shift],
                recv_sem=recv_sem.at[kind, me],
                device_id=(tile, peer),
                device_id_type=mesh_ids,
            )
            copy.start()
            sends.append(copy)
    then()
    for copy in local:
        copy.wait()
    for copy in sends:
        copy.wait_send()
    for shift in range(1, count):
        source_id = lax.rem(me + count - shift, count)
        for kind, (source, target) in enumerate(pairs):
            part = source.at[source_id] if kind == 0 else source
            pltpu.make_async_remote_copy(
                src_ref=part,
                dst_ref=target.at[source_id],
                send_sem=send_sem.at[kind, shift],
                recv_sem=recv_sem.at[kind, source_id],
                device_id=(tile, source_id),
                device_id_type=mesh_ids,
            ).wait_recv()


def align_block(spec, lag, slow, source, real_ref, imag_ref, turn_ref):
    bins, block = spec.shape[0], spec.shape[2]
    first_bin = lax.axis_index("sta") * bins
    bin_rows = (F0 + first_bin + lax.broadcasted_iota(jnp.int32, (bins, block), 0)).astype(jnp.float32)
    cols = pl.ds(pl.multiple_of(source * block, 128), block)
    product = bin_rows * lag.astype(jnp.float32)
    whole = jnp.floor(product * (1.0 / NT))
    left = product - whole * NT
    left = jnp.where(left < 0.0, left + NT, left)
    left = jnp.where(left >= NT, left - NT, left)
    turned = left * (TWO_PI / NT)
    cosine = jnp.cos(turned)
    sine = jnp.sin(turned)
    real_in = spec[:, 0, :].astype(jnp.float32)
    imag_in = spec[:, 1, :].astype(jnp.float32)
    real_ref[:, cols] = (real_in * cosine + imag_in * sine).astype(jnp.bfloat16).astype(jnp.float32)
    imag_ref[:, cols] = (imag_in * cosine - real_in * sine).astype(jnp.bfloat16).astype(jnp.float32)
    turn_ref[:, cols] = slow.astype(jnp.float32)


def complex_times(left, right):
    return left[0] * right[0] - left[1] * right[1], left[0] * right[1] + left[1] * right[0]


def factor_rows(turn_x, turn_y, turn_z, rows8, rows16):
    return (
        exp_neg(turn_x * (rows8 - 3.5)),
        exp_neg(turn_x * (8.0 * (rows8 - 1.5))),
        exp_neg(turn_y * (rows8 - 3.5)),
        exp_neg(turn_z * (rows16 - 7.5)),
        exp_neg(turn_z * (16.0 * (rows8 - 3.5))),
    )


def beam_kernel(spec_ref, lag_ref, slow_ref, out_ref, spec_in, lag_in, slow_in, local_sem, send_sem, recv_sem,
                real_ref, imag_ref, turn_ref, acc_ref, left_ref, right_ref, power_ref, pieces, send_rs, recv_rs,
                send_ag, recv_ag, share_sem):
    count, bins, block = spec_in.shape[0], spec_in.shape[1], spec_in.shape[3]
    me = lax.axis_index("sta")
    first_bin = me * bins
    width = CHUNK
    per_block = block // width
    half_z = CZ // 2
    rows8 = lax.broadcasted_iota(jnp.int32, (8, width), 0).astype(jnp.float32)
    rows16 = lax.broadcasted_iota(jnp.int32, (16, width), 0).astype(jnp.float32)
    omega0 = (F0 + first_bin).astype(jnp.float32) * (TWO_PI / NT)
    step = TWO_PI / NT

    def per_chunk(k, carry, first=False):
        source = lax.rem(me + k // per_block, count)
        cols = pl.ds(pl.multiple_of(source * block + lax.rem(k, per_block) * width, 128), width)
        slow_x = turn_ref[0:1, cols]
        slow_y = turn_ref[1:2, cols]
        slow_z = turn_ref[2:3, cols]
        start = factor_rows(omega0 * slow_x, omega0 * slow_y, omega0 * slow_z, rows8, rows16)
        ratio = factor_rows(step * slow_x, step * slow_y, step * slow_z, rows8, rows16)

        def per_bin(f, state):
            (a_r, a_i), (b_r, b_i), (y_r, y_i), (c_r, c_i), (d_r, d_i) = state
            real_in = real_ref[pl.ds(f, 1), cols]
            imag_in = imag_ref[pl.ds(f, 1), cols]
            q_r = real_in * y_r - imag_in * y_i
            q_i = real_in * y_i + imag_in * y_r
            near = [complex_times((b_r[m : m + 1], b_i[m : m + 1]), (a_r, a_i)) for m in range(CX // 16)]
            cells = CX * CY
            for y in range(CY):
                qq_r, qq_i = q_r[y : y + 1], q_i[y : y + 1]
                lo_r, lo_i, hi_r, hi_i = [], [], [], []
                for x_r, x_i in near:
                    t1, t2 = qq_r * x_r, qq_i * x_i
                    t3, t4 = qq_r * x_i, qq_i * x_r
                    lo_r.append(t1 - t2)
                    lo_i.append(t3 + t4)
                    hi_r.append(t1 + t2)
                    hi_i.append(t4 - t3)
                row = y * CX
                half = CX // 2
                left_ref[row : row + half, :] = jnp.concatenate(lo_r, axis=0).astype(jnp.bfloat16)
                left_ref[row + half : row + CX, :] = jnp.concatenate(hi_r, axis=0).astype(jnp.bfloat16)
                left_ref[cells + row : cells + row + half, :] = jnp.concatenate(lo_i, axis=0).astype(jnp.bfloat16)
                left_ref[cells + row + half : cells + row + CX, :] = jnp.concatenate(hi_i, axis=0).astype(jnp.bfloat16)
            for m in range(half_z // 16):
                z_r, z_i = complex_times((d_r[m : m + 1], d_i[m : m + 1]), (c_r, c_i))
                row = 16 * m
                right_ref[row : row + 16, :] = z_r.astype(jnp.bfloat16)
                right_ref[half_z + row : half_z + row + 16, :] = z_i.astype(jnp.bfloat16)
            product = lax.dot_general(
                left_ref[...], right_ref[...], (((1,), (1,)), ((), ())), preferred_element_type=jnp.float32
            )
            if first:
                acc_ref[f] = product
            else:
                acc_ref[f] += product
            return tuple(complex_times(now, turn) for now, turn in zip(state, ratio))

        lax.fori_loop(0, bins, per_bin, start, unroll=8)
        return carry

    def own_block():
        align_block(spec_ref.at[me], lag_ref[...], slow_ref[...], me, real_ref, imag_ref, turn_ref)
        per_chunk(0, 0, first=True)
        lax.fori_loop(1, per_block, per_chunk, 0)

    exchange_inputs(
        spec_ref, lag_ref, slow_ref, spec_in, lag_in, slow_in, local_sem, send_sem, recv_sem, own_block, out_ref.shape[0] // 2
    )

    def align_other(shift, carry):
        source = lax.rem(me + shift, count)
        align_block(spec_in.at[source], lag_in[source], slow_in[source], source, real_ref, imag_ref, turn_ref)
        return carry

    lax.fori_loop(1, count, align_other, 0)
    lax.fori_loop(per_block, count * per_block, per_chunk, 0)
    cells = CX * CY
    low = jnp.zeros((cells, half_z), jnp.float32)
    high = jnp.zeros((cells, half_z), jnp.float32)
    for f in range(bins):
        sums = acc_ref[f]
        u, w = sums[:cells, :half_z], sums[:cells, half_z:]
        x, v = sums[cells:, :half_z], sums[cells:, half_z:]
        low = low + ((u - v) * (u - v) + (w + x) * (w + x))
        high = high + ((u + v) * (u + v) + (x - w) * (x - w))
    power_ref[:, :half_z] = low
    power_ref[:, half_z:] = high
    share_kernel(power_ref, out_ref, pieces, send_rs, recv_rs, send_ag, recv_ag, share_sem)


def beam_power(spec_send, lag_row, slow_rows, reach):
    count = spec_send.shape[0]
    slots = 2 * reach + 1
    cells = CX * CY
    bins, block = spec_send.shape[1], spec_send.shape[3]
    width = CHUNK
    stations = count * block
    vmem = pl.BlockSpec(memory_space=pltpu.VMEM)
    return pl.pallas_call(
        beam_kernel,
        out_shape=jax.ShapeDtypeStruct((slots, cells, CZ), jnp.float32),
        in_specs=[vmem, vmem, vmem],
        out_specs=vmem,
        scratch_shapes=[
            pltpu.VMEM((count,) + spec_send.shape[1:], jnp.bfloat16),
            pltpu.VMEM((count,) + lag_row.shape, jnp.int32),
            pltpu.VMEM((count,) + slow_rows.shape, jnp.bfloat16),
            pltpu.SemaphoreType.DMA((3,)),
            pltpu.SemaphoreType.DMA((3, count)),
            pltpu.SemaphoreType.DMA((3, count)),
            pltpu.VMEM((bins, stations), jnp.float32),
            pltpu.VMEM((bins, stations), jnp.float32),
            pltpu.VMEM((slow_rows.shape[0], stations), jnp.float32),
            pltpu.VMEM((bins, 2 * CX * CY, CZ), jnp.float32),
            pltpu.VMEM((2 * CX * CY, width), jnp.bfloat16),
            pltpu.VMEM((CZ, width), jnp.bfloat16),
            pltpu.VMEM((cells, CZ), jnp.float32),
            pltpu.VMEM((count, cells // count, CZ), jnp.float32),
            pltpu.SemaphoreType.DMA((count,)),
            pltpu.SemaphoreType.DMA((count,)),
            pltpu.SemaphoreType.DMA((slots, count)),
            pltpu.SemaphoreType.DMA((slots, count)),
            pltpu.SemaphoreType.DMA((1,)),
        ],
        compiler_params=pltpu.CompilerParams(collective_id=1, has_side_effects=True),
    )(spec_send, lag_row, slow_rows)


def share_kernel(part_ref, out_ref, pieces, send_rs, recv_rs, send_ag, recv_ag, local_sem):
    count = pieces.shape[0]
    slots = out_ref.shape[0]
    reach = slots // 2
    rows = pieces.shape[1]
    me = lax.axis_index("sta")
    tile = lax.axis_index("grid")
    tiles = lax.axis_size("grid")
    mesh_ids = pl.DeviceIdType.MESH
    own = pltpu.make_async_copy(part_ref.at[pl.ds(pl.multiple_of(me * rows, 8), rows)], pieces.at[me], local_sem.at[0])
    own.start()
    sends = []
    for shift in range(1, count):
        peer = lax.rem(me + shift, count)
        copy = pltpu.make_async_remote_copy(
            src_ref=part_ref.at[pl.ds(pl.multiple_of(peer * rows, 8), rows)],
            dst_ref=pieces.at[me],
            send_sem=send_rs.at[shift],
            recv_sem=recv_rs.at[me],
            device_id=(tile, peer),
            device_id_type=mesh_ids,
        )
        copy.start()
        sends.append(copy)
    own.wait()
    for copy in sends:
        copy.wait_send()
    for shift in range(1, count):
        source = lax.rem(me + count - shift, count)
        pltpu.make_async_remote_copy(
            src_ref=pieces.at[source],
            dst_ref=pieces.at[source],
            send_sem=send_rs.at[shift],
            recv_sem=recv_rs.at[source],
            device_id=(tile, source),
            device_id_type=mesh_ids,
        ).wait_recv()
    total = pieces[0]
    for source in range(1, count):
        total = total + pieces[source]
    mine = pl.ds(pl.multiple_of(me * rows, 8), rows)
    out_ref[reach, mine] = total
    block = out_ref.at[reach, mine]

    def gather_copy(k, peer, slot):
        return pltpu.make_async_remote_copy(
            src_ref=block,
            dst_ref=out_ref.at[slot, mine],
            send_sem=send_ag.at[slot, peer],
            recv_sem=recv_ag.at[slot, me],
            device_id=(tile + k, peer),
            device_id_type=mesh_ids,
        )

    peers = []
    for shift in range(1, count):
        copy = gather_copy(0, lax.rem(me + shift, count), reach)
        copy.start()
        peers.append(copy)
    for k in range(-reach, reach + 1):
        if k == 0:
            continue

        @pl.when(jnp.logical_not((tile + k >= 0) & (tile + k < tiles)))
        def _():
            out_ref[reach + k] = jnp.zeros(out_ref.shape[1:], out_ref.dtype)

    for copy in peers:
        copy.wait_send()
    for shift in range(1, count):
        source = lax.rem(me + count - shift, count)
        pltpu.make_async_remote_copy(
            src_ref=block,
            dst_ref=out_ref.at[reach, pl.ds(pl.multiple_of(source * rows, 8), rows)],
            send_sem=send_ag.at[reach, source],
            recv_sem=recv_ag.at[reach, source],
            device_id=(tile, source),
            device_id_type=mesh_ids,
        ).wait_recv()

    def halo_copy(k):
        return pltpu.make_async_remote_copy(
            src_ref=out_ref.at[reach],
            dst_ref=out_ref.at[reach - k],
            send_sem=send_ag.at[reach - k, me],
            recv_sem=recv_ag.at[reach - k, me],
            device_id=(tile + k, me),
            device_id_type=mesh_ids,
        )

    for k in range(-reach, reach + 1):
        if k == 0:
            continue

        @pl.when((tile + k >= 0) & (tile + k < tiles))
        def _():
            halo_copy(k).start()

    for k in range(-reach, reach + 1):
        if k == 0:
            continue

        @pl.when((tile + k >= 0) & (tile + k < tiles))
        def _():
            halo_copy(k).wait_send()
            pltpu.make_async_remote_copy(
                src_ref=out_ref.at[reach],
                dst_ref=out_ref.at[reach + k],
                send_sem=send_ag.at[reach + k, me],
                recv_sem=recv_ag.at[reach + k, me],
                device_id=(tile + k, me),
                device_id_type=mesh_ids,
            ).wait_recv()


def share_power(part, reach):
    count = lax.axis_size("sta")
    rows = part.shape[0] // count
    slots = 2 * reach + 1
    return pl.pallas_call(
        share_kernel,
        out_shape=jax.ShapeDtypeStruct((slots,) + part.shape, jnp.float32),
        in_specs=[pl.BlockSpec(memory_space=pltpu.VMEM)],
        out_specs=pl.BlockSpec(memory_space=pltpu.VMEM),
        scratch_shapes=[
            pltpu.VMEM((count, rows, part.shape[1]), jnp.float32),
            pltpu.SemaphoreType.DMA((count,)),
            pltpu.SemaphoreType.DMA((count,)),
            pltpu.SemaphoreType.DMA((slots, count)),
            pltpu.SemaphoreType.DMA((slots, count)),
            pltpu.SemaphoreType.DMA((1,)),
        ],
        compiler_params=pltpu.CompilerParams(collective_id=0, has_side_effects=True),
    )(part)


def freq_beams(freq_ids, aligned_rows, slow_rows):
    return lax.map(lambda pair: beam_freq(pair[0], pair[1], slow_rows), (freq_ids, aligned_rows))


def band_matrix(taps, length):
    rows = jnp.arange(length, dtype=jnp.int32)[:, None]
    columns = jnp.arange(length + 2 * HALF, dtype=jnp.int32)[None, :]
    offset = columns - rows
    picks = jnp.arange(TAPS, dtype=jnp.int32)[:, None, None]
    return jnp.sum(jnp.where(offset[None] == picks, taps[:, None, None], 0.0), axis=0)


def blur(volume, bands):
    band_x, square_y, square_z = bands
    padded = with_halo(volume.astype(jnp.bfloat16), (("grid", 0),), HALF).astype(volume.dtype)
    along_x = jnp.einsum("ip,pyz->iyz", band_x, padded, precision=lax.Precision.HIGHEST)
    along_y = jnp.einsum("jq,xqz->xjz", square_y, along_x, precision=lax.Precision.HIGHEST)
    return jnp.einsum("xyw,kw->xyk", along_y, square_z, precision=lax.Precision.HIGHEST)


def blur_narrowing(volume, taps, square_y, square_z):
    band_x = band_matrix(taps, volume.shape[0] - 2 * HALF)
    along_x = jnp.einsum("ip,pyz->iyz", band_x, volume, precision=lax.Precision.HIGHEST)
    along_y = jnp.einsum("jq,xqz->xjz", square_y, along_x, precision=lax.Precision.HIGHEST)
    return jnp.einsum("xyw,kw->xyk", along_y, square_z, precision=lax.Precision.HIGHEST)


def deblur(observed, halo_tiles, spread_taps):
    tiles = lax.axis_size("grid")
    me = lax.axis_index("grid")
    reach = ITERS * 2 * HALF
    cut = halo_tiles * CX - reach
    observed = observed[cut : observed.shape[0] - cut]
    width = observed.shape[0]
    cell = (me - halo_tiles) * CX + cut + jnp.arange(width, dtype=jnp.int32)
    inside = (cell >= 0) & (cell < tiles * CX)
    square_y = band_matrix(spread_taps[1], CY)[:, HALF : HALF + CY]
    square_z = band_matrix(spread_taps[2], CZ)[:, HALF : HALF + CZ]
    estimate = jnp.where(inside[:, None, None], observed, 0.0)
    for sweep in range(ITERS):
        low = 2 * HALF * sweep + HALF
        blurred = blur_narrowing(estimate, spread_taps[0], square_y, square_z)
        ratio = jnp.where(
            inside[low : width - low, None, None], observed[low : width - low] / blurred, 0.0
        )
        estimate = estimate[2 * HALF : estimate.shape[0] - 2 * HALF] * blur_narrowing(
            ratio, spread_taps[0], square_y, square_z
        )
    return estimate


def band_of(taps_ref, axis, rows, cols):
    offset = cols - rows + HALF
    band = jnp.zeros(offset.shape, jnp.float32)
    for tap in range(TAPS):
        band = jnp.where(offset == tap, taps_ref[axis, tap], band)
    return band


def mirror(index, length):
    return jnp.where(index < length // 2, index, 3 * (length // 2) - 1 - index)


def deblur_kernel(taps_ref, obs_ref, out_ref, kx_ref, kz_ref):
    tiles = lax.axis_size("grid")
    me = lax.axis_index("grid")
    planes, width, depth = obs_ref.shape
    shape_x = kx_ref.shape
    kx_ref[...] = band_of(
        taps_ref, 0, lax.broadcasted_iota(jnp.int32, shape_x, 0) + HALF, lax.broadcasted_iota(jnp.int32, shape_x, 1)
    )
    shape_z = kz_ref.shape
    kz_ref[...] = band_of(
        taps_ref,
        2,
        mirror(lax.broadcasted_iota(jnp.int32, shape_z, 1), depth),
        mirror(lax.broadcasted_iota(jnp.int32, shape_z, 0), depth),
    )
    halo_tiles = (width - CX) // (2 * CX)
    highest = lax.Precision.HIGH

    def inside(low, size):
        cell = (me - halo_tiles) * CX + low + lax.broadcasted_iota(jnp.int32, (size, depth), 0)
        return (cell >= 0) & (cell < tiles * CX)

    lanes = planes * depth

    def blur(volume):
        size_in = volume.shape[0]
        size_out = size_in - 2 * HALF
        band = kx_ref[0:size_out, 0:size_in]
        along_x = jnp.dot(band, volume, precision=highest, preferred_element_type=jnp.float32)
        along_y = []
        for y in range(planes):
            total = None
            for q in range(planes):
                term = taps_ref[1, q - y + HALF] * along_x[:, q * depth : (q + 1) * depth]
                total = term if total is None else total + term
            along_y.append(total)
        joined = jnp.concatenate(along_y, axis=0)
        along_z = jnp.dot(joined, kz_ref[...], precision=highest, preferred_element_type=jnp.float32)
        return jnp.concatenate([along_z[y * size_out : (y + 1) * size_out] for y in range(planes)], axis=1)

    def inside_wide(low, size):
        cell = (me - halo_tiles) * CX + low + lax.broadcasted_iota(jnp.int32, (size, lanes), 0)
        return (cell >= 0) & (cell < tiles * CX)

    observed = jnp.concatenate([obs_ref[y] for y in range(planes)], axis=1)
    estimate = jnp.where(inside_wide(0, width), observed, 0.0)
    for sweep in range(ITERS):
        low = 2 * HALF * sweep + HALF
        blurred = blur(estimate)
        size = blurred.shape[0]
        ratio = jnp.where(inside_wide(low, size), observed[low : low + size] / blurred, 0.0)
        spread = blur(ratio)
        estimate = estimate[2 * HALF : 2 * HALF + spread.shape[0]] * spread
    for y in range(planes):
        out_ref[y] = estimate[:, y * depth : (y + 1) * depth]


def deblur_tile(observed, spread_taps):
    planes, width, depth = observed.shape
    vmem = pl.BlockSpec(memory_space=pltpu.VMEM)
    return pl.pallas_call(
        deblur_kernel,
        out_shape=jax.ShapeDtypeStruct((planes, CX, depth), jnp.float32),
        in_specs=[pl.BlockSpec(memory_space=pltpu.SMEM), vmem],
        out_specs=vmem,
        scratch_shapes=[
            pltpu.VMEM((width - 2 * HALF, width), jnp.float32),
            pltpu.VMEM((depth, depth), jnp.float32),
        ],
    )(spread_taps, observed)


def per_device(spectra, lag_samples, slowness, spread_taps):
    groups = lax.axis_size("sta")
    own_count = FREQS // groups
    first_bin = lax.axis_index("sta") * own_count
    block = spectra.shape[2]
    spec_send = spectra.reshape(groups, own_count, 2, block)
    halo_tiles = -(-(ITERS * 2 * HALF) // CX)
    summed = beam_power(spec_send, lag_samples, slowness[0], halo_tiles)
    observed = summed / (FREQS * STATIONS) + BACKGROUND
    slots = observed.shape[0]
    observed = observed.reshape(slots, CY, CX, CZ)
    observed = jnp.concatenate([observed[:, :, : CX // 2], observed[:, :, CX // 2 :][:, :, ::-1]], axis=2)
    planes = observed.transpose(1, 0, 2, 3).reshape(CY, slots * CX, CZ)
    estimate = deblur_tile(planes, spread_taps)
    both = jnp.stack([observed[halo_tiles], estimate])
    both = jnp.concatenate([both[..., : CZ // 2], both[..., CZ // 2 :][..., ::-1]], axis=-1).transpose(0, 2, 1, 3)
    stacked, estimate = both[0], both[1]
    return (stacked[None], estimate[None])


def solution(mesh):
    placed = (P(None, None, "sta"), P("grid", "sta"), P("grid", None, "sta"), P())
    return jax.shard_map(
        per_device,
        mesh=mesh,
        in_specs=placed,
        out_specs=(P("grid", None, None, None), P("grid", None, None, None)),
        check_vma=False,
    )
```
